32 devices in a mesh: blk: 8 (over y, x, core), head: 4 (over z).
Axes of the slice: x: 2, y: 2, z: 4, core: 2. Of those that a mesh axis runs over, the one named last changes fastest.
Arguments:
- tokens: bfloat16 [2, 8192, 768], P(None, ('blk', 'head')), may hold values from -6 to 6
- seq_lengths: int32 [2, 8], replicated, may hold values from 1 to 4096, 8192 in all within a row
- cluster_perm: int32 [2, 8192], replicated, may hold values from 0 to 8191, as said below
- out_grad: bfloat16 [2, 8192, 768], P(None, ('blk', 'head')), may hold values from -6 to 6
- qkv_weight: bfloat16 [768, 2304], P('blk', 'head'), may hold values from -0.3125 to 0.3125
- query_bias: bfloat16 [768], P('blk'), may hold values from -1.75 to 1.75
- value_bias: bfloat16 [768], P('blk'), may hold values from -1.75 to 1.75
- out_weight: bfloat16 [768, 768], P('blk', 'head'), may hold values from -0.875 to 0.875
- out_bias: bfloat16 [768], P('blk'), may hold values from -1.75 to 1.75
- attn_gain: bfloat16 [768], P('blk'), may hold values from 0.5 to 1.5
- attn_shift: bfloat16 [768], P('blk'), may hold values from -1.75 to 1.75
- up_weight: bfloat16 [768, 3072], P('blk', 'head'), may hold values from -0.21875 to 0.21875
- up_bias: bfloat16 [3072], P('blk'), may hold values from -1.75 to 1.75
- down_weight: bfloat16 [3072, 768], P('blk', 'head'), may hold values from -0.15625 to 0.15625
- down_bias: bfloat16 [768], P('blk'), may hold values from -1.75 to 1.75
- ffn_gain: bfloat16 [768], P('blk'), may hold values from 0.5 to 1.5
- ffn_shift: bfloat16 [768], P('blk'), may hold values from -1.75 to 1.75
Outputs:
- layer_out: bfloat16 [2, 8192, 768], P(None, ('blk', 'head'))
- tokens_grad: float32 [2, 8192, 768], P(None, ('blk', 'head'))
- qkv_weight_grad: float32 [768, 2304], P('blk', 'head')
- query_bias_grad: float32 [768], P('blk')
- value_bias_grad: float32 [768], P('blk')
- out_weight_grad: float32 [768, 768], P('blk', 'head')
- out_bias_grad: float32 [768], P('blk')
- attn_gain_grad: float32 [768], P('blk')
- attn_shift_grad: float32 [768], P('blk')
- up_weight_grad: float32 [768, 3072], P('blk', 'head')
- up_bias_grad: float32 [3072], P('blk')
- down_weight_grad: float32 [3072, 768], P('blk', 'head')
- down_bias_grad: float32 [768], P('blk')
- ffn_gain_grad: float32 [768], P('blk')
- ffn_shift_grad: float32 [768], P('blk')
The draws below stay inside these ranges and needn't reach their ends.
Inputs may be any that keep to these rules, and one draw needn't show every extreme that they name: `seq_lengths`: row m holds the lengths of the 8 sequences of micro-batch m, laid end to end; each row sums to 8192 and its longest sequence has exactly 4096 positions. Each row is a permutation of the slots; position t of micro-batch m lies in cluster cluster_perm[m, t] // 128, so every cluster holds 128 positions. The slots deal positions evenly: for every b and c in 0 .. 7, exactly 128 positions t with t // 1024 == b have cluster_perm[m, t] // 1024 == c.
All inputs are finite; a program needn't handle non-finite values.
Results may differ from the reference program's by a relative error of at most 0.017.
Values may be sent and summed in bfloat16 or wider, within the bound.
A program may use at most 192 MiB of HBM per device.

```python
import math
import jax
import jax.numpy as jnp
import numpy as np
from jax import lax

D = 768
HEADS = 12
HEAD_DIM = 64
FF = 3072
TOK_DEV = 256
MICRO = 2
SEQS = 8
CLUSTER = 128
TOKENS = 8192
SEQ_MAX = 4096
N_BLK = 8
N_HEAD = 4


def draw_cluster_perm(key, part):
    group = TOK_DEV * N_HEAD
    per_pair = group // N_BLK

    def one_row(row_key):
        deal_key, place_key = jax.random.split(row_key)
        codes = jax.vmap(lambda inner: jax.random.permutation(inner, group))(jax.random.split(deal_key, N_BLK))
        places = jax.vmap(lambda inner: jax.random.permutation(inner, group))(jax.random.split(place_key, N_BLK))
        target = codes // per_pair
        within = codes % per_pair
        source = jnp.arange(N_BLK, dtype=jnp.int32)[:, None]
        inner_slot = places[target, source * per_pair + within]
        return (target * group + inner_slot).reshape(-1).astype(jnp.int32)
    return jax.vmap(one_row)(jax.random.split(key, MICRO))


def with_spikes(array, key, source, target, parts, factor):
    owner, partner = [(jnp.arange(array.shape[position]) // (array.shape[position] // parts)).reshape([-1 if axis == position else 1 for axis in range(array.ndim)]) for position in (source, target)]
    chosen = jax.random.permutation(key, parts)[partner]
    strong = (owner == chosen) | (owner == (partner + parts // 2) % parts)
    return jnp.where(strong, factor * array, array)


def levels(stream_key, shape, cuts, smallest, largest):
    def one(axis_at, shards_of):
        steps = jax.random.uniform(jax.random.fold_in(jax.random.fold_in(stream_key, 6), axis_at), (shards_of,), jnp.float32, smallest / len(cuts), largest / len(cuts))
        return jnp.repeat(jnp.exp(steps), shape[axis_at] // shards_of).reshape((-1,) + (1,) * (len(shape) - axis_at - 1))

    factor_of = one(*cuts[0])
    for cut in cuts[1:]:
        factor_of = factor_of * one(*cut)
    return factor_of


def profile(amount, total, most, skew):
    loads = [(1 << 20) // math.isqrt(rank ** skew) + 1 for rank in range(2, amount + 1)]
    surplus, counts = total - most - (amount - 1), [1] * (amount - 1)
    while surplus > 0:
        candidates = [i for i in range(amount - 1) if counts[i] < most]
        whole, left = sum([loads[i] for i in candidates]), surplus
        for i in candidates:
            extra = min(most - counts[i], max(1, left * loads[i] // whole), surplus)
            counts[i] = counts[i] + extra
            surplus = surplus - extra
    return np.array([most] + counts)


def uneven(own_key, number_of, total, reach, lean):
    if number_of == 2:
        one = jax.random.randint(own_key, (), max(1, total - reach), min(reach, total - 1) + 1)
        return jnp.stack([one, total - one])
    lengths = jnp.asarray(profile(number_of, total, reach, lean), jnp.int32)
    twos = (number_of - 1) // 2
    source_of, taker = lengths[1:1 + 2 * twos:2], lengths[2:2 + 2 * twos:2]
    slack = jnp.minimum(source_of - 1, reach - taker)
    shifted = jax.random.randint(jax.random.fold_in(own_key, 1), (twos,), 0, 1 << 20) % (slack + 1)
    lengths = lengths.at[1:1 + 2 * twos:2].set(source_of - shifted).at[2:2 + 2 * twos:2].set(taker + shifted)
    return lengths[jax.random.permutation(jax.random.fold_in(own_key, 2), number_of)]


def scatter_about(rng, shape, scale, bound, pieces=(), kind=jnp.bfloat16):
    level = levels(rng, shape, pieces, -0.22, 0.18) if pieces else 1.0
    values = jax.random.normal(rng, shape, jnp.float32) * scale * level
    return jnp.minimum(jnp.maximum(values, -bound), bound).astype(kind)


def noise_with(stream_key, extent, width, bound, cuts, heavy, kind=jnp.bfloat16):
    values = width * jax.random.normal(stream_key, extent, jnp.float32)
    if cuts:
        values = values * levels(stream_key, extent, cuts, -0.22, 0.18)
    return jnp.clip(with_spikes(values, jax.random.fold_in(stream_key, 3), *heavy), -bound, bound).astype(kind)


def setup_inputs(seed: int = 0) -> dict:
    splits = jax.random.split(jax.random.key(seed), 18)
    return {
        "tokens": noise_with(splits[0], (MICRO, TOKENS, D), 1.0, 6.0, ((1, 32),), (1, 2, 32, 2.75)),
        "seq_lengths": jax.vmap(lambda own: uneven(own, SEQS, TOKENS, SEQ_MAX, 2))(jax.random.split(splits[1], MICRO)).reshape((MICRO, SEQS)).astype(jnp.int32),
        "cluster_perm": draw_cluster_perm(jax.random.fold_in(splits[17], 71), 0),
        "out_grad": noise_with(splits[3], (MICRO, TOKENS, D), 1.0, 6.0, ((1, 32),), (1, 2, 32, 2.75)),
        "qkv_weight": scatter_about(splits[4], (D, 3 * D), (D // 2) ** -0.5, 0.3125, ((0, 8), (1, 4))),
        "query_bias": scatter_about(splits[5], (D,), 0.3, 1.75, ((0, 8),)),
        "value_bias": scatter_about(splits[6], (D,), 0.3, 1.75, ((0, 8),)),
        "out_weight": scatter_about(splits[7], (D, D), (D // 16) ** -0.5, 0.875, ((0, 8), (1, 4))),
        "out_bias": scatter_about(splits[8], (D,), 0.3, 1.75, ((0, 8),)),
        "attn_gain": jnp.clip(1.0 + 0.1 * jax.random.normal(splits[9], (D,), jnp.float32), 0.5, 1.5).astype(jnp.bfloat16),
        "attn_shift": scatter_about(splits[10], (D,), 0.3, 1.75, ((0, 8),)),
        "up_weight": scatter_about(splits[11], (D, FF), D ** -0.5, 0.21875, ((0, 8), (1, 4))),
        "up_bias": scatter_about(splits[12], (FF,), 0.3, 1.75, ((0, 8),)),
        "down_weight": scatter_about(splits[13], (FF, D), (FF // 2) ** -0.5, 0.15625, ((0, 8), (1, 4))),
        "down_bias": scatter_about(splits[14], (D,), 0.3, 1.75, ((0, 8),)),
        "ffn_gain": jnp.clip(1.0 + 0.1 * jax.random.normal(splits[15], (D,), jnp.float32), 0.5, 1.5).astype(jnp.bfloat16),
        "ffn_shift": scatter_about(splits[16], (D,), 0.3, 1.75, ((0, 8),)),
    }


masked_score = -1e+30
norm_epsilon = 1e-05
highest = lax.Precision.HIGHEST

@jax.custom_vjp
def low(v):
    return lax.optimization_barrier(v.astype(jnp.bfloat16)).astype(jnp.float32)

@jax.custom_vjp
def low_back(v):
    return v

def low_keep(v):
    return (low(v), None)

def low_pass(kept, grad):
    return (grad,)

def back_keep(v):
    return (v, None)

def back_low(kept, grad):
    return (low(grad),)
low.defvjp(low_keep, low_pass)
low_back.defvjp(back_keep, back_low)

def layer_norm(hidden, norm_gain, norm_shift):
    center = hidden - lax.optimization_barrier(jnp.mean(hidden, axis=-1, keepdims=True))
    spread = lax.optimization_barrier(jnp.mean(center * center, axis=-1, keepdims=True))
    return center * lax.rsqrt(spread + norm_epsilon) * norm_gain + norm_shift

def segment_of(positions, seq_ends):
    return lax.optimization_barrier(jnp.sum((positions[:, None] >= seq_ends[None, :]).astype(jnp.int32), axis=1))

def product(left, right):
    return jnp.dot(left, right, precision=highest, preferred_element_type=jnp.float32)

def cluster_block(members):
    block_q, block_k, block_v, block_segs = members
    scores = jnp.einsum('cqhd,ckhd->chqk', block_q, block_k, precision=highest) * 0.125
    scores = low_back(scores)
    allowed = block_segs[:, :, None] == block_segs[:, None, :]
    scores = jnp.where(allowed[:, None], scores, masked_score)
    probs = jax.nn.softmax(scores, axis=-1)
    return jnp.einsum('chqk,ckhd->cqhd', low(probs), block_v, precision=highest)

def attend(queries, keys, values, segments, perm_row):
    order = jnp.argsort(perm_row).astype(jnp.int32)
    count = TOKENS // CLUSTER
    per_block = math.gcd(count, 32)
    cluster_shape = (count // per_block, per_block, CLUSTER, HEADS, HEAD_DIM)
    grouped_q = queries[order].reshape(cluster_shape)
    grouped_k = keys[order].reshape(cluster_shape)
    grouped_v = values[order].reshape(cluster_shape)
    grouped_segs = segments[order].reshape(count // per_block, per_block, CLUSTER)
    context = lax.map(jax.checkpoint(cluster_block), (grouped_q, grouped_k, grouped_v, grouped_segs))
    return context.reshape(TOKENS, HEADS * HEAD_DIM)[perm_row]

def layer(inputs, params, segments, perm_row):
    qkv_mat, query_add, value_add, out_mat, out_add, attn_scale, attn_move, up_mat, up_add, down_mat, down_add, ffn_scale, ffn_move = params
    proj = product(inputs, qkv_mat)
    queries = low_back(low(proj[:, 0:D] + query_add))
    keys = low_back(low(proj[:, D:2 * D]))
    values = low_back(low(proj[:, 2 * D:3 * D] + value_add))
    context = low_back(low(attend(queries, keys, values, segments, perm_row)))
    attn_res = inputs + low_back(product(context, out_mat) + out_add)

    def ffn_block(rows):
        normed = layer_norm(rows, attn_scale, attn_move)
        pre_act = low_back(product(low(normed), up_mat) + up_add)
        active = low(jax.nn.gelu(pre_act, approximate=False))
        ffn_res = normed + low_back(product(active, down_mat) + down_add)
        return layer_norm(ffn_res, ffn_scale, ffn_move)
    block_rows = math.gcd(TOKENS, 4096)
    result = lax.map(jax.checkpoint(ffn_block), attn_res.reshape(TOKENS // block_rows, block_rows, D))
    return result.reshape(TOKENS, D)

def reference(tokens, seq_lengths, cluster_perm, out_grad, qkv_weight, query_bias, value_bias, out_weight, out_bias, attn_gain, attn_shift, up_weight, up_bias, down_weight, down_bias, ffn_gain, ffn_shift):
    params = tuple((member.astype(jnp.float32) for member in (qkv_weight, query_bias, value_bias, out_weight, out_bias, attn_gain, attn_shift, up_weight, up_bias, down_weight, down_bias, ffn_gain, ffn_shift)))
    inputs = tokens.astype(jnp.float32)
    positions = jnp.arange(TOKENS, dtype=jnp.int32)
    segment_rows = [segment_of(positions, jnp.cumsum(seq_lengths[micro]).astype(jnp.int32)) for micro in range(MICRO)]

    def forward(inputs, *params):
        rows = [layer(inputs[micro], params, segment_rows[micro], cluster_perm[micro]) for micro in range(MICRO)]
        return jnp.stack(rows)
    outputs, pullback = jax.vjp(forward, inputs, *params)
    grads = pullback(out_grad.astype(jnp.float32))
    return (outputs.astype(jnp.bfloat16), grads[0], grads[1], grads[2], grads[3], grads[4], grads[5], grads[6], grads[7], grads[8], grads[9], grads[10], grads[11], grads[12], grads[13])
```

```python
import functools

import jax
import jax.numpy as jnp
from jax import lax
from jax.experimental import pallas as pl
from jax.experimental.pallas import tpu as pltpu
from jax.sharding import PartitionSpec as P

HEAD_DIM = 64
CLUSTER = 128
MESH = pl.DeviceIdType.MESH
BF16 = jnp.bfloat16
F32 = jnp.float32

masked_score = -1e30
norm_epsilon = 1e-05


def bits_of(index, count):
    return [(index // (1 << i)) % 2 for i in range(count)]


def flip(index, mask, bits):
    for i, bit in enumerate(bits):
        if mask & (1 << i):
            index = index + (1 - 2 * bit) * (1 << i)
    return index


def submasks(dims):
    masks = [0]
    for dim in dims:
        masks = masks + [mask | (1 << dim) for mask in masks]
    return masks


def choose(index, values):
    result = values[-1]
    for position in range(len(values) - 2, -1, -1):
        result = jnp.where(index == position, values[position], result)
    return result


class Sends:
    def __init__(self):
        self.pending = []

    def start(self, make, when=None):
        if when is None:
            make().start()
        else:

            @pl.when(when)
            def _():
                make().start()

        self.pending.append((make, when))

    def finish(self):
        for make, when in self.pending:
            if when is None:
                make().wait_send()
            else:

                @pl.when(when)
                def _(make=make):
                    make().wait_send()


def remote(src, dst, send_sem, recv_sem, device):
    return pltpu.make_async_remote_copy(
        src_ref=src,
        dst_ref=dst,
        send_sem=send_sem,
        recv_sem=recv_sem,
        device_id=device,
        device_id_type=MESH,
    )


def enter(blk, head, blks, heads):
    barrier = pltpu.get_barrier_semaphore()
    for other in range(blks):

        @pl.when(other != blk)
        def _():
            pl.semaphore_signal(barrier, inc=1, device_id=(other, head), device_id_type=MESH)

    for other in range(heads):

        @pl.when(other != head)
        def _():
            pl.semaphore_signal(barrier, inc=1, device_id=(blk, other), device_id_type=MESH)

    pl.semaphore_wait(barrier, blks + heads - 2)


def iota(shape, dim):
    return lax.broadcasted_iota(jnp.int32, shape, dim)


def permute_rows(one_hot_tile, source, target, rows):
    @pl.loop(0, rows // CLUSTER)
    def _(tile):
        start = pl.multiple_of(tile * CLUSTER, CLUSTER)
        chosen = jnp.dot(one_hot_tile(start), source[...], preferred_element_type=F32)
        target[pl.ds(start, CLUSTER), :] = chosen.astype(BF16)


def one_hot_from_row(row_ref):
    def tile(start):
        row = row_ref[0:1, :]
        count = row.shape[1]
        return jnp.where(iota((CLUSTER, count), 0) + start == row, 1.0, 0.0).astype(BF16)

    return tile


def one_hot_from_column(column_ref, count):
    def tile(start):
        column = column_ref[pl.ds(start, CLUSTER), 0:1]
        return jnp.where(iota((CLUSTER, count), 1) == column, 1.0, 0.0).astype(BF16)

    return tile


class RowExchange:
    def __init__(self, sends, blk, head, blks, heads, sems, tensor):
        self.sends, self.blk, self.head, self.blks, self.heads = sends, blk, head, blks, heads
        self.head_send, self.head_recv, self.blk_send, self.blk_recv, self.local = sems
        self.tensor = tensor

    def over_head(self, step, source, target):
        for other in range(self.heads):
            make = lambda other=other: remote(
                source(other),
                target(self.head),
                self.head_send.at[self.tensor, step, other],
                self.head_recv.at[self.tensor, step, self.head],
                (self.blk, other),
            )
            self.sends.start(make, when=other != self.head)

            @pl.when(other == self.head)
            def _():
                pltpu.make_async_copy(
                    source(other), target(other), self.local.at[self.tensor, step]
                ).start()

    def wait_head(self, step, target):
        for other in range(self.heads):

            @pl.when(other != self.head)
            def _():
                remote(
                    target(other),
                    target(other),
                    self.head_send.at[self.tensor, step, other],
                    self.head_recv.at[self.tensor, step, other],
                    (self.blk, other),
                ).wait_recv()

        pltpu.make_async_copy(
            target(self.head), target(self.head), self.local.at[self.tensor, step]
        ).wait()

    def over_blk(self, source, target):
        for other in range(self.blks):
            make = lambda other=other: remote(
                source(other),
                target(self.blk),
                self.blk_send.at[self.tensor, other],
                self.blk_recv.at[self.tensor, self.blk],
                (other, self.head),
            )
            self.sends.start(make, when=other != self.blk)

            @pl.when(other == self.blk)
            def _():
                pltpu.make_async_copy(
                    source(other), target(other), self.local.at[self.tensor, 2]
                ).start()

    def wait_blk(self, target):
        for other in range(self.blks):

            @pl.when(other != self.blk)
            def _():
                remote(
                    target(other),
                    target(other),
                    self.blk_send.at[self.tensor, other],
                    self.blk_recv.at[self.tensor, other],
                    (other, self.head),
                ).wait_recv()

        pltpu.make_async_copy(
            target(self.blk), target(self.blk), self.local.at[self.tensor, 2]
        ).wait()


def exchange_sems(blks, heads):
    dma = pltpu.SemaphoreType.DMA
    return [dma((2, 2, heads)), dma((2, 2, heads)), dma((2, blks)), dma((2, blks)), dma((2, 3))]


def cumulative(ones_ref, sums_ref, count):
    upper = jnp.where(iota((128, 128), 0) <= iota((128, 128), 1), 1.0, 0.0).astype(BF16)
    carry = jnp.zeros((ones_ref.shape[0], 1), F32)
    for tile in range(count // 128):
        part = ones_ref[:, tile * 128 : (tile + 1) * 128].astype(BF16)
        sums = jnp.dot(part, upper, preferred_element_type=F32) + carry
        sums_ref[:, tile * 128 : (tile + 1) * 128] = sums
        carry = sums[:, 127:128]


def gather_kernel(
    blks,
    heads,
    tokens,
    out_grad,
    shard,
    vectors,
    perm,
    full,
    full_vectors,
    slots_x,
    slots_g,
    dest_col,
    slot_col,
    arrived,
    sorted_rows,
    landed,
    ordered,
    dest_row,
    slot_row,
    ones,
    sums,
    rank_rows,
    head_send,
    head_recv,
    blk_send,
    blk_recv,
    local,
    z_send,
    z_recv,
    tree_send,
    tree_recv,
    vec_send,
    vec_recv,
    own_sem,
):
    blk, head = lax.axis_index("blk"), lax.axis_index("head")
    micros, rows, width = tokens.shape
    splits = heads // micros
    part = width // splits
    group = rows * heads
    pair = group // blks
    levels = blks.bit_length() - 1
    bits = bits_of(blk, levels)
    half = shard.shape[1] // 2
    sends = Sends()
    sems = (head_send, head_recv, blk_send, blk_recv, local)

    enter(blk, head, blks, heads)

    exchanges = [RowExchange(sends, blk, head, blks, heads, sems, i) for i in range(2)]
    sources = (tokens, out_grad)

    def send_rows(i):
        exchanges[i].over_head(
            0,
            lambda other: sources[i].at[
                other // splits, :, (other % splits) * part : (other % splits + 1) * part
            ],
            lambda other: arrived.at[i, pl.ds(pl.multiple_of(other * rows, rows), rows), :],
        )

    send_rows(0)

    def vec_copy(other):
        return remote(
            vectors, full_vectors.at[blk], vec_send.at[other], vec_recv.at[blk], (other, head)
        )

    for other in range(blks):
        sends.start(lambda other=other: vec_copy(other), when=other != blk)
    own_vec = pltpu.make_async_copy(vectors, full_vectors.at[blk], own_sem.at[0])
    own_vec.start()

    orders = [list(range(1, levels)) + [0], list(range(2, levels)) + [1, 0]]
    arrival = [
        choose(
            head,
            [
                sorted([x for x in range(heads) if x != own], key=lambda x: (abs(x - own), x))[j - 1]
                for own in range(heads)
            ],
        )
        if j
        else head
        for j in range(heads)
    ]

    def halves(ref, which):
        return ref.at[:, which * half : (which + 1) * half]

    def tree_step(j, step):
        for which in range(2):
            dims = orders[which]
            if step:
                tree_wait(j, which, step - 1)
            other = flip(blk, 1 << dims[step], bits)
            for mask in submasks(dims[:step]):
                piece = flip(blk, mask, bits)
                target = halves(full.at[arrival[j], piece], which)
                source = halves(shard, which) if j == 0 and mask == 0 else target
                slot = (1 << step) - 1 + submasks(dims[:step]).index(mask)
                make = lambda source=source, target=target, piece=piece, other=other, slot=slot, which=which: remote(
                    source,
                    target,
                    tree_send.at[j, which, slot],
                    tree_recv.at[j, which, piece],
                    (other, head),
                )
                sends.start(make)

    def tree_wait(j, which, step):
        dims = orders[which]
        other = flip(blk, 1 << dims[step], bits)
        for mask in submasks(dims[:step]):
            piece = flip(blk, mask | (1 << dims[step]), bits)
            target = halves(full.at[arrival[j], piece], which)
            remote(
                target,
                target,
                tree_send.at[j, which, 0],
                tree_recv.at[j, which, piece],
                (other, head),
            ).wait_recv()

    def chain(j):
        if j == 0:
            source = shard
            left, right = head > 0, head < heads - 1
        else:
            source = full.at[arrival[j], blk]
            left = (arrival[j] > head) & (head > 0)
            right = (arrival[j] < head) & (head < heads - 1)
            remote(
                source, source, z_send.at[0, 0], z_recv.at[arrival[j]], (blk, head)
            ).wait_recv()
        for side, (condition, step) in enumerate(((left, -1), (right, 1))):
            make = lambda source=source, side=side, step=step: remote(
                source,
                full.at[arrival[j], blk],
                z_send.at[j, side],
                z_recv.at[arrival[j]],
                (blk, jnp.clip(head + step, 0, heads - 1)),
            )
            sends.start(make, when=condition)

    tree_step(0, 0)
    chain(0)
    own_shard = pltpu.make_async_copy(shard, full.at[head, blk], own_sem.at[1])
    own_shard.start()
    send_rows(1)

    micro = head // splits
    own_slots = perm[micro, pl.ds(blk, 1), :]
    ones[...] = jnp.where(iota((blks, group), 0) == own_slots // group, 1.0, 0.0)
    cumulative(ones, sums, group)
    rank = jnp.sum(ones[...] * sums[...], axis=0, keepdims=True).astype(jnp.int32) - 1
    dest = own_slots // group * pair + rank
    dest_row[...] = jnp.broadcast_to(dest, dest_row.shape)
    for tile in range(group // 128):
        block = jnp.broadcast_to(dest[:, tile * 128 : (tile + 1) * 128].astype(F32), (128, 128))
        dest_col[tile * 128 : (tile + 1) * 128, :] = block.T.astype(jnp.int32)

    all_slots = perm[micro]
    ones[...] = jnp.where(all_slots // group == blk, 1.0, 0.0)
    cumulative(ones, sums, group)
    rank_rows[...] = jnp.where(ones[...] > 0, sums[...] - 1, -1.0).astype(jnp.int32)

    @pl.loop(0, blks)
    def _(other):
        ranks = rank_rows[pl.ds(other, 1), :]
        inner = (perm[micro, pl.ds(other, 1), :] % group).astype(F32)
        found = jnp.where(iota((pair, group), 0) == ranks, inner, 0.0)
        column = jnp.sum(found, axis=1, keepdims=True).astype(jnp.int32)
        slot_col[pl.ds(pl.multiple_of(other * pair, pair), pair), :] = jnp.broadcast_to(
            column, (pair, 128)
        )

    for tile in range(group // 128):
        block = slot_col[tile * 128 : (tile + 1) * 128, :].astype(F32)
        slot_row[:, tile * 128 : (tile + 1) * 128] = block.T[0:8, :].astype(jnp.int32)

    def to_groups(i):
        exchanges[i].wait_head(
            0, lambda other: arrived.at[i, pl.ds(pl.multiple_of(other * rows, rows), rows), :]
        )
        permute_rows(one_hot_from_row(dest_row), arrived.at[i], sorted_rows.at[i], group)
        exchanges[i].over_blk(
            lambda other: sorted_rows.at[i, pl.ds(other * pair, pair), :],
            lambda other: landed.at[i, pl.ds(pl.multiple_of(other * pair, pair), pair), :],
        )

    outs = (slots_x, slots_g)

    def to_slots(i):
        exchanges[i].wait_blk(
            lambda other: landed.at[i, pl.ds(pl.multiple_of(other * pair, pair), pair), :]
        )
        permute_rows(one_hot_from_row(slot_row), landed.at[i], ordered.at[i], group)
        exchanges[i].over_head(
            1,
            lambda other: ordered.at[i, pl.ds(other * rows, rows), :],
            lambda other: outs[i].at[other],
        )

    to_groups(0)
    for step in range(1, levels):
        tree_step(0, step)
    for j in range(1, heads):
        chain(j)
        tree_step(j, 0)
        if j == 1:
            to_slots(0)
            to_groups(1)
        if j == 2:
            to_slots(1)
        for step in range(1, levels):
            tree_step(j, step)
    for j in range(heads):
        for which in range(2):
            tree_wait(j, which, levels - 1)

    for i in range(2):
        exchanges[i].wait_head(1, lambda other: outs[i].at[other])
    for other in range(blks):

        @pl.when(other != blk)
        def _():
            remote(
                vectors,
                full_vectors.at[other],
                vec_send.at[other],
                vec_recv.at[other],
                (other, head),
            ).wait_recv()

    own_vec.wait()
    own_shard.wait()
    sends.finish()


def gather_all(blks, heads, tokens, out_grad, shard, vectors, perm):
    micros, rows, width = tokens.shape
    part = width * micros // heads
    group = rows * heads
    dma = pltpu.SemaphoreType.DMA
    any_space, vmem = pl.BlockSpec(memory_space=pl.ANY), pl.BlockSpec(memory_space=pltpu.VMEM)
    return pl.pallas_call(
        functools.partial(gather_kernel, blks, heads),
        name="gather_all",
        out_shape=(
            jax.ShapeDtypeStruct((heads, blks) + shard.shape, BF16),
            jax.ShapeDtypeStruct((blks,) + vectors.shape, BF16),
            jax.ShapeDtypeStruct((heads, rows, part), BF16),
            jax.ShapeDtypeStruct((heads, rows, part), BF16),
            jax.ShapeDtypeStruct((group, 128), jnp.int32),
            jax.ShapeDtypeStruct((group, 128), jnp.int32),
        ),
        in_specs=[any_space, any_space, any_space, any_space, vmem],
        out_specs=(any_space, any_space, any_space, any_space, vmem, vmem),
        scratch_shapes=[
            pltpu.VMEM((2, group, part), BF16),
            pltpu.VMEM((2, group, part), BF16),
            pltpu.VMEM((2, group, part), BF16),
            pltpu.VMEM((2, group, part), BF16),
            pltpu.VMEM((8, group), jnp.int32),
            pltpu.VMEM((8, group), jnp.int32),
            pltpu.VMEM((blks, group), F32),
            pltpu.VMEM((blks, group), F32),
            pltpu.VMEM((blks, group), jnp.int32),
        ]
        + exchange_sems(blks, heads)
        + [
            dma((heads, 2)),
            dma((heads,)),
            dma((heads, 2, blks)),
            dma((heads, 2, blks)),
            dma((blks,)),
            dma((blks,)),
            dma((2,)),
        ],
        compiler_params=pltpu.CompilerParams(
            collective_id=0, has_side_effects=True, vmem_limit_bytes=32 << 20
        ),
    )(tokens, out_grad, shard, vectors, perm)


def add_into(target, source, width):
    rows = target.shape[0]
    step = 16 if rows % 16 == 0 else rows

    @pl.loop(0, rows // step)
    def _(i):
        at = pl.ds(pl.multiple_of(i * step, step), step)
        for column in range(0, target.shape[1], width):
            cols = slice(column, column + width)
            target[at, cols] = (
                target[at, cols].astype(F32) + source[at, cols].astype(F32)
            ).astype(BF16)


def reduce_kernel(
    blks,
    heads,
    layer_out,
    x_grad,
    partial,
    vectors,
    dest_col,
    slot_col,
    out_rows,
    grad_rows,
    shard,
    vec_sum,
    total,
    from_core,
    from_tree,
    from_left,
    from_right,
    vec_parts,
    vec_mid,
    vec_heads,
    arrived,
    sorted_rows,
    landed,
    ordered,
    final,
    head_send,
    head_recv,
    blk_send,
    blk_recv,
    local,
    load_sem,
    core_send,
    core_recv,
    tree_send,
    tree_recv,
    left_send,
    left_recv,
    right_send,
    right_recv,
    vec_send,
    vec_recv,
    vec_head_send,
    vec_head_recv,
):
    blk, head = lax.axis_index("blk"), lax.axis_index("head")
    micros, rows, width = out_rows.shape
    splits = heads // micros
    part = width // splits
    group = rows * heads
    pair = group // blks
    levels = blks.bit_length() - 1
    bits = bits_of(blk, levels)
    half = shard.shape[1] // 2
    sends = Sends()
    sems = (head_send, head_recv, blk_send, blk_recv, local)
    exchanges = [RowExchange(sends, blk, head, blks, heads, sems, i) for i in range(2)]
    sources = (layer_out, x_grad)

    enter(blk, head, blks, heads)

    order = []
    for i in range(heads):
        order.append(heads - 1 - i // 2 if i % 2 == 0 else i // 2)

    even = submasks(range(1, levels))
    loads = {}
    for other in order:
        for mask in even:
            piece = flip(blk, mask, bits)
            loads[other, mask] = pltpu.make_async_copy(
                partial.at[other, piece], total.at[other, mask // 2], load_sem.at[other, mask // 2]
            )
            loads[other, mask].start()
            sends.start(
                lambda other=other, mask=mask: remote(
                    partial.at[other, flip(blk, mask | 1, bits)],
                    from_core.at[other, mask // 2],
                    core_send.at[other, mask // 2],
                    core_recv.at[other, mask // 2],
                    (flip(blk, 1, bits), head),
                )
            )

    def rows_to_heads(i):
        exchanges[i].over_head(
            0,
            lambda other: sources[i].at[other],
            lambda other: arrived.at[i, pl.ds(pl.multiple_of(other * rows, rows), rows), :],
        )

    rows_to_heads(0)
    rows_to_heads(1)

    for other in range(blks):
        sends.start(
            lambda other=other: remote(
                vectors.at[other],
                vec_parts.at[blk],
                vec_send.at[other],
                vec_recv.at[blk],
                (other, head),
            ),
            when=other != blk,
        )

    def add_core(other):
        for mask in even:
            loads[other, mask].wait()
            target = from_core.at[other, mask // 2]
            remote(
                target,
                target,
                core_send.at[other, mask // 2],
                core_recv.at[other, mask // 2],
                (flip(blk, 1, bits), head),
            ).wait_recv()
            add_into(total.at[other, mask // 2], target, half)

    orders = [list(range(levels - 1, 0, -1)), [1] + list(range(levels - 1, 1, -1))]

    def cols(ref, which):
        return ref.at[:, which * half : (which + 1) * half]

    def tree_parts(which, step):
        dims = orders[which]
        free = dims[step + 1 :]
        base = sum(1 << (levels - 2 - earlier) for earlier in range(step))
        return dims[step], [(mask, base + i) for i, mask in enumerate(submasks(free))]

    def tree_start(other, step):
        for which in range(2):
            dim, parts = tree_parts(which, step)
            for mask, slot in parts:
                sends.start(
                    lambda which=which, dim=dim, mask=mask, slot=slot: remote(
                        cols(total.at[other, (mask | (1 << dim)) // 2], which),
                        from_tree.at[which, other, slot],
                        tree_send.at[which, other, slot],
                        tree_recv.at[which, other, slot],
                        (flip(blk, 1 << dim, bits), head),
                    )
                )

    def tree_add(other, step):
        for which in range(2):
            dim, parts = tree_parts(which, step)
            for mask, slot in parts:
                source = from_tree.at[which, other, slot]
                remote(
                    source,
                    source,
                    tree_send.at[which, other, slot],
                    tree_recv.at[which, other, slot],
                    (flip(blk, 1 << dim, bits), head),
                ).wait_recv()
                add_into(cols(total.at[other, mask // 2], which), source, half)

    def pass_right(goal):
        target = from_left.at[goal]

        @pl.when((head > 0) & (head <= goal))
        def _():
            remote(
                target, target, left_send.at[goal], left_recv.at[goal], (blk, head)
            ).wait_recv()
            add_into(total.at[goal, 0], target, half)

        sends.start(
            lambda: remote(
                total.at[goal, 0],
                target,
                left_send.at[goal],
                left_recv.at[goal],
                (blk, jnp.minimum(head + 1, heads - 1)),
            ),
            when=head < goal,
        )

    def pass_left(goal):
        target = from_right.at[goal]

        @pl.when((head < heads - 1) & (head >= goal))
        def _():
            remote(
                target, target, right_send.at[goal], right_recv.at[goal], (blk, head)
            ).wait_recv()
            add_into(total.at[goal, 0], target, half)

        sends.start(
            lambda: remote(
                total.at[goal, 0],
                target,
                right_send.at[goal],
                right_recv.at[goal],
                (blk, jnp.maximum(head - 1, 0)),
            ),
            when=head > goal,
        )

    def to_groups(i):
        exchanges[i].wait_head(
            0, lambda other: arrived.at[i, pl.ds(pl.multiple_of(other * rows, rows), rows), :]
        )
        permute_rows(one_hot_from_column(slot_col, group), arrived.at[i], sorted_rows.at[i], group)
        exchanges[i].over_blk(
            lambda other: sorted_rows.at[i, pl.ds(other * pair, pair), :],
            lambda other: landed.at[i, pl.ds(pl.multiple_of(other * pair, pair), pair), :],
        )

    def to_positions(i):
        exchanges[i].wait_blk(
            lambda other: landed.at[i, pl.ds(pl.multiple_of(other * pair, pair), pair), :]
        )
        permute_rows(one_hot_from_column(dest_col, group), landed.at[i], ordered.at[i], group)
        exchanges[i].over_head(
            1,
            lambda other: ordered.at[i, pl.ds(other * rows, rows), :],
            lambda other: final.at[i, other],
        )

    for other in order[:2]:
        add_core(other)
        tree_start(other, 0)
    to_groups(0)
    for other in order[2:]:
        add_core(other)
        tree_start(other, 0)
    to_groups(1)
    for other in order[:2]:
        for step in range(levels - 1):
            tree_add(other, step)
            if step < levels - 2:
                tree_start(other, step + 1)
    to_positions(0)
    for position, other in enumerate(order):
        if position >= 2:
            for step in range(levels - 1):
                tree_add(other, step)
                if step < levels - 2:
                    tree_start(other, step + 1)
        if position == 2:
            to_positions(1)

    vec_mid[...] = vectors[pl.ds(blk, 1)][0]
    for other in range(blks):

        @pl.when(other != blk)
        def _():
            remote(
                vec_parts.at[other],
                vec_parts.at[other],
                vec_send.at[other],
                vec_recv.at[other],
                (other, head),
            ).wait_recv()
            vec_mid[...] += vec_parts[other]

    for other in range(heads):
        sends.start(
            lambda other=other: remote(
                vec_mid,
                vec_heads.at[head],
                vec_head_send.at[other],
                vec_head_recv.at[head],
                (blk, other),
            ),
            when=other != head,
        )

    for i in range(heads):
        goal = heads - 1 - i
        pass_right(goal)
        pass_left(i)

    for own in range(heads):

        @pl.when(own == head)
        def _():
            shard[...] = total[own, 0].astype(F32)

    vec_sum[...] = vec_mid[...]
    for other in range(heads):

        @pl.when(other != head)
        def _():
            remote(
                vec_heads.at[other],
                vec_heads.at[other],
                vec_head_send.at[other],
                vec_head_recv.at[other],
                (blk, other),
            ).wait_recv()
            vec_sum[...] += vec_heads[other]

    for i in range(2):
        exchanges[i].wait_head(1, lambda other: final.at[i, other])
    for source in range(heads):
        micro, which = source // splits, source % splits
        out_rows[micro, :, which * part : (which + 1) * part] = final[0, source]
        grad_rows[micro, :, which * part : (which + 1) * part] = final[1, source].astype(F32)
    sends.finish()


def reduce_all(blks, heads, layer_out, x_grad, partial, vectors, dest_col, slot_col):
    _, rows, part = layer_out.shape
    micros = 2
    group = rows * heads
    width = part * heads // micros
    size = partial.shape[2:]
    half = size[1] // 2
    dma = pltpu.SemaphoreType.DMA
    any_space, vmem = pl.BlockSpec(memory_space=pl.ANY), pl.BlockSpec(memory_space=pltpu.VMEM)
    vec = vectors.shape[1:]
    return pl.pallas_call(
        functools.partial(reduce_kernel, blks, heads),
        name="reduce_all",
        out_shape=(
            jax.ShapeDtypeStruct((micros, rows, width), BF16),
            jax.ShapeDtypeStruct((micros, rows, width), F32),
            jax.ShapeDtypeStruct(size, F32),
            jax.ShapeDtypeStruct(vec, F32),
        ),
        in_specs=[any_space, any_space, any_space, vmem, vmem, vmem],
        out_specs=(vmem, vmem, vmem, vmem),
        scratch_shapes=[
            pltpu.VMEM((heads, blks // 2) + size, BF16),
            pltpu.VMEM((heads, blks // 2) + size, BF16),
            pltpu.VMEM((2, heads, blks // 2 - 1, size[0], half), BF16),
            pltpu.VMEM((heads,) + size, BF16),
            pltpu.VMEM((heads,) + size, BF16),
            pltpu.VMEM((blks,) + vec, F32),
            pltpu.VMEM(vec, F32),
            pltpu.VMEM((heads,) + vec, F32),
            pltpu.VMEM((2, group, part), BF16),
            pltpu.VMEM((2, group, part), BF16),
            pltpu.VMEM((2, group, part), BF16),
            pltpu.VMEM((2, group, part), BF16),
            pltpu.VMEM((2, heads, rows, part), BF16),
        ]
        + exchange_sems(blks, heads)
        + [
            dma((heads, blks // 2)),
            dma((heads, blks // 2)),
            dma((heads, blks // 2)),
            dma((2, heads, blks // 2 - 1)),
            dma((2, heads, blks // 2 - 1)),
            dma((heads,)),
            dma((heads,)),
            dma((heads,)),
            dma((heads,)),
            dma((blks,)),
            dma((blks,)),
            dma((heads,)),
            dma((heads,)),
        ],
        compiler_params=pltpu.CompilerParams(
            collective_id=1, has_side_effects=True, vmem_limit_bytes=56 << 20
        ),
    )(layer_out, x_grad, partial, vectors, dest_col, slot_col)


def layer_norm(hidden, norm_gain, norm_shift):
    center = hidden - jnp.mean(hidden, axis=-1, keepdims=True)
    spread = jnp.mean(center * center, axis=-1, keepdims=True)
    return center * lax.rsqrt(spread + norm_epsilon) * norm_gain + norm_shift


def gelu_exact(values):
    return jax.nn.gelu(values, approximate=False)


def cluster_scores(cluster_q, cluster_k, allowed):
    scores = (
        jnp.einsum("cqhd,ckhd->chqk", cluster_q, cluster_k, preferred_element_type=F32) * 0.125
    )
    return jnp.where(allowed[:, None], scores, masked_score)


def layer_step(x, out_grad, segments, weights, vectors):
    rows, width = x.shape
    full_qkv, full_out, full_up, full_down = weights
    (
        bias_query,
        bias_value,
        bias_out,
        gain_attn,
        shift_attn,
        bias_down,
        gain_ffn,
        shift_ffn,
        bias_up,
    ) = vectors
    heads = width // HEAD_DIM
    cluster_shape = (rows // CLUSTER, CLUSTER, heads, HEAD_DIM)
    proj = jnp.dot(x, full_qkv, preferred_element_type=F32)
    cluster_q = (proj[:, 0:width] + bias_query).astype(BF16).reshape(cluster_shape)
    cluster_k = proj[:, width : 2 * width].astype(BF16).reshape(cluster_shape)
    cluster_v = (proj[:, 2 * width :] + bias_value).astype(BF16).reshape(cluster_shape)
    segments = segments.reshape(rows // CLUSTER, CLUSTER)
    allowed = segments[:, :, None] == segments[:, None, :]
    masked = cluster_scores(cluster_q, cluster_k, allowed)
    probs = jax.nn.softmax(masked, axis=-1)
    context = (
        jnp.einsum("chqk,ckhd->cqhd", probs.astype(BF16), cluster_v, preferred_element_type=F32)
        .astype(BF16)
        .reshape(rows, width)
    )
    attn_res = x.astype(F32) + jnp.dot(context, full_out, preferred_element_type=F32) + bias_out
    normed, norm_back_attn = jax.vjp(layer_norm, attn_res, gain_attn, shift_attn)
    hidden_in = normed.astype(BF16)
    pre_act = jnp.dot(hidden_in, full_up, preferred_element_type=F32) + bias_up
    active_full, gelu_back = jax.vjp(gelu_exact, pre_act)
    active = active_full.astype(BF16)
    ffn_res = normed + jnp.dot(active, full_down, preferred_element_type=F32) + bias_down
    result, norm_back_ffn = jax.vjp(layer_norm, ffn_res, gain_ffn, shift_ffn)
    d_ffn, grad_gain_ffn, grad_shift_ffn = norm_back_ffn(out_grad.astype(F32))
    g_down = d_ffn.astype(BF16)
    grad_down = jnp.einsum("tf,td->fd", active, g_down, preferred_element_type=F32)
    grad_bias_down = jnp.sum(g_down.astype(F32), axis=0)
    d_active = jnp.einsum("td,fd->tf", g_down, full_down, preferred_element_type=F32)
    (d_pre,) = gelu_back(d_active)
    g_pre = d_pre.astype(BF16)
    grad_up = jnp.einsum("td,tf->df", hidden_in, g_pre, preferred_element_type=F32)
    grad_bias_up = jnp.sum(g_pre.astype(F32), axis=0)
    d_normed = d_ffn + jnp.einsum("tf,df->td", g_pre, full_up, preferred_element_type=F32)
    d_attn, grad_gain_attn, grad_shift_attn = norm_back_attn(d_normed)
    g_attn = d_attn.astype(BF16)
    grad_out = jnp.einsum("tc,td->cd", context, g_attn, preferred_element_type=F32)
    grad_bias_out = jnp.sum(g_attn.astype(F32), axis=0)
    cluster_dout = (
        jnp.einsum("td,cd->tc", g_attn, full_out, preferred_element_type=F32)
        .astype(BF16)
        .reshape(cluster_shape)
    )
    dprob = jnp.einsum("cqhd,ckhd->chqk", cluster_dout, cluster_v, preferred_element_type=F32)
    delta = jnp.sum(probs * dprob, axis=-1, keepdims=True)
    dscore = (probs * (dprob - delta)).astype(BF16)
    grad_q = jnp.einsum("chqk,ckhd->cqhd", dscore, cluster_k, preferred_element_type=F32) * 0.125
    grad_k = jnp.einsum("chqk,cqhd->ckhd", dscore, cluster_q, preferred_element_type=F32) * 0.125
    grad_v = jnp.einsum(
        "chqk,cqhd->ckhd", probs.astype(BF16), cluster_dout, preferred_element_type=F32
    )
    g_proj = jnp.concatenate(
        [member.astype(BF16).reshape(rows, width) for member in (grad_q, grad_k, grad_v)], axis=1
    )
    grad_qkv = jnp.einsum("td,tc->dc", x, g_proj, preferred_element_type=F32)
    sums = jnp.sum(g_proj.astype(F32), axis=0)
    x_grad = d_attn + jnp.einsum("tc,dc->td", g_proj, full_qkv, preferred_element_type=F32)
    return (
        result.astype(BF16),
        x_grad.astype(BF16),
        (grad_qkv, grad_out, grad_up, grad_down),
        (
            sums[:width],
            sums[2 * width :],
            grad_bias_out,
            grad_gain_attn,
            grad_shift_attn,
            grad_bias_down,
            grad_gain_ffn,
            grad_shift_ffn,
            grad_bias_up,
        ),
    )


def body(
    tokens,
    seq_lengths,
    cluster_perm,
    out_grad,
    qkv_weight,
    query_bias,
    value_bias,
    out_weight,
    out_bias,
    attn_gain,
    attn_shift,
    up_weight,
    up_bias,
    down_weight,
    down_bias,
    ffn_gain,
    ffn_shift,
):
    blks, heads = lax.axis_size("blk"), lax.axis_size("head")
    blk, head = lax.axis_index("blk"), lax.axis_index("head")
    micros, rows, width = tokens.shape
    group = rows * heads
    total_rows = cluster_perm.shape[1]
    share = qkv_weight.shape[0]
    folds = down_weight.shape[0] // share
    short = down_weight.shape[1]
    widths = [qkv_weight.shape[1], out_weight.shape[1], up_weight.shape[1], folds * short]
    edges = [sum(widths[:i]) for i in range(5)]

    shard = jnp.concatenate(
        [qkv_weight, out_weight, up_weight]
        + [down_weight[i * share : (i + 1) * share] for i in range(folds)],
        axis=1,
    )
    lanes = -(-share // 128) * 128
    small = [
        query_bias,
        value_bias,
        out_bias,
        attn_gain,
        attn_shift,
        down_bias,
        ffn_gain,
        ffn_shift,
    ]
    stacked = jnp.concatenate([jnp.stack(small), up_bias.reshape(folds, share)], axis=0)
    count = stacked.shape[0]
    vectors = jnp.pad(stacked, ((0, -count % 16), (0, lanes - share)))
    perm = cluster_perm.reshape(micros, blks, group)
    full, full_vectors, slots_x, slots_g, dest_col, slot_col = gather_all(
        blks, heads, tokens, out_grad, shard, vectors, perm
    )

    first = blk * group + head * rows
    slots = first + jnp.arange(rows, dtype=jnp.int32)
    ends = jnp.cumsum(seq_lengths, axis=1)
    positions = jnp.arange(total_rows, dtype=jnp.int32)
    segs = jnp.sum((positions[None, :, None] >= ends[:, None, :]).astype(jnp.int32), axis=2)
    slot_segs = jnp.sum(
        jnp.where(cluster_perm[:, None, :] == slots[None, :, None], segs[:, None, :], 0), axis=2
    )

    def unpack(which):
        piece = full[:, :, :, edges[which] : edges[which + 1]]
        if which == 3:
            piece = piece.reshape(heads, blks, share, folds, short)
            return piece.transpose(1, 3, 2, 0, 4).reshape(blks * folds * share, heads * short)
        return piece.transpose(1, 2, 0, 3).reshape(blks * share, heads * widths[which])

    weights = [unpack(i) for i in range(4)]
    spread = full_vectors[:, :count, :share]
    vecs = [spread[:, i].reshape(-1).astype(F32) for i in range(8)]
    vecs.append(spread[:, 8:count].reshape(-1).astype(F32))

    def join(member):
        splits = heads // micros
        return (
            member.reshape(micros, splits, rows, width // splits)
            .transpose(0, 2, 1, 3)
            .reshape(micros * rows, width)
        )

    def split(member):
        splits = heads // micros
        return (
            member.reshape(micros, rows, splits, width // splits)
            .transpose(0, 2, 1, 3)
            .reshape(heads, rows, width // splits)
        )

    result, x_grad, grads, vec_grads = layer_step(
        join(slots_x), join(slots_g), slot_segs.reshape(-1), weights, vecs
    )

    def pack(which, grad):
        grad = grad.astype(BF16)
        if which == 3:
            grad = grad.reshape(blks, folds, share, heads, short).transpose(3, 0, 2, 1, 4)
            return grad.reshape(heads, blks, share, folds * short)
        return grad.reshape(blks, share, heads, widths[which]).transpose(2, 0, 1, 3)

    partial = jnp.concatenate([pack(i, grads[i]) for i in range(4)], axis=3)
    vec_parts = jnp.concatenate(
        [jnp.stack([v.reshape(blks, share) for v in vec_grads[:8]], axis=1)]
        + [vec_grads[8].reshape(blks, folds, share)],
        axis=1,
    )
    vec_parts = jnp.pad(vec_parts, ((0, 0), (0, -count % 16), (0, lanes - share)))
    out_rows, grad_rows, shard_grad, vec_sum = reduce_all(
        blks, heads, split(result), split(x_grad), partial, vec_parts, dest_col, slot_col
    )
    down_grad = shard_grad[:, edges[3] : edges[4]]
    down_grad = jnp.concatenate(
        [down_grad[:, i * short : (i + 1) * short] for i in range(folds)], axis=0
    )
    vec = [vec_sum[i, :share] for i in range(8)]
    return (
        out_rows,
        grad_rows,
        shard_grad[:, edges[0] : edges[1]],
        vec[0],
        vec[1],
        shard_grad[:, edges[1] : edges[2]],
        vec[2],
        vec[3],
        vec[4],
        shard_grad[:, edges[2] : edges[3]],
        vec_sum[8:count, :share].reshape(-1),
        down_grad,
        vec[5],
        vec[6],
        vec[7],
    )


def solution(mesh):
    return jax.shard_map(
        body,
        mesh=mesh,
        in_specs=(
            P(None, ("blk", "head"), None),
            P(),
            P(),
            P(None, ("blk", "head"), None),
            P("blk", "head"),
            P("blk"),
            P("blk"),
            P("blk", "head"),
            P("blk"),
            P("blk"),
            P("blk"),
            P("blk", "head"),
            P("blk"),
            P("blk", "head"),
            P("blk"),
            P("blk"),
            P("blk"),
        ),
        out_specs=(
            P(None, ("blk", "head"), None),
            P(None, ("blk", "head"), None),
            P("blk", "head"),
            P("blk"),
            P("blk"),
            P("blk", "head"),
            P("blk"),
            P("blk"),
            P("blk"),
            P("blk", "head"),
            P("blk"),
            P("blk", "head"),
            P("blk"),
            P("blk"),
            P("blk"),
        ),
        check_vma=False,
    )
```

```python
import functools

import jax
import jax.numpy as jnp
from jax import lax
from jax.experimental import pallas as pl
from jax.experimental.pallas import tpu as pltpu
from jax.sharding import PartitionSpec as P

HEAD_DIM = 64
CLUSTER = 128
MESH = pl.DeviceIdType.MESH
BF16 = jnp.bfloat16
F32 = jnp.float32

masked_score = -1e30
norm_epsilon = 1e-05


def bits_of(index, count):
    return [(index // (1 << i)) % 2 for i in range(count)]


def flip(index, mask, bits):
    for i, bit in enumerate(bits):
        if mask & (1 << i):
            index = index + (1 - 2 * bit) * (1 << i)
    return index


def submasks(dims):
    masks = [0]
    for dim in dims:
        masks = masks + [mask | (1 << dim) for mask in masks]
    return masks


def choose(index, values):
    result = values[-1]
    for position in range(len(values) - 2, -1, -1):
        result = jnp.where(index == position, values[position], result)
    return result


class Sends:
    def __init__(self):
        self.pending = []

    def start(self, make, when=None):
        if when is None:
            make().start()
        else:

            @pl.when(when)
            def _():
                make().start()

        self.pending.append((make, when))

    def finish(self):
        for make, when in self.pending:
            if when is None:
                make().wait_send()
            else:

                @pl.when(when)
                def _(make=make):
                    make().wait_send()


def remote(src, dst, send_sem, recv_sem, device):
    return pltpu.make_async_remote_copy(
        src_ref=src,
        dst_ref=dst,
        send_sem=send_sem,
        recv_sem=recv_sem,
        device_id=device,
        device_id_type=MESH,
    )


def enter(blk, head, blks, heads):
    barrier = pltpu.get_barrier_semaphore()
    for other in range(blks):

        @pl.when(other != blk)
        def _():
            pl.semaphore_signal(barrier, inc=1, device_id=(other, head), device_id_type=MESH)

    for other in range(heads):

        @pl.when(other != head)
        def _():
            pl.semaphore_signal(barrier, inc=1, device_id=(blk, other), device_id_type=MESH)

    pl.semaphore_wait(barrier, blks + heads - 2)


def iota(shape, dim):
    return lax.broadcasted_iota(jnp.int32, shape, dim)


def permute_rows(one_hot_tile, source, target, rows):
    @pl.loop(0, rows // CLUSTER)
    def _(tile):
        start = pl.multiple_of(tile * CLUSTER, CLUSTER)
        chosen = jnp.dot(one_hot_tile(start), source[...], preferred_element_type=F32)
        target[pl.ds(start, CLUSTER), :] = chosen.astype(BF16)


def one_hot_from_row(row_ref):
    def tile(start):
        row = row_ref[0:1, :]
        count = row.shape[1]
        return jnp.where(iota((CLUSTER, count), 0) + start == row, 1.0, 0.0).astype(BF16)

    return tile


def one_hot_from_column(column_ref, count):
    def tile(start):
        column = column_ref[pl.ds(start, CLUSTER), 0:1]
        return jnp.where(iota((CLUSTER, count), 1) == column, 1.0, 0.0).astype(BF16)

    return tile


class RowExchange:
    def __init__(self, sends, blk, head, blks, heads, sems, tensor):
        self.sends, self.blk, self.head, self.blks, self.heads = sends, blk, head, blks, heads
        self.head_send, self.head_recv, self.blk_send, self.blk_recv, self.local = sems
        self.tensor = tensor

    def over_head(self, step, source, target):
        for other in range(self.heads):
            make = lambda other=other: remote(
                source(other),
                target(self.head),
                self.head_send.at[self.tensor, step, other],
                self.head_recv.at[self.tensor, step, self.head],
                (self.blk, other),
            )
            self.sends.start(make, when=other != self.head)

            @pl.when(other == self.head)
            def _():
                pltpu.make_async_copy(
                    source(other), target(other), self.local.at[self.tensor, step]
                ).start()

    def wait_head(self, step, target):
        for other in range(self.heads):

            @pl.when(other != self.head)
            def _():
                remote(
                    target(other),
                    target(other),
                    self.head_send.at[self.tensor, step, other],
                    self.head_recv.at[self.tensor, step, other],
                    (self.blk, other),
                ).wait_recv()

        pltpu.make_async_copy(
            target(self.head), target(self.head), self.local.at[self.tensor, step]
        ).wait()

    def over_blk(self, source, target):
        for other in range(self.blks):
            make = lambda other=other: remote(
                source(other),
                target(self.blk),
                self.blk_send.at[self.tensor, other],
                self.blk_recv.at[self.tensor, self.blk],
                (other, self.head),
            )
            self.sends.start(make, when=other != self.blk)

            @pl.when(other == self.blk)
            def _():
                pltpu.make_async_copy(
                    source(other), target(other), self.local.at[self.tensor, 2]
                ).start()

    def wait_blk(self, target):
        for other in range(self.blks):

            @pl.when(other != self.blk)
            def _():
                remote(
                    target(other),
                    target(other),
                    self.blk_send.at[self.tensor, other],
                    self.blk_recv.at[self.tensor, other],
                    (other, self.head),
                ).wait_recv()

        pltpu.make_async_copy(
            target(self.blk), target(self.blk), self.local.at[self.tensor, 2]
        ).wait()


def exchange_sems(blks, heads):
    dma = pltpu.SemaphoreType.DMA
    return [dma((2, 2, heads)), dma((2, 2, heads)), dma((2, blks)), dma((2, blks)), dma((2, 3))]


def cumulative(ones_ref, sums_ref, count):
    upper = jnp.where(iota((128, 128), 0) <= iota((128, 128), 1), 1.0, 0.0).astype(BF16)
    carry = jnp.zeros((ones_ref.shape[0], 1), F32)
    for tile in range(count // 128):
        part = ones_ref[:, tile * 128 : (tile + 1) * 128].astype(BF16)
        sums = jnp.dot(part, upper, preferred_element_type=F32) + carry
        sums_ref[:, tile * 128 : (tile + 1) * 128] = sums
        carry = sums[:, 127:128]


def gather_kernel(
    blks,
    heads,
    tokens,
    out_grad,
    shard,
    vectors,
    perm,
    full,
    full_vectors,
    slots_x,
    slots_g,
    dest_col,
    slot_col,
    arrived,
    sorted_rows,
    landed,
    ordered,
    dest_row,
    slot_row,
    ones,
    sums,
    rank_rows,
    head_send,
    head_recv,
    blk_send,
    blk_recv,
    local,
    z_send,
    z_recv,
    tree_send,
    tree_recv,
    vec_send,
    vec_recv,
    own_sem,
):
    blk, head = lax.axis_index("blk"), lax.axis_index("head")
    micros, rows, width = tokens.shape
    splits = heads // micros
    part = width // splits
    group = rows * heads
    pair = group // blks
    levels = blks.bit_length() - 1
    bits = bits_of(blk, levels)
    half = shard.shape[1] // 2
    sends = Sends()
    sems = (head_send, head_recv, blk_send, blk_recv, local)

    enter(blk, head, blks, heads)

    exchanges = [RowExchange(sends, blk, head, blks, heads, sems, i) for i in range(2)]
    sources = (tokens, out_grad)

    def send_rows(i):
        exchanges[i].over_head(
            0,
            lambda other: sources[i].at[
                other // splits, :, (other % splits) * part : (other % splits + 1) * part
            ],
            lambda other: arrived.at[i, pl.ds(pl.multiple_of(other * rows, rows), rows), :],
        )

    send_rows(0)

    def vec_copy(other):
        return remote(
            vectors, full_vectors.at[blk], vec_send.at[other], vec_recv.at[blk], (other, head)
        )

    for other in range(blks):
        sends.start(lambda other=other: vec_copy(other), when=other != blk)
    own_vec = pltpu.make_async_copy(vectors, full_vectors.at[blk], own_sem.at[0])
    own_vec.start()

    orders = [list(range(1, levels)) + [0], list(range(2, levels)) + [1, 0]]
    arrival = [
        choose(
            head,
            [
                sorted([x for x in range(heads) if x != own], key=lambda x: (abs(x - own), x))[j - 1]
                for own in range(heads)
            ],
        )
        if j
        else head
        for j in range(heads)
    ]

    def halves(ref, which):
        return ref.at[:, which * half : (which + 1) * half]

    def tree_step(j, step):
        for which in range(2):
            dims = orders[which]
            if step:
                tree_wait(j, which, step - 1)
            other = flip(blk, 1 << dims[step], bits)
            for mask in submasks(dims[:step]):
                piece = flip(blk, mask, bits)
                target = halves(full.at[arrival[j], piece], which)
                source = halves(shard, which) if j == 0 and mask == 0 else target
                slot = (1 << step) - 1 + submasks(dims[:step]).index(mask)
                make = lambda source=source, target=target, piece=piece, other=other, slot=slot, which=which: remote(
                    source,
                    target,
                    tree_send.at[j, which, slot],
                    tree_recv.at[j, which, piece],
                    (other, head),
                )
                sends.start(make)

    def tree_wait(j, which, step):
        dims = orders[which]
        other = flip(blk, 1 << dims[step], bits)
        for mask in submasks(dims[:step]):
            piece = flip(blk, mask | (1 << dims[step]), bits)
            target = halves(full.at[arrival[j], piece], which)
            remote(
                target,
                target,
                tree_send.at[j, which, 0],
                tree_recv.at[j, which, piece],
                (other, head),
            ).wait_recv()

    def chain(j):
        if j == 0:
            source = shard
            left, right = head > 0, head < heads - 1
        else:
            source = full.at[arrival[j], blk]
            left = (arrival[j] > head) & (head > 0)
            right = (arrival[j] < head) & (head < heads - 1)
            remote(
                source, source, z_send.at[0, 0], z_recv.at[arrival[j]], (blk, head)
            ).wait_recv()
        for side, (condition, step) in enumerate(((left, -1), (right, 1))):
            make = lambda source=source, side=side, step=step: remote(
                source,
                full.at[arrival[j], blk],
                z_send.at[j, side],
                z_recv.at[arrival[j]],
                (blk, jnp.clip(head + step, 0, heads - 1)),
            )
            sends.start(make, when=condition)

    tree_step(0, 0)
    chain(0)
    own_shard = pltpu.make_async_copy(shard, full.at[head, blk], own_sem.at[1])
    own_shard.start()
    send_rows(1)

    micro = head // splits
    own_slots = perm[micro, pl.ds(blk, 1), :]
    ones[...] = jnp.where(iota((blks, group), 0) == own_slots // group, 1.0, 0.0)
    cumulative(ones, sums, group)
    rank = jnp.sum(ones[...] * sums[...], axis=0, keepdims=True).astype(jnp.int32) - 1
    dest = own_slots // group * pair + rank
    dest_row[...] = jnp.broadcast_to(dest, dest_row.shape)
    for tile in range(group // 128):
        block = jnp.broadcast_to(dest[:, tile * 128 : (tile + 1) * 128].astype(F32), (128, 128))
        dest_col[tile * 128 : (tile + 1) * 128, :] = block.T.astype(jnp.int32)

    all_slots = perm[micro]
    ones[...] = jnp.where(all_slots // group == blk, 1.0, 0.0)
    cumulative(ones, sums, group)
    rank_rows[...] = jnp.where(ones[...] > 0, sums[...] - 1, -1.0).astype(jnp.int32)

    @pl.loop(0, blks)
    def _(other):
        ranks = rank_rows[pl.ds(other, 1), :]
        inner = (perm[micro, pl.ds(other, 1), :] % group).astype(F32)
        found = jnp.where(iota((pair, group), 0) == ranks, inner, 0.0)
        column = jnp.sum(found, axis=1, keepdims=True).astype(jnp.int32)
        slot_col[pl.ds(pl.multiple_of(other * pair, pair), pair), :] = jnp.broadcast_to(
            column, (pair, 128)
        )

    for tile in range(group // 128):
        block = slot_col[tile * 128 : (tile + 1) * 128, :].astype(F32)
        slot_row[:, tile * 128 : (tile + 1) * 128] = block.T[0:8, :].astype(jnp.int32)

    def to_groups(i):
        exchanges[i].wait_head(
            0, lambda other: arrived.at[i, pl.ds(pl.multiple_of(other * rows, rows), rows), :]
        )
        permute_rows(one_hot_from_row(dest_row), arrived.at[i], sorted_rows.at[i], group)
        exchanges[i].over_blk(
            lambda other: sorted_rows.at[i, pl.ds(other * pair, pair), :],
            lambda other: landed.at[i, pl.ds(pl.multiple_of(other * pair, pair), pair), :],
        )

    outs = (slots_x, slots_g)

    def to_slots(i):
        exchanges[i].wait_blk(
            lambda other: landed.at[i, pl.ds(pl.multiple_of(other * pair, pair), pair), :]
        )
        permute_rows(one_hot_from_row(slot_row), landed.at[i], ordered.at[i], group)
        exchanges[i].over_head(
            1,
            lambda other: ordered.at[i, pl.ds(other * rows, rows), :],
            lambda other: outs[i].at[other],
        )

    to_groups(0)
    for step in range(1, levels):
        tree_step(0, step)
    for j in range(1, heads):
        chain(j)
        tree_step(j, 0)
        if j == 1:
            to_slots(0)
            to_groups(1)
        if j == 2:
            to_slots(1)
        for step in range(1, levels):
            tree_step(j, step)
    for j in range(heads):
        for which in range(2):
            tree_wait(j, which, levels - 1)

    for i in range(2):
        exchanges[i].wait_head(1, lambda other: outs[i].at[other])
    for other in range(blks):

        @pl.when(other != blk)
        def _():
            remote(
                vectors,
                full_vectors.at[other],
                vec_send.at[other],
                vec_recv.at[other],
                (other, head),
            ).wait_recv()

    own_vec.wait()
    own_shard.wait()
    sends.finish()


def gather_all(blks, heads, tokens, out_grad, shard, vectors, perm):
    micros, rows, width = tokens.shape
    part = width * micros // heads
    group = rows * heads
    dma = pltpu.SemaphoreType.DMA
    any_space, vmem = pl.BlockSpec(memory_space=pl.ANY), pl.BlockSpec(memory_space=pltpu.VMEM)
    return pl.pallas_call(
        functools.partial(gather_kernel, blks, heads),
        name="gather_all",
        out_shape=(
            jax.ShapeDtypeStruct((heads, blks) + shard.shape, BF16),
            jax.ShapeDtypeStruct((blks,) + vectors.shape, BF16),
            jax.ShapeDtypeStruct((heads, rows, part), BF16),
            jax.ShapeDtypeStruct((heads, rows, part), BF16),
            jax.ShapeDtypeStruct((group, 128), jnp.int32),
            jax.ShapeDtypeStruct((group, 128), jnp.int32),
        ),
        in_specs=[any_space, any_space, any_space, any_space, vmem],
        out_specs=(any_space, any_space, any_space, any_space, vmem, vmem),
        scratch_shapes=[
            pltpu.VMEM((2, group, part), BF16),
            pltpu.VMEM((2, group, part), BF16),
            pltpu.VMEM((2, group, part), BF16),
            pltpu.VMEM((2, group, part), BF16),
            pltpu.VMEM((8, group), jnp.int32),
            pltpu.VMEM((8, group), jnp.int32),
            pltpu.VMEM((blks, group), F32),
            pltpu.VMEM((blks, group), F32),
            pltpu.VMEM((blks, group), jnp.int32),
        ]
        + exchange_sems(blks, heads)
        + [
            dma((heads, 2)),
            dma((heads,)),
            dma((heads, 2, blks)),
            dma((heads, 2, blks)),
            dma((blks,)),
            dma((blks,)),
            dma((2,)),
        ],
        compiler_params=pltpu.CompilerParams(
            collective_id=0, has_side_effects=True, vmem_limit_bytes=32 << 20
        ),
    )(tokens, out_grad, shard, vectors, perm)


def add_into(target, source, width):
    rows = target.shape[0]
    step = 16 if rows % 16 == 0 else rows

    @pl.loop(0, rows // step)
    def _(i):
        at = pl.ds(pl.multiple_of(i * step, step), step)
        for column in range(0, target.shape[1], width):
            cols = slice(column, column + width)
            target[at, cols] = (
                target[at, cols].astype(F32) + source[at, cols].astype(F32)
            ).astype(BF16)


def reduce_kernel(
    blks,
    heads,
    layer_out,
    x_grad,
    partial,
    vectors,
    dest_col,
    slot_col,
    out_rows,
    grad_rows,
    shard,
    vec_sum,
    total,
    from_core,
    from_tree,
    from_left,
    from_right,
    vec_parts,
    vec_mid,
    vec_heads,
    arrived,
    sorted_rows,
    landed,
    ordered,
    final,
    head_send,
    head_recv,
    blk_send,
    blk_recv,
    local,
    load_sem,
    core_send,
    core_recv,
    tree_send,
    tree_recv,
    left_send,
    left_recv,
    right_send,
    right_recv,
    vec_send,
    vec_recv,
    vec_head_send,
    vec_head_recv,
):
    blk, head = lax.axis_index("blk"), lax.axis_index("head")
    micros, rows, width = out_rows.shape
    splits = heads // micros
    part = width // splits
    group = rows * heads
    pair = group // blks
    levels = blks.bit_length() - 1
    bits = bits_of(blk, levels)
    half = shard.shape[1] // 2
    sends = Sends()
    sems = (head_send, head_recv, blk_send, blk_recv, local)
    exchanges = [RowExchange(sends, blk, head, blks, heads, sems, i) for i in range(2)]
    sources = (layer_out, x_grad)

    enter(blk, head, blks, heads)

    order = []
    for i in range(heads):
        order.append(heads - 1 - i // 2 if i % 2 == 0 else i // 2)

    even = submasks(range(1, levels))
    loads = {}
    for other in order:
        for mask in even:
            piece = flip(blk, mask, bits)
            loads[other, mask] = pltpu.make_async_copy(
                partial.at[other, piece], total.at[other, mask // 2], load_sem.at[other, mask // 2]
            )
            loads[other, mask].start()
            sends.start(
                lambda other=other, mask=mask: remote(
                    partial.at[other, flip(blk, mask | 1, bits)],
                    from_core.at[other, mask // 2],
                    core_send.at[other, mask // 2],
                    core_recv.at[other, mask // 2],
                    (flip(blk, 1, bits), head),
                )
            )

    def rows_to_heads(i):
        exchanges[i].over_head(
            0,
            lambda other: sources[i].at[other],
            lambda other: arrived.at[i, pl.ds(pl.multiple_of(other * rows, rows), rows), :],
        )

    rows_to_heads(0)
    rows_to_heads(1)

    for other in range(blks):
        sends.start(
            lambda other=other: remote(
                vectors.at[other],
                vec_parts.at[blk],
                vec_send.at[other],
                vec_recv.at[blk],
                (other, head),
            ),
            when=other != blk,
        )

    def add_core(other):
        for mask in even:
            loads[other, mask].wait()
            target = from_core.at[other, mask // 2]
            remote(
                target,
                target,
                core_send.at[other, mask // 2],
                core_recv.at[other, mask // 2],
                (flip(blk, 1, bits), head),
            ).wait_recv()
            add_into(total.at[other, mask // 2], target, half)

    orders = [list(range(levels - 1, 0, -1)), [1] + list(range(levels - 1, 1, -1))]

    def cols(ref, which):
        return ref.at[:, which * half : (which + 1) * half]

    def tree_parts(which, step):
        dims = orders[which]
        free = dims[step + 1 :]
        base = sum(1 << (levels - 2 - earlier) for earlier in range(step))
        return dims[step], [(mask, base + i) for i, mask in enumerate(submasks(free))]

    def tree_start(other, step):
        for which in range(2):
            dim, parts = tree_parts(which, step)
            for mask, slot in parts:
                sends.start(
                    lambda which=which, dim=dim, mask=mask, slot=slot: remote(
                        cols(total.at[other, (mask | (1 << dim)) // 2], which),
                        from_tree.at[which, other, slot],
                        tree_send.at[which, other, slot],
                        tree_recv.at[which, other, slot],
                        (flip(blk, 1 << dim, bits), head),
                    )
                )

    def tree_add(other, step):
        for which in range(2):
            dim, parts = tree_parts(which, step)
            for mask, slot in parts:
                source = from_tree.at[which, other, slot]
                remote(
                    source,
                    source,
                    tree_send.at[which, other, slot],
                    tree_recv.at[which, other, slot],
                    (flip(blk, 1 << dim, bits), head),
                ).wait_recv()
                add_into(cols(total.at[other, mask // 2], which), source, half)

    def pass_right(goal):
        target = from_left.at[goal]

        @pl.when((head > 0) & (head <= goal))
        def _():
            remote(
                target, target, left_send.at[goal], left_recv.at[goal], (blk, head)
            ).wait_recv()
            add_into(total.at[goal, 0], target, half)

        sends.start(
            lambda: remote(
                total.at[goal, 0],
                target,
                left_send.at[goal],
                left_recv.at[goal],
                (blk, jnp.minimum(head + 1, heads - 1)),
            ),
            when=head < goal,
        )

    def pass_left(goal):
        target = from_right.at[goal]

        @pl.when((head < heads - 1) & (head >= goal))
        def _():
            remote(
                target, target, right_send.at[goal], right_recv.at[goal], (blk, head)
            ).wait_recv()
            add_into(total.at[goal, 0], target, half)

        sends.start(
            lambda: remote(
                total.at[goal, 0],
                target,
                right_send.at[goal],
                right_recv.at[goal],
                (blk, jnp.maximum(head - 1, 0)),
            ),
            when=head > goal,
        )

    def to_groups(i):
        exchanges[i].wait_head(
            0, lambda other: arrived.at[i, pl.ds(pl.multiple_of(other * rows, rows), rows), :]
        )
        permute_rows(one_hot_from_column(slot_col, group), arrived.at[i], sorted_rows.at[i], group)
        exchanges[i].over_blk(
            lambda other: sorted_rows.at[i, pl.ds(other * pair, pair), :],
            lambda other: landed.at[i, pl.ds(pl.multiple_of(other * pair, pair), pair), :],
        )

    def to_positions(i):
        exchanges[i].wait_blk(
            lambda other: landed.at[i, pl.ds(pl.multiple_of(other * pair, pair), pair), :]
        )
        permute_rows(one_hot_from_column(dest_col, group), landed.at[i], ordered.at[i], group)
        exchanges[i].over_head(
            1,
            lambda other: ordered.at[i, pl.ds(other * rows, rows), :],
            lambda other: final.at[i, other],
        )

    for other in order[:2]:
        add_core(other)
        tree_start(other, 0)
    to_groups(0)
    for other in order[2:]:
        add_core(other)
        tree_start(other, 0)
    to_groups(1)
    for other in order[:2]:
        for step in range(levels - 1):
            tree_add(other, step)
            if step < levels - 2:
                tree_start(other, step + 1)
    to_positions(0)
    for position, other in enumerate(order):
        if position >= 2:
            for step in range(levels - 1):
                tree_add(other, step)
                if step < levels - 2:
                    tree_start(other, step + 1)
        if position == 2:
            to_positions(1)

    vec_mid[...] = vectors[pl.ds(blk, 1)][0]
    for other in range(blks):

        @pl.when(other != blk)
        def _():
            remote(
                vec_parts.at[other],
                vec_parts.at[other],
                vec_send.at[other],
                vec_recv.at[other],
                (other, head),
            ).wait_recv()
            vec_mid[...] += vec_parts[other]

    for other in range(heads):
        sends.start(
            lambda other=other: remote(
                vec_mid,
                vec_heads.at[head],
                vec_head_send.at[other],
                vec_head_recv.at[head],
                (blk, other),
            ),
            when=other != head,
        )

    for i in range(heads):
        goal = heads - 1 - i
        pass_right(goal)
        pass_left(i)

    for own in range(heads):

        @pl.when(own == head)
        def _():
            shard[...] = total[own, 0].astype(F32)

    vec_sum[...] = vec_mid[...]
    for other in range(heads):

        @pl.when(other != head)
        def _():
            remote(
                vec_heads.at[other],
                vec_heads.at[other],
                vec_head_send.at[other],
                vec_head_recv.at[other],
                (blk, other),
            ).wait_recv()
            vec_sum[...] += vec_heads[other]

    for i in range(2):
        exchanges[i].wait_head(1, lambda other: final.at[i, other])
    for source in range(heads):
        micro, which = source // splits, source % splits
        out_rows[micro, :, which * part : (which + 1) * part] = final[0, source]
        grad_rows[micro, :, which * part : (which + 1) * part] = final[1, source].astype(F32)
    sends.finish()


def reduce_all(blks, heads, layer_out, x_grad, partial, vectors, dest_col, slot_col):
    _, rows, part = layer_out.shape
    micros = 2
    group = rows * heads
    width = part * heads // micros
    size = partial.shape[2:]
    half = size[1] // 2
    dma = pltpu.SemaphoreType.DMA
    any_space, vmem = pl.BlockSpec(memory_space=pl.ANY), pl.BlockSpec(memory_space=pltpu.VMEM)
    vec = vectors.shape[1:]
    return pl.pallas_call(
        functools.partial(reduce_kernel, blks, heads),
        name="reduce_all",
        out_shape=(
            jax.ShapeDtypeStruct((micros, rows, width), BF16),
            jax.ShapeDtypeStruct((micros, rows, width), F32),
            jax.ShapeDtypeStruct(size, F32),
            jax.ShapeDtypeStruct(vec, F32),
        ),
        in_specs=[any_space, any_space, any_space, vmem, vmem, vmem],
        out_specs=(vmem, vmem, vmem, vmem),
        scratch_shapes=[
            pltpu.VMEM((heads, blks // 2) + size, BF16),
            pltpu.VMEM((heads, blks // 2) + size, BF16),
            pltpu.VMEM((2, heads, blks // 2 - 1, size[0], half), BF16),
            pltpu.VMEM((heads,) + size, BF16),
            pltpu.VMEM((heads,) + size, BF16),
            pltpu.VMEM((blks,) + vec, F32),
            pltpu.VMEM(vec, F32),
            pltpu.VMEM((heads,) + vec, F32),
            pltpu.VMEM((2, group, part), BF16),
            pltpu.VMEM((2, group, part), BF16),
            pltpu.VMEM((2, group, part), BF16),
            pltpu.VMEM((2, group, part), BF16),
            pltpu.VMEM((2, heads, rows, part), BF16),
        ]
        + exchange_sems(blks, heads)
        + [
            dma((heads, blks // 2)),
            dma((heads, blks // 2)),
            dma((heads, blks // 2)),
            dma((2, heads, blks // 2 - 1)),
            dma((2, heads, blks // 2 - 1)),
            dma((heads,)),
            dma((heads,)),
            dma((heads,)),
            dma((heads,)),
            dma((blks,)),
            dma((blks,)),
            dma((heads,)),
            dma((heads,)),
        ],
        compiler_params=pltpu.CompilerParams(
            collective_id=1, has_side_effects=True, vmem_limit_bytes=56 << 20
        ),
    )(layer_out, x_grad, partial, vectors, dest_col, slot_col)


def contract(left, right, dims):
    return lax.dot_general(left, right, ((dims[:1], dims[1:]), ((), ())), preferred_element_type=F32)


def assemble_attention(packed, qkv, out):
    heads, width, _ = packed.shape
    wide, narrow = qkv.shape[1] // heads, out.shape[1] // heads

    @pl.loop(0, width // CLUSTER)
    def _(tile):
        rows = pl.ds(pl.multiple_of(tile * CLUSTER, CLUSTER), CLUSTER)
        for head in range(heads):
            qkv[rows, head * wide : (head + 1) * wide] = packed[head, rows, 0:wide]
            out[rows, head * narrow : (head + 1) * narrow] = packed[
                head, rows, wide : wide + narrow
            ]


def column_sum(values):
    return jnp.sum(values, axis=0, keepdims=True)


def row_mean(values):
    return jnp.mean(values, axis=1, keepdims=True)


def normalize(hidden):
    center = hidden - row_mean(hidden)
    scale = lax.rsqrt(row_mean(center * center) + norm_epsilon)
    return center * scale, scale


def norm_derivative(normal, scale, cotangent, gain):
    scaled = cotangent * gain
    return scale * (scaled - row_mean(scaled) - normal * row_mean(scaled * normal))


def forward_kernel(
    slots_x,
    weights,
    bias_qkv,
    vectors,
    seg_col,
    seg_row,
    x,
    proj,
    probs,
    context,
    attn_res,
    qkv,
    out,
    packed,
    sem,
):
    heads, rows, part = slots_x.shape
    tokens, width = x.shape
    splits = width // part
    load = pltpu.make_async_copy(weights.at[:, :, 0 : packed.shape[2]], packed, sem.at[0])
    load.start()
    for source in range(heads):
        micro, which = source // splits, source % splits
        x[micro * rows : (micro + 1) * rows, which * part : (which + 1) * part] = slots_x[source]
    load.wait()
    assemble_attention(packed, qkv, out)
    project(x, qkv, bias_qkv, proj)
    attend(proj, probs, context, seg_col, seg_row)
    leave_attention(x, context, out, vectors, attn_res)


def project(x, qkv, bias_qkv, proj):
    @pl.loop(0, proj.shape[1] // 256)
    def _(tile):
        cols = pl.ds(pl.multiple_of(tile * 256, 256), 256)
        sums = jnp.dot(x[...], qkv[:, cols], preferred_element_type=F32)
        proj[:, cols] = (sums + bias_qkv[:, cols]).astype(BF16)


def two_heads(tile, first):
    zero = jnp.zeros_like(tile)
    return jnp.concatenate([jnp.where(first, tile, zero), jnp.where(first, zero, tile)], axis=0)


def attend(proj, probs, context, seg_col, seg_row):
    tokens, width = context.shape
    first = iota((CLUSTER, 128), 1) < HEAD_DIM

    @pl.loop(0, tokens // CLUSTER)
    def _(cluster):
        rows = pl.ds(pl.multiple_of(cluster * CLUSTER, CLUSTER), CLUSTER)
        column = seg_col[rows, 0:1]
        allowed = jnp.concatenate([column, column], axis=0) == seg_row[pl.ds(cluster, 1), :]
        for pair in range(width // 128):
            at = pair * 128
            q = two_heads(proj[rows, at : at + 128], first)
            k = proj[rows, width + at : width + at + 128]
            v = proj[rows, 2 * width + at : 2 * width + at + 128]
            scores = contract(q, k, (1, 1)) * 0.125
            scores = jnp.where(allowed, scores, masked_score)
            weight = jnp.exp(scores - jnp.max(scores, axis=1, keepdims=True))
            p = (weight / jnp.sum(weight, axis=1, keepdims=True)).astype(BF16)
            probs[cluster, pair] = p
            both = jnp.dot(p, v, preferred_element_type=F32)
            context[rows, at : at + 128] = jnp.where(
                first, both[:CLUSTER], both[CLUSTER:]
            ).astype(BF16)


def leave_attention(x, context, out, vectors, attn_res):
    @pl.loop(0, x.shape[1] // 256)
    def _(tile):
        cols = pl.ds(pl.multiple_of(tile * 256, 256), 256)
        sums = jnp.dot(context[...], out[:, cols], preferred_element_type=F32)
        attn_res[:, cols] = x[:, cols].astype(F32) + sums + vectors[2:3, cols]


def forward_part(slots_x, weights, bias_qkv, vectors, seg_col, seg_row):
    heads, rows, part = slots_x.shape
    width = weights.shape[1]
    tokens = heads * part * rows // width
    vmem = pl.BlockSpec(memory_space=pltpu.VMEM)
    return pl.pallas_call(
        forward_kernel,
        name="forward_part",
        out_shape=(
            jax.ShapeDtypeStruct((tokens, width), BF16),
            jax.ShapeDtypeStruct((tokens, 3 * width), BF16),
            jax.ShapeDtypeStruct((tokens // CLUSTER, width // 128, 2 * CLUSTER, CLUSTER), BF16),
            jax.ShapeDtypeStruct((tokens, width), BF16),
            jax.ShapeDtypeStruct((tokens, width), F32),
            jax.ShapeDtypeStruct((width, 3 * width), BF16),
            jax.ShapeDtypeStruct((width, width), BF16),
        ),
        in_specs=[vmem, pl.BlockSpec(memory_space=pl.ANY), vmem, vmem, vmem, vmem],
        out_specs=(vmem,) * 7,
        scratch_shapes=[
            pltpu.VMEM((heads, width, width), BF16),
            pltpu.SemaphoreType.DMA((1,)),
        ],
        compiler_params=pltpu.CompilerParams(vmem_limit_bytes=48 << 20),
    )(slots_x, weights, bias_qkv, vectors, seg_col, seg_row)


def ffn_kernel(
    share,
    attn_res,
    slots_g,
    weights,
    vectors,
    up_bias,
    layer_out,
    d_attn,
    g_attn,
    partial,
    vec_grads,
    up_bias_grad,
    packed,
    down,
    normed,
    hidden,
    hidden_t,
    active,
    slope,
    g_pre,
    ffn_res,
    g_down,
    sem,
):
    heads, rows, part = slots_g.shape
    tokens, width = attn_res.shape
    ff = active.shape[1]
    fold = ff // width
    short = width // heads
    splits = width // part
    load = pltpu.make_async_copy(weights.at[:, :, width : 3 * width], packed, sem.at[0])
    load.start()
    gain_attn, shift_attn = vectors[3:4, :], vectors[4:5, :]
    bias_down, gain_ffn, shift_ffn = vectors[5:6, :], vectors[6:7, :], vectors[7:8, :]
    vec_grads[...] = jnp.zeros_like(vec_grads)

    def row_tiles(body):
        @pl.loop(0, tokens // CLUSTER)
        def _(tile):
            body(tile, pl.ds(pl.multiple_of(tile * CLUSTER, CLUSTER), CLUSTER))

    def first_norm(tile, at):
        normal, _ = normalize(attn_res[at, :])
        values = normal * gain_attn + shift_attn
        normed[at, :] = values
        hidden[at, :] = values.astype(BF16)

    row_tiles(first_norm)
    hidden_t[...] = hidden[...].T
    load.wait()

    blks = width // share

    @pl.loop(0, blks)
    def _(blk):
        source = pl.ds(pl.multiple_of(blk * share, share), share)
        for j in range(fold):
            target = pl.ds(pl.multiple_of(blk * share * fold + j * share, share), share)
            for head in range(heads):
                down[target, head * short : (head + 1) * short] = packed[
                    head, source, width + j * short : width + (j + 1) * short
                ]

    per_head = width // 256

    @pl.loop(0, ff // 256)
    def _(tile):
        cols = pl.ds(pl.multiple_of(tile * 256, 256), 256)
        inner = pl.ds(pl.multiple_of(tile % per_head * 256, 256), 256)
        pre = jnp.dot(
            hidden[...], packed[tile // per_head, :, inner], preferred_element_type=F32
        )
        pre = pre + up_bias[:, cols]
        below = 0.5 + 0.5 * lax.erf(pre * (0.5**0.5))
        active[:, cols] = (pre * below).astype(BF16)
        slope[:, cols] = below + pre * jnp.exp(-0.5 * pre * pre) * (0.5 / jnp.pi) ** 0.5

    @pl.loop(0, width // 256)
    def _(tile):
        cols = pl.ds(pl.multiple_of(tile * 256, 256), 256)
        sums = jnp.dot(active[...], down[:, cols], preferred_element_type=F32)
        ffn_res[:, cols] = normed[:, cols] + sums + vectors[5:6, cols]

    def second_norm(tile, at):
        normal, scale = normalize(ffn_res[at, :])
        result = (normal * gain_ffn + shift_ffn).astype(BF16)
        micro = tile * CLUSTER // rows
        inner = pl.ds(pl.multiple_of(tile * CLUSTER % rows, CLUSTER), CLUSTER)
        for which in range(splits):
            layer_out[micro * splits + which, inner, :] = result[
                :, which * part : (which + 1) * part
            ]
        cotangent = jnp.concatenate(
            [slots_g[micro * splits + which, inner, :] for which in range(splits)], axis=1
        ).astype(F32)
        d_ffn = norm_derivative(normal, scale, cotangent, gain_ffn)
        low = d_ffn.astype(BF16)
        g_down[at, :] = low
        ffn_res[at, :] = d_ffn
        vec_grads[5:6, :] += column_sum(low.astype(F32))
        vec_grads[6:7, :] += column_sum(cotangent * normal)
        vec_grads[7:8, :] += column_sum(cotangent)

    row_tiles(second_norm)

    @pl.loop(0, ff // 256)
    def _(tile):
        cols = pl.ds(pl.multiple_of(tile * 256, 256), 256)
        inner = pl.ds(pl.multiple_of(tile % per_head * 256, 256), 256)
        d_active = contract(g_down[...], down[cols, :], (1, 1))
        low = (d_active * slope[:, cols]).astype(BF16)
        g_pre[:, cols] = low
        up_bias_grad[:, cols] = column_sum(low.astype(F32))
        up_grad = jnp.dot(hidden_t[...], low, preferred_element_type=F32)
        partial[tile // per_head, :, inner] = up_grad.astype(BF16)

    @pl.loop(0, blks)
    def _(blk):
        wide = share * fold
        cols = pl.ds(pl.multiple_of(blk * wide, wide), wide)
        down_grad = contract(active[:, cols], g_down[...], (0, 0)).astype(BF16)
        target = pl.ds(pl.multiple_of(blk * share, share), share)
        for j in range(fold):
            for head in range(heads):
                partial[head, target, width + j * short : width + (j + 1) * short] = down_grad[
                    j * share : (j + 1) * share, head * short : (head + 1) * short
                ]

    @pl.loop(0, width // 256)
    def _(tile):
        cols = pl.ds(pl.multiple_of(tile * 256, 256), 256)
        sums = ffn_res[:, cols]
        for head in range(heads):
            sums = sums + contract(
                g_pre[:, head * width : (head + 1) * width], packed[head, cols, 0:width], (1, 1)
            )
        normed[:, cols] = sums

    def first_norm_back(tile, at):
        normal, scale = normalize(attn_res[at, :])
        cotangent = normed[at, :]
        grad = norm_derivative(normal, scale, cotangent, gain_attn)
        low = grad.astype(BF16)
        d_attn[at, :] = grad
        g_attn[at, :] = low
        vec_grads[2:3, :] += column_sum(low.astype(F32))
        vec_grads[3:4, :] += column_sum(cotangent * normal)
        vec_grads[4:5, :] += column_sum(cotangent)

    row_tiles(first_norm_back)


def ffn_part(share, attn_res, slots_g, weights, vectors, up_bias):
    heads = weights.shape[0]
    tokens, width = attn_res.shape
    ff = up_bias.shape[1]
    vmem = pl.BlockSpec(memory_space=pltpu.VMEM)
    return pl.pallas_call(
        functools.partial(ffn_kernel, share),
        name="ffn_part",
        out_shape=(
            jax.ShapeDtypeStruct(slots_g.shape, BF16),
            jax.ShapeDtypeStruct((tokens, width), F32),
            jax.ShapeDtypeStruct((tokens, width), BF16),
            jax.ShapeDtypeStruct((heads, width, 2 * width), BF16),
            jax.ShapeDtypeStruct((8, width), F32),
            jax.ShapeDtypeStruct((1, ff), F32),
        ),
        in_specs=[vmem, vmem, pl.BlockSpec(memory_space=pl.ANY), vmem, vmem],
        out_specs=(vmem,) * 6,
        scratch_shapes=[
            pltpu.VMEM((heads, width, 2 * width), BF16),
            pltpu.VMEM((ff, width), BF16),
            pltpu.VMEM((tokens, width), F32),
            pltpu.VMEM((tokens, width), BF16),
            pltpu.VMEM((width, tokens), BF16),
            pltpu.VMEM((tokens, ff), BF16),
            pltpu.VMEM((tokens, ff), F32),
            pltpu.VMEM((tokens, ff), BF16),
            pltpu.VMEM((tokens, width), F32),
            pltpu.VMEM((tokens, width), BF16),
            pltpu.SemaphoreType.DMA((1,)),
        ],
        compiler_params=pltpu.CompilerParams(vmem_limit_bytes=60 << 20),
    )(attn_res, slots_g, weights, vectors, up_bias)


def attend_back(proj, probs, g_context, g_proj):
    tokens, width = g_context.shape
    first = iota((CLUSTER, 128), 1) < HEAD_DIM

    @pl.loop(0, tokens // CLUSTER)
    def _(cluster):
        rows = pl.ds(pl.multiple_of(cluster * CLUSTER, CLUSTER), CLUSTER)
        for pair in range(width // 128):
            at = pair * 128
            q = two_heads(proj[rows, at : at + 128], first)
            k = proj[rows, width + at : width + at + 128]
            v = proj[rows, 2 * width + at : 2 * width + at + 128]
            g = two_heads(g_context[rows, at : at + 128], first)
            low = probs[cluster, pair]
            p = low.astype(F32)
            dprob = contract(g, v, (1, 1))
            delta = jnp.sum(p * dprob, axis=1, keepdims=True)
            dscore = (p * (dprob - delta)).astype(BF16)
            both = jnp.dot(dscore, k, preferred_element_type=F32)
            g_q = jnp.where(first, both[:CLUSTER], both[CLUSTER:]) * 0.125
            g_k = contract(dscore, q, (0, 0)) * 0.125
            g_v = contract(low, g, (0, 0))
            g_proj[rows, at : at + 128] = g_q.astype(BF16)
            g_proj[rows, width + at : width + at + 128] = g_k.astype(BF16)
            g_proj[rows, 2 * width + at : 2 * width + at + 128] = g_v.astype(BF16)


def backward_kernel(
    x,
    proj,
    probs,
    context,
    qkv,
    out,
    d_attn,
    g_attn,
    x_grad,
    partial,
    vec_grads,
    g_context,
    g_proj,
    x_t,
    natural,
):
    heads, rows, part = x_grad.shape
    tokens, width = x.shape
    splits = width // part
    wide, narrow = 3 * width // heads, width // heads
    g_context[...] = contract(g_attn[...], out[...], (1, 1)).astype(BF16)
    x_t[...] = context[...].T

    def tiles(count, body):
        @pl.loop(0, count)
        def _(tile):
            body(pl.ds(pl.multiple_of(tile * 256, 256), 256))

    def out_grad(cols):
        natural[:, cols] = jnp.dot(
            x_t[...], g_attn[:, cols], preferred_element_type=F32
        ).astype(BF16)

    tiles(width // 256, out_grad)

    @pl.loop(0, width // CLUSTER)
    def _(tile):
        at = pl.ds(pl.multiple_of(tile * CLUSTER, CLUSTER), CLUSTER)
        for head in range(heads):
            partial[head, at, wide : wide + narrow] = natural[
                at, head * narrow : (head + 1) * narrow
            ]

    attend_back(proj, probs, g_context, g_proj)
    x_t[...] = x[...].T

    def qkv_grad(cols):
        natural[:, cols] = jnp.dot(
            x_t[...], g_proj[:, cols], preferred_element_type=F32
        ).astype(BF16)

    tiles(3 * width // 256, qkv_grad)

    @pl.loop(0, width // CLUSTER)
    def _(tile):
        at = pl.ds(pl.multiple_of(tile * CLUSTER, CLUSTER), CLUSTER)
        for head in range(heads):
            partial[head, at, 0:wide] = natural[at, head * wide : (head + 1) * wide]

    vec_grads[...] = jnp.zeros_like(vec_grads)
    vec_grads[0:1, :] = column_sum(g_proj[:, 0:width].astype(F32))
    vec_grads[1:2, :] = column_sum(g_proj[:, 2 * width :].astype(F32))
    for which in range(splits):
        for piece in range(part // 128):
            at = which * part + piece * 128
            sums = d_attn[:, at : at + 128] + contract(g_proj[...], qkv[at : at + 128, :], (1, 1))
            for micro in range(heads // splits):
                x_grad[micro * splits + which, :, piece * 128 : (piece + 1) * 128] = sums[
                    micro * rows : (micro + 1) * rows
                ].astype(BF16)


def backward_part(heads, rows, x, proj, probs, context, qkv, out, d_attn, g_attn):
    tokens, width = x.shape
    part = tokens * width // (heads * rows)
    vmem = pl.BlockSpec(memory_space=pltpu.VMEM)
    return pl.pallas_call(
        backward_kernel,
        name="backward_part",
        out_shape=(
            jax.ShapeDtypeStruct((heads, rows, part), BF16),
            jax.ShapeDtypeStruct((heads, width, width), BF16),
            jax.ShapeDtypeStruct((8, width), F32),
        ),
        in_specs=[vmem] * 8,
        out_specs=(vmem,) * 3,
        scratch_shapes=[
            pltpu.VMEM((tokens, width), BF16),
            pltpu.VMEM((tokens, 3 * width), BF16),
            pltpu.VMEM((width, tokens), BF16),
            pltpu.VMEM((width, 3 * width), BF16),
        ],
        compiler_params=pltpu.CompilerParams(vmem_limit_bytes=48 << 20),
    )(x, proj, probs, context, qkv, out, d_attn, g_attn)


def refold(packed, share, other, fold):
    if share == other:
        return packed
    heads, width, wide = packed.shape
    short = wide // fold
    rows = packed.reshape(heads, width // share, share, fold, short).transpose(0, 1, 3, 2, 4)
    rows = rows.reshape(heads, width // other, fold, other, short).transpose(0, 1, 3, 2, 4)
    return rows.reshape(packed.shape)


def body(
    tokens,
    seq_lengths,
    cluster_perm,
    out_grad,
    qkv_weight,
    query_bias,
    value_bias,
    out_weight,
    out_bias,
    attn_gain,
    attn_shift,
    up_weight,
    up_bias,
    down_weight,
    down_bias,
    ffn_gain,
    ffn_shift,
):
    blks, heads = lax.axis_size("blk"), lax.axis_size("head")
    blk, head = lax.axis_index("blk"), lax.axis_index("head")
    micros, rows, width = tokens.shape
    group = rows * heads
    total_rows = cluster_perm.shape[1]
    share = qkv_weight.shape[0]
    folds = down_weight.shape[0] // share
    short = down_weight.shape[1]
    widths = [qkv_weight.shape[1], out_weight.shape[1], up_weight.shape[1], folds * short]
    edges = [sum(widths[:i]) for i in range(5)]

    shard = jnp.concatenate(
        [qkv_weight, out_weight, up_weight]
        + [down_weight[i * share : (i + 1) * share] for i in range(folds)],
        axis=1,
    )
    lanes = -(-share // 128) * 128
    small = [
        query_bias,
        value_bias,
        out_bias,
        attn_gain,
        attn_shift,
        down_bias,
        ffn_gain,
        ffn_shift,
    ]
    stacked = jnp.concatenate([jnp.stack(small), up_bias.reshape(folds, share)], axis=0)
    count = stacked.shape[0]
    vectors = jnp.pad(stacked, ((0, -count % 16), (0, lanes - share)))
    perm = cluster_perm.reshape(micros, blks, group)
    full, full_vectors, slots_x, slots_g, dest_col, slot_col = gather_all(
        blks, heads, tokens, out_grad, shard, vectors, perm
    )

    first = blk * group + head * rows
    slots = first + jnp.arange(rows, dtype=jnp.int32)
    ends = jnp.cumsum(seq_lengths, axis=1)
    positions = jnp.arange(total_rows, dtype=jnp.int32)
    segs = jnp.sum((positions[None, :, None] >= ends[:, None, :]).astype(jnp.int32), axis=2)
    slot_segs = jnp.sum(
        jnp.where(cluster_perm[:, None, :] == slots[None, :, None], segs[:, None, :], 0), axis=2
    )

    weights = full.reshape(heads, blks * share, -1)
    tall = share if share % 16 == 0 else width // 8
    if tall != share:
        weights = jnp.concatenate(
            [weights[:, :, : edges[3]], refold(weights[:, :, edges[3] :], share, tall, folds)],
            axis=2,
        )
    spread = full_vectors[:, :count, :share].astype(F32)
    vecs = spread[:, :8].transpose(1, 0, 2).reshape(8, width)
    up_vec = spread[:, 8:count].reshape(1, -1)
    bias_qkv = jnp.concatenate([vecs[0:1], jnp.zeros((1, width), F32), vecs[1:2]], axis=1)
    seg_col = jnp.broadcast_to(slot_segs.reshape(-1, 1), (micros * rows, 128))
    seg_row = slot_segs.reshape(-1, CLUSTER)
    x, proj, probs, context, attn_res, qkv, out = forward_part(
        slots_x, weights, bias_qkv, vecs, seg_col, seg_row
    )
    layer_out, d_attn, g_attn, partial_ffn, vec_ffn, up_vec_grad = ffn_part(
        tall, attn_res, slots_g, weights, vecs, up_vec
    )
    x_grad, partial_attn, vec_attn = backward_part(
        heads, rows, x, proj, probs, context, qkv, out, d_attn, g_attn
    )
    if tall != share:
        partial_ffn = jnp.concatenate(
            [partial_ffn[:, :, :width], refold(partial_ffn[:, :, width:], tall, share, folds)],
            axis=2,
        )
    partial = jnp.concatenate([partial_attn, partial_ffn], axis=2).reshape(full.shape)
    vec_grads = vec_ffn + vec_attn
    vec_parts = jnp.concatenate(
        [vec_grads.reshape(8, blks, share).transpose(1, 0, 2), up_vec_grad.reshape(blks, folds, share)],
        axis=1,
    )
    vec_parts = jnp.pad(vec_parts, ((0, 0), (0, -count % 16), (0, lanes - share)))
    out_rows, grad_rows, shard_grad, vec_sum = reduce_all(
        blks, heads, layer_out, x_grad, partial, vec_parts, dest_col, slot_col
    )
    down_grad = shard_grad[:, edges[3] : edges[4]]
    down_grad = jnp.concatenate(
        [down_grad[:, i * short : (i + 1) * short] for i in range(folds)], axis=0
    )
    vec = [vec_sum[i, :share] for i in range(8)]
    return (
        out_rows,
        grad_rows,
        shard_grad[:, edges[0] : edges[1]],
        vec[0],
        vec[1],
        shard_grad[:, edges[1] : edges[2]],
        vec[2],
        vec[3],
        vec[4],
        shard_grad[:, edges[2] : edges[3]],
        vec_sum[8:count, :share].reshape(-1),
        down_grad,
        vec[5],
        vec[6],
        vec[7],
    )


def solution(mesh):
    return jax.shard_map(
        body,
        mesh=mesh,
        in_specs=(
            P(None, ("blk", "head"), None),
            P(),
            P(),
            P(None, ("blk", "head"), None),
            P("blk", "head"),
            P("blk"),
            P("blk"),
            P("blk", "head"),
            P("blk"),
            P("blk"),
            P("blk"),
            P("blk", "head"),
            P("blk"),
            P("blk", "head"),
            P("blk"),
            P("blk"),
            P("blk"),
        ),
        out_specs=(
            P(None, ("blk", "head"), None),
            P(None, ("blk", "head"), None),
            P("blk", "head"),
            P("blk"),
            P("blk"),
            P("blk", "head"),
            P("blk"),
            P("blk"),
            P("blk"),
            P("blk", "head"),
            P("blk"),
            P("blk", "head"),
            P("blk"),
            P("blk"),
            P("blk"),
        ),
        check_vma=False,
    )
```

```python
import functools
import types

import jax
import jax.numpy as jnp
from jax import lax
from jax.experimental import pallas as pl
from jax.experimental.pallas import tpu as pltpu
from jax.sharding import PartitionSpec as P

HEAD_DIM = 64
CLUSTER = 128
MESH = pl.DeviceIdType.MESH
BF16 = jnp.bfloat16
F32 = jnp.float32

masked_score = -1e30
norm_epsilon = 1e-05


def bits_of(index, count):
    return [(index // (1 << i)) % 2 for i in range(count)]


def flip(index, mask, bits):
    for i, bit in enumerate(bits):
        if mask & (1 << i):
            index = index + (1 - 2 * bit) * (1 << i)
    return index


def submasks(dims):
    masks = [0]
    for dim in dims:
        masks = masks + [mask | (1 << dim) for mask in masks]
    return masks


def choose(index, values):
    result = values[-1]
    for position in range(len(values) - 2, -1, -1):
        result = jnp.where(index == position, values[position], result)
    return result


class Sends:
    def __init__(self):
        self.pending = []

    def start(self, make, when=None):
        if when is None:
            make().start()
        else:

            @pl.when(when)
            def _():
                make().start()

        self.pending.append((make, when))

    def finish(self):
        pending, self.pending = self.pending, []
        for make, when in pending:
            if when is None:
                make().wait_send()
            else:

                @pl.when(when)
                def _(make=make):
                    make().wait_send()


def remote(src, dst, send_sem, recv_sem, device):
    return pltpu.make_async_remote_copy(
        src_ref=src,
        dst_ref=dst,
        send_sem=send_sem,
        recv_sem=recv_sem,
        device_id=device,
        device_id_type=MESH,
    )


def enter(blk, head, blks, heads):
    barrier = pltpu.get_barrier_semaphore()
    for other in range(blks):

        @pl.when(other != blk)
        def _():
            pl.semaphore_signal(barrier, inc=1, device_id=(other, head), device_id_type=MESH)

    for other in range(heads):

        @pl.when(other != head)
        def _():
            pl.semaphore_signal(barrier, inc=1, device_id=(blk, other), device_id_type=MESH)

    pl.semaphore_wait(barrier, blks + heads - 2)


def iota(shape, dim):
    return lax.broadcasted_iota(jnp.int32, shape, dim)


def permute_rows(one_hot_tile, source, target, rows):
    @pl.loop(0, rows // CLUSTER)
    def _(tile):
        start = pl.multiple_of(tile * CLUSTER, CLUSTER)
        chosen = jnp.dot(one_hot_tile(start), source[...], preferred_element_type=F32)
        target[pl.ds(start, CLUSTER), :] = chosen.astype(BF16)


def one_hot_from_row(row_ref):
    def tile(start):
        row = row_ref[0:1, :]
        count = row.shape[1]
        return jnp.where(iota((CLUSTER, count), 0) + start == row, 1.0, 0.0).astype(BF16)

    return tile


def one_hot_from_column(column_ref, count):
    def tile(start):
        column = column_ref[pl.ds(start, CLUSTER), 0:1]
        return jnp.where(iota((CLUSTER, count), 1) == column, 1.0, 0.0).astype(BF16)

    return tile


class RowExchange:
    def __init__(self, sends, blk, head, blks, heads, sems, tensor):
        self.sends, self.blk, self.head, self.blks, self.heads = sends, blk, head, blks, heads
        self.head_send, self.head_recv, self.blk_send, self.blk_recv, self.local = sems
        self.tensor = tensor

    def over_head(self, step, source, target):
        for other in range(self.heads):
            make = lambda other=other: remote(
                source(other),
                target(self.head),
                self.head_send.at[self.tensor, step, other],
                self.head_recv.at[self.tensor, step, self.head],
                (self.blk, other),
            )
            self.sends.start(make, when=other != self.head)

            @pl.when(other == self.head)
            def _():
                pltpu.make_async_copy(
                    source(other), target(other), self.local.at[self.tensor, step]
                ).start()

    def wait_head(self, step, target):
        for other in range(self.heads):

            @pl.when(other != self.head)
            def _():
                remote(
                    target(other),
                    target(other),
                    self.head_send.at[self.tensor, step, other],
                    self.head_recv.at[self.tensor, step, other],
                    (self.blk, other),
                ).wait_recv()

        pltpu.make_async_copy(
            target(self.head), target(self.head), self.local.at[self.tensor, step]
        ).wait()

    def over_blk(self, source, target):
        for other in range(self.blks):
            make = lambda other=other: remote(
                source(other),
                target(self.blk),
                self.blk_send.at[self.tensor, other],
                self.blk_recv.at[self.tensor, self.blk],
                (other, self.head),
            )
            self.sends.start(make, when=other != self.blk)

            @pl.when(other == self.blk)
            def _():
                pltpu.make_async_copy(
                    source(other), target(other), self.local.at[self.tensor, 2]
                ).start()

    def wait_blk(self, target):
        for other in range(self.blks):

            @pl.when(other != self.blk)
            def _():
                remote(
                    target(other),
                    target(other),
                    self.blk_send.at[self.tensor, other],
                    self.blk_recv.at[self.tensor, other],
                    (other, self.head),
                ).wait_recv()

        pltpu.make_async_copy(
            target(self.blk), target(self.blk), self.local.at[self.tensor, 2]
        ).wait()


def exchange_sems(blks, heads):
    dma = pltpu.SemaphoreType.DMA
    return [dma((2, 2, heads)), dma((2, 2, heads)), dma((2, blks)), dma((2, blks)), dma((2, 3))]


def cumulative(ones_ref, sums_ref, count):
    upper = jnp.where(iota((128, 128), 0) <= iota((128, 128), 1), 1.0, 0.0).astype(BF16)
    carry = jnp.zeros((ones_ref.shape[0], 1), F32)
    for tile in range(count // 128):
        part = ones_ref[:, tile * 128 : (tile + 1) * 128].astype(BF16)
        sums = jnp.dot(part, upper, preferred_element_type=F32) + carry
        sums_ref[:, tile * 128 : (tile + 1) * 128] = sums
        carry = sums[:, 127:128]


def gather_kernel(
    blks,
    heads,
    tokens,
    out_grad,
    shard,
    vectors,
    perm,
    full,
    full_vectors,
    slots_x,
    slots_g,
    dest_col,
    slot_col,
    arrived,
    sorted_rows,
    landed,
    ordered,
    dest_row,
    slot_row,
    ones,
    sums,
    rank_rows,
    head_send,
    head_recv,
    blk_send,
    blk_recv,
    local,
    z_send,
    z_recv,
    tree_send,
    tree_recv,
    vec_send,
    vec_recv,
    own_sem,
):
    blk, head = lax.axis_index("blk"), lax.axis_index("head")
    micros, rows, width = tokens.shape
    splits = heads // micros
    part = width // splits
    group = rows * heads
    pair = group // blks
    levels = blks.bit_length() - 1
    bits = bits_of(blk, levels)
    half = shard.shape[1] // 2
    sends = Sends()
    sems = (head_send, head_recv, blk_send, blk_recv, local)

    enter(blk, head, blks, heads)

    exchanges = [RowExchange(sends, blk, head, blks, heads, sems, i) for i in range(2)]
    sources = (tokens, out_grad)

    def send_rows(i):
        exchanges[i].over_head(
            0,
            lambda other: sources[i].at[
                other // splits, :, (other % splits) * part : (other % splits + 1) * part
            ],
            lambda other: arrived.at[i, pl.ds(pl.multiple_of(other * rows, rows), rows), :],
        )

    send_rows(0)

    def vec_copy(other):
        return remote(
            vectors, full_vectors.at[blk], vec_send.at[other], vec_recv.at[blk], (other, head)
        )

    for other in range(blks):
        sends.start(lambda other=other: vec_copy(other), when=other != blk)
    own_vec = pltpu.make_async_copy(vectors, full_vectors.at[blk], own_sem.at[0])
    own_vec.start()

    orders = [list(range(1, levels)) + [0], list(range(2, levels)) + [1, 0]]
    arrival = [
        choose(
            head,
            [
                sorted([x for x in range(heads) if x != own], key=lambda x: (abs(x - own), x))[j - 1]
                for own in range(heads)
            ],
        )
        if j
        else head
        for j in range(heads)
    ]

    def halves(ref, which):
        return ref.at[:, which * half : (which + 1) * half]

    def tree_step(j, step):
        for which in range(2):
            dims = orders[which]
            if step:
                tree_wait(j, which, step - 1)
            other = flip(blk, 1 << dims[step], bits)
            for mask in submasks(dims[:step]):
                piece = flip(blk, mask, bits)
                target = halves(full.at[arrival[j], piece], which)
                source = halves(shard, which) if j == 0 and mask == 0 else target
                slot = (1 << step) - 1 + submasks(dims[:step]).index(mask)
                make = lambda source=source, target=target, piece=piece, other=other, slot=slot, which=which: remote(
                    source,
                    target,
                    tree_send.at[j, which, slot],
                    tree_recv.at[j, which, piece],
                    (other, head),
                )
                sends.start(make)

    def tree_wait(j, which, step):
        dims = orders[which]
        other = flip(blk, 1 << dims[step], bits)
        for mask in submasks(dims[:step]):
            piece = flip(blk, mask | (1 << dims[step]), bits)
            target = halves(full.at[arrival[j], piece], which)
            remote(
                target,
                target,
                tree_send.at[j, which, 0],
                tree_recv.at[j, which, piece],
                (other, head),
            ).wait_recv()

    def chain(j):
        if j == 0:
            source = shard
            left, right = head > 0, head < heads - 1
        else:
            source = full.at[arrival[j], blk]
            left = (arrival[j] > head) & (head > 0)
            right = (arrival[j] < head) & (head < heads - 1)
            remote(
                source, source, z_send.at[0, 0], z_recv.at[arrival[j]], (blk, head)
            ).wait_recv()
        for side, (condition, step) in enumerate(((left, -1), (right, 1))):
            make = lambda source=source, side=side, step=step: remote(
                source,
                full.at[arrival[j], blk],
                z_send.at[j, side],
                z_recv.at[arrival[j]],
                (blk, jnp.clip(head + step, 0, heads - 1)),
            )
            sends.start(make, when=condition)

    tree_step(0, 0)
    chain(0)
    own_shard = pltpu.make_async_copy(shard, full.at[head, blk], own_sem.at[1])
    own_shard.start()
    send_rows(1)

    micro = head // splits
    own_slots = perm[micro, pl.ds(blk, 1), :]
    ones[...] = jnp.where(iota((blks, group), 0) == own_slots // group, 1.0, 0.0)
    cumulative(ones, sums, group)
    rank = jnp.sum(ones[...] * sums[...], axis=0, keepdims=True).astype(jnp.int32) - 1
    dest = own_slots // group * pair + rank
    dest_row[...] = jnp.broadcast_to(dest, dest_row.shape)
    for tile in range(group // 128):
        block = jnp.broadcast_to(dest[:, tile * 128 : (tile + 1) * 128].astype(F32), (128, 128))
        dest_col[tile * 128 : (tile + 1) * 128, :] = block.T.astype(jnp.int32)

    all_slots = perm[micro]
    ones[...] = jnp.where(all_slots // group == blk, 1.0, 0.0)
    cumulative(ones, sums, group)
    rank_rows[...] = jnp.where(ones[...] > 0, sums[...] - 1, -1.0).astype(jnp.int32)

    @pl.loop(0, blks)
    def _(other):
        ranks = rank_rows[pl.ds(other, 1), :]
        inner = (perm[micro, pl.ds(other, 1), :] % group).astype(F32)
        found = jnp.where(iota((pair, group), 0) == ranks, inner, 0.0)
        column = jnp.sum(found, axis=1, keepdims=True).astype(jnp.int32)
        slot_col[pl.ds(pl.multiple_of(other * pair, pair), pair), :] = jnp.broadcast_to(
            column, (pair, 128)
        )

    for tile in range(group // 128):
        block = slot_col[tile * 128 : (tile + 1) * 128, :].astype(F32)
        slot_row[:, tile * 128 : (tile + 1) * 128] = block.T[0:8, :].astype(jnp.int32)

    def to_groups(i):
        exchanges[i].wait_head(
            0, lambda other: arrived.at[i, pl.ds(pl.multiple_of(other * rows, rows), rows), :]
        )
        permute_rows(one_hot_from_row(dest_row), arrived.at[i], sorted_rows.at[i], group)
        exchanges[i].over_blk(
            lambda other: sorted_rows.at[i, pl.ds(other * pair, pair), :],
            lambda other: landed.at[i, pl.ds(pl.multiple_of(other * pair, pair), pair), :],
        )

    outs = (slots_x, slots_g)

    def to_slots(i):
        exchanges[i].wait_blk(
            lambda other: landed.at[i, pl.ds(pl.multiple_of(other * pair, pair), pair), :]
        )
        permute_rows(one_hot_from_row(slot_row), landed.at[i], ordered.at[i], group)
        exchanges[i].over_head(
            1,
            lambda other: ordered.at[i, pl.ds(other * rows, rows), :],
            lambda other: outs[i].at[other],
        )

    to_groups(0)
    for step in range(1, levels):
        tree_step(0, step)
    for j in range(1, heads):
        chain(j)
        tree_step(j, 0)
        if j == 1:
            to_slots(0)
            to_groups(1)
        if j == 2:
            to_slots(1)
        for step in range(1, levels):
            tree_step(j, step)
    for j in range(heads):
        for which in range(2):
            tree_wait(j, which, levels - 1)

    for i in range(2):
        exchanges[i].wait_head(1, lambda other: outs[i].at[other])
    for other in range(blks):

        @pl.when(other != blk)
        def _():
            remote(
                vectors,
                full_vectors.at[other],
                vec_send.at[other],
                vec_recv.at[other],
                (other, head),
            ).wait_recv()

    own_vec.wait()
    own_shard.wait()
    sends.finish()


def gather_all(blks, heads, tokens, out_grad, shard, vectors, perm):
    micros, rows, width = tokens.shape
    part = width * micros // heads
    group = rows * heads
    dma = pltpu.SemaphoreType.DMA
    any_space, vmem = pl.BlockSpec(memory_space=pl.ANY), pl.BlockSpec(memory_space=pltpu.VMEM)
    return pl.pallas_call(
        functools.partial(gather_kernel, blks, heads),
        name="gather_all",
        out_shape=(
            jax.ShapeDtypeStruct((heads, blks) + shard.shape, BF16),
            jax.ShapeDtypeStruct((blks,) + vectors.shape, BF16),
            jax.ShapeDtypeStruct((heads, rows, part), BF16),
            jax.ShapeDtypeStruct((heads, rows, part), BF16),
            jax.ShapeDtypeStruct((group, 128), jnp.int32),
            jax.ShapeDtypeStruct((group, 128), jnp.int32),
        ),
        in_specs=[any_space, any_space, any_space, any_space, vmem],
        out_specs=(any_space, any_space, any_space, any_space, vmem, vmem),
        scratch_shapes=[
            pltpu.VMEM((2, group, part), BF16),
            pltpu.VMEM((2, group, part), BF16),
            pltpu.VMEM((2, group, part), BF16),
            pltpu.VMEM((2, group, part), BF16),
            pltpu.VMEM((8, group), jnp.int32),
            pltpu.VMEM((8, group), jnp.int32),
            pltpu.VMEM((blks, group), F32),
            pltpu.VMEM((blks, group), F32),
            pltpu.VMEM((blks, group), jnp.int32),
        ]
        + exchange_sems(blks, heads)
        + [
            dma((heads, 2)),
            dma((heads,)),
            dma((heads, 2, blks)),
            dma((heads, 2, blks)),
            dma((blks,)),
            dma((blks,)),
            dma((2,)),
        ],
        compiler_params=pltpu.CompilerParams(
            collective_id=0, has_side_effects=True, vmem_limit_bytes=32 << 20
        ),
    )(tokens, out_grad, shard, vectors, perm)


def add_into(target, source, width):
    rows = target.shape[0]
    step = 16 if rows % 16 == 0 else rows

    @pl.loop(0, rows // step)
    def _(i):
        at = pl.ds(pl.multiple_of(i * step, step), step)
        for column in range(0, target.shape[1], width):
            cols = slice(column, column + width)
            target[at, cols] = (
                target[at, cols].astype(F32) + source[at, cols].astype(F32)
            ).astype(BF16)


def reduce_kernel(
    blks,
    heads,
    layer_out,
    x_grad,
    partial,
    vectors,
    dest_col,
    slot_col,
    out_rows,
    grad_rows,
    shard,
    vec_sum,
    total,
    from_core,
    from_tree,
    from_left,
    from_right,
    vec_parts,
    vec_mid,
    vec_heads,
    arrived,
    sorted_rows,
    landed,
    ordered,
    final,
    head_send,
    head_recv,
    blk_send,
    blk_recv,
    local,
    load_sem,
    core_send,
    core_recv,
    tree_send,
    tree_recv,
    left_send,
    left_recv,
    right_send,
    right_recv,
    vec_send,
    vec_recv,
    vec_head_send,
    vec_head_recv,
):
    blk, head = lax.axis_index("blk"), lax.axis_index("head")
    micros, rows, width = out_rows.shape
    splits = heads // micros
    part = width // splits
    group = rows * heads
    pair = group // blks
    levels = blks.bit_length() - 1
    bits = bits_of(blk, levels)
    half = shard.shape[1] // 2
    sends = Sends()
    sems = (head_send, head_recv, blk_send, blk_recv, local)
    exchanges = [RowExchange(sends, blk, head, blks, heads, sems, i) for i in range(2)]
    sources = (layer_out, x_grad)

    enter(blk, head, blks, heads)

    order = []
    for i in range(heads):
        order.append(heads - 1 - i // 2 if i % 2 == 0 else i // 2)

    even = submasks(range(1, levels))
    loads = {}
    for other in order:
        for mask in even:
            piece = flip(blk, mask, bits)
            loads[other, mask] = pltpu.make_async_copy(
                partial.at[other, piece], total.at[other, mask // 2], load_sem.at[other, mask // 2]
            )
            loads[other, mask].start()
            sends.start(
                lambda other=other, mask=mask: remote(
                    partial.at[other, flip(blk, mask | 1, bits)],
                    from_core.at[other, mask // 2],
                    core_send.at[other, mask // 2],
                    core_recv.at[other, mask // 2],
                    (flip(blk, 1, bits), head),
                )
            )

    def rows_to_heads(i):
        exchanges[i].over_head(
            0,
            lambda other: sources[i].at[other],
            lambda other: arrived.at[i, pl.ds(pl.multiple_of(other * rows, rows), rows), :],
        )

    rows_to_heads(0)
    rows_to_heads(1)

    for other in range(blks):
        sends.start(
            lambda other=other: remote(
                vectors.at[other],
                vec_parts.at[blk],
                vec_send.at[other],
                vec_recv.at[blk],
                (other, head),
            ),
            when=other != blk,
        )

    def add_core(other):
        for mask in even:
            loads[other, mask].wait()
            target = from_core.at[other, mask // 2]
            remote(
                target,
                target,
                core_send.at[other, mask // 2],
                core_recv.at[other, mask // 2],
                (flip(blk, 1, bits), head),
            ).wait_recv()
            add_into(total.at[other, mask // 2], target, half)

    orders = [list(range(levels - 1, 0, -1)), [1] + list(range(levels - 1, 1, -1))]

    def cols(ref, which):
        return ref.at[:, which * half : (which + 1) * half]

    def tree_parts(which, step):
        dims = orders[which]
        free = dims[step + 1 :]
        base = sum(1 << (levels - 2 - earlier) for earlier in range(step))
        return dims[step], [(mask, base + i) for i, mask in enumerate(submasks(free))]

    def tree_start(other, step):
        for which in range(2):
            dim, parts = tree_parts(which, step)
            for mask, slot in parts:
                sends.start(
                    lambda which=which, dim=dim, mask=mask, slot=slot: remote(
                        cols(total.at[other, (mask | (1 << dim)) // 2], which),
                        from_tree.at[which, other, slot],
                        tree_send.at[which, other, slot],
                        tree_recv.at[which, other, slot],
                        (flip(blk, 1 << dim, bits), head),
                    )
                )

    def tree_add(other, step):
        for which in range(2):
            dim, parts = tree_parts(which, step)
            for mask, slot in parts:
                source = from_tree.at[which, other, slot]
                remote(
                    source,
                    source,
                    tree_send.at[which, other, slot],
                    tree_recv.at[which, other, slot],
                    (flip(blk, 1 << dim, bits), head),
                ).wait_recv()
                add_into(cols(total.at[other, mask // 2], which), source, half)

    def pass_right(goal):
        target = from_left.at[goal]

        @pl.when((head > 0) & (head <= goal))
        def _():
            remote(
                target, target, left_send.at[goal], left_recv.at[goal], (blk, head)
            ).wait_recv()
            add_into(total.at[goal, 0], target, half)

        sends.start(
            lambda: remote(
                total.at[goal, 0],
                target,
                left_send.at[goal],
                left_recv.at[goal],
                (blk, jnp.minimum(head + 1, heads - 1)),
            ),
            when=head < goal,
        )

    def pass_left(goal):
        target = from_right.at[goal]

        @pl.when((head < heads - 1) & (head >= goal))
        def _():
            remote(
                target, target, right_send.at[goal], right_recv.at[goal], (blk, head)
            ).wait_recv()
            add_into(total.at[goal, 0], target, half)

        sends.start(
            lambda: remote(
                total.at[goal, 0],
                target,
                right_send.at[goal],
                right_recv.at[goal],
                (blk, jnp.maximum(head - 1, 0)),
            ),
            when=head > goal,
        )

    def to_groups(i):
        exchanges[i].wait_head(
            0, lambda other: arrived.at[i, pl.ds(pl.multiple_of(other * rows, rows), rows), :]
        )
        permute_rows(one_hot_from_column(slot_col, group), arrived.at[i], sorted_rows.at[i], group)
        exchanges[i].over_blk(
            lambda other: sorted_rows.at[i, pl.ds(other * pair, pair), :],
            lambda other: landed.at[i, pl.ds(pl.multiple_of(other * pair, pair), pair), :],
        )

    def to_positions(i):
        exchanges[i].wait_blk(
            lambda other: landed.at[i, pl.ds(pl.multiple_of(other * pair, pair), pair), :]
        )
        permute_rows(one_hot_from_column(dest_col, group), landed.at[i], ordered.at[i], group)
        exchanges[i].over_head(
            1,
            lambda other: ordered.at[i, pl.ds(other * rows, rows), :],
            lambda other: final.at[i, other],
        )

    for other in order[:2]:
        add_core(other)
        tree_start(other, 0)
    to_groups(0)
    for other in order[2:]:
        add_core(other)
        tree_start(other, 0)
    to_groups(1)
    for other in order[:2]:
        for step in range(levels - 1):
            tree_add(other, step)
            if step < levels - 2:
                tree_start(other, step + 1)
    to_positions(0)
    for position, other in enumerate(order):
        if position >= 2:
            for step in range(levels - 1):
                tree_add(other, step)
                if step < levels - 2:
                    tree_start(other, step + 1)
        if position == 2:
            to_positions(1)

    vec_mid[...] = vectors[pl.ds(blk, 1)][0]
    for other in range(blks):

        @pl.when(other != blk)
        def _():
            remote(
                vec_parts.at[other],
                vec_parts.at[other],
                vec_send.at[other],
                vec_recv.at[other],
                (other, head),
            ).wait_recv()
            vec_mid[...] += vec_parts[other]

    for other in range(heads):
        sends.start(
            lambda other=other: remote(
                vec_mid,
                vec_heads.at[head],
                vec_head_send.at[other],
                vec_head_recv.at[head],
                (blk, other),
            ),
            when=other != head,
        )

    for i in range(heads):
        goal = heads - 1 - i
        pass_right(goal)
        pass_left(i)

    for own in range(heads):

        @pl.when(own == head)
        def _():
            shard[...] = total[own, 0].astype(F32)

    vec_sum[...] = vec_mid[...]
    for other in range(heads):

        @pl.when(other != head)
        def _():
            remote(
                vec_heads.at[other],
                vec_heads.at[other],
                vec_head_send.at[other],
                vec_head_recv.at[other],
                (blk, other),
            ).wait_recv()
            vec_sum[...] += vec_heads[other]

    for i in range(2):
        exchanges[i].wait_head(1, lambda other: final.at[i, other])
    for source in range(heads):
        micro, which = source // splits, source % splits
        out_rows[micro, :, which * part : (which + 1) * part] = final[0, source]
        grad_rows[micro, :, which * part : (which + 1) * part] = final[1, source].astype(F32)
    sends.finish()


def reduce_all(blks, heads, layer_out, x_grad, partial, vectors, dest_col, slot_col):
    _, rows, part = layer_out.shape
    micros = 2
    group = rows * heads
    width = part * heads // micros
    size = partial.shape[2:]
    half = size[1] // 2
    dma = pltpu.SemaphoreType.DMA
    any_space, vmem = pl.BlockSpec(memory_space=pl.ANY), pl.BlockSpec(memory_space=pltpu.VMEM)
    vec = vectors.shape[1:]
    return pl.pallas_call(
        functools.partial(reduce_kernel, blks, heads),
        name="reduce_all",
        out_shape=(
            jax.ShapeDtypeStruct((micros, rows, width), BF16),
            jax.ShapeDtypeStruct((micros, rows, width), F32),
            jax.ShapeDtypeStruct(size, F32),
            jax.ShapeDtypeStruct(vec, F32),
        ),
        in_specs=[any_space, any_space, any_space, vmem, vmem, vmem],
        out_specs=(vmem, vmem, vmem, vmem),
        scratch_shapes=[
            pltpu.VMEM((heads, blks // 2) + size, BF16),
            pltpu.VMEM((heads, blks // 2) + size, BF16),
            pltpu.VMEM((2, heads, blks // 2 - 1, size[0], half), BF16),
            pltpu.VMEM((heads,) + size, BF16),
            pltpu.VMEM((heads,) + size, BF16),
            pltpu.VMEM((blks,) + vec, F32),
            pltpu.VMEM(vec, F32),
            pltpu.VMEM((heads,) + vec, F32),
            pltpu.VMEM((2, group, part), BF16),
            pltpu.VMEM((2, group, part), BF16),
            pltpu.VMEM((2, group, part), BF16),
            pltpu.VMEM((2, group, part), BF16),
            pltpu.VMEM((2, heads, rows, part), BF16),
        ]
        + exchange_sems(blks, heads)
        + [
            dma((heads, blks // 2)),
            dma((heads, blks // 2)),
            dma((heads, blks // 2)),
            dma((2, heads, blks // 2 - 1)),
            dma((2, heads, blks // 2 - 1)),
            dma((heads,)),
            dma((heads,)),
            dma((heads,)),
            dma((heads,)),
            dma((blks,)),
            dma((blks,)),
            dma((heads,)),
            dma((heads,)),
        ],
        compiler_params=pltpu.CompilerParams(
            collective_id=1, has_side_effects=True, vmem_limit_bytes=56 << 20
        ),
    )(layer_out, x_grad, partial, vectors, dest_col, slot_col)


def contract(left, right, dims):
    return lax.dot_general(left, right, ((dims[:1], dims[1:]), ((), ())), preferred_element_type=F32)


def assemble_attention(packed, qkv, out):
    heads, width, _ = packed.shape
    wide, narrow = qkv.shape[1] // heads, out.shape[1] // heads

    @pl.loop(0, width // CLUSTER)
    def _(tile):
        rows = pl.ds(pl.multiple_of(tile * CLUSTER, CLUSTER), CLUSTER)
        for head in range(heads):
            qkv[rows, head * wide : (head + 1) * wide] = packed[head, rows, 0:wide]
            out[rows, head * narrow : (head + 1) * narrow] = packed[
                head, rows, wide : wide + narrow
            ]


def column_sum(values):
    return jnp.sum(values, axis=0, keepdims=True)


def row_mean(values):
    return jnp.mean(values, axis=1, keepdims=True)


def normalize(hidden):
    center = hidden - row_mean(hidden)
    scale = lax.rsqrt(row_mean(center * center) + norm_epsilon)
    return center * scale, scale


def norm_derivative(normal, scale, cotangent, gain):
    scaled = cotangent * gain
    return scale * (scaled - row_mean(scaled) - normal * row_mean(scaled * normal))


def forward_kernel(
    slots_x,
    weights,
    bias_qkv,
    vectors,
    seg_col,
    seg_row,
    x,
    proj,
    probs,
    context,
    attn_res,
    qkv,
    out,
    packed,
    sem,
):
    heads, rows, part = slots_x.shape
    tokens, width = x.shape
    splits = width // part
    load = pltpu.make_async_copy(weights.at[:, :, 0 : packed.shape[2]], packed, sem.at[0])
    load.start()
    for source in range(heads):
        micro, which = source // splits, source % splits
        x[micro * rows : (micro + 1) * rows, which * part : (which + 1) * part] = slots_x[source]
    load.wait()
    assemble_attention(packed, qkv, out)
    project(x, qkv, bias_qkv, proj)
    attend(proj, probs, context, seg_col, seg_row)
    leave_attention(x, context, out, vectors, attn_res)


def project(x, qkv, bias_qkv, proj):
    @pl.loop(0, proj.shape[1] // 256)
    def _(tile):
        cols = pl.ds(pl.multiple_of(tile * 256, 256), 256)
        sums = jnp.dot(x[...], qkv[:, cols], preferred_element_type=F32)
        proj[:, cols] = (sums + bias_qkv[:, cols]).astype(BF16)


def two_heads(tile, first):
    zero = jnp.zeros_like(tile)
    return jnp.concatenate([jnp.where(first, tile, zero), jnp.where(first, zero, tile)], axis=0)


def attend(proj, probs, context, seg_col, seg_row):
    tokens, width = context.shape
    first = iota((CLUSTER, 128), 1) < HEAD_DIM

    @pl.loop(0, tokens // CLUSTER)
    def _(cluster):
        rows = pl.ds(pl.multiple_of(cluster * CLUSTER, CLUSTER), CLUSTER)
        column = seg_col[rows, 0:1]
        allowed = jnp.concatenate([column, column], axis=0) == seg_row[pl.ds(cluster, 1), :]
        for pair in range(width // 128):
            at = pair * 128
            q = two_heads(proj[rows, at : at + 128], first)
            k = proj[rows, width + at : width + at + 128]
            v = proj[rows, 2 * width + at : 2 * width + at + 128]
            scores = contract(q, k, (1, 1)) * 0.125
            scores = jnp.where(allowed, scores, masked_score)
            weight = jnp.exp(scores - jnp.max(scores, axis=1, keepdims=True))
            p = (weight / jnp.sum(weight, axis=1, keepdims=True)).astype(BF16)
            probs[cluster, pair] = p
            both = jnp.dot(p, v, preferred_element_type=F32)
            context[rows, at : at + 128] = jnp.where(
                first, both[:CLUSTER], both[CLUSTER:]
            ).astype(BF16)


def leave_attention(x, context, out, vectors, attn_res):
    @pl.loop(0, x.shape[1] // 256)
    def _(tile):
        cols = pl.ds(pl.multiple_of(tile * 256, 256), 256)
        sums = jnp.dot(context[...], out[:, cols], preferred_element_type=F32)
        attn_res[:, cols] = x[:, cols].astype(F32) + sums + vectors[2:3, cols]


def forward_part(slots_x, weights, bias_qkv, vectors, seg_col, seg_row):
    heads, rows, part = slots_x.shape
    width = weights.shape[1]
    tokens = heads * part * rows // width
    vmem = pl.BlockSpec(memory_space=pltpu.VMEM)
    return pl.pallas_call(
        forward_kernel,
        name="forward_part",
        out_shape=(
            jax.ShapeDtypeStruct((tokens, width), BF16),
            jax.ShapeDtypeStruct((tokens, 3 * width), BF16),
            jax.ShapeDtypeStruct((tokens // CLUSTER, width // 128, 2 * CLUSTER, CLUSTER), BF16),
            jax.ShapeDtypeStruct((tokens, width), BF16),
            jax.ShapeDtypeStruct((tokens, width), F32),
            jax.ShapeDtypeStruct((width, 3 * width), BF16),
            jax.ShapeDtypeStruct((width, width), BF16),
        ),
        in_specs=[vmem, pl.BlockSpec(memory_space=pl.ANY), vmem, vmem, vmem, vmem],
        out_specs=(vmem,) * 7,
        scratch_shapes=[
            pltpu.VMEM((heads, width, width), BF16),
            pltpu.SemaphoreType.DMA((1,)),
        ],
        compiler_params=pltpu.CompilerParams(vmem_limit_bytes=48 << 20),
    )(slots_x, weights, bias_qkv, vectors, seg_col, seg_row)


def ffn_kernel(
    share,
    attn_res,
    slots_g,
    weights,
    vectors,
    up_bias,
    layer_out,
    d_attn,
    g_attn,
    partial,
    vec_grads,
    up_bias_grad,
    packed,
    down,
    normed,
    hidden,
    hidden_t,
    active,
    slope,
    g_pre,
    ffn_res,
    g_down,
    sem,
):
    heads, rows, part = slots_g.shape
    tokens, width = attn_res.shape
    ff = active.shape[1]
    fold = ff // width
    short = width // heads
    splits = width // part
    load = pltpu.make_async_copy(weights.at[:, :, width : 3 * width], packed, sem.at[0])
    load.start()
    gain_attn, shift_attn = vectors[3:4, :], vectors[4:5, :]
    bias_down, gain_ffn, shift_ffn = vectors[5:6, :], vectors[6:7, :], vectors[7:8, :]
    vec_grads[...] = jnp.zeros_like(vec_grads)

    def row_tiles(body):
        @pl.loop(0, tokens // CLUSTER)
        def _(tile):
            body(tile, pl.ds(pl.multiple_of(tile * CLUSTER, CLUSTER), CLUSTER))

    def first_norm(tile, at):
        normal, _ = normalize(attn_res[at, :])
        values = normal * gain_attn + shift_attn
        normed[at, :] = values
        hidden[at, :] = values.astype(BF16)

    row_tiles(first_norm)
    hidden_t[...] = hidden[...].T
    load.wait()

    blks = width // share

    @pl.loop(0, blks)
    def _(blk):
        source = pl.ds(pl.multiple_of(blk * share, share), share)
        for j in range(fold):
            target = pl.ds(pl.multiple_of(blk * share * fold + j * share, share), share)
            for head in range(heads):
                down[target, head * short : (head + 1) * short] = packed[
                    head, source, width + j * short : width + (j + 1) * short
                ]

    per_head = width // 256

    @pl.loop(0, ff // 256)
    def _(tile):
        cols = pl.ds(pl.multiple_of(tile * 256, 256), 256)
        inner = pl.ds(pl.multiple_of(tile % per_head * 256, 256), 256)
        pre = jnp.dot(
            hidden[...], packed[tile // per_head, :, inner], preferred_element_type=F32
        )
        pre = pre + up_bias[:, cols]
        below = 0.5 + 0.5 * lax.erf(pre * (0.5**0.5))
        active[:, cols] = (pre * below).astype(BF16)
        slope[:, cols] = below + pre * jnp.exp(-0.5 * pre * pre) * (0.5 / jnp.pi) ** 0.5

    @pl.loop(0, width // 256)
    def _(tile):
        cols = pl.ds(pl.multiple_of(tile * 256, 256), 256)
        sums = jnp.dot(active[...], down[:, cols], preferred_element_type=F32)
        ffn_res[:, cols] = normed[:, cols] + sums + vectors[5:6, cols]

    def second_norm(tile, at):
        normal, scale = normalize(ffn_res[at, :])
        result = (normal * gain_ffn + shift_ffn).astype(BF16)
        micro = tile * CLUSTER // rows
        inner = pl.ds(pl.multiple_of(tile * CLUSTER % rows, CLUSTER), CLUSTER)
        for which in range(splits):
            layer_out[micro * splits + which, inner, :] = result[
                :, which * part : (which + 1) * part
            ]
        cotangent = jnp.concatenate(
            [slots_g[micro * splits + which, inner, :] for which in range(splits)], axis=1
        ).astype(F32)
        d_ffn = norm_derivative(normal, scale, cotangent, gain_ffn)
        low = d_ffn.astype(BF16)
        g_down[at, :] = low
        ffn_res[at, :] = d_ffn
        vec_grads[5:6, :] += column_sum(low.astype(F32))
        vec_grads[6:7, :] += column_sum(cotangent * normal)
        vec_grads[7:8, :] += column_sum(cotangent)

    row_tiles(second_norm)

    @pl.loop(0, ff // 256)
    def _(tile):
        cols = pl.ds(pl.multiple_of(tile * 256, 256), 256)
        inner = pl.ds(pl.multiple_of(tile % per_head * 256, 256), 256)
        d_active = contract(g_down[...], down[cols, :], (1, 1))
        low = (d_active * slope[:, cols]).astype(BF16)
        g_pre[:, cols] = low
        up_bias_grad[:, cols] = column_sum(low.astype(F32))
        up_grad = jnp.dot(hidden_t[...], low, preferred_element_type=F32)
        partial[tile // per_head, :, inner] = up_grad.astype(BF16)

    @pl.loop(0, blks)
    def _(blk):
        wide = share * fold
        cols = pl.ds(pl.multiple_of(blk * wide, wide), wide)
        down_grad = contract(active[:, cols], g_down[...], (0, 0)).astype(BF16)
        target = pl.ds(pl.multiple_of(blk * share, share), share)
        for j in range(fold):
            for head in range(heads):
                partial[head, target, width + j * short : width + (j + 1) * short] = down_grad[
                    j * share : (j + 1) * share, head * short : (head + 1) * short
                ]

    @pl.loop(0, width // 256)
    def _(tile):
        cols = pl.ds(pl.multiple_of(tile * 256, 256), 256)
        sums = ffn_res[:, cols]
        for head in range(heads):
            sums = sums + contract(
                g_pre[:, head * width : (head + 1) * width], packed[head, cols, 0:width], (1, 1)
            )
        normed[:, cols] = sums

    def first_norm_back(tile, at):
        normal, scale = normalize(attn_res[at, :])
        cotangent = normed[at, :]
        grad = norm_derivative(normal, scale, cotangent, gain_attn)
        low = grad.astype(BF16)
        d_attn[at, :] = grad
        g_attn[at, :] = low
        vec_grads[2:3, :] += column_sum(low.astype(F32))
        vec_grads[3:4, :] += column_sum(cotangent * normal)
        vec_grads[4:5, :] += column_sum(cotangent)

    row_tiles(first_norm_back)


def ffn_part(share, attn_res, slots_g, weights, vectors, up_bias):
    heads = weights.shape[0]
    tokens, width = attn_res.shape
    ff = up_bias.shape[1]
    vmem = pl.BlockSpec(memory_space=pltpu.VMEM)
    return pl.pallas_call(
        functools.partial(ffn_kernel, share),
        name="ffn_part",
        out_shape=(
            jax.ShapeDtypeStruct(slots_g.shape, BF16),
            jax.ShapeDtypeStruct((tokens, width), F32),
            jax.ShapeDtypeStruct((tokens, width), BF16),
            jax.ShapeDtypeStruct((heads, width, 2 * width), BF16),
            jax.ShapeDtypeStruct((8, width), F32),
            jax.ShapeDtypeStruct((1, ff), F32),
        ),
        in_specs=[vmem, vmem, pl.BlockSpec(memory_space=pl.ANY), vmem, vmem],
        out_specs=(vmem,) * 6,
        scratch_shapes=[
            pltpu.VMEM((heads, width, 2 * width), BF16),
            pltpu.VMEM((ff, width), BF16),
            pltpu.VMEM((tokens, width), F32),
            pltpu.VMEM((tokens, width), BF16),
            pltpu.VMEM((width, tokens), BF16),
            pltpu.VMEM((tokens, ff), BF16),
            pltpu.VMEM((tokens, ff), F32),
            pltpu.VMEM((tokens, ff), BF16),
            pltpu.VMEM((tokens, width), F32),
            pltpu.VMEM((tokens, width), BF16),
            pltpu.SemaphoreType.DMA((1,)),
        ],
        compiler_params=pltpu.CompilerParams(vmem_limit_bytes=60 << 20),
    )(attn_res, slots_g, weights, vectors, up_bias)


def attend_back(proj, probs, g_context, g_proj):
    tokens, width = g_context.shape
    first = iota((CLUSTER, 128), 1) < HEAD_DIM

    @pl.loop(0, tokens // CLUSTER)
    def _(cluster):
        rows = pl.ds(pl.multiple_of(cluster * CLUSTER, CLUSTER), CLUSTER)
        for pair in range(width // 128):
            at = pair * 128
            q = two_heads(proj[rows, at : at + 128], first)
            k = proj[rows, width + at : width + at + 128]
            v = proj[rows, 2 * width + at : 2 * width + at + 128]
            g = two_heads(g_context[rows, at : at + 128], first)
            low = probs[cluster, pair]
            p = low.astype(F32)
            dprob = contract(g, v, (1, 1))
            delta = jnp.sum(p * dprob, axis=1, keepdims=True)
            dscore = (p * (dprob - delta)).astype(BF16)
            both = jnp.dot(dscore, k, preferred_element_type=F32)
            g_q = jnp.where(first, both[:CLUSTER], both[CLUSTER:]) * 0.125
            g_k = contract(dscore, q, (0, 0)) * 0.125
            g_v = contract(low, g, (0, 0))
            g_proj[rows, at : at + 128] = g_q.astype(BF16)
            g_proj[rows, width + at : width + at + 128] = g_k.astype(BF16)
            g_proj[rows, 2 * width + at : 2 * width + at + 128] = g_v.astype(BF16)


def backward_kernel(
    x,
    proj,
    probs,
    context,
    qkv,
    out,
    d_attn,
    g_attn,
    x_grad,
    partial,
    vec_grads,
    g_context,
    g_proj,
    x_t,
    natural,
):
    heads, rows, part = x_grad.shape
    tokens, width = x.shape
    splits = width // part
    wide, narrow = 3 * width // heads, width // heads
    g_context[...] = contract(g_attn[...], out[...], (1, 1)).astype(BF16)
    x_t[...] = context[...].T

    def tiles(count, body):
        @pl.loop(0, count)
        def _(tile):
            body(pl.ds(pl.multiple_of(tile * 256, 256), 256))

    def out_grad(cols):
        natural[:, cols] = jnp.dot(
            x_t[...], g_attn[:, cols], preferred_element_type=F32
        ).astype(BF16)

    tiles(width // 256, out_grad)

    @pl.loop(0, width // CLUSTER)
    def _(tile):
        at = pl.ds(pl.multiple_of(tile * CLUSTER, CLUSTER), CLUSTER)
        for head in range(heads):
            partial[head, at, wide : wide + narrow] = natural[
                at, head * narrow : (head + 1) * narrow
            ]

    attend_back(proj, probs, g_context, g_proj)
    x_t[...] = x[...].T

    def qkv_grad(cols):
        natural[:, cols] = jnp.dot(
            x_t[...], g_proj[:, cols], preferred_element_type=F32
        ).astype(BF16)

    tiles(3 * width // 256, qkv_grad)

    @pl.loop(0, width // CLUSTER)
    def _(tile):
        at = pl.ds(pl.multiple_of(tile * CLUSTER, CLUSTER), CLUSTER)
        for head in range(heads):
            partial[head, at, 0:wide] = natural[at, head * wide : (head + 1) * wide]

    vec_grads[...] = jnp.zeros_like(vec_grads)
    vec_grads[0:1, :] = column_sum(g_proj[:, 0:width].astype(F32))
    vec_grads[1:2, :] = column_sum(g_proj[:, 2 * width :].astype(F32))
    for which in range(splits):
        for piece in range(part // 128):
            at = which * part + piece * 128
            sums = d_attn[:, at : at + 128] + contract(g_proj[...], qkv[at : at + 128, :], (1, 1))
            for micro in range(heads // splits):
                x_grad[micro * splits + which, :, piece * 128 : (piece + 1) * 128] = sums[
                    micro * rows : (micro + 1) * rows
                ].astype(BF16)


def backward_part(heads, rows, x, proj, probs, context, qkv, out, d_attn, g_attn):
    tokens, width = x.shape
    part = tokens * width // (heads * rows)
    vmem = pl.BlockSpec(memory_space=pltpu.VMEM)
    return pl.pallas_call(
        backward_kernel,
        name="backward_part",
        out_shape=(
            jax.ShapeDtypeStruct((heads, rows, part), BF16),
            jax.ShapeDtypeStruct((heads, width, width), BF16),
            jax.ShapeDtypeStruct((8, width), F32),
        ),
        in_specs=[vmem] * 8,
        out_specs=(vmem,) * 3,
        scratch_shapes=[
            pltpu.VMEM((tokens, width), BF16),
            pltpu.VMEM((tokens, 3 * width), BF16),
            pltpu.VMEM((width, tokens), BF16),
            pltpu.VMEM((width, 3 * width), BF16),
        ],
        compiler_params=pltpu.CompilerParams(vmem_limit_bytes=48 << 20),
    )(x, proj, probs, context, qkv, out, d_attn, g_attn)


def fused_scratch(micros, rows, width, blks, heads, share, fold):
    dma = pltpu.SemaphoreType.DMA
    vmem = pltpu.VMEM
    tokens = micros * rows
    part = width * micros // heads
    group = rows * heads
    ff = width * fold
    half = width // 2
    kept = blks // 2
    levels = blks.bit_length() - 1
    return dict(
        arrived=vmem((2, group, part), BF16),
        sorted_rows=vmem((2, group, part), BF16),
        landed=vmem((2, group, part), BF16),
        ordered=vmem((2, group, part), BF16),
        slots=vmem((2, heads, rows, part), BF16),
        dest_row=vmem((8, group), jnp.int32),
        slot_row=vmem((8, group), jnp.int32),
        dest_col=vmem((group, 128), jnp.int32),
        slot_col=vmem((group, 128), jnp.int32),
        ones=vmem((blks, group), F32),
        sums=vmem((blks, group), F32),
        rank_rows=vmem((blks, group), jnp.int32),
        seg_col=vmem((tokens, 128), F32),
        seg_row=vmem((8 * (-(-tokens // CLUSTER // 8)), CLUSTER), F32),
        packed=vmem((heads, width, 3 * width), BF16),
        qkv=vmem((width, 3 * width), BF16),
        out=vmem((width, width), BF16),
        down=vmem((ff, width), BF16),
        full_vectors=vmem((blks, 16, 128), BF16),
        vectors=vmem((8, width), F32),
        bias_qkv=vmem((1, 3 * width), F32),
        up_bias=vmem((1, ff), F32),
        vec_grads=vmem((8, width), F32),
        up_bias_grad=vmem((1, ff), F32),
        x=vmem((tokens, width), BF16),
        proj=vmem((tokens, 3 * width), BF16),
        probs=vmem((tokens // CLUSTER, width // 128, 2 * CLUSTER, CLUSTER), BF16),
        context=vmem((tokens, width), BF16),
        attn_res=vmem((tokens, width), F32),
        normed=vmem((tokens, width), F32),
        hidden=vmem((tokens, width), BF16),
        turned=vmem((width, tokens), BF16),
        active=vmem((tokens, ff), BF16),
        slope=vmem((tokens, ff), BF16),
        ffn_res=vmem((tokens, width), F32),
        g_down=vmem((tokens, width), BF16),
        g_attn=vmem((tokens, width), BF16),
        staged=vmem((2, kept, share, width), BF16),
        from_tree=vmem((3, 2, heads, kept - 1, share, half), BF16),
        from_left=vmem((3, heads, share, width), BF16),
        from_right=vmem((3, heads, share, width), BF16),
        vec_split=vmem((blks, 16, 128), F32),
        vec_parts=vmem((blks, 16, 128), F32),
        vec_mid=vmem((16, 128), F32),
        vec_heads=vmem((heads, 16, 128), F32),
        head_send=dma((4, 2, heads)),
        head_recv=dma((4, 2, heads)),
        blk_send=dma((4, blks)),
        blk_recv=dma((4, blks)),
        local=dma((4, 3)),
        z_send=dma((2, heads, 2)),
        z_recv=dma((2, heads)),
        tree_send=dma((2, heads, 2, blks)),
        tree_recv=dma((2, heads, 2, blks)),
        gain_send=dma((blks,)),
        gain_recv=dma((blks,)),
        own_sem=dma((2,)),
        core_send=dma((3, heads, kept)),
        core_recv=dma((3, heads, kept)),
        stage_sem=dma((3, heads)),
        down_send=dma((3, 2, heads, kept)),
        down_recv=dma((3, 2, heads, kept)),
        left_send=dma((3, heads)),
        left_recv=dma((3, heads)),
        right_send=dma((3, heads)),
        right_recv=dma((3, heads)),
        vec_send=dma((blks,)),
        vec_recv=dma((blks,)),
        vec_head_send=dma((heads,)),
        vec_head_recv=dma((heads,)),
        out_sem=dma((3, max(heads, 3))),
    )


def fused_kernel(names, blks, heads, share, fold, *refs):
    r = types.SimpleNamespace(**dict(zip(names, refs)))
    blk, head = lax.axis_index("blk"), lax.axis_index("head")
    micros, rows, width = r.tokens.shape
    tokens = micros * rows
    splits = heads // micros
    part = width // splits
    group = rows * heads
    pair = group // blks
    ff = width * fold
    short = width // heads
    levels = blks.bit_length() - 1
    bits = bits_of(blk, levels)
    sends = Sends()
    sems = (r.head_send, r.head_recv, r.blk_send, r.blk_recv, r.local)
    exchanges = [RowExchange(sends, blk, head, blks, heads, sems, i) for i in range(4)]

    def tiles(count, size):
        def run(body):
            @pl.loop(0, count)
            def _(tile):
                body(tile, pl.ds(pl.multiple_of(tile * size, size), size))

        return run

    row_tiles = tiles(tokens // CLUSTER, CLUSTER)


    def head_block(ref, i):
        return lambda other: ref.at[i, pl.ds(pl.multiple_of(other * rows, rows), rows), :]

    def blk_block(ref, i):
        return lambda other: ref.at[i, pl.ds(pl.multiple_of(other * pair, pair), pair), :]

    def row_source(ref):
        return lambda other: ref.at[
            other // splits, :, (other % splits) * part : (other % splits + 1) * part
        ]

    def own_rows(ref):
        return lambda other: ref.at[
            other // splits * rows : (other // splits + 1) * rows,
            (other % splits) * part : (other % splits + 1) * part,
        ]

    def to_heads(i, source):
        exchanges[i].over_head(0, source, head_block(r.arrived, i % 2))

    def to_groups(i, one_hot):
        exchanges[i].wait_head(0, head_block(r.arrived, i % 2))
        permute_rows(one_hot, r.arrived.at[i % 2], r.sorted_rows.at[i % 2], group)
        exchanges[i].over_blk(blk_block(r.sorted_rows, i % 2), blk_block(r.landed, i % 2))

    def to_owners(i, one_hot):
        exchanges[i].wait_blk(blk_block(r.landed, i % 2))
        permute_rows(one_hot, r.landed.at[i % 2], r.ordered.at[i % 2], group)
        exchanges[i].over_head(
            1, head_block(r.ordered, i % 2), lambda other: r.slots.at[i % 2, other]
        )

    def rows_here(i):
        exchanges[i].wait_head(1, lambda other: r.slots.at[i % 2, other])


    parts = ((0, width), (width, 2 * width))
    orders = [list(range(1, levels)) + [0], list(range(2, levels)) + [1, 0]]
    arrival = [
        choose(
            head,
            [
                sorted([x for x in range(heads) if x != own], key=lambda x: (abs(x - own), x))[j - 1]
                for own in range(heads)
            ],
        )
        if j
        else head
        for j in range(heads)
    ]

    def piece_rows(piece):
        return pl.ds(pl.multiple_of(piece * share, share), share)

    def part_cols(p, which=None):
        base, size = parts[p]
        if which is None:
            return slice(base, base + size)
        return slice(base + which * size // 2, base + (which + 1) * size // 2)

    def tree_wait(p, j, which, step):
        dims = orders[which]
        other = flip(blk, 1 << dims[step], bits)
        for mask in submasks(dims[:step]):
            piece = flip(blk, mask | (1 << dims[step]), bits)
            target = r.packed.at[arrival[j], piece_rows(piece), part_cols(p, which)]
            remote(
                target,
                target,
                r.tree_send.at[p, j, which, 0],
                r.tree_recv.at[p, j, which, piece],
                (other, head),
            ).wait_recv()

    def tree_step(p, j, step):
        for which in range(2):
            dims = orders[which]
            if step:
                tree_wait(p, j, which, step - 1)
            if step == levels:
                continue
            other = flip(blk, 1 << dims[step], bits)
            for index, mask in enumerate(submasks(dims[:step])):
                piece = flip(blk, mask, bits)
                target = r.packed.at[arrival[j], piece_rows(piece), part_cols(p, which)]
                first = j == 0 and mask == 0
                source = r.shard.at[:, part_cols(p, which)] if first else target
                sends.start(
                    lambda source=source, target=target, piece=piece, other=other, which=which, slot=(1 << step) - 1 + index: remote(
                        source,
                        target,
                        r.tree_send.at[p, j, which, slot],
                        r.tree_recv.at[p, j, which, piece],
                        (other, head),
                    )
                )

    def chain(p, j):
        target = r.packed.at[arrival[j], piece_rows(blk), part_cols(p)]
        if j == 0:
            source = r.shard.at[:, part_cols(p)]
            left, right = head > 0, head < heads - 1
        else:
            source = target
            left = (arrival[j] > head) & (head > 0)
            right = (arrival[j] < head) & (head < heads - 1)
            remote(
                target, target, r.z_send.at[p, 0, 0], r.z_recv.at[p, arrival[j]], (blk, head)
            ).wait_recv()
        for side, (condition, step) in enumerate(((left, -1), (right, 1))):
            sends.start(
                lambda side=side, step=step: remote(
                    source,
                    target,
                    r.z_send.at[p, j, side],
                    r.z_recv.at[p, arrival[j]],
                    (blk, jnp.clip(head + step, 0, heads - 1)),
                ),
                when=condition,
            )

    def gain_copy(other, slot):
        return remote(
            r.small, r.full_vectors.at[slot], r.gain_send.at[other], r.gain_recv.at[slot], (other, head)
        )


    order = []
    for i in range(heads):
        order.append(heads - 1 - i // 2 if i % 2 == 0 else i // 2)
    even = submasks(range(1, levels))
    down_orders = [list(range(levels - 1, 0, -1)), [1] + list(range(levels - 1, 1, -1))]
    sibling = flip(blk, 1, bits)

    def group_cols(g, which=None):
        if which is None:
            return slice(g * width, (g + 1) * width)
        return slice(g * width + which * width // 2, g * width + (which + 1) * width // 2)

    def total(g, other, mask, which=None):
        return r.packed.at[other, piece_rows(flip(blk, mask, bits)), group_cols(g, which)]

    def core_start(g):
        for other in order:
            for mask in even:
                sends.start(
                    lambda other=other, mask=mask: remote(
                        total(g, other, mask | 1),
                        r.from_core.at[g, other, mask // 2],
                        r.core_send.at[g, other, mask // 2],
                        r.core_recv.at[g, other, mask // 2],
                        (sibling, head),
                    )
                )

    def core_load(g, i):
        other = order[i]
        return pltpu.make_async_copy(
            r.from_core.at[g, other], r.staged.at[i % 2], r.stage_sem.at[g, i]
        )

    def core_arrived(g, i):
        other = order[i]
        for mask in even:
            target = r.from_core.at[g, other, mask // 2]
            remote(
                target,
                target,
                r.core_send.at[g, other, mask // 2],
                r.core_recv.at[g, other, mask // 2],
                (sibling, head),
            ).wait_recv()
        core_load(g, i).start()

    def core_add(g):
        core_arrived(g, 0)
        for i, other in enumerate(order):
            if i + 1 < heads:
                core_arrived(g, i + 1)
            core_load(g, i).wait()
            for mask in even:
                add_into(total(g, other, mask), r.staged.at[i % 2, mask // 2], width)
            tree_start(g, other, 0)

    def tree_slots(which, step):
        dims = down_orders[which]
        base = sum(1 << (levels - 2 - earlier) for earlier in range(step))
        return dims[step], [(mask, base + i) for i, mask in enumerate(submasks(dims[step + 1 :]))]

    def tree_copy(g, other, which, dim, mask, slot):
        return remote(
            total(g, other, mask | (1 << dim), which),
            r.from_tree.at[g, which, other, slot],
            r.down_send.at[g, which, other, slot],
            r.down_recv.at[g, which, other, slot],
            (flip(blk, 1 << dim, bits), head),
        )

    def tree_start(g, other, step):
        for which in range(2):
            dim, slots = tree_slots(which, step)
            for mask, slot in slots:
                sends.start(
                    lambda which=which, dim=dim, mask=mask, slot=slot: tree_copy(
                        g, other, which, dim, mask, slot
                    )
                )

    def tree_add(g, other, step):
        for which in range(2):
            dim, slots = tree_slots(which, step)
            for mask, slot in slots:
                tree_copy(g, other, which, dim, mask, slot).wait_recv()
                add_into(
                    total(g, other, mask, which), r.from_tree.at[g, which, other, slot], width // 2
                )
        if step < levels - 2:
            tree_start(g, other, step + 1)

    def tree_down(g, step):
        for other in order:
            tree_add(g, other, step)

    def pass_on(g, goal):
        for target, send_sem, recv_sem, step in (
            (r.from_left.at[g, goal], r.left_send, r.left_recv, 1),
            (r.from_right.at[g, goal], r.right_send, r.right_recv, -1),
        ):
            if step == 1:
                arrives = (head > 0) & (head <= goal)
                leaves = head < goal
            else:
                arrives = (head < heads - 1) & (head >= goal)
                leaves = head > goal

            @pl.when(arrives)
            def _(target=target, send_sem=send_sem, recv_sem=recv_sem):
                remote(
                    target, target, send_sem.at[g, goal], recv_sem.at[g, goal], (blk, head)
                ).wait_recv()
                add_into(total(g, goal, 0), target, width)

            sends.start(
                lambda target=target, send_sem=send_sem, recv_sem=recv_sem, step=step: remote(
                    total(g, goal, 0),
                    target,
                    send_sem.at[g, goal],
                    recv_sem.at[g, goal],
                    (blk, jnp.clip(head + step, 0, heads - 1)),
                ),
                when=leaves,
            )


    micro = head // splits

    def find_destinations():
        own_slots = r.perm[micro, pl.ds(blk, 1), :]
        r.ones[...] = jnp.where(iota((blks, group), 0) == own_slots // group, 1.0, 0.0)
        cumulative(r.ones, r.sums, group)
        rank = column_sum(r.ones[...] * r.sums[...]).astype(jnp.int32) - 1
        dest = own_slots // group * pair + rank
        r.dest_row[...] = jnp.broadcast_to(dest, r.dest_row.shape)
        for tile in range(group // 128):
            block = jnp.broadcast_to(dest[:, tile * 128 : (tile + 1) * 128].astype(F32), (128, 128))
            r.dest_col[tile * 128 : (tile + 1) * 128, :] = block.T.astype(jnp.int32)

    def find_slots():
        r.ones[...] = jnp.where(r.perm[micro] // group == blk, 1.0, 0.0)
        cumulative(r.ones, r.sums, group)
        r.rank_rows[...] = jnp.where(r.ones[...] > 0, r.sums[...] - 1, -1.0).astype(jnp.int32)

        @pl.loop(0, blks)
        def _(other):
            ranks = r.rank_rows[pl.ds(other, 1), :]
            inner = (r.perm[micro, pl.ds(other, 1), :] % group).astype(F32)
            found = jnp.where(iota((pair, group), 0) == ranks, inner, 0.0)
            column = jnp.sum(found, axis=1, keepdims=True).astype(jnp.int32)
            r.slot_col[pl.ds(pl.multiple_of(other * pair, pair), pair), :] = jnp.broadcast_to(
                column, (pair, 128)
            )

        for tile in range(group // 128):
            block = r.slot_col[tile * 128 : (tile + 1) * 128, :].astype(F32)
            r.slot_row[:, tile * 128 : (tile + 1) * 128] = block.T[0:8, :].astype(jnp.int32)

    def find_segments():
        first = blk * group + head * rows
        for m in range(micros):
            ends = []
            for s in range(r.seq_lengths.shape[1]):
                ends.append(r.seq_lengths[m, s] + (ends[-1] if ends else 0))
            for tile in range(rows // CLUSTER):
                slot = iota((CLUSTER, group), 0) + (first + tile * CLUSTER)

                def add(other, sums):
                    position = iota((1, group), 1) + other * group
                    segment = jnp.zeros((1, group), F32)
                    for end in ends:
                        segment = segment + jnp.where(position >= end, 1.0, 0.0)
                    here = r.perm[m, pl.ds(other, 1), :] == slot
                    found = jnp.where(here, segment, 0.0)
                    return sums + sum(
                        found[:, i * 128 : (i + 1) * 128] for i in range(group // 128)
                    )

                sums = lax.fori_loop(0, blks, add, jnp.zeros((CLUSTER, 128), F32))
                column = jnp.broadcast_to(
                    jnp.sum(sums, axis=1, keepdims=True), (CLUSTER, 128)
                )
                cluster = m * (rows // CLUSTER) + tile
                r.seg_col[cluster * CLUSTER : (cluster + 1) * CLUSTER, :] = column
                r.seg_row[cluster : cluster + 1, :] = column.T[0:1, :]

    def spread_vectors():
        for b in range(blks):
            small = r.full_vectors[b].astype(F32)
            r.vectors[:, b * share : (b + 1) * share] = small[0:8, 0:share]
            for j in range(fold):
                at = (b * fold + j) * share
                r.up_bias[:, at : at + share] = small[8 + j : 9 + j, 0:share]
        r.bias_qkv[:, 0:width] = r.vectors[0:1, :]
        r.bias_qkv[:, width : 2 * width] = jnp.zeros((1, width), F32)
        r.bias_qkv[:, 2 * width :] = r.vectors[1:2, :]


    def take_rows():
        for source in range(heads):
            m, which = source // splits, source % splits
            r.x[m * rows : (m + 1) * rows, which * part : (which + 1) * part] = r.slots[0, source]

    def assemble_down():
        @pl.loop(0, width // share)
        def _(b):
            source = piece_rows(b)
            for j in range(fold):
                at = b * share * fold + j * share
                target = pl.ds(pl.multiple_of(at, share), share)
                for h in range(heads):
                    base = 2 * width + j * short
                    r.down[target, h * short : (h + 1) * short] = r.packed[
                        h, source, base : base + short
                    ]

    per_head = width // 256

    def first_norm():
        @row_tiles
        def _(tile, at):
            normal, _ = normalize(r.attn_res[at, :])
            values = normal * r.vectors[3:4, :] + r.vectors[4:5, :]
            r.normed[at, :] = values
            r.hidden[at, :] = values.astype(BF16)

        r.turned[...] = r.hidden[...].T

    def ffn_up(h):
        @tiles(per_head, 256)
        def _(tile, inner):
            inner = pl.ds(pl.multiple_of(width + tile * 256, 256), 256)
            cols = pl.ds(pl.multiple_of(h * width + tile * 256, 256), 256)
            pre = jnp.dot(r.hidden[...], r.packed[h, :, inner], preferred_element_type=F32)
            pre = pre + r.up_bias[:, cols]
            below = 0.5 + 0.5 * lax.erf(pre * (0.5**0.5))
            r.active[:, cols] = (pre * below).astype(BF16)
            bell = jnp.exp(-0.5 * pre * pre) * (0.5 / jnp.pi) ** 0.5
            r.slope[:, cols] = (below + pre * bell).astype(BF16)

    def ffn_down():
        @tiles(width // 256, 256)
        def _(tile, cols):
            sums = jnp.dot(r.active[...], r.down[:, cols], preferred_element_type=F32)
            r.ffn_res[:, cols] = r.normed[:, cols] + sums + r.vectors[5:6, cols]

    def inner_rows(tile):
        return tile * CLUSTER // rows, pl.ds(pl.multiple_of(tile * CLUSTER % rows, CLUSTER), CLUSTER)

    def second_norm():
        @row_tiles
        def _(tile, at):
            normal, _ = normalize(r.ffn_res[at, :])
            result = (normal * r.vectors[6:7, :] + r.vectors[7:8, :]).astype(BF16)
            r.hidden[at, :] = result

    def second_norm_back():
        @row_tiles
        def _(tile, at):
            normal, scale = normalize(r.ffn_res[at, :])
            m, inner = inner_rows(tile)
            cotangent = jnp.concatenate(
                [r.slots[1, m * splits + which, inner, :] for which in range(splits)], axis=1
            ).astype(F32)
            d_ffn = norm_derivative(normal, scale, cotangent, r.vectors[6:7, :])
            low = d_ffn.astype(BF16)
            r.g_down[at, :] = low
            r.ffn_res[at, :] = d_ffn
            r.vec_grads[5:6, :] += column_sum(low.astype(F32))
            r.vec_grads[6:7, :] += column_sum(cotangent * normal)
            r.vec_grads[7:8, :] += column_sum(cotangent)

    def down_gradient():
        @pl.loop(0, width // share)
        def _(b):
            wide = share * fold
            cols = pl.ds(pl.multiple_of(b * wide, wide), wide)
            turned = r.active[:, cols].T
            target = piece_rows(b)
            for which in range(2):
                grad = jnp.dot(
                    turned,
                    r.g_down[:, which * width // 2 : (which + 1) * width // 2],
                    preferred_element_type=F32,
                ).astype(BF16)
                for j in range(fold):
                    for h in range(heads // 2):
                        base = 2 * width + j * short
                        r.packed[which * heads // 2 + h, target, base : base + short] = grad[
                            j * share : (j + 1) * share, h * short : (h + 1) * short
                        ]

    def ffn_up_back():
        @tiles(ff // 256, 256)
        def _(tile, cols):
            d_active = contract(r.g_down[...], r.down[cols, :], (1, 1))
            low = (d_active * r.slope[:, cols].astype(F32)).astype(BF16)
            r.slope[:, cols] = low
            r.up_bias_grad[:, cols] = column_sum(low.astype(F32))

    def norm_cotangent():
        @tiles(width // 256, 256)
        def _(tile, cols):
            sums = r.ffn_res[:, cols]
            for h in range(heads):
                sums = sums + contract(
                    r.slope[:, h * width : (h + 1) * width],
                    r.packed[h, cols, width : 2 * width],
                    (1, 1),
                )
            r.normed[:, cols] = sums

    def up_gradient():
        @tiles(ff // 256, 256)
        def _(tile, cols):
            inner = pl.ds(pl.multiple_of(width + tile % per_head * 256, 256), 256)
            grad = jnp.dot(r.turned[...], r.slope[:, cols], preferred_element_type=F32)
            r.packed[tile // per_head, :, inner] = grad.astype(BF16)

    def first_norm_back():
        @row_tiles
        def _(tile, at):
            normal, scale = normalize(r.attn_res[at, :])
            cotangent = r.normed[at, :]
            grad = norm_derivative(normal, scale, cotangent, r.vectors[3:4, :])
            low = grad.astype(BF16)
            r.attn_res[at, :] = grad
            r.g_attn[at, :] = low
            r.vec_grads[2:3, :] += column_sum(low.astype(F32))
            r.vec_grads[3:4, :] += column_sum(cotangent * normal)
            r.vec_grads[4:5, :] += column_sum(cotangent)

    g_context = r.g_down
    x_grad = r.g_down
    g_proj = r.active
    wide = 3 * width // heads

    def out_gradient():
        r.turned[...] = r.context[...].T
        for h in range(heads):
            grad = jnp.dot(
                r.turned[...],
                r.g_attn[:, h * short : (h + 1) * short],
                preferred_element_type=F32,
            )
            r.packed[h, :, wide : wide + short] = grad.astype(BF16)

    def context_cotangent():
        @tiles(width // 256, 256)
        def _(tile, cols):
            g_context[:, cols] = contract(r.g_attn[...], r.out[cols, :], (1, 1)).astype(BF16)

    def qkv_gradient():
        r.turned[...] = r.x[...].T

        @tiles(width // 256, 256)
        def _(tile, at):
            for h in range(heads):
                grad = jnp.dot(
                    r.turned[at, :], g_proj[:, h * wide : (h + 1) * wide], preferred_element_type=F32
                )
                r.packed[h, at, 0:wide] = grad.astype(BF16)

        r.vec_grads[0:1, :] = column_sum(g_proj[:, 0:width].astype(F32))
        r.vec_grads[1:2, :] = column_sum(g_proj[:, 2 * width : 3 * width].astype(F32))

    def row_gradient():
        for which in range(splits):
            for piece in range(part // 128):
                at = which * part + piece * 128
                sums = r.attn_res[:, at : at + 128] + contract(
                    g_proj[:, 0 : 3 * width], r.qkv[at : at + 128, :], (1, 1)
                )
                x_grad[:, at : at + 128] = sums.astype(BF16)


    def split_vectors():
        r.vec_split[...] = jnp.zeros_like(r.vec_split)
        for b in range(blks):
            r.vec_split[b, 0:8, 0:share] = r.vec_grads[:, b * share : (b + 1) * share]
            for j in range(fold):
                at = (b * fold + j) * share
                r.vec_split[b, 8 + j : 9 + j, 0:share] = r.up_bias_grad[:, at : at + share]

    def vec_copy(other, slot):
        return remote(
            r.vec_split.at[other],
            r.vec_parts.at[slot],
            r.vec_send.at[other],
            r.vec_recv.at[slot],
            (other, head),
        )

    def vec_head_copy(other, slot):
        return remote(
            r.vec_mid,
            r.vec_heads.at[slot],
            r.vec_head_send.at[other],
            r.vec_head_recv.at[slot],
            (blk, other),
        )


    enter(blk, head, blks, heads)
    to_heads(0, row_source(r.tokens))
    for other in range(blks):
        sends.start(lambda other=other: gain_copy(other, blk), when=other != blk)
    own_gain = pltpu.make_async_copy(r.small, r.full_vectors.at[blk], r.own_sem.at[0])
    own_gain.start()
    for p in range(2):
        tree_step(p, 0, 0)
        chain(p, 0)
    own_shard = pltpu.make_async_copy(r.shard, r.packed.at[head, piece_rows(blk), :], r.own_sem.at[1])
    own_shard.start()
    find_destinations()
    to_groups(0, one_hot_from_row(r.dest_row))
    to_heads(1, row_source(r.out_grad))
    tree_step(0, 0, 1)
    chain(0, 1)
    tree_step(0, 1, 0)
    find_slots()
    tree_step(0, 0, 2)
    tree_step(0, 1, 1)
    chain(0, 2)
    tree_step(0, 2, 0)
    to_owners(0, one_hot_from_row(r.slot_row))
    find_segments()
    tree_step(0, 1, 2)
    tree_step(0, 2, 1)
    chain(0, 3)
    tree_step(0, 3, 0)
    tree_step(1, 0, 1)
    chain(1, 1)
    tree_step(1, 1, 0)
    tree_step(0, 2, 2)
    tree_step(0, 3, 1)
    to_groups(1, one_hot_from_row(r.dest_row))
    tree_step(1, 0, 2)
    tree_step(1, 1, 1)
    tree_step(0, 3, 2)
    for other in range(blks):

        @pl.when(other != blk)
        def _():
            gain_copy(other, other).wait_recv()

    own_gain.wait()
    own_shard.wait()
    spread_vectors()
    for j in range(heads):
        tree_step(0, j, 3)
    assemble_attention(r.packed, r.qkv, r.out)
    chain(1, 2)
    tree_step(1, 2, 0)
    rows_here(0)
    take_rows()
    project(r.x, r.qkv, r.bias_qkv, r.proj)
    tree_step(1, 1, 2)
    tree_step(1, 2, 1)
    chain(1, 3)
    tree_step(1, 3, 0)
    to_owners(1, one_hot_from_row(r.slot_row))
    attend(r.proj, r.probs, r.context, r.seg_col, r.seg_row)
    tree_step(1, 2, 2)
    tree_step(1, 3, 1)
    leave_attention(r.x, r.context, r.out, r.vectors, r.attn_res)
    first_norm()
    tree_step(1, 0, 3)
    ffn_up(arrival[0])
    tree_step(1, 3, 2)
    tree_step(1, 1, 3)
    ffn_up(arrival[1])
    tree_step(1, 2, 3)
    ffn_up(arrival[2])
    tree_step(1, 3, 3)
    ffn_up(arrival[3])
    assemble_down()
    ffn_down()
    second_norm()
    sends.finish()
    to_heads(2, own_rows(r.hidden))
    r.vec_grads[...] = jnp.zeros_like(r.vec_grads)
    rows_here(1)
    second_norm_back()
    down_gradient()
    core_start(2)
    ffn_up_back()
    norm_cotangent()
    core_add(2)
    up_gradient()
    core_start(1)
    to_groups(2, one_hot_from_column(r.slot_col, group))
    first_norm_back()
    tree_down(2, 0)
    context_cotangent()
    core_add(1)
    attend_back(r.proj, r.probs, g_context, g_proj)
    tree_down(2, 1)
    row_gradient()
    to_heads(3, own_rows(x_grad))
    to_owners(2, one_hot_from_column(r.dest_col, group))
    tree_down(1, 0)
    out_gradient()
    qkv_gradient()
    core_start(0)
    split_vectors()
    for other in range(blks):
        sends.start(lambda other=other: vec_copy(other, blk), when=other != blk)
    for i in range(heads):
        pass_on(2, order[i])
    tree_down(1, 1)
    core_add(0)
    to_groups(3, one_hot_from_column(r.slot_col, group))
    for i in range(heads):
        pass_on(1, order[i])
    tree_down(0, 0)
    r.vec_mid[...] = r.vec_split[pl.ds(blk, 1)][0]
    for other in range(blks):

        @pl.when(other != blk)
        def _():
            vec_copy(other, other).wait_recv()
            r.vec_mid[...] += r.vec_parts[other]

    for other in range(heads):
        sends.start(lambda other=other: vec_head_copy(other, head), when=other != head)
    to_owners(3, one_hot_from_column(r.dest_col, group))
    tree_down(0, 1)
    for i in range(heads):
        pass_on(0, order[i])

    def out_copy(source):
        m, which = source // splits, source % splits
        return pltpu.make_async_copy(
            r.slots.at[0, source],
            r.out_rows.at[m, :, which * part : (which + 1) * part],
            r.out_sem.at[0, source],
        )

    rows_here(2)
    for source in range(heads):
        out_copy(source).start()
    r.vec_sum[...] = r.vec_mid[...]
    for other in range(heads):

        @pl.when(other != head)
        def _():
            vec_head_copy(other, other).wait_recv()
            r.vec_sum[...] += r.vec_heads[other]

    copies = []
    for g in range(3):
        at = slice(g * share, (g + 1) * share)
        r.ffn_res[at, :] = r.packed[head, piece_rows(blk), group_cols(g)].astype(F32)
        copies.append(
            pltpu.make_async_copy(
                r.ffn_res.at[at, :], r.shard_grad.at[:, group_cols(g)], r.out_sem.at[1, g]
            )
        )
        copies[-1].start()
    rows_here(3)
    for m in range(micros):
        at = slice(m * rows, (m + 1) * rows)
        for which in range(splits):
            r.normed[at, which * part : (which + 1) * part] = r.slots[
                1, m * splits + which
            ].astype(F32)
        copies.append(
            pltpu.make_async_copy(r.normed.at[at, :], r.grad_rows.at[m], r.out_sem.at[2, m])
        )
        copies[-1].start()
    for source in range(heads):
        out_copy(source).wait()
    for copy in copies:
        copy.wait()
    sends.finish()


def fused(blks, heads, fold, tokens, out_grad, shard, small, perm, seq_lengths):
    micros, rows, width = tokens.shape
    share = shard.shape[0]
    scratch = fused_scratch(micros, rows, width, blks, heads, share, fold)
    any_space, vmem = pl.BlockSpec(memory_space=pl.ANY), pl.BlockSpec(memory_space=pltpu.VMEM)
    names = ["tokens", "out_grad", "shard", "small", "perm", "seq_lengths"]
    names += ["out_rows", "grad_rows", "shard_grad", "vec_sum", "from_core"]
    names += list(scratch)
    return pl.pallas_call(
        functools.partial(fused_kernel, names, blks, heads, share, fold),
        name="fused",
        out_shape=(
            jax.ShapeDtypeStruct((micros, rows, width), BF16),
            jax.ShapeDtypeStruct((micros, rows, width), F32),
            jax.ShapeDtypeStruct(shard.shape, F32),
            jax.ShapeDtypeStruct((16, 128), F32),
            jax.ShapeDtypeStruct((3, heads, blks // 2, share, width), BF16),
        ),
        in_specs=[any_space] * 4 + [vmem, pl.BlockSpec(memory_space=pltpu.SMEM)],
        out_specs=(any_space, any_space, any_space, vmem, any_space),
        scratch_shapes=list(scratch.values()),
        compiler_params=pltpu.CompilerParams(
            collective_id=2, has_side_effects=True, vmem_limit_bytes=64 << 20
        ),
    )(tokens, out_grad, shard, small, perm, seq_lengths)[:4]


def refold(packed, share, other, fold):
    if share == other:
        return packed
    heads, width, wide = packed.shape
    short = wide // fold
    rows = packed.reshape(heads, width // share, share, fold, short).transpose(0, 1, 3, 2, 4)
    rows = rows.reshape(heads, width // other, fold, other, short).transpose(0, 1, 3, 2, 4)
    return rows.reshape(packed.shape)


def body(
    tokens,
    seq_lengths,
    cluster_perm,
    out_grad,
    qkv_weight,
    query_bias,
    value_bias,
    out_weight,
    out_bias,
    attn_gain,
    attn_shift,
    up_weight,
    up_bias,
    down_weight,
    down_bias,
    ffn_gain,
    ffn_shift,
):
    blks, heads = lax.axis_size("blk"), lax.axis_size("head")
    blk, head = lax.axis_index("blk"), lax.axis_index("head")
    micros, rows, width = tokens.shape
    group = rows * heads
    total_rows = cluster_perm.shape[1]
    share = qkv_weight.shape[0]
    folds = down_weight.shape[0] // share
    short = down_weight.shape[1]
    widths = [qkv_weight.shape[1], out_weight.shape[1], up_weight.shape[1], folds * short]
    edges = [sum(widths[:i]) for i in range(5)]

    shard = jnp.concatenate(
        [qkv_weight, out_weight, up_weight]
        + [down_weight[i * share : (i + 1) * share] for i in range(folds)],
        axis=1,
    )
    lanes = -(-share // 128) * 128
    small = [
        query_bias,
        value_bias,
        out_bias,
        attn_gain,
        attn_shift,
        down_bias,
        ffn_gain,
        ffn_shift,
    ]
    stacked = jnp.concatenate([jnp.stack(small), up_bias.reshape(folds, share)], axis=0)
    count = stacked.shape[0]
    vectors = jnp.pad(stacked, ((0, -count % 16), (0, lanes - share)))
    perm = cluster_perm.reshape(micros, blks, group)
    if share % 16 == 0:
        out_rows, grad_rows, shard_grad, vec_sum = fused(
            blks, heads, folds, tokens, out_grad, shard, vectors, perm, seq_lengths
        )
    else:
        full, full_vectors, slots_x, slots_g, dest_col, slot_col = gather_all(
            blks, heads, tokens, out_grad, shard, vectors, perm
        )

        first = blk * group + head * rows
        slots = first + jnp.arange(rows, dtype=jnp.int32)
        ends = jnp.cumsum(seq_lengths, axis=1)
        positions = jnp.arange(total_rows, dtype=jnp.int32)
        segs = jnp.sum((positions[None, :, None] >= ends[:, None, :]).astype(jnp.int32), axis=2)
        slot_segs = jnp.sum(
            jnp.where(cluster_perm[:, None, :] == slots[None, :, None], segs[:, None, :], 0), axis=2
        )

        weights = full.reshape(heads, blks * share, -1)
        tall = share if share % 16 == 0 else width // 8
        if tall != share:
            weights = jnp.concatenate(
                [weights[:, :, : edges[3]], refold(weights[:, :, edges[3] :], share, tall, folds)],
                axis=2,
            )
        spread = full_vectors[:, :count, :share].astype(F32)
        vecs = spread[:, :8].transpose(1, 0, 2).reshape(8, width)
        up_vec = spread[:, 8:count].reshape(1, -1)
        bias_qkv = jnp.concatenate([vecs[0:1], jnp.zeros((1, width), F32), vecs[1:2]], axis=1)
        seg_col = jnp.broadcast_to(slot_segs.reshape(-1, 1), (micros * rows, 128))
        seg_row = slot_segs.reshape(-1, CLUSTER)
        x, proj, probs, context, attn_res, qkv, out = forward_part(
            slots_x, weights, bias_qkv, vecs, seg_col, seg_row
        )
        layer_out, d_attn, g_attn, partial_ffn, vec_ffn, up_vec_grad = ffn_part(
            tall, attn_res, slots_g, weights, vecs, up_vec
        )
        x_grad, partial_attn, vec_attn = backward_part(
            heads, rows, x, proj, probs, context, qkv, out, d_attn, g_attn
        )
        if tall != share:
            partial_ffn = jnp.concatenate(
                [partial_ffn[:, :, :width], refold(partial_ffn[:, :, width:], tall, share, folds)],
                axis=2,
            )
        partial = jnp.concatenate([partial_attn, partial_ffn], axis=2).reshape(full.shape)
        vec_grads = vec_ffn + vec_attn
        vec_parts = jnp.concatenate(
            [vec_grads.reshape(8, blks, share).transpose(1, 0, 2), up_vec_grad.reshape(blks, folds, share)],
            axis=1,
        )
        vec_parts = jnp.pad(vec_parts, ((0, 0), (0, -count % 16), (0, lanes - share)))
        out_rows, grad_rows, shard_grad, vec_sum = reduce_all(
            blks, heads, layer_out, x_grad, partial, vec_parts, dest_col, slot_col
        )
    down_grad = shard_grad[:, edges[3] : edges[4]]
    down_grad = jnp.concatenate(
        [down_grad[:, i * short : (i + 1) * short] for i in range(folds)], axis=0
    )
    vec = [vec_sum[i, :share] for i in range(8)]
    return (
        out_rows,
        grad_rows,
        shard_grad[:, edges[0] : edges[1]],
        vec[0],
        vec[1],
        shard_grad[:, edges[1] : edges[2]],
        vec[2],
        vec[3],
        vec[4],
        shard_grad[:, edges[2] : edges[3]],
        vec_sum[8:count, :share].reshape(-1),
        down_grad,
        vec[5],
        vec[6],
        vec[7],
    )


def solution(mesh):
    return jax.shard_map(
        body,
        mesh=mesh,
        in_specs=(
            P(None, ("blk", "head"), None),
            P(),
            P(),
            P(None, ("blk", "head"), None),
            P("blk", "head"),
            P("blk"),
            P("blk"),
            P("blk", "head"),
            P("blk"),
            P("blk"),
            P("blk"),
            P("blk", "head"),
            P("blk"),
            P("blk", "head"),
            P("blk"),
            P("blk"),
            P("blk"),
        ),
        out_specs=(
            P(None, ("blk", "head"), None),
            P(None, ("blk", "head"), None),
            P("blk", "head"),
            P("blk"),
            P("blk"),
            P("blk", "head"),
            P("blk"),
            P("blk"),
            P("blk"),
            P("blk", "head"),
            P("blk"),
            P("blk", "head"),
            P("blk"),
            P("blk"),
            P("blk"),
        ),
        check_vma=False,
    )
```

```python
import functools
import types

import jax
import jax.numpy as jnp
from jax import lax
from jax.experimental import pallas as pl
from jax.experimental.pallas import tpu as pltpu
from jax.sharding import PartitionSpec as P

HEAD_DIM = 64
CLUSTER = 128
TILE = 256
MESH = pl.DeviceIdType.MESH
BF16 = jnp.bfloat16
F32 = jnp.float32

masked_score = -1e30
norm_epsilon = 1e-05


def bits_of(index, count):
    return [(index // (1 << i)) % 2 for i in range(count)]


def flip(index, mask, bits):
    for i, bit in enumerate(bits):
        if mask & (1 << i):
            index = index + (1 - 2 * bit) * (1 << i)
    return index


def submasks(dims):
    masks = [0]
    for dim in dims:
        masks = masks + [mask | (1 << dim) for mask in masks]
    return masks


def choose(index, values):
    result = values[-1]
    for position in range(len(values) - 2, -1, -1):
        result = jnp.where(index == position, values[position], result)
    return result


class Sends:
    def __init__(self):
        self.pending = []

    def start(self, make, when=None, tag=None):
        if when is None:
            make().start()
        else:

            @pl.when(when)
            def _():
                make().start()

        self.pending.append((make, when, tag))

    def finish(self, *tags):
        pending, self.pending = self.pending, []
        for make, when, tag in pending:
            if tags and tag not in tags:
                self.pending.append((make, when, tag))
            elif when is None:
                make().wait_send()
            else:

                @pl.when(when)
                def _(make=make):
                    make().wait_send()


def remote(src, dst, send_sem, recv_sem, device):
    return pltpu.make_async_remote_copy(
        src_ref=src,
        dst_ref=dst,
        send_sem=send_sem,
        recv_sem=recv_sem,
        device_id=device,
        device_id_type=MESH,
    )


def enter(blk, head, blks, heads):
    barrier = pltpu.get_barrier_semaphore()
    for other in range(blks):

        @pl.when(other != blk)
        def _():
            pl.semaphore_signal(barrier, inc=1, device_id=(other, head), device_id_type=MESH)

    for other in range(heads):

        @pl.when(other != head)
        def _():
            pl.semaphore_signal(barrier, inc=1, device_id=(blk, other), device_id_type=MESH)

    pl.semaphore_wait(barrier, blks + heads - 2)


def iota(shape, dim):
    return lax.broadcasted_iota(jnp.int32, shape, dim)


def permute_rows(one_hot_tile, source, target, rows):
    @pl.loop(0, rows // TILE)
    def _(tile):
        start = pl.multiple_of(tile * TILE, TILE)
        chosen = jnp.dot(one_hot_tile(start), source[...], preferred_element_type=F32)
        target[pl.ds(start, TILE), :] = chosen.astype(BF16)


def one_hot_from_row(row_ref):
    def tile(start):
        row = row_ref[0:1, :]
        count = row.shape[1]
        return jnp.where(iota((TILE, count), 0) + start == row, 1.0, 0.0).astype(BF16)

    return tile


def one_hot_from_column(column_ref, count):
    def tile(start):
        column = column_ref[pl.ds(start, TILE), 0:1]
        return jnp.where(iota((TILE, count), 1) == column, 1.0, 0.0).astype(BF16)

    return tile


class RowExchange:
    def __init__(self, sends, blk, head, blks, heads, sems, tensor):
        self.sends, self.blk, self.head, self.blks, self.heads = sends, blk, head, blks, heads
        self.head_send, self.head_recv, self.blk_send, self.blk_recv, self.local = sems
        self.tensor = tensor

    def over_head(self, step, source, target):
        for other in range(self.heads):
            make = lambda other=other: remote(
                source(other),
                target(self.head),
                self.head_send.at[self.tensor, step, other],
                self.head_recv.at[self.tensor, step, self.head],
                (self.blk, other),
            )
            self.sends.start(make, when=other != self.head, tag=self.tensor)

            @pl.when(other == self.head)
            def _():
                pltpu.make_async_copy(
                    source(other), target(other), self.local.at[self.tensor, step]
                ).start()

    def wait_head(self, step, target):
        for other in range(self.heads):

            @pl.when(other != self.head)
            def _():
                remote(
                    target(other),
                    target(other),
                    self.head_send.at[self.tensor, step, other],
                    self.head_recv.at[self.tensor, step, other],
                    (self.blk, other),
                ).wait_recv()

        pltpu.make_async_copy(
            target(self.head), target(self.head), self.local.at[self.tensor, step]
        ).wait()

    def over_blk(self, source, target):
        for other in range(self.blks):
            make = lambda other=other: remote(
                source(other),
                target(self.blk),
                self.blk_send.at[self.tensor, other],
                self.blk_recv.at[self.tensor, self.blk],
                (other, self.head),
            )
            self.sends.start(make, when=other != self.blk, tag=self.tensor)

            @pl.when(other == self.blk)
            def _():
                pltpu.make_async_copy(
                    source(other), target(other), self.local.at[self.tensor, 2]
                ).start()

    def wait_blk(self, target):
        for other in range(self.blks):

            @pl.when(other != self.blk)
            def _():
                remote(
                    target(other),
                    target(other),
                    self.blk_send.at[self.tensor, other],
                    self.blk_recv.at[self.tensor, other],
                    (other, self.head),
                ).wait_recv()

        pltpu.make_async_copy(
            target(self.blk), target(self.blk), self.local.at[self.tensor, 2]
        ).wait()


def exchange_sems(blks, heads):
    dma = pltpu.SemaphoreType.DMA
    return [dma((2, 2, heads)), dma((2, 2, heads)), dma((2, blks)), dma((2, blks)), dma((2, 3))]


def cumulative(ones_ref, sums_ref, count):
    upper = jnp.where(iota((128, 128), 0) <= iota((128, 128), 1), 1.0, 0.0).astype(BF16)
    carry = jnp.zeros((ones_ref.shape[0], 1), F32)
    for tile in range(count // 128):
        part = ones_ref[:, tile * 128 : (tile + 1) * 128].astype(BF16)
        sums = jnp.dot(part, upper, preferred_element_type=F32) + carry
        sums_ref[:, tile * 128 : (tile + 1) * 128] = sums
        carry = sums[:, 127:128]


def gather_kernel(
    blks,
    heads,
    tokens,
    out_grad,
    shard,
    vectors,
    perm,
    full,
    full_vectors,
    slots_x,
    slots_g,
    dest_col,
    slot_col,
    arrived,
    sorted_rows,
    landed,
    ordered,
    dest_row,
    slot_row,
    ones,
    sums,
    rank_rows,
    head_send,
    head_recv,
    blk_send,
    blk_recv,
    local,
    z_send,
    z_recv,
    tree_send,
    tree_recv,
    vec_send,
    vec_recv,
    own_sem,
):
    blk, head = lax.axis_index("blk"), lax.axis_index("head")
    micros, rows, width = tokens.shape
    splits = heads // micros
    part = width // splits
    group = rows * heads
    pair = group // blks
    levels = blks.bit_length() - 1
    bits = bits_of(blk, levels)
    half = shard.shape[1] // 2
    sends = Sends()
    sems = (head_send, head_recv, blk_send, blk_recv, local)

    enter(blk, head, blks, heads)

    exchanges = [RowExchange(sends, blk, head, blks, heads, sems, i) for i in range(2)]
    sources = (tokens, out_grad)

    def send_rows(i):
        exchanges[i].over_head(
            0,
            lambda other: sources[i].at[
                other // splits, :, (other % splits) * part : (other % splits + 1) * part
            ],
            lambda other: arrived.at[i, pl.ds(pl.multiple_of(other * rows, rows), rows), :],
        )

    send_rows(0)

    def vec_copy(other):
        return remote(
            vectors, full_vectors.at[blk], vec_send.at[other], vec_recv.at[blk], (other, head)
        )

    for other in range(blks):
        sends.start(lambda other=other: vec_copy(other), when=other != blk)
    own_vec = pltpu.make_async_copy(vectors, full_vectors.at[blk], own_sem.at[0])
    own_vec.start()

    orders = [list(range(1, levels)) + [0], list(range(2, levels)) + [1, 0]]
    arrival = [
        choose(
            head,
            [
                sorted([x for x in range(heads) if x != own], key=lambda x: (abs(x - own), x))[j - 1]
                for own in range(heads)
            ],
        )
        if j
        else head
        for j in range(heads)
    ]

    def halves(ref, which):
        return ref.at[:, which * half : (which + 1) * half]

    def tree_step(j, step):
        for which in range(2):
            dims = orders[which]
            if step:
                tree_wait(j, which, step - 1)
            other = flip(blk, 1 << dims[step], bits)
            for mask in submasks(dims[:step]):
                piece = flip(blk, mask, bits)
                target = halves(full.at[arrival[j], piece], which)
                source = halves(shard, which) if j == 0 and mask == 0 else target
                slot = (1 << step) - 1 + submasks(dims[:step]).index(mask)
                make = lambda source=source, target=target, piece=piece, other=other, slot=slot, which=which: remote(
                    source,
                    target,
                    tree_send.at[j, which, slot],
                    tree_recv.at[j, which, piece],
                    (other, head),
                )
                sends.start(make)

    def tree_wait(j, which, step):
        dims = orders[which]
        other = flip(blk, 1 << dims[step], bits)
        for mask in submasks(dims[:step]):
            piece = flip(blk, mask | (1 << dims[step]), bits)
            target = halves(full.at[arrival[j], piece], which)
            remote(
                target,
                target,
                tree_send.at[j, which, 0],
                tree_recv.at[j, which, piece],
                (other, head),
            ).wait_recv()

    def chain(j):
        if j == 0:
            source = shard
            left, right = head > 0, head < heads - 1
        else:
            source = full.at[arrival[j], blk]
            left = (arrival[j] > head) & (head > 0)
            right = (arrival[j] < head) & (head < heads - 1)
            remote(
                source, source, z_send.at[0, 0], z_recv.at[arrival[j]], (blk, head)
            ).wait_recv()
        for side, (condition, step) in enumerate(((left, -1), (right, 1))):
            make = lambda source=source, side=side, step=step: remote(
                source,
                full.at[arrival[j], blk],
                z_send.at[j, side],
                z_recv.at[arrival[j]],
                (blk, jnp.clip(head + step, 0, heads - 1)),
            )
            sends.start(make, when=condition)

    tree_step(0, 0)
    chain(0)
    own_shard = pltpu.make_async_copy(shard, full.at[head, blk], own_sem.at[1])
    own_shard.start()
    send_rows(1)

    micro = head // splits
    own_slots = perm[micro, pl.ds(blk, 1), :]
    ones[...] = jnp.where(iota((blks, group), 0) == own_slots // group, 1.0, 0.0)
    cumulative(ones, sums, group)
    rank = jnp.sum(ones[...] * sums[...], axis=0, keepdims=True).astype(jnp.int32) - 1
    dest = own_slots // group * pair + rank
    dest_row[...] = jnp.broadcast_to(dest, dest_row.shape)
    for tile in range(group // 128):
        block = jnp.broadcast_to(dest[:, tile * 128 : (tile + 1) * 128].astype(F32), (128, 128))
        dest_col[tile * 128 : (tile + 1) * 128, :] = block.T.astype(jnp.int32)

    all_slots = perm[micro]
    ones[...] = jnp.where(all_slots // group == blk, 1.0, 0.0)
    cumulative(ones, sums, group)
    rank_rows[...] = jnp.where(ones[...] > 0, sums[...] - 1, -1.0).astype(jnp.int32)

    @pl.loop(0, blks)
    def _(other):
        ranks = rank_rows[pl.ds(other, 1), :]
        inner = (perm[micro, pl.ds(other, 1), :] % group).astype(F32)
        found = jnp.where(iota((pair, group), 0) == ranks, inner, 0.0)
        column = jnp.sum(found, axis=1, keepdims=True).astype(jnp.int32)
        slot_col[pl.ds(pl.multiple_of(other * pair, pair), pair), :] = jnp.broadcast_to(
            column, (pair, 128)
        )

    for tile in range(group // 128):
        block = slot_col[tile * 128 : (tile + 1) * 128, :].astype(F32)
        slot_row[:, tile * 128 : (tile + 1) * 128] = block.T[0:8, :].astype(jnp.int32)

    def to_groups(i):
        exchanges[i].wait_head(
            0, lambda other: arrived.at[i, pl.ds(pl.multiple_of(other * rows, rows), rows), :]
        )
        permute_rows(one_hot_from_row(dest_row), arrived.at[i], sorted_rows.at[i], group)
        exchanges[i].over_blk(
            lambda other: sorted_rows.at[i, pl.ds(other * pair, pair), :],
            lambda other: landed.at[i, pl.ds(pl.multiple_of(other * pair, pair), pair), :],
        )

    outs = (slots_x, slots_g)

    def to_slots(i):
        exchanges[i].wait_blk(
            lambda other: landed.at[i, pl.ds(pl.multiple_of(other * pair, pair), pair), :]
        )
        permute_rows(one_hot_from_row(slot_row), landed.at[i], ordered.at[i], group)
        exchanges[i].over_head(
            1,
            lambda other: ordered.at[i, pl.ds(other * rows, rows), :],
            lambda other: outs[i].at[other],
        )

    to_groups(0)
    for step in range(1, levels):
        tree_step(0, step)
    for j in range(1, heads):
        chain(j)
        tree_step(j, 0)
        if j == 1:
            to_slots(0)
            to_groups(1)
        if j == 2:
            to_slots(1)
        for step in range(1, levels):
            tree_step(j, step)
    for j in range(heads):
        for which in range(2):
            tree_wait(j, which, levels - 1)

    for i in range(2):
        exchanges[i].wait_head(1, lambda other: outs[i].at[other])
    for other in range(blks):

        @pl.when(other != blk)
        def _():
            remote(
                vectors,
                full_vectors.at[other],
                vec_send.at[other],
                vec_recv.at[other],
                (other, head),
            ).wait_recv()

    own_vec.wait()
    own_shard.wait()
    sends.finish()


def gather_all(blks, heads, tokens, out_grad, shard, vectors, perm):
    micros, rows, width = tokens.shape
    part = width * micros // heads
    group = rows * heads
    dma = pltpu.SemaphoreType.DMA
    any_space, vmem = pl.BlockSpec(memory_space=pl.ANY), pl.BlockSpec(memory_space=pltpu.VMEM)
    return pl.pallas_call(
        functools.partial(gather_kernel, blks, heads),
        name="gather_all",
        out_shape=(
            jax.ShapeDtypeStruct((heads, blks) + shard.shape, BF16),
            jax.ShapeDtypeStruct((blks,) + vectors.shape, BF16),
            jax.ShapeDtypeStruct((heads, rows, part), BF16),
            jax.ShapeDtypeStruct((heads, rows, part), BF16),
            jax.ShapeDtypeStruct((group, 128), jnp.int32),
            jax.ShapeDtypeStruct((group, 128), jnp.int32),
        ),
        in_specs=[any_space, any_space, any_space, any_space, vmem],
        out_specs=(any_space, any_space, any_space, any_space, vmem, vmem),
        scratch_shapes=[
            pltpu.VMEM((2, group, part), BF16),
            pltpu.VMEM((2, group, part), BF16),
            pltpu.VMEM((2, group, part), BF16),
            pltpu.VMEM((2, group, part), BF16),
            pltpu.VMEM((8, group), jnp.int32),
            pltpu.VMEM((8, group), jnp.int32),
            pltpu.VMEM((blks, group), F32),
            pltpu.VMEM((blks, group), F32),
            pltpu.VMEM((blks, group), jnp.int32),
        ]
        + exchange_sems(blks, heads)
        + [
            dma((heads, 2)),
            dma((heads,)),
            dma((heads, 2, blks)),
            dma((heads, 2, blks)),
            dma((blks,)),
            dma((blks,)),
            dma((2,)),
        ],
        compiler_params=pltpu.CompilerParams(
            collective_id=0, has_side_effects=True, vmem_limit_bytes=32 << 20
        ),
    )(tokens, out_grad, shard, vectors, perm)


def add_into(target, source, width):
    rows = target.shape[0]
    step = 16 if rows % 16 == 0 else rows

    @pl.loop(0, rows // step)
    def _(i):
        at = pl.ds(pl.multiple_of(i * step, step), step)
        for column in range(0, target.shape[1], width):
            cols = slice(column, column + width)
            target[at, cols] = (
                target[at, cols].astype(F32) + source[at, cols].astype(F32)
            ).astype(BF16)


def reduce_kernel(
    blks,
    heads,
    layer_out,
    x_grad,
    partial,
    vectors,
    dest_col,
    slot_col,
    out_rows,
    grad_rows,
    shard,
    vec_sum,
    total,
    from_core,
    from_tree,
    from_left,
    from_right,
    vec_parts,
    vec_mid,
    vec_heads,
    arrived,
    sorted_rows,
    landed,
    ordered,
    final,
    head_send,
    head_recv,
    blk_send,
    blk_recv,
    local,
    load_sem,
    core_send,
    core_recv,
    tree_send,
    tree_recv,
    left_send,
    left_recv,
    right_send,
    right_recv,
    vec_send,
    vec_recv,
    vec_head_send,
    vec_head_recv,
):
    blk, head = lax.axis_index("blk"), lax.axis_index("head")
    micros, rows, width = out_rows.shape
    splits = heads // micros
    part = width // splits
    group = rows * heads
    pair = group // blks
    levels = blks.bit_length() - 1
    bits = bits_of(blk, levels)
    half = shard.shape[1] // 2
    sends = Sends()
    sems = (head_send, head_recv, blk_send, blk_recv, local)
    exchanges = [RowExchange(sends, blk, head, blks, heads, sems, i) for i in range(2)]
    sources = (layer_out, x_grad)

    enter(blk, head, blks, heads)

    order = []
    for i in range(heads):
        order.append(heads - 1 - i // 2 if i % 2 == 0 else i // 2)

    even = submasks(range(1, levels))
    loads = {}
    for other in order:
        for mask in even:
            piece = flip(blk, mask, bits)
            loads[other, mask] = pltpu.make_async_copy(
                partial.at[other, piece], total.at[other, mask // 2], load_sem.at[other, mask // 2]
            )
            loads[other, mask].start()
            sends.start(
                lambda other=other, mask=mask: remote(
                    partial.at[other, flip(blk, mask | 1, bits)],
                    from_core.at[other, mask // 2],
                    core_send.at[other, mask // 2],
                    core_recv.at[other, mask // 2],
                    (flip(blk, 1, bits), head),
                )
            )

    def rows_to_heads(i):
        exchanges[i].over_head(
            0,
            lambda other: sources[i].at[other],
            lambda other: arrived.at[i, pl.ds(pl.multiple_of(other * rows, rows), rows), :],
        )

    rows_to_heads(0)
    rows_to_heads(1)

    for other in range(blks):
        sends.start(
            lambda other=other: remote(
                vectors.at[other],
                vec_parts.at[blk],
                vec_send.at[other],
                vec_recv.at[blk],
                (other, head),
            ),
            when=other != blk,
        )

    def add_core(other):
        for mask in even:
            loads[other, mask].wait()
            target = from_core.at[other, mask // 2]
            remote(
                target,
                target,
                core_send.at[other, mask // 2],
                core_recv.at[other, mask // 2],
                (flip(blk, 1, bits), head),
            ).wait_recv()
            add_into(total.at[other, mask // 2], target, half)

    orders = [list(range(levels - 1, 0, -1)), [1] + list(range(levels - 1, 1, -1))]

    def cols(ref, which):
        return ref.at[:, which * half : (which + 1) * half]

    def tree_parts(which, step):
        dims = orders[which]
        free = dims[step + 1 :]
        base = sum(1 << (levels - 2 - earlier) for earlier in range(step))
        return dims[step], [(mask, base + i) for i, mask in enumerate(submasks(free))]

    def tree_start(other, step):
        for which in range(2):
            dim, parts = tree_parts(which, step)
            for mask, slot in parts:
                sends.start(
                    lambda which=which, dim=dim, mask=mask, slot=slot: remote(
                        cols(total.at[other, (mask | (1 << dim)) // 2], which),
                        from_tree.at[which, other, slot],
                        tree_send.at[which, other, slot],
                        tree_recv.at[which, other, slot],
                        (flip(blk, 1 << dim, bits), head),
                    )
                )

    def tree_add(other, step):
        for which in range(2):
            dim, parts = tree_parts(which, step)
            for mask, slot in parts:
                source = from_tree.at[which, other, slot]
                remote(
                    source,
                    source,
                    tree_send.at[which, other, slot],
                    tree_recv.at[which, other, slot],
                    (flip(blk, 1 << dim, bits), head),
                ).wait_recv()
                add_into(cols(total.at[other, mask // 2], which), source, half)

    def pass_right(goal):
        target = from_left.at[goal]

        @pl.when((head > 0) & (head <= goal))
        def _():
            remote(
                target, target, left_send.at[goal], left_recv.at[goal], (blk, head)
            ).wait_recv()
            add_into(total.at[goal, 0], target, half)

        sends.start(
            lambda: remote(
                total.at[goal, 0],
                target,
                left_send.at[goal],
                left_recv.at[goal],
                (blk, jnp.minimum(head + 1, heads - 1)),
            ),
            when=head < goal,
        )

    def pass_left(goal):
        target = from_right.at[goal]

        @pl.when((head < heads - 1) & (head >= goal))
        def _():
            remote(
                target, target, right_send.at[goal], right_recv.at[goal], (blk, head)
            ).wait_recv()
            add_into(total.at[goal, 0], target, half)

        sends.start(
            lambda: remote(
                total.at[goal, 0],
                target,
                right_send.at[goal],
                right_recv.at[goal],
                (blk, jnp.maximum(head - 1, 0)),
            ),
            when=head > goal,
        )

    def to_groups(i):
        exchanges[i].wait_head(
            0, lambda other: arrived.at[i, pl.ds(pl.multiple_of(other * rows, rows), rows), :]
        )
        permute_rows(one_hot_from_column(slot_col, group), arrived.at[i], sorted_rows.at[i], group)
        exchanges[i].over_blk(
            lambda other: sorted_rows.at[i, pl.ds(other * pair, pair), :],
            lambda other: landed.at[i, pl.ds(pl.multiple_of(other * pair, pair), pair), :],
        )

    def to_positions(i):
        exchanges[i].wait_blk(
            lambda other: landed.at[i, pl.ds(pl.multiple_of(other * pair, pair), pair), :]
        )
        permute_rows(one_hot_from_column(dest_col, group), landed.at[i], ordered.at[i], group)
        exchanges[i].over_head(
            1,
            lambda other: ordered.at[i, pl.ds(other * rows, rows), :],
            lambda other: final.at[i, other],
        )

    for other in order[:2]:
        add_core(other)
        tree_start(other, 0)
    to_groups(0)
    for other in order[2:]:
        add_core(other)
        tree_start(other, 0)
    to_groups(1)
    for other in order[:2]:
        for step in range(levels - 1):
            tree_add(other, step)
            if step < levels - 2:
                tree_start(other, step + 1)
    to_positions(0)
    for position, other in enumerate(order):
        if position >= 2:
            for step in range(levels - 1):
                tree_add(other, step)
                if step < levels - 2:
                    tree_start(other, step + 1)
        if position == 2:
            to_positions(1)

    vec_mid[...] = vectors[pl.ds(blk, 1)][0]
    for other in range(blks):

        @pl.when(other != blk)
        def _():
            remote(
                vec_parts.at[other],
                vec_parts.at[other],
                vec_send.at[other],
                vec_recv.at[other],
                (other, head),
            ).wait_recv()
            vec_mid[...] += vec_parts[other]

    for other in range(heads):
        sends.start(
            lambda other=other: remote(
                vec_mid,
                vec_heads.at[head],
                vec_head_send.at[other],
                vec_head_recv.at[head],
                (blk, other),
            ),
            when=other != head,
        )

    for i in range(heads):
        goal = heads - 1 - i
        pass_right(goal)
        pass_left(i)

    for own in range(heads):

        @pl.when(own == head)
        def _():
            shard[...] = total[own, 0].astype(F32)

    vec_sum[...] = vec_mid[...]
    for other in range(heads):

        @pl.when(other != head)
        def _():
            remote(
                vec_heads.at[other],
                vec_heads.at[other],
                vec_head_send.at[other],
                vec_head_recv.at[other],
                (blk, other),
            ).wait_recv()
            vec_sum[...] += vec_heads[other]

    for i in range(2):
        exchanges[i].wait_head(1, lambda other: final.at[i, other])
    for source in range(heads):
        micro, which = source // splits, source % splits
        out_rows[micro, :, which * part : (which + 1) * part] = final[0, source]
        grad_rows[micro, :, which * part : (which + 1) * part] = final[1, source].astype(F32)
    sends.finish()


def reduce_all(blks, heads, layer_out, x_grad, partial, vectors, dest_col, slot_col):
    _, rows, part = layer_out.shape
    micros = 2
    group = rows * heads
    width = part * heads // micros
    size = partial.shape[2:]
    half = size[1] // 2
    dma = pltpu.SemaphoreType.DMA
    any_space, vmem = pl.BlockSpec(memory_space=pl.ANY), pl.BlockSpec(memory_space=pltpu.VMEM)
    vec = vectors.shape[1:]
    return pl.pallas_call(
        functools.partial(reduce_kernel, blks, heads),
        name="reduce_all",
        out_shape=(
            jax.ShapeDtypeStruct((micros, rows, width), BF16),
            jax.ShapeDtypeStruct((micros, rows, width), F32),
            jax.ShapeDtypeStruct(size, F32),
            jax.ShapeDtypeStruct(vec, F32),
        ),
        in_specs=[any_space, any_space, any_space, vmem, vmem, vmem],
        out_specs=(vmem, vmem, vmem, vmem),
        scratch_shapes=[
            pltpu.VMEM((heads, blks // 2) + size, BF16),
            pltpu.VMEM((heads, blks // 2) + size, BF16),
            pltpu.VMEM((2, heads, blks // 2 - 1, size[0], half), BF16),
            pltpu.VMEM((heads,) + size, BF16),
            pltpu.VMEM((heads,) + size, BF16),
            pltpu.VMEM((blks,) + vec, F32),
            pltpu.VMEM(vec, F32),
            pltpu.VMEM((heads,) + vec, F32),
            pltpu.VMEM((2, group, part), BF16),
            pltpu.VMEM((2, group, part), BF16),
            pltpu.VMEM((2, group, part), BF16),
            pltpu.VMEM((2, group, part), BF16),
            pltpu.VMEM((2, heads, rows, part), BF16),
        ]
        + exchange_sems(blks, heads)
        + [
            dma((heads, blks // 2)),
            dma((heads, blks // 2)),
            dma((heads, blks // 2)),
            dma((2, heads, blks // 2 - 1)),
            dma((2, heads, blks // 2 - 1)),
            dma((heads,)),
            dma((heads,)),
            dma((heads,)),
            dma((heads,)),
            dma((blks,)),
            dma((blks,)),
            dma((heads,)),
            dma((heads,)),
        ],
        compiler_params=pltpu.CompilerParams(
            collective_id=1, has_side_effects=True, vmem_limit_bytes=56 << 20
        ),
    )(layer_out, x_grad, partial, vectors, dest_col, slot_col)


def contract(left, right, dims):
    return lax.dot_general(left, right, ((dims[:1], dims[1:]), ((), ())), preferred_element_type=F32)


def assemble_attention(packed, qkv, out):
    heads, width, _ = packed.shape
    wide, narrow = qkv.shape[1] // heads, out.shape[1] // heads

    @pl.loop(0, width // CLUSTER)
    def _(tile):
        rows = pl.ds(pl.multiple_of(tile * CLUSTER, CLUSTER), CLUSTER)
        for head in range(heads):
            qkv[rows, head * wide : (head + 1) * wide] = packed[head, rows, 0:wide]
            out[rows, head * narrow : (head + 1) * narrow] = packed[
                head, rows, wide : wide + narrow
            ]


def column_sum(values):
    return jnp.sum(values, axis=0, keepdims=True)


def row_mean(values):
    return jnp.mean(values, axis=1, keepdims=True)


def normalize(hidden):
    center = hidden - row_mean(hidden)
    scale = lax.rsqrt(row_mean(center * center) + norm_epsilon)
    return center * scale, scale


def norm_derivative(normal, scale, cotangent, gain):
    scaled = cotangent * gain
    return scale * (scaled - row_mean(scaled) - normal * row_mean(scaled * normal))


def forward_kernel(
    slots_x,
    weights,
    bias_qkv,
    vectors,
    seg_col,
    seg_row,
    x,
    proj,
    probs,
    context,
    attn_res,
    qkv,
    out,
    packed,
    sem,
):
    heads, rows, part = slots_x.shape
    tokens, width = x.shape
    splits = width // part
    load = pltpu.make_async_copy(weights.at[:, :, 0 : packed.shape[2]], packed, sem.at[0])
    load.start()
    for source in range(heads):
        micro, which = source // splits, source % splits
        x[micro * rows : (micro + 1) * rows, which * part : (which + 1) * part] = slots_x[source]
    load.wait()
    assemble_attention(packed, qkv, out)
    project(x, qkv, bias_qkv, proj)
    attend(proj, probs, context, seg_col, seg_row)
    leave_attention(x, context, out, vectors, attn_res)


def project(x, qkv, bias_qkv, proj):
    @pl.loop(0, proj.shape[1] // 256)
    def _(tile):
        cols = pl.ds(pl.multiple_of(tile * 256, 256), 256)
        sums = jnp.dot(x[...], qkv[:, cols], preferred_element_type=F32)
        proj[:, cols] = (sums + bias_qkv[:, cols]).astype(BF16)


def two_heads(tile, first):
    zero = jnp.zeros_like(tile)
    return jnp.concatenate([jnp.where(first, tile, zero), jnp.where(first, zero, tile)], axis=0)


def attend(proj, probs, context, seg_col, seg_row):
    tokens, width = context.shape
    first = iota((CLUSTER, 128), 1) < HEAD_DIM

    @pl.loop(0, tokens // CLUSTER)
    def _(cluster):
        rows = pl.ds(pl.multiple_of(cluster * CLUSTER, CLUSTER), CLUSTER)
        column = seg_col[rows, 0:1]
        allowed = jnp.concatenate([column, column], axis=0) == seg_row[pl.ds(cluster, 1), :]
        for pair in range(width // 128):
            at = pair * 128
            q = two_heads(proj[rows, at : at + 128], first)
            k = proj[rows, width + at : width + at + 128]
            v = proj[rows, 2 * width + at : 2 * width + at + 128]
            scores = contract(q, k, (1, 1)) * 0.125
            scores = jnp.where(allowed, scores, masked_score)
            weight = jnp.exp(scores - jnp.max(scores, axis=1, keepdims=True))
            p = (weight / jnp.sum(weight, axis=1, keepdims=True)).astype(BF16)
            probs[cluster, pair] = p
            both = jnp.dot(p, v, preferred_element_type=F32)
            context[rows, at : at + 128] = jnp.where(
                first, both[:CLUSTER], both[CLUSTER:]
            ).astype(BF16)


def leave_attention(x, context, out, vectors, attn_res):
    @pl.loop(0, x.shape[1] // 256)
    def _(tile):
        cols = pl.ds(pl.multiple_of(tile * 256, 256), 256)
        sums = jnp.dot(context[...], out[:, cols], preferred_element_type=F32)
        attn_res[:, cols] = x[:, cols].astype(F32) + sums + vectors[2:3, cols]


def forward_part(slots_x, weights, bias_qkv, vectors, seg_col, seg_row):
    heads, rows, part = slots_x.shape
    width = weights.shape[1]
    tokens = heads * part * rows // width
    vmem = pl.BlockSpec(memory_space=pltpu.VMEM)
    return pl.pallas_call(
        forward_kernel,
        name="forward_part",
        out_shape=(
            jax.ShapeDtypeStruct((tokens, width), BF16),
            jax.ShapeDtypeStruct((tokens, 3 * width), BF16),
            jax.ShapeDtypeStruct((tokens // CLUSTER, width // 128, 2 * CLUSTER, CLUSTER), BF16),
            jax.ShapeDtypeStruct((tokens, width), BF16),
            jax.ShapeDtypeStruct((tokens, width), F32),
            jax.ShapeDtypeStruct((width, 3 * width), BF16),
            jax.ShapeDtypeStruct((width, width), BF16),
        ),
        in_specs=[vmem, pl.BlockSpec(memory_space=pl.ANY), vmem, vmem, vmem, vmem],
        out_specs=(vmem,) * 7,
        scratch_shapes=[
            pltpu.VMEM((heads, width, width), BF16),
            pltpu.SemaphoreType.DMA((1,)),
        ],
        compiler_params=pltpu.CompilerParams(vmem_limit_bytes=48 << 20),
    )(slots_x, weights, bias_qkv, vectors, seg_col, seg_row)


def ffn_kernel(
    share,
    attn_res,
    slots_g,
    weights,
    vectors,
    up_bias,
    layer_out,
    d_attn,
    g_attn,
    partial,
    vec_grads,
    up_bias_grad,
    packed,
    down,
    normed,
    hidden,
    hidden_t,
    active,
    slope,
    g_pre,
    ffn_res,
    g_down,
    sem,
):
    heads, rows, part = slots_g.shape
    tokens, width = attn_res.shape
    ff = active.shape[1]
    fold = ff // width
    short = width // heads
    splits = width // part
    load = pltpu.make_async_copy(weights.at[:, :, width : 3 * width], packed, sem.at[0])
    load.start()
    gain_attn, shift_attn = vectors[3:4, :], vectors[4:5, :]
    bias_down, gain_ffn, shift_ffn = vectors[5:6, :], vectors[6:7, :], vectors[7:8, :]
    vec_grads[...] = jnp.zeros_like(vec_grads)

    def row_tiles(body):
        @pl.loop(0, tokens // CLUSTER)
        def _(tile):
            body(tile, pl.ds(pl.multiple_of(tile * CLUSTER, CLUSTER), CLUSTER))

    def first_norm(tile, at):
        normal, _ = normalize(attn_res[at, :])
        values = normal * gain_attn + shift_attn
        normed[at, :] = values
        hidden[at, :] = values.astype(BF16)

    row_tiles(first_norm)
    hidden_t[...] = hidden[...].T
    load.wait()

    blks = width // share

    @pl.loop(0, blks)
    def _(blk):
        source = pl.ds(pl.multiple_of(blk * share, share), share)
        for j in range(fold):
            target = pl.ds(pl.multiple_of(blk * share * fold + j * share, share), share)
            for head in range(heads):
                down[target, head * short : (head + 1) * short] = packed[
                    head, source, width + j * short : width + (j + 1) * short
                ]

    per_head = width // 256

    @pl.loop(0, ff // 256)
    def _(tile):
        cols = pl.ds(pl.multiple_of(tile * 256, 256), 256)
        inner = pl.ds(pl.multiple_of(tile % per_head * 256, 256), 256)
        pre = jnp.dot(
            hidden[...], packed[tile // per_head, :, inner], preferred_element_type=F32
        )
        pre = pre + up_bias[:, cols]
        below = 0.5 + 0.5 * lax.erf(pre * (0.5**0.5))
        active[:, cols] = (pre * below).astype(BF16)
        slope[:, cols] = below + pre * jnp.exp(-0.5 * pre * pre) * (0.5 / jnp.pi) ** 0.5

    @pl.loop(0, width // 256)
    def _(tile):
        cols = pl.ds(pl.multiple_of(tile * 256, 256), 256)
        sums = jnp.dot(active[...], down[:, cols], preferred_element_type=F32)
        ffn_res[:, cols] = normed[:, cols] + sums + vectors[5:6, cols]

    def second_norm(tile, at):
        normal, scale = normalize(ffn_res[at, :])
        result = (normal * gain_ffn + shift_ffn).astype(BF16)
        micro = tile * CLUSTER // rows
        inner = pl.ds(pl.multiple_of(tile * CLUSTER % rows, CLUSTER), CLUSTER)
        for which in range(splits):
            layer_out[micro * splits + which, inner, :] = result[
                :, which * part : (which + 1) * part
            ]
        cotangent = jnp.concatenate(
            [slots_g[micro * splits + which, inner, :] for which in range(splits)], axis=1
        ).astype(F32)
        d_ffn = norm_derivative(normal, scale, cotangent, gain_ffn)
        low = d_ffn.astype(BF16)
        g_down[at, :] = low
        ffn_res[at, :] = d_ffn
        vec_grads[5:6, :] += column_sum(low.astype(F32))
        vec_grads[6:7, :] += column_sum(cotangent * normal)
        vec_grads[7:8, :] += column_sum(cotangent)

    row_tiles(second_norm)

    @pl.loop(0, ff // 256)
    def _(tile):
        cols = pl.ds(pl.multiple_of(tile * 256, 256), 256)
        inner = pl.ds(pl.multiple_of(tile % per_head * 256, 256), 256)
        d_active = contract(g_down[...], down[cols, :], (1, 1))
        low = (d_active * slope[:, cols]).astype(BF16)
        g_pre[:, cols] = low
        up_bias_grad[:, cols] = column_sum(low.astype(F32))
        up_grad = jnp.dot(hidden_t[...], low, preferred_element_type=F32)
        partial[tile // per_head, :, inner] = up_grad.astype(BF16)

    @pl.loop(0, blks)
    def _(blk):
        wide = share * fold
        cols = pl.ds(pl.multiple_of(blk * wide, wide), wide)
        down_grad = contract(active[:, cols], g_down[...], (0, 0)).astype(BF16)
        target = pl.ds(pl.multiple_of(blk * share, share), share)
        for j in range(fold):
            for head in range(heads):
                partial[head, target, width + j * short : width + (j + 1) * short] = down_grad[
                    j * share : (j + 1) * share, head * short : (head + 1) * short
                ]

    @pl.loop(0, width // 256)
    def _(tile):
        cols = pl.ds(pl.multiple_of(tile * 256, 256), 256)
        sums = ffn_res[:, cols]
        for head in range(heads):
            sums = sums + contract(
                g_pre[:, head * width : (head + 1) * width], packed[head, cols, 0:width], (1, 1)
            )
        normed[:, cols] = sums

    def first_norm_back(tile, at):
        normal, scale = normalize(attn_res[at, :])
        cotangent = normed[at, :]
        grad = norm_derivative(normal, scale, cotangent, gain_attn)
        low = grad.astype(BF16)
        d_attn[at, :] = grad
        g_attn[at, :] = low
        vec_grads[2:3, :] += column_sum(low.astype(F32))
        vec_grads[3:4, :] += column_sum(cotangent * normal)
        vec_grads[4:5, :] += column_sum(cotangent)

    row_tiles(first_norm_back)


def ffn_part(share, attn_res, slots_g, weights, vectors, up_bias):
    heads = weights.shape[0]
    tokens, width = attn_res.shape
    ff = up_bias.shape[1]
    vmem = pl.BlockSpec(memory_space=pltpu.VMEM)
    return pl.pallas_call(
        functools.partial(ffn_kernel, share),
        name="ffn_part",
        out_shape=(
            jax.ShapeDtypeStruct(slots_g.shape, BF16),
            jax.ShapeDtypeStruct((tokens, width), F32),
            jax.ShapeDtypeStruct((tokens, width), BF16),
            jax.ShapeDtypeStruct((heads, width, 2 * width), BF16),
            jax.ShapeDtypeStruct((8, width), F32),
            jax.ShapeDtypeStruct((1, ff), F32),
        ),
        in_specs=[vmem, vmem, pl.BlockSpec(memory_space=pl.ANY), vmem, vmem],
        out_specs=(vmem,) * 6,
        scratch_shapes=[
            pltpu.VMEM((heads, width, 2 * width), BF16),
            pltpu.VMEM((ff, width), BF16),
            pltpu.VMEM((tokens, width), F32),
            pltpu.VMEM((tokens, width), BF16),
            pltpu.VMEM((width, tokens), BF16),
            pltpu.VMEM((tokens, ff), BF16),
            pltpu.VMEM((tokens, ff), F32),
            pltpu.VMEM((tokens, ff), BF16),
            pltpu.VMEM((tokens, width), F32),
            pltpu.VMEM((tokens, width), BF16),
            pltpu.SemaphoreType.DMA((1,)),
        ],
        compiler_params=pltpu.CompilerParams(vmem_limit_bytes=60 << 20),
    )(attn_res, slots_g, weights, vectors, up_bias)


def attend_back(proj, probs, g_context, g_proj, begin=0, end=None):
    tokens, width = g_context.shape
    first = iota((CLUSTER, 128), 1) < HEAD_DIM

    @pl.loop(begin, tokens // CLUSTER if end is None else end)
    def _(cluster):
        rows = pl.ds(pl.multiple_of(cluster * CLUSTER, CLUSTER), CLUSTER)
        for pair in range(width // 128):
            at = pair * 128
            q = two_heads(proj[rows, at : at + 128], first)
            k = proj[rows, width + at : width + at + 128]
            v = proj[rows, 2 * width + at : 2 * width + at + 128]
            g = two_heads(g_context[rows, at : at + 128], first)
            low = probs[cluster, pair]
            p = low.astype(F32)
            dprob = contract(g, v, (1, 1))
            delta = jnp.sum(p * dprob, axis=1, keepdims=True)
            dscore = (p * (dprob - delta)).astype(BF16)
            both = jnp.dot(dscore, k, preferred_element_type=F32)
            g_q = jnp.where(first, both[:CLUSTER], both[CLUSTER:]) * 0.125
            g_k = contract(dscore, q, (0, 0)) * 0.125
            g_v = contract(low, g, (0, 0))
            g_proj[rows, at : at + 128] = g_q.astype(BF16)
            g_proj[rows, width + at : width + at + 128] = g_k.astype(BF16)
            g_proj[rows, 2 * width + at : 2 * width + at + 128] = g_v.astype(BF16)


def backward_kernel(
    x,
    proj,
    probs,
    context,
    qkv,
    out,
    d_attn,
    g_attn,
    x_grad,
    partial,
    vec_grads,
    g_context,
    g_proj,
    x_t,
    natural,
):
    heads, rows, part = x_grad.shape
    tokens, width = x.shape
    splits = width // part
    wide, narrow = 3 * width // heads, width // heads
    g_context[...] = contract(g_attn[...], out[...], (1, 1)).astype(BF16)
    x_t[...] = context[...].T

    def tiles(count, body):
        @pl.loop(0, count)
        def _(tile):
            body(pl.ds(pl.multiple_of(tile * 256, 256), 256))

    def out_grad(cols):
        natural[:, cols] = jnp.dot(
            x_t[...], g_attn[:, cols], preferred_element_type=F32
        ).astype(BF16)

    tiles(width // 256, out_grad)

    @pl.loop(0, width // CLUSTER)
    def _(tile):
        at = pl.ds(pl.multiple_of(tile * CLUSTER, CLUSTER), CLUSTER)
        for head in range(heads):
            partial[head, at, wide : wide + narrow] = natural[
                at, head * narrow : (head + 1) * narrow
            ]

    attend_back(proj, probs, g_context, g_proj)
    x_t[...] = x[...].T

    def qkv_grad(cols):
        natural[:, cols] = jnp.dot(
            x_t[...], g_proj[:, cols], preferred_element_type=F32
        ).astype(BF16)

    tiles(3 * width // 256, qkv_grad)

    @pl.loop(0, width // CLUSTER)
    def _(tile):
        at = pl.ds(pl.multiple_of(tile * CLUSTER, CLUSTER), CLUSTER)
        for head in range(heads):
            partial[head, at, 0:wide] = natural[at, head * wide : (head + 1) * wide]

    vec_grads[...] = jnp.zeros_like(vec_grads)
    vec_grads[0:1, :] = column_sum(g_proj[:, 0:width].astype(F32))
    vec_grads[1:2, :] = column_sum(g_proj[:, 2 * width :].astype(F32))
    for which in range(splits):
        for piece in range(part // 128):
            at = which * part + piece * 128
            sums = d_attn[:, at : at + 128] + contract(g_proj[...], qkv[at : at + 128, :], (1, 1))
            for micro in range(heads // splits):
                x_grad[micro * splits + which, :, piece * 128 : (piece + 1) * 128] = sums[
                    micro * rows : (micro + 1) * rows
                ].astype(BF16)


def backward_part(heads, rows, x, proj, probs, context, qkv, out, d_attn, g_attn):
    tokens, width = x.shape
    part = tokens * width // (heads * rows)
    vmem = pl.BlockSpec(memory_space=pltpu.VMEM)
    return pl.pallas_call(
        backward_kernel,
        name="backward_part",
        out_shape=(
            jax.ShapeDtypeStruct((heads, rows, part), BF16),
            jax.ShapeDtypeStruct((heads, width, width), BF16),
            jax.ShapeDtypeStruct((8, width), F32),
        ),
        in_specs=[vmem] * 8,
        out_specs=(vmem,) * 3,
        scratch_shapes=[
            pltpu.VMEM((tokens, width), BF16),
            pltpu.VMEM((tokens, 3 * width), BF16),
            pltpu.VMEM((width, tokens), BF16),
            pltpu.VMEM((width, 3 * width), BF16),
        ],
        compiler_params=pltpu.CompilerParams(vmem_limit_bytes=48 << 20),
    )(x, proj, probs, context, qkv, out, d_attn, g_attn)


def fused_scratch(micros, rows, width, blks, heads, share, fold):
    dma = pltpu.SemaphoreType.DMA
    vmem = pltpu.VMEM
    tokens = micros * rows
    part = width * micros // heads
    group = rows * heads
    ff = width * fold
    half = width // 2
    kept = blks // 2
    levels = blks.bit_length() - 1
    return dict(
        arrived=vmem((2, group, part), BF16),
        sorted_rows=vmem((2, group, part), BF16),
        landed=vmem((2, group, part), BF16),
        ordered=vmem((2, group, part), BF16),
        slots=vmem((2, heads, rows, part), BF16),
        dest_row=vmem((8, group), jnp.int32),
        slot_row=vmem((8, group), jnp.int32),
        dest_col=vmem((group, 128), jnp.int32),
        slot_col=vmem((group, 128), jnp.int32),
        ones=vmem((blks, group), F32),
        sums=vmem((blks, group), F32),
        rank_rows=vmem((blks, group), jnp.int32),
        seg_col=vmem((tokens, 128), F32),
        seg_row=vmem((8 * (-(-tokens // CLUSTER // 8)), CLUSTER), F32),
        perm=vmem((micros, blks, group), jnp.int32),
        shard=vmem((share, 3 * width), BF16),
        small_sums=vmem((16, 128), F32),
        small=vmem((16, 128), BF16),
        packed=vmem((heads, width, 3 * width), BF16),
        qkv=vmem((width, 3 * width), BF16),
        out=vmem((width, width), BF16),
        down=vmem((ff, width), BF16),
        full_vectors=vmem((blks, 16, 128), BF16),
        vectors=vmem((8, width), F32),
        bias_qkv=vmem((1, 3 * width), F32),
        up_bias=vmem((1, ff), F32),
        vec_grads=vmem((8, width), F32),
        up_bias_grad=vmem((1, ff), F32),
        x=vmem((tokens, width), BF16),
        proj=vmem((tokens, 3 * width), BF16),
        probs=vmem((tokens // CLUSTER, width // 128, 2 * CLUSTER, CLUSTER), BF16),
        context=vmem((tokens, width), BF16),
        attn_res=vmem((tokens, width), F32),
        normed=vmem((tokens, width), F32),
        hidden=vmem((tokens, width), BF16),
        turned=vmem((width, tokens), BF16),
        active=vmem((tokens, ff), BF16),
        slope=vmem((tokens, ff), BF16),
        ffn_res=vmem((tokens, width), F32),
        g_down=vmem((tokens, width), BF16),
        g_attn=vmem((tokens, width), BF16),
        staged=vmem((2, kept, share, width), BF16),
        from_tree=vmem((3, 2, heads, kept - 1, share, half), BF16),
        from_head=vmem((3, heads, share, width), BF16),
        vec_split=vmem((blks, 16, 128), F32),
        vec_parts=vmem((blks, 16, 128), F32),
        vec_mid=vmem((16, 128), F32),
        vec_heads=vmem((heads, 16, 128), F32),
        head_send=dma((4, 2, heads)),
        head_recv=dma((4, 2, heads)),
        blk_send=dma((4, blks)),
        blk_recv=dma((4, blks)),
        local=dma((4, 3)),
        z_send=dma((2, heads, 2)),
        z_recv=dma((2, heads)),
        tree_send=dma((2, heads, 2, blks)),
        tree_recv=dma((2, heads, 2, blks)),
        gain_send=dma((blks,)),
        gain_recv=dma((blks,)),
        own_sem=dma((2,)),
        core_send=dma((3, heads, kept)),
        core_recv=dma((3, heads, kept)),
        stage_sem=dma((3, heads)),
        down_send=dma((3, 2, heads, kept)),
        down_recv=dma((3, 2, heads, kept)),
        left_send=dma((3, heads)),
        left_recv=dma((3, heads)),
        vec_send=dma((blks,)),
        vec_recv=dma((blks,)),
        vec_head_send=dma((heads,)),
        vec_head_recv=dma((heads,)),
        out_sem=dma((2, 3)),
    )


def fused_kernel(names, blks, heads, share, fold, *refs):
    r = types.SimpleNamespace(**dict(zip(names, refs)))
    blk, head = lax.axis_index("blk"), lax.axis_index("head")
    micros, rows, width = r.tokens.shape
    tokens = micros * rows
    splits = heads // micros
    part = width // splits
    group = rows * heads
    pair = group // blks
    ff = width * fold
    short = width // heads
    levels = blks.bit_length() - 1
    bits = bits_of(blk, levels)
    sends = Sends()
    sems = (r.head_send, r.head_recv, r.blk_send, r.blk_recv, r.local)
    exchanges = [RowExchange(sends, blk, head, blks, heads, sems, i) for i in range(4)]

    def tiles(count, size):
        def run(body):
            @pl.loop(0, count)
            def _(tile):
                body(tile, pl.ds(pl.multiple_of(tile * size, size), size))

        return run

    row_tiles = tiles(tokens // CLUSTER, CLUSTER)


    def head_block(ref, i):
        return lambda other: ref.at[i, pl.ds(pl.multiple_of(other * rows, rows), rows), :]

    def blk_block(ref, i):
        return lambda other: ref.at[i, pl.ds(pl.multiple_of(other * pair, pair), pair), :]

    def row_source(ref):
        return lambda other: ref.at[
            other // splits, :, (other % splits) * part : (other % splits + 1) * part
        ]

    def own_rows(ref):
        return lambda other: ref.at[
            other // splits * rows : (other // splits + 1) * rows,
            (other % splits) * part : (other % splits + 1) * part,
        ]

    def to_heads(i, source):
        exchanges[i].over_head(0, source, head_block(r.arrived, i % 2))

    def to_groups(i, one_hot):
        exchanges[i].wait_head(0, head_block(r.arrived, i % 2))
        permute_rows(one_hot, r.arrived.at[i % 2], r.sorted_rows.at[i % 2], group)
        exchanges[i].over_blk(blk_block(r.sorted_rows, i % 2), blk_block(r.landed, i % 2))

    def to_owners(i, one_hot):
        exchanges[i].wait_blk(blk_block(r.landed, i % 2))
        permute_rows(one_hot, r.landed.at[i % 2], r.ordered.at[i % 2], group)
        exchanges[i].over_head(
            1, head_block(r.ordered, i % 2), lambda other: r.slots.at[i % 2, other]
        )

    def rows_here(i):
        exchanges[i].wait_head(1, lambda other: r.slots.at[i % 2, other])


    parts = ((0, width), (width, 2 * width))
    orders = [list(range(1, levels)) + [0], list(range(2, levels)) + [1, 0]]
    arrival = [
        choose(
            head,
            [
                sorted([x for x in range(heads) if x != own], key=lambda x: (abs(x - own), x))[j - 1]
                for own in range(heads)
            ],
        )
        if j
        else head
        for j in range(heads)
    ]

    def piece_rows(piece):
        return pl.ds(pl.multiple_of(piece * share, share), share)

    def part_cols(p, which=None):
        base, size = parts[p]
        if which is None:
            return slice(base, base + size)
        return slice(base + which * size // 2, base + (which + 1) * size // 2)

    def tree_wait(p, j, which, step):
        dims = orders[which]
        other = flip(blk, 1 << dims[step], bits)
        for mask in submasks(dims[:step]):
            piece = flip(blk, mask | (1 << dims[step]), bits)
            target = r.packed.at[arrival[j], piece_rows(piece), part_cols(p, which)]
            remote(
                target,
                target,
                r.tree_send.at[p, j, which, 0],
                r.tree_recv.at[p, j, which, piece],
                (other, head),
            ).wait_recv()

    def forwards(j):
        left = (arrival[j] > head) & (head > 0)
        right = (arrival[j] < head) & (head < heads - 1)
        return left, right

    def chain_wait(p, j):
        target = r.packed.at[arrival[j], piece_rows(blk), part_cols(p)]
        remote(
            target, target, r.z_send.at[p, 0, 0], r.z_recv.at[p, arrival[j]], (blk, head)
        ).wait_recv()

    def tree_step(p, j, step):
        if step == 0 and j:
            left, right = forwards(j)

            @pl.when(jnp.logical_not(left | right))
            def _():
                chain_wait(p, j)

        for which in range(2):
            dims = orders[which]
            if step:
                tree_wait(p, j, which, step - 1)
            if step == levels:
                continue
            other = flip(blk, 1 << dims[step], bits)
            for index, mask in enumerate(submasks(dims[:step])):
                piece = flip(blk, mask, bits)
                target = r.packed.at[arrival[j], piece_rows(piece), part_cols(p, which)]
                first = j == 0 and mask == 0
                source = r.shard.at[:, part_cols(p, which)] if first else target
                sends.start(
                    lambda source=source, target=target, piece=piece, other=other, which=which, slot=(1 << step) - 1 + index: remote(
                        source,
                        target,
                        r.tree_send.at[p, j, which, slot],
                        r.tree_recv.at[p, j, which, piece],
                        (other, head),
                    ),
                    tag="weights",
                )

    def chain(p, j):
        target = r.packed.at[arrival[j], piece_rows(blk), part_cols(p)]
        if j == 0:
            source = r.shard.at[:, part_cols(p)]
            left, right = head > 0, head < heads - 1
        else:
            source = target
            left, right = forwards(j)

            @pl.when(left | right)
            def _():
                chain_wait(p, j)

        for side, (condition, step) in enumerate(((left, -1), (right, 1))):
            sends.start(
                lambda side=side, step=step: remote(
                    source,
                    target,
                    r.z_send.at[p, j, side],
                    r.z_recv.at[p, arrival[j]],
                    (blk, jnp.clip(head + step, 0, heads - 1)),
                ),
                when=condition,
                tag="weights",
            )

    def gain_copy(other, slot):
        return remote(
            r.small, r.full_vectors.at[slot], r.gain_send.at[other], r.gain_recv.at[slot], (other, head)
        )


    order = []
    for i in range(heads):
        order.append(heads - 1 - i // 2 if i % 2 == 0 else i // 2)
    even = submasks(range(1, levels))
    down_orders = [list(range(levels - 1, 0, -1)), [1] + list(range(levels - 1, 1, -1))]
    sibling = flip(blk, 1, bits)

    def group_cols(g, which=None):
        if which is None:
            return slice(g * width, (g + 1) * width)
        return slice(g * width + which * width // 2, g * width + (which + 1) * width // 2)

    def total(g, other, mask, which=None):
        return r.packed.at[other, piece_rows(flip(blk, mask, bits)), group_cols(g, which)]

    def core_start(g):
        for other in order:
            for mask in even:
                sends.start(
                    lambda other=other, mask=mask: remote(
                        total(g, other, mask | 1),
                        r.from_core.at[g, other, mask // 2],
                        r.core_send.at[g, other, mask // 2],
                        r.core_recv.at[g, other, mask // 2],
                        (sibling, head),
                    )
                )

    def core_load(g, i):
        other = order[i]
        return pltpu.make_async_copy(
            r.from_core.at[g, other], r.staged.at[i % 2], r.stage_sem.at[g, i]
        )

    def core_arrived(g, i):
        other = order[i]
        for mask in even:
            target = r.from_core.at[g, other, mask // 2]
            remote(
                target,
                target,
                r.core_send.at[g, other, mask // 2],
                r.core_recv.at[g, other, mask // 2],
                (sibling, head),
            ).wait_recv()
        core_load(g, i).start()

    def core_add(g):
        core_arrived(g, 0)
        for i, other in enumerate(order):
            if i + 1 < heads:
                core_arrived(g, i + 1)
            core_load(g, i).wait()
            for mask in even:
                add_into(total(g, other, mask), r.staged.at[i % 2, mask // 2], width)
            tree_start(g, other, 0)

    def tree_slots(which, step):
        dims = down_orders[which]
        base = sum(1 << (levels - 2 - earlier) for earlier in range(step))
        return dims[step], [(mask, base + i) for i, mask in enumerate(submasks(dims[step + 1 :]))]

    def tree_copy(g, other, which, dim, mask, slot):
        return remote(
            total(g, other, mask | (1 << dim), which),
            r.from_tree.at[g, which, other, slot],
            r.down_send.at[g, which, other, slot],
            r.down_recv.at[g, which, other, slot],
            (flip(blk, 1 << dim, bits), head),
        )

    def tree_start(g, other, step):
        for which in range(2):
            dim, slots = tree_slots(which, step)
            for mask, slot in slots:
                sends.start(
                    lambda which=which, dim=dim, mask=mask, slot=slot: tree_copy(
                        g, other, which, dim, mask, slot
                    )
                )

    def tree_add(g, other, step):
        for which in range(2):
            dim, slots = tree_slots(which, step)
            for mask, slot in slots:
                tree_copy(g, other, which, dim, mask, slot).wait_recv()
                add_into(
                    total(g, other, mask, which), r.from_tree.at[g, which, other, slot], width // 2
                )
        if step < levels - 2:
            tree_start(g, other, step + 1)

    def tree_down(g, step):
        for other in order:
            tree_add(g, other, step)

    def direct_copy(g, goal, source):
        return remote(
            total(g, goal, 0),
            r.from_head.at[g, source],
            r.left_send.at[g, goal],
            r.left_recv.at[g, source],
            (blk, goal),
        )

    def direct_start(g):
        for goal in range(heads):
            sends.start(lambda goal=goal: direct_copy(g, goal, head), when=goal != head)

    def direct_add(g):
        for source in range(heads):

            @pl.when(source != head)
            def _():
                direct_copy(g, source, source).wait_recv()
                add_into(total(g, head, 0), r.from_head.at[g, source], width)


    micro = head // splits

    def find_destinations():
        own_slots = r.perm[micro, pl.ds(blk, 1), :]
        r.ones[...] = jnp.where(iota((blks, group), 0) == own_slots // group, 1.0, 0.0)
        cumulative(r.ones, r.sums, group)
        rank = column_sum(r.ones[...] * r.sums[...]).astype(jnp.int32) - 1
        dest = own_slots // group * pair + rank
        r.dest_row[...] = jnp.broadcast_to(dest, r.dest_row.shape)
        for tile in range(group // 128):
            block = jnp.broadcast_to(dest[:, tile * 128 : (tile + 1) * 128].astype(F32), (128, 128))
            r.dest_col[tile * 128 : (tile + 1) * 128, :] = block.T.astype(jnp.int32)

    def find_slots():
        r.ones[...] = jnp.where(r.perm[micro] // group == blk, 1.0, 0.0)
        cumulative(r.ones, r.sums, group)
        r.rank_rows[...] = jnp.where(r.ones[...] > 0, r.sums[...] - 1, -1.0).astype(jnp.int32)

        @pl.loop(0, blks)
        def _(other):
            ranks = r.rank_rows[pl.ds(other, 1), :]
            inner = (r.perm[micro, pl.ds(other, 1), :] % group).astype(F32)
            found = jnp.where(iota((pair, group), 0) == ranks, inner, 0.0)
            column = jnp.sum(found, axis=1, keepdims=True).astype(jnp.int32)
            r.slot_col[pl.ds(pl.multiple_of(other * pair, pair), pair), :] = jnp.broadcast_to(
                column, (pair, 128)
            )

        for tile in range(group // 128):
            block = r.slot_col[tile * 128 : (tile + 1) * 128, :].astype(F32)
            r.slot_row[:, tile * 128 : (tile + 1) * 128] = block.T[0:8, :].astype(jnp.int32)

    def find_segments():
        first = blk * group + head * rows
        for m in range(micros):
            ends = []
            for s in range(r.seq_lengths.shape[1]):
                ends.append(r.seq_lengths[m, s] + (ends[-1] if ends else 0))
            for tile in range(rows // CLUSTER):
                slot = iota((CLUSTER, group), 0) + (first + tile * CLUSTER)

                def add(other, sums):
                    position = iota((1, group), 1) + other * group
                    segment = jnp.zeros((1, group), F32)
                    for end in ends:
                        segment = segment + jnp.where(position >= end, 1.0, 0.0)
                    here = r.perm[m, pl.ds(other, 1), :] == slot
                    found = jnp.where(here, segment, 0.0)
                    return sums + sum(
                        found[:, i * 128 : (i + 1) * 128] for i in range(group // 128)
                    )

                sums = lax.fori_loop(0, blks, add, jnp.zeros((CLUSTER, 128), F32))
                column = jnp.broadcast_to(
                    jnp.sum(sums, axis=1, keepdims=True), (CLUSTER, 128)
                )
                cluster = m * (rows // CLUSTER) + tile
                r.seg_col[cluster * CLUSTER : (cluster + 1) * CLUSTER, :] = column
                r.seg_row[cluster : cluster + 1, :] = column.T[0:1, :]

    def spread_vectors():
        for b in range(blks):
            small = r.full_vectors[b].astype(F32)
            r.vectors[:, b * share : (b + 1) * share] = small[0:8, 0:share]
            for j in range(fold):
                at = (b * fold + j) * share
                r.up_bias[:, at : at + share] = small[8 + j : 9 + j, 0:share]
        r.bias_qkv[:, 0:width] = r.vectors[0:1, :]
        r.bias_qkv[:, width : 2 * width] = jnp.zeros((1, width), F32)
        r.bias_qkv[:, 2 * width :] = r.vectors[1:2, :]


    def take_rows():
        for source in range(heads):
            m, which = source // splits, source % splits
            r.x[m * rows : (m + 1) * rows, which * part : (which + 1) * part] = r.slots[0, source]

    def assemble_down():
        @pl.loop(0, width // share)
        def _(b):
            source = piece_rows(b)
            for j in range(fold):
                at = b * share * fold + j * share
                target = pl.ds(pl.multiple_of(at, share), share)
                for h in range(heads):
                    base = 2 * width + j * short
                    r.down[target, h * short : (h + 1) * short] = r.packed[
                        h, source, base : base + short
                    ]

    per_head = width // 256

    def first_norm():
        @row_tiles
        def _(tile, at):
            normal, _ = normalize(r.attn_res[at, :])
            values = normal * r.vectors[3:4, :] + r.vectors[4:5, :]
            r.normed[at, :] = values
            r.hidden[at, :] = values.astype(BF16)

        r.turned[...] = r.hidden[...].T

    def ffn_up(h):
        @tiles(per_head, 256)
        def _(tile, inner):
            inner = pl.ds(pl.multiple_of(width + tile * 256, 256), 256)
            cols = pl.ds(pl.multiple_of(h * width + tile * 256, 256), 256)
            pre = jnp.dot(r.hidden[...], r.packed[h, :, inner], preferred_element_type=F32)
            pre = pre + r.up_bias[:, cols]
            below = 0.5 + 0.5 * lax.erf(pre * (0.5**0.5))
            r.active[:, cols] = (pre * below).astype(BF16)
            bell = jnp.exp(-0.5 * pre * pre) * (0.5 / jnp.pi) ** 0.5
            r.slope[:, cols] = (below + pre * bell).astype(BF16)

    def ffn_down():
        @tiles(width // 256, 256)
        def _(tile, cols):
            sums = jnp.dot(r.active[...], r.down[:, cols], preferred_element_type=F32)
            r.ffn_res[:, cols] = r.normed[:, cols] + sums + r.vectors[5:6, cols]

    def inner_rows(tile):
        return tile * CLUSTER // rows, pl.ds(pl.multiple_of(tile * CLUSTER % rows, CLUSTER), CLUSTER)

    def second_norm():
        @row_tiles
        def _(tile, at):
            normal, _ = normalize(r.ffn_res[at, :])
            result = (normal * r.vectors[6:7, :] + r.vectors[7:8, :]).astype(BF16)
            r.hidden[at, :] = result

    def second_norm_back():
        @row_tiles
        def _(tile, at):
            normal, scale = normalize(r.ffn_res[at, :])
            m, inner = inner_rows(tile)
            cotangent = jnp.concatenate(
                [r.slots[1, m * splits + which, inner, :] for which in range(splits)], axis=1
            ).astype(F32)
            d_ffn = norm_derivative(normal, scale, cotangent, r.vectors[6:7, :])
            low = d_ffn.astype(BF16)
            r.g_down[at, :] = low
            r.ffn_res[at, :] = d_ffn
            r.vec_grads[5:6, :] += column_sum(low.astype(F32))
            r.vec_grads[6:7, :] += column_sum(cotangent * normal)
            r.vec_grads[7:8, :] += column_sum(cotangent)

    def down_gradient():
        @pl.loop(0, width // share)
        def _(b):
            wide = share * fold
            cols = pl.ds(pl.multiple_of(b * wide, wide), wide)
            turned = r.active[:, cols].T
            target = piece_rows(b)
            for which in range(2):
                grad = jnp.dot(
                    turned,
                    r.g_down[:, which * width // 2 : (which + 1) * width // 2],
                    preferred_element_type=F32,
                ).astype(BF16)
                for j in range(fold):
                    for h in range(heads // 2):
                        base = 2 * width + j * short
                        r.packed[which * heads // 2 + h, target, base : base + short] = grad[
                            j * share : (j + 1) * share, h * short : (h + 1) * short
                        ]

    def ffn_up_back():
        @tiles(ff // 256, 256)
        def _(tile, cols):
            d_active = contract(r.g_down[...], r.down[cols, :], (1, 1))
            low = (d_active * r.slope[:, cols].astype(F32)).astype(BF16)
            r.slope[:, cols] = low
            r.up_bias_grad[:, cols] = column_sum(low.astype(F32))

    def norm_cotangent():
        @tiles(width // 256, 256)
        def _(tile, cols):
            sums = r.ffn_res[:, cols]
            for h in range(heads):
                sums = sums + contract(
                    r.slope[:, h * width : (h + 1) * width],
                    r.packed[h, cols, width : 2 * width],
                    (1, 1),
                )
            r.normed[:, cols] = sums

    def up_gradient():
        @tiles(ff // 256, 256)
        def _(tile, cols):
            inner = pl.ds(pl.multiple_of(width + tile % per_head * 256, 256), 256)
            grad = jnp.dot(r.turned[...], r.slope[:, cols], preferred_element_type=F32)
            r.packed[tile // per_head, :, inner] = grad.astype(BF16)

    def first_norm_back():
        @row_tiles
        def _(tile, at):
            normal, scale = normalize(r.attn_res[at, :])
            cotangent = r.normed[at, :]
            grad = norm_derivative(normal, scale, cotangent, r.vectors[3:4, :])
            low = grad.astype(BF16)
            r.attn_res[at, :] = grad
            r.g_attn[at, :] = low
            r.vec_grads[2:3, :] += column_sum(low.astype(F32))
            r.vec_grads[3:4, :] += column_sum(cotangent * normal)
            r.vec_grads[4:5, :] += column_sum(cotangent)

    g_context = r.g_down
    x_grad = r.g_down
    g_proj = r.active
    wide = 3 * width // heads

    def out_gradient():
        r.turned[...] = r.context[...].T
        for h in range(heads):
            grad = jnp.dot(
                r.turned[...],
                r.g_attn[:, h * short : (h + 1) * short],
                preferred_element_type=F32,
            )
            r.packed[h, :, wide : wide + short] = grad.astype(BF16)

    def context_cotangent():
        @tiles(width // 256, 256)
        def _(tile, cols):
            g_context[:, cols] = contract(r.g_attn[...], r.out[cols, :], (1, 1)).astype(BF16)

    def qkv_gradient():
        r.turned[...] = r.x[...].T

        @tiles(width // 256, 256)
        def _(tile, at):
            for h in range(heads):
                grad = jnp.dot(
                    r.turned[at, :], g_proj[:, h * wide : (h + 1) * wide], preferred_element_type=F32
                )
                r.packed[h, at, 0:wide] = grad.astype(BF16)

        r.vec_grads[0:1, :] = column_sum(g_proj[:, 0:width].astype(F32))
        r.vec_grads[1:2, :] = column_sum(g_proj[:, 2 * width : 3 * width].astype(F32))

    def row_gradient():
        for which in range(splits):
            for piece in range(part // 128):
                at = which * part + piece * 128
                sums = r.attn_res[:, at : at + 128] + contract(
                    g_proj[:, 0 : 3 * width], r.qkv[at : at + 128, :], (1, 1)
                )
                x_grad[:, at : at + 128] = sums.astype(BF16)


    def split_vectors():
        r.vec_split[...] = jnp.zeros_like(r.vec_split)
        for b in range(blks):
            r.vec_split[b, 0:8, 0:share] = r.vec_grads[:, b * share : (b + 1) * share]
            for j in range(fold):
                at = (b * fold + j) * share
                r.vec_split[b, 8 + j : 9 + j, 0:share] = r.up_bias_grad[:, at : at + share]

    def vec_copy(other, slot):
        return remote(
            r.vec_split.at[other],
            r.vec_parts.at[slot],
            r.vec_send.at[other],
            r.vec_recv.at[slot],
            (other, head),
        )

    def vec_head_copy(other, slot):
        return remote(
            r.vec_mid,
            r.vec_heads.at[slot],
            r.vec_head_send.at[other],
            r.vec_head_recv.at[slot],
            (blk, other),
        )

    def place_slots():
        for m in range(micros):
            for b in range(blks):
                r.perm[m, b : b + 1, :] = r.perm_rows[m : m + 1, b * group : (b + 1) * group]

    def pack_shard():
        at = 0
        for source in (r.qkv_weight, r.out_weight, r.up_weight):
            r.shard[:, at : at + source.shape[1]] = source[...]
            at += source.shape[1]
        turned = r.down_weight[...].T
        for j in range(fold):
            r.shard[:, at + j * short : at + (j + 1) * short] = turned[
                j * share : (j + 1) * share
            ]

    def pack_small():
        r.small_sums[...] = jnp.zeros_like(r.small_sums)
        for i in range(8):
            r.small_sums[i : i + 1, 0:share] = getattr(r, "vector%d" % i)[...].astype(F32)
        for j in range(fold):
            r.small_sums[8 + j : 9 + j, 0:share] = r.up_bias_here[
                :, j * share : (j + 1) * share
            ].astype(F32)
        r.small[...] = r.small_sums[...].astype(BF16)

    def send_small():
        for other in range(blks):
            sends.start(lambda other=other: gain_copy(other, blk), when=other != blk)
        own_gain.start()
        own_shard.start()

    def take_small():
        for other in range(blks):

            @pl.when(other != blk)
            def _():
                gain_copy(other, other).wait_recv()

        own_gain.wait()
        own_shard.wait()
        spread_vectors()

    def send_vectors():
        split_vectors()
        for other in range(blks):
            sends.start(lambda other=other: vec_copy(other, blk), when=other != blk)

    def sum_vectors_over_blk():
        r.vec_mid[...] = r.vec_split[pl.ds(blk, 1)][0]
        for other in range(blks):

            @pl.when(other != blk)
            def _():
                vec_copy(other, other).wait_recv()
                r.vec_mid[...] += r.vec_parts[other]

        for other in range(heads):
            sends.start(lambda other=other: vec_head_copy(other, head), when=other != head)

    def sum_vectors_over_head():
        r.vec_sum[...] = r.vec_mid[...]
        for other in range(heads):

            @pl.when(other != head)
            def _():
                vec_head_copy(other, other).wait_recv()
                r.vec_sum[...] += r.vec_heads[other]

    own_gain = pltpu.make_async_copy(r.small, r.full_vectors.at[blk], r.own_sem.at[0])
    own_shard = pltpu.make_async_copy(
        r.shard, r.packed.at[head, piece_rows(blk), :], r.own_sem.at[1]
    )

    def start_backward():
        r.vec_grads[...] = jnp.zeros_like(r.vec_grads)

    clusters = tokens // CLUSTER

    def attention_back(begin, end):
        attend_back(r.proj, r.probs, g_context, g_proj, begin, end)

    def row_copy(i):
        return pltpu.make_async_copy(r.slots.at[i], r.row_results.at[i], r.out_sem.at[0, i])

    def shard_copy(g):
        return pltpu.make_async_copy(
            r.packed.at[head, piece_rows(blk), group_cols(g)],
            r.shard_grad.at[:, group_cols(g)],
            r.out_sem.at[1, g],
        )

    def finish():
        for i in range(2):
            row_copy(i).wait()
        for g in range(3):
            shard_copy(g).wait()
        sends.finish()


    enter(blk, head, blks, heads)
    to_heads(0, row_source(r.tokens))
    pack_shard()
    chain(0, 0)
    tree_step(0, 0, 0)
    tree_step(1, 0, 0)
    pack_small()
    send_small()
    place_slots()
    find_destinations()
    tree_step(0, 0, 1)
    chain(1, 0)
    tree_step(1, 0, 1)
    find_slots()
    tree_step(0, 0, 2)
    tree_step(1, 0, 2)
    find_segments()
    chain(0, 1)
    to_groups(0, one_hot_from_row(r.dest_row))
    chain(0, 2)
    chain(1, 1)
    tree_step(0, 1, 0)
    chain(1, 2)
    tree_step(1, 1, 0)
    chain(0, 3)
    tree_step(0, 2, 0)
    tree_step(0, 1, 1)
    to_owners(0, one_hot_from_row(r.slot_row))
    chain(1, 3)
    tree_step(0, 3, 0)
    tree_step(1, 2, 0)
    tree_step(0, 2, 1)
    tree_step(0, 1, 2)
    to_heads(1, row_source(r.out_grad))
    tree_step(1, 1, 1)
    tree_step(0, 3, 1)
    tree_step(0, 2, 2)
    take_small()
    tree_step(1, 3, 0)
    tree_step(1, 2, 1)
    tree_step(0, 3, 2)
    tree_step(1, 1, 2)
    tree_step(0, 0, 3)
    tree_step(0, 1, 3)
    tree_step(0, 2, 3)
    tree_step(0, 3, 3)
    assemble_attention(r.packed, r.qkv, r.out)
    tree_step(1, 3, 1)
    tree_step(1, 2, 2)
    rows_here(0)
    take_rows()
    project(r.x, r.qkv, r.bias_qkv, r.proj)
    to_groups(1, one_hot_from_row(r.dest_row))
    tree_step(1, 3, 2)
    attend(r.proj, r.probs, r.context, r.seg_col, r.seg_row)
    leave_attention(r.x, r.context, r.out, r.vectors, r.attn_res)
    first_norm()
    to_owners(1, one_hot_from_row(r.slot_row))
    tree_step(1, 0, 3)
    ffn_up(arrival[0])
    tree_step(1, 1, 3)
    ffn_up(arrival[1])
    tree_step(1, 2, 3)
    ffn_up(arrival[2])
    tree_step(1, 3, 3)
    ffn_up(arrival[3])
    assemble_down()
    ffn_down()
    second_norm()
    to_heads(2, own_rows(r.hidden))
    start_backward()
    rows_here(1)
    second_norm_back()
    sends.finish("weights")
    down_gradient()
    core_start(2)
    ffn_up_back()
    norm_cotangent()
    sends.finish(0)
    to_groups(2, one_hot_from_column(r.slot_col, group))
    core_add(2)
    up_gradient()
    core_start(1)
    first_norm_back()
    context_cotangent()
    to_owners(2, one_hot_from_column(r.dest_col, group))
    attention_back(0, clusters // 2)
    core_add(1)
    attention_back(clusters // 2, clusters)
    tree_down(2, 0)
    row_gradient()
    to_heads(3, own_rows(x_grad))
    out_gradient()
    qkv_gradient()
    core_start(0)
    send_vectors()
    tree_down(2, 1)
    direct_start(2)
    tree_down(1, 0)
    core_add(0)
    sends.finish(1)
    sum_vectors_over_blk()
    to_groups(3, one_hot_from_column(r.slot_col, group))
    tree_down(1, 1)
    direct_start(1)
    direct_add(2)
    shard_copy(2).start()
    to_owners(3, one_hot_from_column(r.dest_col, group))
    tree_down(0, 0)
    sum_vectors_over_head()
    tree_down(0, 1)
    direct_start(0)
    rows_here(2)
    row_copy(0).start()
    direct_add(1)
    shard_copy(1).start()
    direct_add(0)
    shard_copy(0).start()
    rows_here(3)
    row_copy(1).start()
    finish()


def fused(blks, heads, fold, tokens, out_grad, weights, vectors, up_bias, perm, seq_lengths):
    micros, rows, width = tokens.shape
    share = weights[0].shape[0]
    part = width * micros // heads
    scratch = fused_scratch(micros, rows, width, blks, heads, share, fold)
    any_space, vmem = pl.BlockSpec(memory_space=pl.ANY), pl.BlockSpec(memory_space=pltpu.VMEM)
    names = ["tokens", "out_grad", "qkv_weight", "out_weight", "up_weight", "down_weight"]
    names += ["vector%d" % i for i in range(8)] + ["up_bias_here", "perm_rows", "seq_lengths"]
    names += ["row_results", "shard_grad", "vec_sum", "from_core"]
    names += list(scratch)
    return pl.pallas_call(
        functools.partial(fused_kernel, names, blks, heads, share, fold),
        name="fused",
        out_shape=(
            jax.ShapeDtypeStruct((2, heads, rows, part), BF16),
            jax.ShapeDtypeStruct((share, 3 * width), BF16),
            jax.ShapeDtypeStruct((16, 128), F32),
            jax.ShapeDtypeStruct((3, heads, blks // 2, share, width), BF16),
        ),
        in_specs=[any_space] * 2 + [vmem] * 14 + [pl.BlockSpec(memory_space=pltpu.SMEM)],
        out_specs=(any_space, any_space, vmem, any_space),
        scratch_shapes=list(scratch.values()),
        compiler_params=pltpu.CompilerParams(
            collective_id=2, has_side_effects=True, vmem_limit_bytes=64 << 20
        ),
    )(
        tokens,
        out_grad,
        *weights[:3],
        weights[3].T,
        *[vector.reshape(1, -1) for vector in vectors],
        up_bias.reshape(1, -1),
        perm,
        seq_lengths,
    )[:3]


def unpack_kernel(
    row_results, shard, sums, layer_out, x_grad, qkv, out, up, down, up_bias, *vectors
):
    micros, rows, width = layer_out.shape
    _, heads, _, part = row_results.shape
    splits = heads // micros
    share, short = out.shape
    fold = down.shape[1] // share
    for source in range(heads):
        m, which = source // splits, source % splits
        cols = slice(which * part, (which + 1) * part)
        layer_out[m, :, cols] = row_results[0, source]
        x_grad[m, :, cols] = row_results[1, source].astype(F32)
    at = 0
    for target in (qkv, out, up):
        target[...] = shard[:, at : at + target.shape[1]].astype(F32)
        at += target.shape[1]
    pieces = [
        shard[:, at + j * short : at + (j + 1) * short].astype(F32) for j in range(fold)
    ]
    down[...] = jnp.concatenate(pieces, axis=0).T
    for i, vector in enumerate(vectors):
        vector[...] = sums[i : i + 1, 0:share]
    for j in range(fold):
        up_bias[:, j * share : (j + 1) * share] = sums[8 + j : 9 + j, 0:share]


def unpack(micros, width, widths, row_results, shard, sums):
    _, heads, rows, part = row_results.shape
    share = shard.shape[0]
    vmem = pl.BlockSpec(memory_space=pltpu.VMEM)
    shapes = [(share, widths[0]), (share, widths[1]), (share, widths[2])]
    shapes += [(widths[1], widths[3] // widths[1] * share), (1, widths[3] // widths[1] * share)]
    shapes += [(1, share)] * 8
    results = pl.pallas_call(
        unpack_kernel,
        name="unpack",
        out_shape=(
            jax.ShapeDtypeStruct((micros, rows, width), BF16),
            jax.ShapeDtypeStruct((micros, rows, width), F32),
        )
        + tuple(jax.ShapeDtypeStruct(shape, F32) for shape in shapes),
        in_specs=[vmem] * 3,
        out_specs=(vmem,) * (2 + len(shapes)),
        compiler_params=pltpu.CompilerParams(vmem_limit_bytes=32 << 20),
    )(row_results, shard, sums)
    layer_out, x_grad, qkv, out, up, down, up_bias = results[:7]
    vec = [member.reshape(-1) for member in results[7:]]
    return (
        layer_out,
        x_grad,
        qkv,
        vec[0],
        vec[1],
        out,
        vec[2],
        vec[3],
        vec[4],
        up,
        up_bias.reshape(-1),
        down.T,
        vec[5],
        vec[6],
        vec[7],
    )


def refold(packed, share, other, fold):
    if share == other:
        return packed
    heads, width, wide = packed.shape
    short = wide // fold
    rows = packed.reshape(heads, width // share, share, fold, short).transpose(0, 1, 3, 2, 4)
    rows = rows.reshape(heads, width // other, fold, other, short).transpose(0, 1, 3, 2, 4)
    return rows.reshape(packed.shape)


def body(
    tokens,
    seq_lengths,
    cluster_perm,
    out_grad,
    qkv_weight,
    query_bias,
    value_bias,
    out_weight,
    out_bias,
    attn_gain,
    attn_shift,
    up_weight,
    up_bias,
    down_weight,
    down_bias,
    ffn_gain,
    ffn_shift,
):
    blks, heads = lax.axis_size("blk"), lax.axis_size("head")
    blk, head = lax.axis_index("blk"), lax.axis_index("head")
    micros, rows, width = tokens.shape
    group = rows * heads
    total_rows = cluster_perm.shape[1]
    share = qkv_weight.shape[0]
    folds = down_weight.shape[0] // share
    short = down_weight.shape[1]
    widths = [qkv_weight.shape[1], out_weight.shape[1], up_weight.shape[1], folds * short]
    edges = [sum(widths[:i]) for i in range(5)]

    small = [
        query_bias,
        value_bias,
        out_bias,
        attn_gain,
        attn_shift,
        down_bias,
        ffn_gain,
        ffn_shift,
    ]
    if share % 16 == 0:
        results = fused(
            blks,
            heads,
            folds,
            tokens,
            out_grad,
            (qkv_weight, out_weight, up_weight, down_weight),
            small,
            up_bias,
            cluster_perm,
            seq_lengths,
        )
        return unpack(micros, width, widths, *results)

    shard = jnp.concatenate(
        [qkv_weight, out_weight, up_weight]
        + [down_weight[i * share : (i + 1) * share] for i in range(folds)],
        axis=1,
    )
    lanes = -(-share // 128) * 128
    stacked = jnp.concatenate([jnp.stack(small), up_bias.reshape(folds, share)], axis=0)
    count = stacked.shape[0]
    vectors = jnp.pad(stacked, ((0, -count % 16), (0, lanes - share)))
    perm = cluster_perm.reshape(micros, blks, group)
    full, full_vectors, slots_x, slots_g, dest_col, slot_col = gather_all(
        blks, heads, tokens, out_grad, shard, vectors, perm
    )

    first = blk * group + head * rows
    slots = first + jnp.arange(rows, dtype=jnp.int32)
    ends = jnp.cumsum(seq_lengths, axis=1)
    positions = jnp.arange(total_rows, dtype=jnp.int32)
    segs = jnp.sum((positions[None, :, None] >= ends[:, None, :]).astype(jnp.int32), axis=2)
    slot_segs = jnp.sum(
        jnp.where(cluster_perm[:, None, :] == slots[None, :, None], segs[:, None, :], 0), axis=2
    )

    weights = full.reshape(heads, blks * share, -1)
    tall = share if share % 16 == 0 else width // 8
    if tall != share:
        weights = jnp.concatenate(
            [weights[:, :, : edges[3]], refold(weights[:, :, edges[3] :], share, tall, folds)],
            axis=2,
        )
    spread = full_vectors[:, :count, :share].astype(F32)
    vecs = spread[:, :8].transpose(1, 0, 2).reshape(8, width)
    up_vec = spread[:, 8:count].reshape(1, -1)
    bias_qkv = jnp.concatenate([vecs[0:1], jnp.zeros((1, width), F32), vecs[1:2]], axis=1)
    seg_col = jnp.broadcast_to(slot_segs.reshape(-1, 1), (micros * rows, 128))
    seg_row = slot_segs.reshape(-1, CLUSTER)
    x, proj, probs, context, attn_res, qkv, out = forward_part(
        slots_x, weights, bias_qkv, vecs, seg_col, seg_row
    )
    layer_out, d_attn, g_attn, partial_ffn, vec_ffn, up_vec_grad = ffn_part(
        tall, attn_res, slots_g, weights, vecs, up_vec
    )
    x_grad, partial_attn, vec_attn = backward_part(
        heads, rows, x, proj, probs, context, qkv, out, d_attn, g_attn
    )
    if tall != share:
        partial_ffn = jnp.concatenate(
            [partial_ffn[:, :, :width], refold(partial_ffn[:, :, width:], tall, share, folds)],
            axis=2,
        )
    partial = jnp.concatenate([partial_attn, partial_ffn], axis=2).reshape(full.shape)
    vec_grads = vec_ffn + vec_attn
    vec_parts = jnp.concatenate(
        [vec_grads.reshape(8, blks, share).transpose(1, 0, 2), up_vec_grad.reshape(blks, folds, share)],
        axis=1,
    )
    vec_parts = jnp.pad(vec_parts, ((0, 0), (0, -count % 16), (0, lanes - share)))
    out_rows, grad_rows, shard_grad, vec_sum = reduce_all(
        blks, heads, layer_out, x_grad, partial, vec_parts, dest_col, slot_col
    )
    down_grad = shard_grad[:, edges[3] : edges[4]]
    down_grad = jnp.concatenate(
        [down_grad[:, i * short : (i + 1) * short] for i in range(folds)], axis=0
    )
    vec = [vec_sum[i, :share] for i in range(8)]
    return (
        out_rows,
        grad_rows,
        shard_grad[:, edges[0] : edges[1]],
        vec[0],
        vec[1],
        shard_grad[:, edges[1] : edges[2]],
        vec[2],
        vec[3],
        vec[4],
        shard_grad[:, edges[2] : edges[3]],
        vec_sum[8:count, :share].reshape(-1),
        down_grad,
        vec[5],
        vec[6],
        vec[7],
    )


def solution(mesh):
    return jax.shard_map(
        body,
        mesh=mesh,
        in_specs=(
            P(None, ("blk", "head"), None),
            P(),
            P(),
            P(None, ("blk", "head"), None),
            P("blk", "head"),
            P("blk"),
            P("blk"),
            P("blk", "head"),
            P("blk"),
            P("blk"),
            P("blk"),
            P("blk", "head"),
            P("blk"),
            P("blk", "head"),
            P("blk"),
            P("blk"),
            P("blk"),
        ),
        out_specs=(
            P(None, ("blk", "head"), None),
            P(None, ("blk", "head"), None),
            P("blk", "head"),
            P("blk"),
            P("blk"),
            P("blk", "head"),
            P("blk"),
            P("blk"),
            P("blk"),
            P("blk", "head"),
            P("blk"),
            P("blk", "head"),
            P("blk"),
            P("blk"),
            P("blk"),
        ),
        check_vma=False,
    )
```

```python
import functools
import types

import jax
import jax.numpy as jnp
from jax import lax
from jax.experimental import pallas as pl
from jax.experimental.pallas import tpu as pltpu
from jax.sharding import PartitionSpec as P

HEAD_DIM = 64
CLUSTER = 128
TILE = 256
MESH = pl.DeviceIdType.MESH
BF16 = jnp.bfloat16
F32 = jnp.float32

masked_score = -1e30
norm_epsilon = 1e-05


def bits_of(index, count):
    return [(index // (1 << i)) % 2 for i in range(count)]


def flip(index, mask, bits):
    for i, bit in enumerate(bits):
        if mask & (1 << i):
            index = index + (1 - 2 * bit) * (1 << i)
    return index


def submasks(dims):
    masks = [0]
    for dim in dims:
        masks = masks + [mask | (1 << dim) for mask in masks]
    return masks


def choose(index, values):
    result = values[-1]
    for position in range(len(values) - 2, -1, -1):
        result = jnp.where(index == position, values[position], result)
    return result


class Sends:
    def __init__(self):
        self.pending = []
        self.shared = {}

    def start(self, make, when=None, tag=None, shared=None):
        if when is None:
            make().start()
        else:

            @pl.when(when)
            def _():
                make().start()

        if shared is None:
            self.pending.append((make, when, tag))
        else:
            key, wait = shared
            self.shared[tag, key] = wait

    def finish(self, *tags):
        pending, self.pending = self.pending, []
        for make, when, tag in pending:
            if tags and tag not in tags:
                self.pending.append((make, when, tag))
            elif when is None:
                make().wait_send()
            else:

                @pl.when(when)
                def _(make=make):
                    make().wait_send()

        shared, self.shared = self.shared, {}
        for (tag, key), wait in shared.items():
            if tags and tag not in tags:
                self.shared[tag, key] = wait
            else:
                wait()


def await_bytes(ref, sem):
    pltpu.make_async_copy(ref, ref, sem).wait()


def remote(src, dst, send_sem, recv_sem, device):
    return pltpu.make_async_remote_copy(
        src_ref=src,
        dst_ref=dst,
        send_sem=send_sem,
        recv_sem=recv_sem,
        device_id=device,
        device_id_type=MESH,
    )


def enter(blk, head, blks, heads):
    barrier = pltpu.get_barrier_semaphore()
    for other in range(blks):

        @pl.when(other != blk)
        def _():
            pl.semaphore_signal(barrier, inc=1, device_id=(other, head), device_id_type=MESH)

    for other in range(heads):

        @pl.when(other != head)
        def _():
            pl.semaphore_signal(barrier, inc=1, device_id=(blk, other), device_id_type=MESH)

    pl.semaphore_wait(barrier, blks + heads - 2)


def iota(shape, dim):
    return lax.broadcasted_iota(jnp.int32, shape, dim)


def permute_rows(one_hot_tile, source, target, rows):
    @pl.loop(0, rows // TILE)
    def _(tile):
        start = pl.multiple_of(tile * TILE, TILE)
        chosen = jnp.dot(one_hot_tile(start), source[...], preferred_element_type=F32)
        target[pl.ds(start, TILE), :] = chosen.astype(BF16)


def one_hot_from_row(row_ref):
    def tile(start):
        row = row_ref[0:1, :]
        count = row.shape[1]
        return jnp.where(iota((TILE, count), 0) + start == row, 1.0, 0.0).astype(BF16)

    return tile


def one_hot_from_column(column_ref, count):
    def tile(start):
        column = column_ref[pl.ds(start, TILE), 0:1]
        return jnp.where(iota((TILE, count), 1) == column, 1.0, 0.0).astype(BF16)

    return tile


class RowExchange:
    def __init__(self, sends, blk, head, blks, heads, sems, tensor):
        self.sends, self.blk, self.head, self.blks, self.heads = sends, blk, head, blks, heads
        self.head_send, self.head_recv, self.blk_send, self.blk_recv, self.local = sems
        self.tensor = tensor

    def over_head(self, step, source, target, all_but_one):
        send_sem = self.head_send.at[self.tensor, step]
        for other in range(self.heads):
            make = lambda other=other: remote(
                source(other),
                target(self.head),
                send_sem,
                self.head_recv.at[self.tensor, step],
                (self.blk, other),
            )
            self.sends.start(
                make,
                when=other != self.head,
                tag=self.tensor,
                shared=(("head", step), lambda: await_bytes(all_but_one, send_sem)),
            )

            @pl.when(other == self.head)
            def _():
                pltpu.make_async_copy(
                    source(other), target(other), self.local.at[self.tensor, step]
                ).start()

    def wait_head(self, step, target, all_but_one):
        await_bytes(all_but_one, self.head_recv.at[self.tensor, step])
        await_bytes(target(self.head), self.local.at[self.tensor, step])

    def over_blk(self, source, target, all_but_one):
        send_sem = self.blk_send.at[self.tensor]
        for other in range(self.blks):
            make = lambda other=other: remote(
                source(other),
                target(self.blk),
                send_sem,
                self.blk_recv.at[self.tensor],
                (other, self.head),
            )
            self.sends.start(
                make,
                when=other != self.blk,
                tag=self.tensor,
                shared=("blk", lambda: await_bytes(all_but_one, send_sem)),
            )

            @pl.when(other == self.blk)
            def _():
                pltpu.make_async_copy(
                    source(other), target(other), self.local.at[self.tensor, 2]
                ).start()

    def wait_blk(self, target, all_but_one):
        await_bytes(all_but_one, self.blk_recv.at[self.tensor])
        await_bytes(target(self.blk), self.local.at[self.tensor, 2])


def exchange_sems(blks, heads):
    dma = pltpu.SemaphoreType.DMA
    return [dma((2, 2)), dma((2, 2)), dma((2,)), dma((2,)), dma((2, 3))]


def cumulative(ones_ref, sums_ref, count):
    upper = jnp.where(iota((128, 128), 0) <= iota((128, 128), 1), 1.0, 0.0).astype(BF16)
    carry = jnp.zeros((ones_ref.shape[0], 1), F32)
    for tile in range(count // 128):
        part = ones_ref[:, tile * 128 : (tile + 1) * 128].astype(BF16)
        sums = jnp.dot(part, upper, preferred_element_type=F32) + carry
        sums_ref[:, tile * 128 : (tile + 1) * 128] = sums
        carry = sums[:, 127:128]


def gather_kernel(
    blks,
    heads,
    tokens,
    out_grad,
    shard,
    vectors,
    perm,
    full,
    full_vectors,
    slots_x,
    slots_g,
    dest_col,
    slot_col,
    arrived,
    sorted_rows,
    landed,
    ordered,
    dest_row,
    slot_row,
    ones,
    sums,
    rank_rows,
    head_send,
    head_recv,
    blk_send,
    blk_recv,
    local,
    z_send,
    z_recv,
    tree_send,
    tree_recv,
    vec_send,
    vec_recv,
    own_sem,
):
    blk, head = lax.axis_index("blk"), lax.axis_index("head")
    micros, rows, width = tokens.shape
    splits = heads // micros
    part = width // splits
    group = rows * heads
    pair = group // blks
    levels = blks.bit_length() - 1
    bits = bits_of(blk, levels)
    half = shard.shape[1] // 2
    sends = Sends()
    sems = (head_send, head_recv, blk_send, blk_recv, local)

    enter(blk, head, blks, heads)

    exchanges = [RowExchange(sends, blk, head, blks, heads, sems, i) for i in range(2)]
    sources = (tokens, out_grad)

    def send_rows(i):
        exchanges[i].over_head(
            0,
            lambda other: sources[i].at[
                other // splits, :, (other % splits) * part : (other % splits + 1) * part
            ],
            lambda other: arrived.at[i, pl.ds(pl.multiple_of(other * rows, rows), rows), :],
            arrived.at[i, 0 : group - rows, :],
        )

    send_rows(0)

    def vec_copy(other):
        return remote(
            vectors, full_vectors.at[blk], vec_send.at[other], vec_recv.at[blk], (other, head)
        )

    for other in range(blks):
        sends.start(lambda other=other: vec_copy(other), when=other != blk)
    own_vec = pltpu.make_async_copy(vectors, full_vectors.at[blk], own_sem.at[0])
    own_vec.start()

    orders = [list(range(1, levels)) + [0], list(range(2, levels)) + [1, 0]]
    arrival = [
        choose(
            head,
            [
                sorted([x for x in range(heads) if x != own], key=lambda x: (abs(x - own), x))[j - 1]
                for own in range(heads)
            ],
        )
        if j
        else head
        for j in range(heads)
    ]

    def halves(ref, which):
        return ref.at[:, which * half : (which + 1) * half]

    def tree_step(j, step):
        for which in range(2):
            dims = orders[which]
            if step:
                tree_wait(j, which, step - 1)
            other = flip(blk, 1 << dims[step], bits)
            for mask in submasks(dims[:step]):
                piece = flip(blk, mask, bits)
                target = halves(full.at[arrival[j], piece], which)
                source = halves(shard, which) if j == 0 and mask == 0 else target
                slot = (1 << step) - 1 + submasks(dims[:step]).index(mask)
                make = lambda source=source, target=target, piece=piece, other=other, slot=slot, which=which: remote(
                    source,
                    target,
                    tree_send.at[j, which, slot],
                    tree_recv.at[j, which, piece],
                    (other, head),
                )
                sends.start(make)

    def tree_wait(j, which, step):
        dims = orders[which]
        other = flip(blk, 1 << dims[step], bits)
        for mask in submasks(dims[:step]):
            piece = flip(blk, mask | (1 << dims[step]), bits)
            target = halves(full.at[arrival[j], piece], which)
            remote(
                target,
                target,
                tree_send.at[j, which, 0],
                tree_recv.at[j, which, piece],
                (other, head),
            ).wait_recv()

    def chain(j):
        if j == 0:
            source = shard
            left, right = head > 0, head < heads - 1
        else:
            source = full.at[arrival[j], blk]
            left = (arrival[j] > head) & (head > 0)
            right = (arrival[j] < head) & (head < heads - 1)
            remote(
                source, source, z_send.at[0, 0], z_recv.at[arrival[j]], (blk, head)
            ).wait_recv()
        for side, (condition, step) in enumerate(((left, -1), (right, 1))):
            make = lambda source=source, side=side, step=step: remote(
                source,
                full.at[arrival[j], blk],
                z_send.at[j, side],
                z_recv.at[arrival[j]],
                (blk, jnp.clip(head + step, 0, heads - 1)),
            )
            sends.start(make, when=condition)

    tree_step(0, 0)
    chain(0)
    own_shard = pltpu.make_async_copy(shard, full.at[head, blk], own_sem.at[1])
    own_shard.start()
    send_rows(1)

    micro = head // splits
    own_slots = perm[micro, pl.ds(blk, 1), :]
    ones[...] = jnp.where(iota((blks, group), 0) == own_slots // group, 1.0, 0.0)
    cumulative(ones, sums, group)
    rank = jnp.sum(ones[...] * sums[...], axis=0, keepdims=True).astype(jnp.int32) - 1
    dest = own_slots // group * pair + rank
    dest_row[...] = jnp.broadcast_to(dest, dest_row.shape)
    for tile in range(group // 128):
        block = jnp.broadcast_to(dest[:, tile * 128 : (tile + 1) * 128].astype(F32), (128, 128))
        dest_col[tile * 128 : (tile + 1) * 128, :] = block.T.astype(jnp.int32)

    all_slots = perm[micro]
    ones[...] = jnp.where(all_slots // group == blk, 1.0, 0.0)
    cumulative(ones, sums, group)
    rank_rows[...] = jnp.where(ones[...] > 0, sums[...] - 1, -1.0).astype(jnp.int32)

    @pl.loop(0, blks)
    def _(other):
        ranks = rank_rows[pl.ds(other, 1), :]
        inner = (perm[micro, pl.ds(other, 1), :] % group).astype(F32)
        found = jnp.where(iota((pair, group), 0) == ranks, inner, 0.0)
        column = jnp.sum(found, axis=1, keepdims=True).astype(jnp.int32)
        slot_col[pl.ds(pl.multiple_of(other * pair, pair), pair), :] = jnp.broadcast_to(
            column, (pair, 128)
        )

    for tile in range(group // 128):
        block = slot_col[tile * 128 : (tile + 1) * 128, :].astype(F32)
        slot_row[:, tile * 128 : (tile + 1) * 128] = block.T[0:8, :].astype(jnp.int32)

    def to_groups(i):
        exchanges[i].wait_head(
            0,
            lambda other: arrived.at[i, pl.ds(pl.multiple_of(other * rows, rows), rows), :],
            arrived.at[i, 0 : group - rows, :],
        )
        permute_rows(one_hot_from_row(dest_row), arrived.at[i], sorted_rows.at[i], group)
        exchanges[i].over_blk(
            lambda other: sorted_rows.at[i, pl.ds(other * pair, pair), :],
            lambda other: landed.at[i, pl.ds(pl.multiple_of(other * pair, pair), pair), :],
            landed.at[i, 0 : group - pair, :],
        )

    outs = (slots_x, slots_g)

    def to_slots(i):
        exchanges[i].wait_blk(
            lambda other: landed.at[i, pl.ds(pl.multiple_of(other * pair, pair), pair), :],
            landed.at[i, 0 : group - pair, :],
        )
        permute_rows(one_hot_from_row(slot_row), landed.at[i], ordered.at[i], group)
        exchanges[i].over_head(
            1,
            lambda other: ordered.at[i, pl.ds(other * rows, rows), :],
            lambda other: outs[i].at[other],
            outs[i].at[0 : heads - 1],
        )

    to_groups(0)
    for step in range(1, levels):
        tree_step(0, step)
    for j in range(1, heads):
        chain(j)
        tree_step(j, 0)
        if j == 1:
            to_slots(0)
            to_groups(1)
        if j == 2:
            to_slots(1)
        for step in range(1, levels):
            tree_step(j, step)
    for j in range(heads):
        for which in range(2):
            tree_wait(j, which, levels - 1)

    for i in range(2):
        exchanges[i].wait_head(1, lambda other: outs[i].at[other], outs[i].at[0 : heads - 1])
    for other in range(blks):

        @pl.when(other != blk)
        def _():
            remote(
                vectors,
                full_vectors.at[other],
                vec_send.at[other],
                vec_recv.at[other],
                (other, head),
            ).wait_recv()

    own_vec.wait()
    own_shard.wait()
    sends.finish()


def gather_all(blks, heads, tokens, out_grad, shard, vectors, perm):
    micros, rows, width = tokens.shape
    part = width * micros // heads
    group = rows * heads
    dma = pltpu.SemaphoreType.DMA
    any_space, vmem = pl.BlockSpec(memory_space=pl.ANY), pl.BlockSpec(memory_space=pltpu.VMEM)
    return pl.pallas_call(
        functools.partial(gather_kernel, blks, heads),
        name="gather_all",
        out_shape=(
            jax.ShapeDtypeStruct((heads, blks) + shard.shape, BF16),
            jax.ShapeDtypeStruct((blks,) + vectors.shape, BF16),
            jax.ShapeDtypeStruct((heads, rows, part), BF16),
            jax.ShapeDtypeStruct((heads, rows, part), BF16),
            jax.ShapeDtypeStruct((group, 128), jnp.int32),
            jax.ShapeDtypeStruct((group, 128), jnp.int32),
        ),
        in_specs=[any_space, any_space, any_space, any_space, vmem],
        out_specs=(any_space, any_space, any_space, any_space, vmem, vmem),
        scratch_shapes=[
            pltpu.VMEM((2, group, part), BF16),
            pltpu.VMEM((2, group, part), BF16),
            pltpu.VMEM((2, group, part), BF16),
            pltpu.VMEM((2, group, part), BF16),
            pltpu.VMEM((8, group), jnp.int32),
            pltpu.VMEM((8, group), jnp.int32),
            pltpu.VMEM((blks, group), F32),
            pltpu.VMEM((blks, group), F32),
            pltpu.VMEM((blks, group), jnp.int32),
        ]
        + exchange_sems(blks, heads)
        + [
            dma((heads, 2)),
            dma((heads,)),
            dma((heads, 2, blks)),
            dma((heads, 2, blks)),
            dma((blks,)),
            dma((blks,)),
            dma((2,)),
        ],
        compiler_params=pltpu.CompilerParams(
            collective_id=0, has_side_effects=True, vmem_limit_bytes=32 << 20
        ),
    )(tokens, out_grad, shard, vectors, perm)


def add_into(target, source, width):
    rows = target.shape[0]
    step = 16 if rows % 16 == 0 else rows

    @pl.loop(0, rows // step)
    def _(i):
        at = pl.ds(pl.multiple_of(i * step, step), step)
        for column in range(0, target.shape[1], width):
            cols = slice(column, column + width)
            target[at, cols] = target[at, cols] + source[at, cols]


def reduce_kernel(
    blks,
    heads,
    layer_out,
    x_grad,
    partial,
    vectors,
    dest_col,
    slot_col,
    out_rows,
    grad_rows,
    shard,
    vec_sum,
    total,
    from_core,
    from_tree,
    from_left,
    from_right,
    vec_parts,
    vec_mid,
    vec_heads,
    arrived,
    sorted_rows,
    landed,
    ordered,
    final,
    head_send,
    head_recv,
    blk_send,
    blk_recv,
    local,
    load_sem,
    core_send,
    core_recv,
    tree_send,
    tree_recv,
    left_send,
    left_recv,
    right_send,
    right_recv,
    vec_send,
    vec_recv,
    vec_head_send,
    vec_head_recv,
):
    blk, head = lax.axis_index("blk"), lax.axis_index("head")
    micros, rows, width = out_rows.shape
    splits = heads // micros
    part = width // splits
    group = rows * heads
    pair = group // blks
    levels = blks.bit_length() - 1
    bits = bits_of(blk, levels)
    half = shard.shape[1] // 2
    sends = Sends()
    sems = (head_send, head_recv, blk_send, blk_recv, local)
    exchanges = [RowExchange(sends, blk, head, blks, heads, sems, i) for i in range(2)]
    sources = (layer_out, x_grad)

    enter(blk, head, blks, heads)

    order = []
    for i in range(heads):
        order.append(heads - 1 - i // 2 if i % 2 == 0 else i // 2)

    even = submasks(range(1, levels))
    loads = {}
    for other in order:
        for mask in even:
            piece = flip(blk, mask, bits)
            loads[other, mask] = pltpu.make_async_copy(
                partial.at[other, piece], total.at[other, mask // 2], load_sem.at[other, mask // 2]
            )
            loads[other, mask].start()
            sends.start(
                lambda other=other, mask=mask: remote(
                    partial.at[other, flip(blk, mask | 1, bits)],
                    from_core.at[other, mask // 2],
                    core_send.at[other, mask // 2],
                    core_recv.at[other, mask // 2],
                    (flip(blk, 1, bits), head),
                )
            )

    def rows_to_heads(i):
        exchanges[i].over_head(
            0,
            lambda other: sources[i].at[other],
            lambda other: arrived.at[i, pl.ds(pl.multiple_of(other * rows, rows), rows), :],
            arrived.at[i, 0 : group - rows, :],
        )

    rows_to_heads(0)
    rows_to_heads(1)

    for other in range(blks):
        sends.start(
            lambda other=other: remote(
                vectors.at[other],
                vec_parts.at[blk],
                vec_send.at[other],
                vec_recv.at[blk],
                (other, head),
            ),
            when=other != blk,
        )

    def add_core(other):
        for mask in even:
            loads[other, mask].wait()
            target = from_core.at[other, mask // 2]
            remote(
                target,
                target,
                core_send.at[other, mask // 2],
                core_recv.at[other, mask // 2],
                (flip(blk, 1, bits), head),
            ).wait_recv()
            add_into(total.at[other, mask // 2], target, half)

    orders = [list(range(levels - 1, 0, -1)), [1] + list(range(levels - 1, 1, -1))]

    def cols(ref, which):
        return ref.at[:, which * half : (which + 1) * half]

    def tree_parts(which, step):
        dims = orders[which]
        free = dims[step + 1 :]
        base = sum(1 << (levels - 2 - earlier) for earlier in range(step))
        return dims[step], [(mask, base + i) for i, mask in enumerate(submasks(free))]

    def tree_start(other, step):
        for which in range(2):
            dim, parts = tree_parts(which, step)
            for mask, slot in parts:
                sends.start(
                    lambda which=which, dim=dim, mask=mask, slot=slot: remote(
                        cols(total.at[other, (mask | (1 << dim)) // 2], which),
                        from_tree.at[which, other, slot],
                        tree_send.at[which, other, slot],
                        tree_recv.at[which, other, slot],
                        (flip(blk, 1 << dim, bits), head),
                    )
                )

    def tree_add(other, step):
        for which in range(2):
            dim, parts = tree_parts(which, step)
            for mask, slot in parts:
                source = from_tree.at[which, other, slot]
                remote(
                    source,
                    source,
                    tree_send.at[which, other, slot],
                    tree_recv.at[which, other, slot],
                    (flip(blk, 1 << dim, bits), head),
                ).wait_recv()
                add_into(cols(total.at[other, mask // 2], which), source, half)

    def pass_right(goal):
        target = from_left.at[goal]

        @pl.when((head > 0) & (head <= goal))
        def _():
            remote(
                target, target, left_send.at[goal], left_recv.at[goal], (blk, head)
            ).wait_recv()
            add_into(total.at[goal, 0], target, half)

        sends.start(
            lambda: remote(
                total.at[goal, 0],
                target,
                left_send.at[goal],
                left_recv.at[goal],
                (blk, jnp.minimum(head + 1, heads - 1)),
            ),
            when=head < goal,
        )

    def pass_left(goal):
        target = from_right.at[goal]

        @pl.when((head < heads - 1) & (head >= goal))
        def _():
            remote(
                target, target, right_send.at[goal], right_recv.at[goal], (blk, head)
            ).wait_recv()
            add_into(total.at[goal, 0], target, half)

        sends.start(
            lambda: remote(
                total.at[goal, 0],
                target,
                right_send.at[goal],
                right_recv.at[goal],
                (blk, jnp.maximum(head - 1, 0)),
            ),
            when=head > goal,
        )

    def to_groups(i):
        exchanges[i].wait_head(
            0,
            lambda other: arrived.at[i, pl.ds(pl.multiple_of(other * rows, rows), rows), :],
            arrived.at[i, 0 : group - rows, :],
        )
        permute_rows(one_hot_from_column(slot_col, group), arrived.at[i], sorted_rows.at[i], group)
        exchanges[i].over_blk(
            lambda other: sorted_rows.at[i, pl.ds(other * pair, pair), :],
            lambda other: landed.at[i, pl.ds(pl.multiple_of(other * pair, pair), pair), :],
            landed.at[i, 0 : group - pair, :],
        )

    def to_positions(i):
        exchanges[i].wait_blk(
            lambda other: landed.at[i, pl.ds(pl.multiple_of(other * pair, pair), pair), :],
            landed.at[i, 0 : group - pair, :],
        )
        permute_rows(one_hot_from_column(dest_col, group), landed.at[i], ordered.at[i], group)
        exchanges[i].over_head(
            1,
            lambda other: ordered.at[i, pl.ds(other * rows, rows), :],
            lambda other: final.at[i, other],
            final.at[i, 0 : heads - 1],
        )

    for other in order[:2]:
        add_core(other)
        tree_start(other, 0)
    to_groups(0)
    for other in order[2:]:
        add_core(other)
        tree_start(other, 0)
    to_groups(1)
    for other in order[:2]:
        for step in range(levels - 1):
            tree_add(other, step)
            if step < levels - 2:
                tree_start(other, step + 1)
    to_positions(0)
    for position, other in enumerate(order):
        if position >= 2:
            for step in range(levels - 1):
                tree_add(other, step)
                if step < levels - 2:
                    tree_start(other, step + 1)
        if position == 2:
            to_positions(1)

    vec_mid[...] = vectors[pl.ds(blk, 1)][0]
    for other in range(blks):

        @pl.when(other != blk)
        def _():
            remote(
                vec_parts.at[other],
                vec_parts.at[other],
                vec_send.at[other],
                vec_recv.at[other],
                (other, head),
            ).wait_recv()
            vec_mid[...] += vec_parts[other]

    for other in range(heads):
        sends.start(
            lambda other=other: remote(
                vec_mid,
                vec_heads.at[head],
                vec_head_send.at[other],
                vec_head_recv.at[head],
                (blk, other),
            ),
            when=other != head,
        )

    for i in range(heads):
        goal = heads - 1 - i
        pass_right(goal)
        pass_left(i)

    for own in range(heads):

        @pl.when(own == head)
        def _():
            shard[...] = total[own, 0].astype(F32)

    vec_sum[...] = vec_mid[...]
    for other in range(heads):

        @pl.when(other != head)
        def _():
            remote(
                vec_heads.at[other],
                vec_heads.at[other],
                vec_head_send.at[other],
                vec_head_recv.at[other],
                (blk, other),
            ).wait_recv()
            vec_sum[...] += vec_heads[other]

    for i in range(2):
        exchanges[i].wait_head(1, lambda other: final.at[i, other], final.at[i, 0 : heads - 1])
    for source in range(heads):
        micro, which = source // splits, source % splits
        out_rows[micro, :, which * part : (which + 1) * part] = final[0, source]
        grad_rows[micro, :, which * part : (which + 1) * part] = final[1, source].astype(F32)
    sends.finish()


def reduce_all(blks, heads, layer_out, x_grad, partial, vectors, dest_col, slot_col):
    _, rows, part = layer_out.shape
    micros = 2
    group = rows * heads
    width = part * heads // micros
    size = partial.shape[2:]
    half = size[1] // 2
    dma = pltpu.SemaphoreType.DMA
    any_space, vmem = pl.BlockSpec(memory_space=pl.ANY), pl.BlockSpec(memory_space=pltpu.VMEM)
    vec = vectors.shape[1:]
    return pl.pallas_call(
        functools.partial(reduce_kernel, blks, heads),
        name="reduce_all",
        out_shape=(
            jax.ShapeDtypeStruct((micros, rows, width), BF16),
            jax.ShapeDtypeStruct((micros, rows, width), F32),
            jax.ShapeDtypeStruct(size, F32),
            jax.ShapeDtypeStruct(vec, F32),
        ),
        in_specs=[any_space, any_space, any_space, vmem, vmem, vmem],
        out_specs=(vmem, vmem, vmem, vmem),
        scratch_shapes=[
            pltpu.VMEM((heads, blks // 2) + size, BF16),
            pltpu.VMEM((heads, blks // 2) + size, BF16),
            pltpu.VMEM((2, heads, blks // 2 - 1, size[0], half), BF16),
            pltpu.VMEM((heads,) + size, BF16),
            pltpu.VMEM((heads,) + size, BF16),
            pltpu.VMEM((blks,) + vec, F32),
            pltpu.VMEM(vec, F32),
            pltpu.VMEM((heads,) + vec, F32),
            pltpu.VMEM((2, group, part), BF16),
            pltpu.VMEM((2, group, part), BF16),
            pltpu.VMEM((2, group, part), BF16),
            pltpu.VMEM((2, group, part), BF16),
            pltpu.VMEM((2, heads, rows, part), BF16),
        ]
        + exchange_sems(blks, heads)
        + [
            dma((heads, blks // 2)),
            dma((heads, blks // 2)),
            dma((heads, blks // 2)),
            dma((2, heads, blks // 2 - 1)),
            dma((2, heads, blks // 2 - 1)),
            dma((heads,)),
            dma((heads,)),
            dma((heads,)),
            dma((heads,)),
            dma((blks,)),
            dma((blks,)),
            dma((heads,)),
            dma((heads,)),
        ],
        compiler_params=pltpu.CompilerParams(
            collective_id=1, has_side_effects=True, vmem_limit_bytes=56 << 20
        ),
    )(layer_out, x_grad, partial, vectors, dest_col, slot_col)


def contract(left, right, dims):
    return lax.dot_general(left, right, ((dims[:1], dims[1:]), ((), ())), preferred_element_type=F32)


def assemble_attention(packed, qkv, out):
    heads, width, _ = packed.shape
    wide, narrow = qkv.shape[1] // heads, out.shape[1] // heads

    @pl.loop(0, width // CLUSTER)
    def _(tile):
        rows = pl.ds(pl.multiple_of(tile * CLUSTER, CLUSTER), CLUSTER)
        for head in range(heads):
            qkv[rows, head * wide : (head + 1) * wide] = packed[head, rows, 0:wide]
            out[rows, head * narrow : (head + 1) * narrow] = packed[
                head, rows, wide : wide + narrow
            ]


def column_sum(values):
    return jnp.sum(values, axis=0, keepdims=True)


def row_mean(values):
    return jnp.mean(values, axis=1, keepdims=True)


def normalize(hidden):
    center = hidden - row_mean(hidden)
    scale = lax.rsqrt(row_mean(center * center) + norm_epsilon)
    return center * scale, scale


def norm_derivative(normal, scale, cotangent, gain):
    scaled = cotangent * gain
    return scale * (scaled - row_mean(scaled) - normal * row_mean(scaled * normal))


def forward_kernel(
    slots_x,
    weights,
    bias_qkv,
    vectors,
    seg_col,
    seg_row,
    x,
    proj,
    probs,
    context,
    attn_res,
    qkv,
    out,
    packed,
    sem,
):
    heads, rows, part = slots_x.shape
    tokens, width = x.shape
    splits = width // part
    load = pltpu.make_async_copy(weights.at[:, :, 0 : packed.shape[2]], packed, sem.at[0])
    load.start()
    for source in range(heads):
        micro, which = source // splits, source % splits
        x[micro * rows : (micro + 1) * rows, which * part : (which + 1) * part] = slots_x[source]
    load.wait()
    assemble_attention(packed, qkv, out)
    project(x, qkv, bias_qkv, proj)
    attend(proj, probs, context, seg_col, seg_row)
    leave_attention(x, context, out, vectors, attn_res)


def project(x, qkv, bias_qkv, proj):
    @pl.loop(0, proj.shape[1] // 256)
    def _(tile):
        cols = pl.ds(pl.multiple_of(tile * 256, 256), 256)
        sums = jnp.dot(x[...], qkv[:, cols], preferred_element_type=F32)
        proj[:, cols] = (sums + bias_qkv[:, cols]).astype(BF16)


def two_heads(tile, first):
    zero = jnp.zeros_like(tile)
    return jnp.concatenate([jnp.where(first, tile, zero), jnp.where(first, zero, tile)], axis=0)


def attend(proj, probs, context, seg_col, seg_row):
    tokens, width = context.shape
    first = iota((CLUSTER, 128), 1) < HEAD_DIM

    @pl.loop(0, tokens // CLUSTER)
    def _(cluster):
        rows = pl.ds(pl.multiple_of(cluster * CLUSTER, CLUSTER), CLUSTER)
        column = seg_col[rows, 0:1]
        allowed = jnp.concatenate([column, column], axis=0) == seg_row[pl.ds(cluster, 1), :]
        for pair in range(width // 128):
            at = pair * 128
            q = two_heads(proj[rows, at : at + 128], first)
            k = proj[rows, width + at : width + at + 128]
            v = proj[rows, 2 * width + at : 2 * width + at + 128]
            scores = contract(q, k, (1, 1)) * 0.125
            scores = jnp.where(allowed, scores, masked_score)
            weight = jnp.exp(scores - jnp.max(scores, axis=1, keepdims=True))
            p = (weight / jnp.sum(weight, axis=1, keepdims=True)).astype(BF16)
            probs[cluster, pair] = p
            both = jnp.dot(p, v, preferred_element_type=F32)
            context[rows, at : at + 128] = jnp.where(
                first, both[:CLUSTER], both[CLUSTER:]
            ).astype(BF16)


def leave_attention(x, context, out, vectors, attn_res):
    @pl.loop(0, x.shape[1] // 256)
    def _(tile):
        cols = pl.ds(pl.multiple_of(tile * 256, 256), 256)
        sums = jnp.dot(context[...], out[:, cols], preferred_element_type=F32)
        attn_res[:, cols] = x[:, cols].astype(F32) + sums + vectors[2:3, cols]


def forward_part(slots_x, weights, bias_qkv, vectors, seg_col, seg_row):
    heads, rows, part = slots_x.shape
    width = weights.shape[1]
    tokens = heads * part * rows // width
    vmem = pl.BlockSpec(memory_space=pltpu.VMEM)
    return pl.pallas_call(
        forward_kernel,
        name="forward_part",
        out_shape=(
            jax.ShapeDtypeStruct((tokens, width), BF16),
            jax.ShapeDtypeStruct((tokens, 3 * width), BF16),
            jax.ShapeDtypeStruct((tokens // CLUSTER, width // 128, 2 * CLUSTER, CLUSTER), BF16),
            jax.ShapeDtypeStruct((tokens, width), BF16),
            jax.ShapeDtypeStruct((tokens, width), F32),
            jax.ShapeDtypeStruct((width, 3 * width), BF16),
            jax.ShapeDtypeStruct((width, width), BF16),
        ),
        in_specs=[vmem, pl.BlockSpec(memory_space=pl.ANY), vmem, vmem, vmem, vmem],
        out_specs=(vmem,) * 7,
        scratch_shapes=[
            pltpu.VMEM((heads, width, width), BF16),
            pltpu.SemaphoreType.DMA((1,)),
        ],
        compiler_params=pltpu.CompilerParams(vmem_limit_bytes=48 << 20),
    )(slots_x, weights, bias_qkv, vectors, seg_col, seg_row)


def ffn_kernel(
    share,
    attn_res,
    slots_g,
    weights,
    vectors,
    up_bias,
    layer_out,
    d_attn,
    g_attn,
    partial,
    vec_grads,
    up_bias_grad,
    packed,
    down,
    normed,
    hidden,
    hidden_t,
    active,
    slope,
    g_pre,
    ffn_res,
    g_down,
    sem,
):
    heads, rows, part = slots_g.shape
    tokens, width = attn_res.shape
    ff = active.shape[1]
    fold = ff // width
    short = width // heads
    splits = width // part
    load = pltpu.make_async_copy(weights.at[:, :, width : 3 * width], packed, sem.at[0])
    load.start()
    gain_attn, shift_attn = vectors[3:4, :], vectors[4:5, :]
    bias_down, gain_ffn, shift_ffn = vectors[5:6, :], vectors[6:7, :], vectors[7:8, :]
    vec_grads[...] = jnp.zeros_like(vec_grads)

    def row_tiles(body):
        @pl.loop(0, tokens // CLUSTER)
        def _(tile):
            body(tile, pl.ds(pl.multiple_of(tile * CLUSTER, CLUSTER), CLUSTER))

    def first_norm(tile, at):
        normal, _ = normalize(attn_res[at, :])
        values = normal * gain_attn + shift_attn
        normed[at, :] = values
        hidden[at, :] = values.astype(BF16)

    row_tiles(first_norm)
    hidden_t[...] = hidden[...].T
    load.wait()

    blks = width // share

    @pl.loop(0, blks)
    def _(blk):
        source = pl.ds(pl.multiple_of(blk * share, share), share)
        for j in range(fold):
            target = pl.ds(pl.multiple_of(blk * share * fold + j * share, share), share)
            for head in range(heads):
                down[target, head * short : (head + 1) * short] = packed[
                    head, source, width + j * short : width + (j + 1) * short
                ]

    per_head = width // 256

    @pl.loop(0, ff // 256)
    def _(tile):
        cols = pl.ds(pl.multiple_of(tile * 256, 256), 256)
        inner = pl.ds(pl.multiple_of(tile % per_head * 256, 256), 256)
        pre = jnp.dot(
            hidden[...], packed[tile // per_head, :, inner], preferred_element_type=F32
        )
        pre = pre + up_bias[:, cols]
        below = 0.5 + 0.5 * lax.erf(pre * (0.5**0.5))
        active[:, cols] = (pre * below).astype(BF16)
        slope[:, cols] = below + pre * jnp.exp(-0.5 * pre * pre) * (0.5 / jnp.pi) ** 0.5

    @pl.loop(0, width // 256)
    def _(tile):
        cols = pl.ds(pl.multiple_of(tile * 256, 256), 256)
        sums = jnp.dot(active[...], down[:, cols], preferred_element_type=F32)
        ffn_res[:, cols] = normed[:, cols] + sums + vectors[5:6, cols]

    def second_norm(tile, at):
        normal, scale = normalize(ffn_res[at, :])
        result = (normal * gain_ffn + shift_ffn).astype(BF16)
        micro = tile * CLUSTER // rows
        inner = pl.ds(pl.multiple_of(tile * CLUSTER % rows, CLUSTER), CLUSTER)
        for which in range(splits):
            layer_out[micro * splits + which, inner, :] = result[
                :, which * part : (which + 1) * part
            ]
        cotangent = jnp.concatenate(
            [slots_g[micro * splits + which, inner, :] for which in range(splits)], axis=1
        ).astype(F32)
        d_ffn = norm_derivative(normal, scale, cotangent, gain_ffn)
        low = d_ffn.astype(BF16)
        g_down[at, :] = low
        ffn_res[at, :] = d_ffn
        vec_grads[5:6, :] += column_sum(low.astype(F32))
        vec_grads[6:7, :] += column_sum(cotangent * normal)
        vec_grads[7:8, :] += column_sum(cotangent)

    row_tiles(second_norm)

    @pl.loop(0, ff // 256)
    def _(tile):
        cols = pl.ds(pl.multiple_of(tile * 256, 256), 256)
        inner = pl.ds(pl.multiple_of(tile % per_head * 256, 256), 256)
        d_active = contract(g_down[...], down[cols, :], (1, 1))
        low = (d_active * slope[:, cols]).astype(BF16)
        g_pre[:, cols] = low
        up_bias_grad[:, cols] = column_sum(low.astype(F32))
        up_grad = jnp.dot(hidden_t[...], low, preferred_element_type=F32)
        partial[tile // per_head, :, inner] = up_grad.astype(BF16)

    @pl.loop(0, blks)
    def _(blk):
        wide = share * fold
        cols = pl.ds(pl.multiple_of(blk * wide, wide), wide)
        down_grad = contract(active[:, cols], g_down[...], (0, 0)).astype(BF16)
        target = pl.ds(pl.multiple_of(blk * share, share), share)
        for j in range(fold):
            for head in range(heads):
                partial[head, target, width + j * short : width + (j + 1) * short] = down_grad[
                    j * share : (j + 1) * share, head * short : (head + 1) * short
                ]

    @pl.loop(0, width // 256)
    def _(tile):
        cols = pl.ds(pl.multiple_of(tile * 256, 256), 256)
        sums = ffn_res[:, cols]
        for head in range(heads):
            sums = sums + contract(
                g_pre[:, head * width : (head + 1) * width], packed[head, cols, 0:width], (1, 1)
            )
        normed[:, cols] = sums

    def first_norm_back(tile, at):
        normal, scale = normalize(attn_res[at, :])
        cotangent = normed[at, :]
        grad = norm_derivative(normal, scale, cotangent, gain_attn)
        low = grad.astype(BF16)
        d_attn[at, :] = grad
        g_attn[at, :] = low
        vec_grads[2:3, :] += column_sum(low.astype(F32))
        vec_grads[3:4, :] += column_sum(cotangent * normal)
        vec_grads[4:5, :] += column_sum(cotangent)

    row_tiles(first_norm_back)


def ffn_part(share, attn_res, slots_g, weights, vectors, up_bias):
    heads = weights.shape[0]
    tokens, width = attn_res.shape
    ff = up_bias.shape[1]
    vmem = pl.BlockSpec(memory_space=pltpu.VMEM)
    return pl.pallas_call(
        functools.partial(ffn_kernel, share),
        name="ffn_part",
        out_shape=(
            jax.ShapeDtypeStruct(slots_g.shape, BF16),
            jax.ShapeDtypeStruct((tokens, width), F32),
            jax.ShapeDtypeStruct((tokens, width), BF16),
            jax.ShapeDtypeStruct((heads, width, 2 * width), BF16),
            jax.ShapeDtypeStruct((8, width), F32),
            jax.ShapeDtypeStruct((1, ff), F32),
        ),
        in_specs=[vmem, vmem, pl.BlockSpec(memory_space=pl.ANY), vmem, vmem],
        out_specs=(vmem,) * 6,
        scratch_shapes=[
            pltpu.VMEM((heads, width, 2 * width), BF16),
            pltpu.VMEM((ff, width), BF16),
            pltpu.VMEM((tokens, width), F32),
            pltpu.VMEM((tokens, width), BF16),
            pltpu.VMEM((width, tokens), BF16),
            pltpu.VMEM((tokens, ff), BF16),
            pltpu.VMEM((tokens, ff), F32),
            pltpu.VMEM((tokens, ff), BF16),
            pltpu.VMEM((tokens, width), F32),
            pltpu.VMEM((tokens, width), BF16),
            pltpu.SemaphoreType.DMA((1,)),
        ],
        compiler_params=pltpu.CompilerParams(vmem_limit_bytes=60 << 20),
    )(attn_res, slots_g, weights, vectors, up_bias)


def attend_back(proj, probs, g_context, g_proj, begin=0, end=None):
    tokens, width = g_context.shape
    first = iota((CLUSTER, 128), 1) < HEAD_DIM

    @pl.loop(begin, tokens // CLUSTER if end is None else end)
    def _(cluster):
        rows = pl.ds(pl.multiple_of(cluster * CLUSTER, CLUSTER), CLUSTER)
        for pair in range(width // 128):
            at = pair * 128
            q = two_heads(proj[rows, at : at + 128], first)
            k = proj[rows, width + at : width + at + 128]
            v = proj[rows, 2 * width + at : 2 * width + at + 128]
            g = two_heads(g_context[rows, at : at + 128], first)
            low = probs[cluster, pair]
            p = low.astype(F32)
            dprob = contract(g, v, (1, 1))
            delta = jnp.sum(p * dprob, axis=1, keepdims=True)
            dscore = (p * (dprob - delta)).astype(BF16)
            both = jnp.dot(dscore, k, preferred_element_type=F32)
            g_q = jnp.where(first, both[:CLUSTER], both[CLUSTER:]) * 0.125
            g_k = contract(dscore, q, (0, 0)) * 0.125
            g_v = contract(low, g, (0, 0))
            g_proj[rows, at : at + 128] = g_q.astype(BF16)
            g_proj[rows, width + at : width + at + 128] = g_k.astype(BF16)
            g_proj[rows, 2 * width + at : 2 * width + at + 128] = g_v.astype(BF16)


def backward_kernel(
    x,
    proj,
    probs,
    context,
    qkv,
    out,
    d_attn,
    g_attn,
    x_grad,
    partial,
    vec_grads,
    g_context,
    g_proj,
    x_t,
    natural,
):
    heads, rows, part = x_grad.shape
    tokens, width = x.shape
    splits = width // part
    wide, narrow = 3 * width // heads, width // heads
    g_context[...] = contract(g_attn[...], out[...], (1, 1)).astype(BF16)
    x_t[...] = context[...].T

    def tiles(count, body):
        @pl.loop(0, count)
        def _(tile):
            body(pl.ds(pl.multiple_of(tile * 256, 256), 256))

    def out_grad(cols):
        natural[:, cols] = jnp.dot(
            x_t[...], g_attn[:, cols], preferred_element_type=F32
        ).astype(BF16)

    tiles(width // 256, out_grad)

    @pl.loop(0, width // CLUSTER)
    def _(tile):
        at = pl.ds(pl.multiple_of(tile * CLUSTER, CLUSTER), CLUSTER)
        for head in range(heads):
            partial[head, at, wide : wide + narrow] = natural[
                at, head * narrow : (head + 1) * narrow
            ]

    attend_back(proj, probs, g_context, g_proj)
    x_t[...] = x[...].T

    def qkv_grad(cols):
        natural[:, cols] = jnp.dot(
            x_t[...], g_proj[:, cols], preferred_element_type=F32
        ).astype(BF16)

    tiles(3 * width // 256, qkv_grad)

    @pl.loop(0, width // CLUSTER)
    def _(tile):
        at = pl.ds(pl.multiple_of(tile * CLUSTER, CLUSTER), CLUSTER)
        for head in range(heads):
            partial[head, at, 0:wide] = natural[at, head * wide : (head + 1) * wide]

    vec_grads[...] = jnp.zeros_like(vec_grads)
    vec_grads[0:1, :] = column_sum(g_proj[:, 0:width].astype(F32))
    vec_grads[1:2, :] = column_sum(g_proj[:, 2 * width :].astype(F32))
    for which in range(splits):
        for piece in range(part // 128):
            at = which * part + piece * 128
            sums = d_attn[:, at : at + 128] + contract(g_proj[...], qkv[at : at + 128, :], (1, 1))
            for micro in range(heads // splits):
                x_grad[micro * splits + which, :, piece * 128 : (piece + 1) * 128] = sums[
                    micro * rows : (micro + 1) * rows
                ].astype(BF16)


def backward_part(heads, rows, x, proj, probs, context, qkv, out, d_attn, g_attn):
    tokens, width = x.shape
    part = tokens * width // (heads * rows)
    vmem = pl.BlockSpec(memory_space=pltpu.VMEM)
    return pl.pallas_call(
        backward_kernel,
        name="backward_part",
        out_shape=(
            jax.ShapeDtypeStruct((heads, rows, part), BF16),
            jax.ShapeDtypeStruct((heads, width, width), BF16),
            jax.ShapeDtypeStruct((8, width), F32),
        ),
        in_specs=[vmem] * 8,
        out_specs=(vmem,) * 3,
        scratch_shapes=[
            pltpu.VMEM((tokens, width), BF16),
            pltpu.VMEM((tokens, 3 * width), BF16),
            pltpu.VMEM((width, tokens), BF16),
            pltpu.VMEM((width, 3 * width), BF16),
        ],
        compiler_params=pltpu.CompilerParams(vmem_limit_bytes=48 << 20),
    )(x, proj, probs, context, qkv, out, d_attn, g_attn)


def fused_scratch(micros, rows, width, blks, heads, share, fold):
    dma = pltpu.SemaphoreType.DMA
    vmem = pltpu.VMEM
    tokens = micros * rows
    part = width * micros // heads
    group = rows * heads
    ff = width * fold
    half = width // 2
    kept = blks // 2
    levels = blks.bit_length() - 1
    return dict(
        arrived=vmem((2, group, part), BF16),
        sorted_rows=vmem((2, group, part), BF16),
        landed=vmem((2, group, part), BF16),
        ordered=vmem((2, group, part), BF16),
        slots=vmem((2, heads, rows, part), BF16),
        dest_row=vmem((8, group), jnp.int32),
        slot_row=vmem((8, group), jnp.int32),
        dest_col=vmem((group, 128), jnp.int32),
        slot_col=vmem((group, 128), jnp.int32),
        ones=vmem((blks, group), F32),
        sums=vmem((blks, group), F32),
        rank_rows=vmem((blks, group), jnp.int32),
        seg_col=vmem((tokens, 128), F32),
        seg_row=vmem((8 * (-(-tokens // CLUSTER // 8)), CLUSTER), F32),
        perm=vmem((micros, blks, group), jnp.int32),
        shard=vmem((share, 3 * width), BF16),
        small_sums=vmem((16, 128), F32),
        small=vmem((16, 128), BF16),
        packed=vmem((heads, width, 3 * width), BF16),
        qkv=vmem((width, 3 * width), BF16),
        out=vmem((width, width), BF16),
        down=vmem((ff, width), BF16),
        full_vectors=vmem((blks, 16, 128), BF16),
        vectors=vmem((8, width), F32),
        bias_qkv=vmem((1, 3 * width), F32),
        up_bias=vmem((1, ff), F32),
        vec_grads=vmem((8, width), F32),
        up_bias_grad=vmem((1, ff), F32),
        x=vmem((tokens, width), BF16),
        proj=vmem((tokens, 3 * width), BF16),
        probs=vmem((tokens // CLUSTER, width // 128, 2 * CLUSTER, CLUSTER), BF16),
        context=vmem((tokens, width), BF16),
        attn_res=vmem((tokens, width), F32),
        normed=vmem((tokens, width), F32),
        hidden=vmem((tokens, width), BF16),
        turned=vmem((width, tokens), BF16),
        active=vmem((tokens, ff), BF16),
        slope=vmem((tokens, ff), BF16),
        ffn_res=vmem((tokens, width), F32),
        g_down=vmem((tokens, width), BF16),
        g_attn=vmem((tokens, width), BF16),
        staged=vmem((2, kept, share, width), BF16),
        from_tree=vmem((3, 2, heads, kept - 1, share, half), BF16),
        from_head=vmem((3, heads, share, width), BF16),
        vec_split=vmem((blks, 16, 128), F32),
        vec_parts=vmem((blks, 16, 128), F32),
        vec_mid=vmem((16, 128), F32),
        vec_heads=vmem((heads, 16, 128), F32),
        head_send=dma((4, 2)),
        head_recv=dma((4, 2)),
        blk_send=dma((4,)),
        blk_recv=dma((4,)),
        local=dma((4, 3)),
        z_send=dma((2, heads, 2)),
        z_recv=dma((2, heads)),
        tree_send=dma((2,)),
        tree_recv=dma((2, heads, 2, levels)),
        small_send=dma((3,)),
        small_recv=dma((3,)),
        own_sem=dma((2,)),
        core_send=dma((3,)),
        core_recv=dma((3, heads)),
        stage_sem=dma((2,)),
        down_send=dma((3,)),
        down_recv=dma((3, 2, heads, levels - 1)),
        pair_send=dma((3,)),
        pair_recv=dma((3, heads)),
        out_sem=dma((2, 3)),
    )


def fused_kernel(names, blks, heads, share, fold, *refs):
    r = types.SimpleNamespace(**dict(zip(names, refs)))
    blk, head = lax.axis_index("blk"), lax.axis_index("head")
    micros, rows, width = r.tokens.shape
    tokens = micros * rows
    splits = heads // micros
    part = width // splits
    group = rows * heads
    pair = group // blks
    ff = width * fold
    short = width // heads
    levels = blks.bit_length() - 1
    bits = bits_of(blk, levels)
    sends = Sends()
    sems = (r.head_send, r.head_recv, r.blk_send, r.blk_recv, r.local)
    exchanges = [RowExchange(sends, blk, head, blks, heads, sems, i) for i in range(4)]

    def tiles(count, size):
        def run(body):
            @pl.loop(0, count)
            def _(tile):
                body(tile, pl.ds(pl.multiple_of(tile * size, size), size))

        return run

    row_tiles = tiles(tokens // CLUSTER, CLUSTER)


    def head_block(ref, i):
        return lambda other: ref.at[i, pl.ds(pl.multiple_of(other * rows, rows), rows), :]

    def blk_block(ref, i):
        return lambda other: ref.at[i, pl.ds(pl.multiple_of(other * pair, pair), pair), :]

    def head_blocks(ref, i):
        return ref.at[i, 0 : group - rows, :]

    def blk_blocks(ref, i):
        return ref.at[i, 0 : group - pair, :]

    def row_source(ref):
        return lambda other: ref.at[
            other // splits, :, (other % splits) * part : (other % splits + 1) * part
        ]

    def own_rows(ref):
        return lambda other: ref.at[
            other // splits * rows : (other // splits + 1) * rows,
            (other % splits) * part : (other % splits + 1) * part,
        ]

    def to_heads(i, source):
        exchanges[i].over_head(0, source, head_block(r.arrived, i % 2), head_blocks(r.arrived, i % 2))

    def to_groups(i, one_hot):
        exchanges[i].wait_head(0, head_block(r.arrived, i % 2), head_blocks(r.arrived, i % 2))
        permute_rows(one_hot, r.arrived.at[i % 2], r.sorted_rows.at[i % 2], group)
        exchanges[i].over_blk(
            blk_block(r.sorted_rows, i % 2), blk_block(r.landed, i % 2), blk_blocks(r.landed, i % 2)
        )

    def to_owners(i, one_hot):
        exchanges[i].wait_blk(blk_block(r.landed, i % 2), blk_blocks(r.landed, i % 2))
        permute_rows(one_hot, r.landed.at[i % 2], r.ordered.at[i % 2], group)
        exchanges[i].over_head(
            1,
            head_block(r.ordered, i % 2),
            lambda other: r.slots.at[i % 2, other],
            r.slots.at[i % 2, 0 : heads - 1],
        )

    def rows_here(i):
        exchanges[i].wait_head(
            1, lambda other: r.slots.at[i % 2, other], r.slots.at[i % 2, 0 : heads - 1]
        )


    parts = ((0, width), (width, 2 * width))
    orders = [list(range(1, levels)) + [0], list(range(2, levels)) + [1, 0]]
    arrival = [
        choose(
            head,
            [
                sorted([x for x in range(heads) if x != own], key=lambda x: (abs(x - own), x))[j - 1]
                for own in range(heads)
            ],
        )
        if j
        else head
        for j in range(heads)
    ]

    def piece_rows(piece):
        return pl.ds(pl.multiple_of(piece * share, share), share)

    def part_cols(p, which=None):
        base, size = parts[p]
        if which is None:
            return slice(base, base + size)
        return slice(base + which * size // 2, base + (which + 1) * size // 2)

    def tree_wait(p, j, which, step):
        pieces = slice(0, share << step)
        await_bytes(
            r.packed.at[arrival[j], pieces, part_cols(p, which)], r.tree_recv.at[p, j, which, step]
        )

    def forwards(j):
        left = (arrival[j] > head) & (head > 0)
        right = (arrival[j] < head) & (head < heads - 1)
        return left, right

    def chain_wait(p, j):
        target = r.packed.at[arrival[j], piece_rows(blk), part_cols(p)]
        remote(
            target, target, r.z_send.at[p, 0, 0], r.z_recv.at[p, arrival[j]], (blk, head)
        ).wait_recv()

    def tree_step(p, j, step):
        if step == 0 and j:
            left, right = forwards(j)

            @pl.when(jnp.logical_not(left | right))
            def _():
                chain_wait(p, j)

        for which in range(2):
            dims = orders[which]
            if step:
                tree_wait(p, j, which, step - 1)
            if step == levels:
                continue
            other = flip(blk, 1 << dims[step], bits)
            sent = r.packed.at[:, 0 : (blks - 1) * share, part_cols(p)]
            for mask in submasks(dims[:step]):
                piece = flip(blk, mask, bits)
                target = r.packed.at[arrival[j], piece_rows(piece), part_cols(p, which)]
                first = j == 0 and mask == 0
                source = r.shard.at[:, part_cols(p, which)] if first else target
                sends.start(
                    lambda source=source, target=target, other=other, which=which: remote(
                        source,
                        target,
                        r.tree_send.at[p],
                        r.tree_recv.at[p, j, which, step],
                        (other, head),
                    ),
                    tag="weights",
                    shared=(p, lambda: await_bytes(sent, r.tree_send.at[p])),
                )

    def chain(p, j):
        target = r.packed.at[arrival[j], piece_rows(blk), part_cols(p)]
        if j == 0:
            source = r.shard.at[:, part_cols(p)]
            left, right = head > 0, head < heads - 1
        else:
            source = target
            left, right = forwards(j)

            @pl.when(left | right)
            def _():
                chain_wait(p, j)

        for side, (condition, step) in enumerate(((left, -1), (right, 1))):
            sends.start(
                lambda side=side, step=step: remote(
                    source,
                    target,
                    r.z_send.at[p, j, side],
                    r.z_recv.at[p, arrival[j]],
                    (blk, jnp.clip(head + step, 0, heads - 1)),
                ),
                when=condition,
                tag="weights",
            )

    def gain_copy(other, slot):
        return remote(
            r.small, r.full_vectors.at[slot], r.small_send.at[0], r.small_recv.at[0], (other, head)
        )


    order = []
    for i in range(heads):
        order.append(heads - 1 - i // 2 if i % 2 == 0 else i // 2)
    even = submasks(range(1, levels))
    down_orders = [list(range(levels - 1, 0, -1)), [1] + list(range(levels - 1, 1, -1))]
    sibling = flip(blk, 1, bits)

    def group_cols(g, which=None):
        if which is None:
            return slice(g * width, (g + 1) * width)
        return slice(g * width + which * width // 2, g * width + (which + 1) * width // 2)

    def total(g, other, mask, which=None):
        return r.packed.at[other, piece_rows(flip(blk, mask, bits)), group_cols(g, which)]

    def core_start(g):
        sent = r.packed.at[:, 0 : blks // 2 * share, group_cols(g)]
        for other in order:
            for mask in even:
                sends.start(
                    lambda other=other, mask=mask: remote(
                        total(g, other, mask | 1),
                        r.from_core.at[g, other, mask // 2],
                        r.core_send.at[g],
                        r.core_recv.at[g, other],
                        (sibling, head),
                    ),
                    shared=(("core", g), lambda: await_bytes(sent, r.core_send.at[g])),
                )

    def core_load(g, i):
        return pltpu.make_async_copy(
            r.from_core.at[g, order[i]], r.staged.at[i % 2], r.stage_sem.at[i % 2]
        )

    def core_arrived(g, i):
        await_bytes(r.from_core.at[g, order[i]], r.core_recv.at[g, order[i]])
        core_load(g, i).start()

    def core_add(g):
        core_arrived(g, 0)
        for i, other in enumerate(order):
            if i + 1 < heads:
                core_arrived(g, i + 1)
            core_load(g, i).wait()
            for mask in even:
                add_into(total(g, other, mask), r.staged.at[i % 2, mask // 2], width)
            tree_start(g, other, 0)

    def tree_slots(which, step):
        dims = down_orders[which]
        base = sum(1 << (levels - 2 - earlier) for earlier in range(step))
        return dims[step], [(mask, base + i) for i, mask in enumerate(submasks(dims[step + 1 :]))]

    def tree_start(g, other, step):
        sent = r.packed.at[:, 0 : (blks // 2 - 1) * share, group_cols(g)]
        for which in range(2):
            dim, slots = tree_slots(which, step)
            for mask, slot in slots:
                sends.start(
                    lambda which=which, dim=dim, mask=mask, slot=slot: remote(
                        total(g, other, mask | (1 << dim), which),
                        r.from_tree.at[g, which, other, slot],
                        r.down_send.at[g],
                        r.down_recv.at[g, which, other, step],
                        (flip(blk, 1 << dim, bits), head),
                    ),
                    shared=(("down", g), lambda: await_bytes(sent, r.down_send.at[g])),
                )

    def tree_add(g, other, step):
        for which in range(2):
            _, slots = tree_slots(which, step)
            first, count = slots[0][1], len(slots)
            await_bytes(
                r.from_tree.at[g, which, other, first : first + count],
                r.down_recv.at[g, which, other, step],
            )
            for mask, slot in slots:
                add_into(
                    total(g, other, mask, which), r.from_tree.at[g, which, other, slot], width // 2
                )
        if step < levels - 2:
            tree_start(g, other, step + 1)

    def tree_down(g, step):
        for other in order:
            tree_add(g, other, step)

    partner = head + 1 - 2 * (head % 2)
    others = range(1, heads // 2)

    def far(distance):
        return (head + 2 * distance) % heads

    def far_partner(distance):
        return (partner + 2 * distance) % heads

    def sum_copy(g, goal, slot, device):
        return remote(
            total(g, goal, 0),
            r.from_head.at[g, slot],
            r.pair_send.at[g],
            r.pair_recv.at[g, slot],
            (blk, device),
        )

    def sum_start(g, goal, slot, device, when=None):
        sent = r.packed.at[0, 0 : (heads - 1) * share, group_cols(g)]
        sends.start(
            lambda: sum_copy(g, goal, slot, device),
            when=when,
            shared=(("pair", g), lambda: await_bytes(sent, r.pair_send.at[g])),
        )

    def sum_add(g, goal, slot):
        await_bytes(r.from_head.at[g, slot], r.pair_recv.at[g, slot])
        add_into(total(g, goal, 0), r.from_head.at[g, slot], width)

    def direct_start(g):
        for goal in range(heads):
            sum_start(g, goal, head, goal, when=goal != head)

    def direct_add(g):
        for source in range(heads):

            @pl.when(source != head)
            def _():
                sum_add(g, head, source)

    def pair_start(g):
        sum_start(g, partner, 0, partner)
        for distance in others:
            sum_start(g, far_partner(distance), distance, partner)

    def pair_forward(g):
        for distance in others:
            sum_add(g, far(distance), distance)
            sum_start(g, far(distance), heads // 2 + distance, far(distance))

    def pair_add(g):
        sum_add(g, head, 0)
        for distance in others:
            sum_add(g, head, heads // 2 + distance)


    micro = head // splits

    def find_destinations():
        own_slots = r.perm[micro, pl.ds(blk, 1), :]
        r.ones[...] = jnp.where(iota((blks, group), 0) == own_slots // group, 1.0, 0.0)
        cumulative(r.ones, r.sums, group)
        rank = column_sum(r.ones[...] * r.sums[...]).astype(jnp.int32) - 1
        dest = own_slots // group * pair + rank
        r.dest_row[...] = jnp.broadcast_to(dest, r.dest_row.shape)
        for tile in range(group // 128):
            block = jnp.broadcast_to(dest[:, tile * 128 : (tile + 1) * 128].astype(F32), (128, 128))
            r.dest_col[tile * 128 : (tile + 1) * 128, :] = block.T.astype(jnp.int32)

    def find_slots():
        r.ones[...] = jnp.where(r.perm[micro] // group == blk, 1.0, 0.0)
        cumulative(r.ones, r.sums, group)
        r.rank_rows[...] = jnp.where(r.ones[...] > 0, r.sums[...] - 1, -1.0).astype(jnp.int32)

        @pl.loop(0, blks)
        def _(other):
            ranks = r.rank_rows[pl.ds(other, 1), :]
            inner = (r.perm[micro, pl.ds(other, 1), :] % group).astype(F32)
            found = jnp.where(iota((pair, group), 0) == ranks, inner, 0.0)
            column = jnp.sum(found, axis=1, keepdims=True).astype(jnp.int32)
            r.slot_col[pl.ds(pl.multiple_of(other * pair, pair), pair), :] = jnp.broadcast_to(
                column, (pair, 128)
            )

        for tile in range(group // 128):
            block = r.slot_col[tile * 128 : (tile + 1) * 128, :].astype(F32)
            r.slot_row[:, tile * 128 : (tile + 1) * 128] = block.T[0:8, :].astype(jnp.int32)

    def find_segments():
        first = blk * group + head * rows
        for m in range(micros):
            ends = []
            for s in range(r.seq_lengths.shape[1]):
                ends.append(r.seq_lengths[m, s] + (ends[-1] if ends else 0))
            for tile in range(rows // CLUSTER):
                slot = iota((CLUSTER, group), 0) + (first + tile * CLUSTER)

                def add(other, sums):
                    position = iota((1, group), 1) + other * group
                    segment = jnp.zeros((1, group), F32)
                    for end in ends:
                        segment = segment + jnp.where(position >= end, 1.0, 0.0)
                    here = r.perm[m, pl.ds(other, 1), :] == slot
                    found = jnp.where(here, segment, 0.0)
                    return sums + sum(
                        found[:, i * 128 : (i + 1) * 128] for i in range(group // 128)
                    )

                sums = lax.fori_loop(0, blks, add, jnp.zeros((CLUSTER, 128), F32))
                column = jnp.broadcast_to(
                    jnp.sum(sums, axis=1, keepdims=True), (CLUSTER, 128)
                )
                cluster = m * (rows // CLUSTER) + tile
                r.seg_col[cluster * CLUSTER : (cluster + 1) * CLUSTER, :] = column
                r.seg_row[cluster : cluster + 1, :] = column.T[0:1, :]

    def spread_vectors():
        for b in range(blks):
            small = r.full_vectors[b].astype(F32)
            r.vectors[:, b * share : (b + 1) * share] = small[0:8, 0:share]
            for j in range(fold):
                at = (b * fold + j) * share
                r.up_bias[:, at : at + share] = small[8 + j : 9 + j, 0:share]
        r.bias_qkv[:, 0:width] = r.vectors[0:1, :]
        r.bias_qkv[:, width : 2 * width] = jnp.zeros((1, width), F32)
        r.bias_qkv[:, 2 * width :] = r.vectors[1:2, :]


    def take_rows():
        for source in range(heads):
            m, which = source // splits, source % splits
            r.x[m * rows : (m + 1) * rows, which * part : (which + 1) * part] = r.slots[0, source]

    def assemble_down():
        @pl.loop(0, width // share)
        def _(b):
            source = piece_rows(b)
            for j in range(fold):
                at = b * share * fold + j * share
                target = pl.ds(pl.multiple_of(at, share), share)
                for h in range(heads):
                    base = 2 * width + j * short
                    r.down[target, h * short : (h + 1) * short] = r.packed[
                        h, source, base : base + short
                    ]

    per_head = width // 256

    def first_norm():
        @row_tiles
        def _(tile, at):
            normal, _ = normalize(r.attn_res[at, :])
            values = normal * r.vectors[3:4, :] + r.vectors[4:5, :]
            r.normed[at, :] = values
            r.hidden[at, :] = values.astype(BF16)

        r.turned[...] = r.hidden[...].T

    def ffn_up(h):
        @tiles(per_head, 256)
        def _(tile, inner):
            inner = pl.ds(pl.multiple_of(width + tile * 256, 256), 256)
            cols = pl.ds(pl.multiple_of(h * width + tile * 256, 256), 256)
            pre = jnp.dot(r.hidden[...], r.packed[h, :, inner], preferred_element_type=F32)
            pre = pre + r.up_bias[:, cols]
            below = 0.5 + 0.5 * lax.erf(pre * (0.5**0.5))
            r.active[:, cols] = (pre * below).astype(BF16)
            bell = jnp.exp(-0.5 * pre * pre) * (0.5 / jnp.pi) ** 0.5
            r.slope[:, cols] = (below + pre * bell).astype(BF16)

    def ffn_down():
        @tiles(width // 256, 256)
        def _(tile, cols):
            sums = jnp.dot(r.active[...], r.down[:, cols], preferred_element_type=F32)
            r.ffn_res[:, cols] = r.normed[:, cols] + sums + r.vectors[5:6, cols]

    def inner_rows(tile):
        return tile * CLUSTER // rows, pl.ds(pl.multiple_of(tile * CLUSTER % rows, CLUSTER), CLUSTER)

    def second_norm():
        @row_tiles
        def _(tile, at):
            normal, _ = normalize(r.ffn_res[at, :])
            result = (normal * r.vectors[6:7, :] + r.vectors[7:8, :]).astype(BF16)
            r.hidden[at, :] = result

    def second_norm_back():
        @row_tiles
        def _(tile, at):
            normal, scale = normalize(r.ffn_res[at, :])
            m, inner = inner_rows(tile)
            cotangent = jnp.concatenate(
                [r.slots[1, m * splits + which, inner, :] for which in range(splits)], axis=1
            ).astype(F32)
            d_ffn = norm_derivative(normal, scale, cotangent, r.vectors[6:7, :])
            low = d_ffn.astype(BF16)
            r.g_down[at, :] = low
            r.ffn_res[at, :] = d_ffn
            r.vec_grads[5:6, :] += column_sum(low.astype(F32))
            r.vec_grads[6:7, :] += column_sum(cotangent * normal)
            r.vec_grads[7:8, :] += column_sum(cotangent)

    def down_gradient():
        @pl.loop(0, width // share)
        def _(b):
            wide = share * fold
            cols = pl.ds(pl.multiple_of(b * wide, wide), wide)
            turned = r.active[:, cols].T
            target = piece_rows(b)
            for which in range(2):
                grad = jnp.dot(
                    turned,
                    r.g_down[:, which * width // 2 : (which + 1) * width // 2],
                    preferred_element_type=F32,
                ).astype(BF16)
                for j in range(fold):
                    for h in range(heads // 2):
                        base = 2 * width + j * short
                        r.packed[which * heads // 2 + h, target, base : base + short] = grad[
                            j * share : (j + 1) * share, h * short : (h + 1) * short
                        ]

    def ffn_up_back():
        @tiles(ff // 256, 256)
        def _(tile, cols):
            d_active = contract(r.g_down[...], r.down[cols, :], (1, 1))
            low = (d_active * r.slope[:, cols].astype(F32)).astype(BF16)
            r.slope[:, cols] = low
            r.up_bias_grad[:, cols] = column_sum(low.astype(F32))

    def norm_cotangent():
        @tiles(width // 256, 256)
        def _(tile, cols):
            sums = r.ffn_res[:, cols]
            for h in range(heads):
                sums = sums + contract(
                    r.slope[:, h * width : (h + 1) * width],
                    r.packed[h, cols, width : 2 * width],
                    (1, 1),
                )
            r.normed[:, cols] = sums

    def up_gradient():
        @tiles(ff // 256, 256)
        def _(tile, cols):
            inner = pl.ds(pl.multiple_of(width + tile % per_head * 256, 256), 256)
            grad = jnp.dot(r.turned[...], r.slope[:, cols], preferred_element_type=F32)
            r.packed[tile // per_head, :, inner] = grad.astype(BF16)

    def first_norm_back():
        @row_tiles
        def _(tile, at):
            normal, scale = normalize(r.attn_res[at, :])
            cotangent = r.normed[at, :]
            grad = norm_derivative(normal, scale, cotangent, r.vectors[3:4, :])
            low = grad.astype(BF16)
            r.attn_res[at, :] = grad
            r.g_attn[at, :] = low
            r.vec_grads[2:3, :] += column_sum(low.astype(F32))
            r.vec_grads[3:4, :] += column_sum(cotangent * normal)
            r.vec_grads[4:5, :] += column_sum(cotangent)

    g_context = r.g_down
    x_grad = r.g_down
    g_proj = r.active
    wide = 3 * width // heads

    def out_gradient():
        r.turned[...] = r.context[...].T
        for h in range(heads):
            grad = jnp.dot(
                r.turned[...],
                r.g_attn[:, h * short : (h + 1) * short],
                preferred_element_type=F32,
            )
            r.packed[h, :, wide : wide + short] = grad.astype(BF16)

    def context_cotangent():
        @tiles(width // 256, 256)
        def _(tile, cols):
            g_context[:, cols] = contract(r.g_attn[...], r.out[cols, :], (1, 1)).astype(BF16)

    def qkv_gradient():
        r.turned[...] = r.x[...].T

        @tiles(width // 256, 256)
        def _(tile, at):
            for h in range(heads):
                grad = jnp.dot(
                    r.turned[at, :], g_proj[:, h * wide : (h + 1) * wide], preferred_element_type=F32
                )
                r.packed[h, at, 0:wide] = grad.astype(BF16)

        r.vec_grads[0:1, :] = column_sum(g_proj[:, 0:width].astype(F32))
        r.vec_grads[1:2, :] = column_sum(g_proj[:, 2 * width : 3 * width].astype(F32))

    def row_gradient():
        for which in range(splits):
            for piece in range(part // 128):
                at = which * part + piece * 128
                sums = r.attn_res[:, at : at + 128] + contract(
                    g_proj[:, 0 : 3 * width], r.qkv[at : at + 128, :], (1, 1)
                )
                x_grad[:, at : at + 128] = sums.astype(BF16)


    def split_vectors():
        r.vec_split[...] = jnp.zeros_like(r.vec_split)
        for b in range(blks):
            r.vec_split[b, 0:8, 0:share] = r.vec_grads[:, b * share : (b + 1) * share]
            for j in range(fold):
                at = (b * fold + j) * share
                r.vec_split[b, 8 + j : 9 + j, 0:share] = r.up_bias_grad[:, at : at + share]

    def vec_copy(other, slot):
        return remote(
            r.vec_split.at[other],
            r.vec_parts.at[slot],
            r.small_send.at[1],
            r.small_recv.at[1],
            (other, head),
        )

    def vec_head_copy(other, slot):
        return remote(
            r.vec_mid,
            r.vec_heads.at[slot],
            r.small_send.at[2],
            r.small_recv.at[2],
            (blk, other),
        )

    def place_slots():
        for m in range(micros):
            for b in range(blks):
                r.perm[m, b : b + 1, :] = r.perm_rows[m : m + 1, b * group : (b + 1) * group]

    def pack_shard():
        at = 0
        for source in (r.qkv_weight, r.out_weight, r.up_weight):
            r.shard[:, at : at + source.shape[1]] = source[...]
            at += source.shape[1]
        turned = r.down_weight[...].T
        for j in range(fold):
            r.shard[:, at + j * short : at + (j + 1) * short] = turned[
                j * share : (j + 1) * share
            ]

    def pack_small():
        r.small_sums[...] = jnp.zeros_like(r.small_sums)
        for i in range(8):
            r.small_sums[i : i + 1, 0:share] = getattr(r, "vector%d" % i)[...].astype(F32)
        bias = r.up_bias_here[...].astype(F32)
        bias = jnp.concatenate([bias[i : i + 1] for i in range(bias.shape[0])], axis=1)
        for j in range(fold):
            r.small_sums[8 + j : 9 + j, 0:share] = bias[:, j * share : (j + 1) * share]
        r.small[...] = r.small_sums[...].astype(BF16)

    def send_small():
        sent = r.full_vectors.at[0 : blks - 1]
        for other in range(blks):
            sends.start(
                lambda other=other: gain_copy(other, blk),
                when=other != blk,
                shared=("gain", lambda: await_bytes(sent, r.small_send.at[0])),
            )
        own_gain.start()
        own_shard.start()

    def take_small():
        await_bytes(r.full_vectors.at[0 : blks - 1], r.small_recv.at[0])
        own_gain.wait()
        own_shard.wait()
        spread_vectors()

    def send_vectors():
        split_vectors()
        sent = r.vec_parts.at[0 : blks - 1]
        for other in range(blks):
            sends.start(
                lambda other=other: vec_copy(other, blk),
                when=other != blk,
                shared=("vec", lambda: await_bytes(sent, r.small_send.at[1])),
            )

    def sum_vectors_over_blk():
        await_bytes(r.vec_parts.at[0 : blks - 1], r.small_recv.at[1])
        r.vec_mid[...] = jnp.zeros_like(r.vec_mid)
        for other in range(blks):

            @pl.when(other != blk)
            def _():
                r.vec_mid[...] += r.vec_parts[other]

        r.vec_mid[...] += r.vec_split[pl.ds(blk, 1)][0]
        sent = r.vec_heads.at[0 : heads - 1]
        for other in range(heads):
            sends.start(
                lambda other=other: vec_head_copy(other, head),
                when=other != head,
                shared=("vec head", lambda: await_bytes(sent, r.small_send.at[2])),
            )

    def sum_vectors_over_head():
        await_bytes(r.vec_heads.at[0 : heads - 1], r.small_recv.at[2])
        r.vec_sum[...] = r.vec_mid[...]
        for other in range(heads):

            @pl.when(other != head)
            def _():
                r.vec_sum[...] += r.vec_heads[other]

    own_gain = pltpu.make_async_copy(r.small, r.full_vectors.at[blk], r.own_sem.at[0])
    own_shard = pltpu.make_async_copy(
        r.shard, r.packed.at[head, piece_rows(blk), :], r.own_sem.at[1]
    )

    def start_backward():
        r.vec_grads[...] = jnp.zeros_like(r.vec_grads)

    clusters = tokens // CLUSTER

    def attention_back(begin, end):
        attend_back(r.proj, r.probs, g_context, g_proj, begin, end)

    def row_copy(i):
        return pltpu.make_async_copy(r.slots.at[i], r.row_results.at[i], r.out_sem.at[0, i])

    def shard_copy(g):
        return pltpu.make_async_copy(
            r.packed.at[head, piece_rows(blk), group_cols(g)],
            r.shard_grad.at[:, group_cols(g)],
            r.out_sem.at[1, g],
        )

    def finish():
        for i in range(2):
            row_copy(i).wait()
        for g in range(3):
            shard_copy(g).wait()
        sends.finish()


    enter(blk, head, blks, heads)
    to_heads(0, row_source(r.tokens))
    pack_shard()
    chain(0, 0)
    tree_step(0, 0, 0)
    tree_step(1, 0, 0)
    pack_small()
    send_small()
    place_slots()
    find_destinations()
    tree_step(0, 0, 1)
    chain(1, 0)
    tree_step(1, 0, 1)
    find_slots()
    tree_step(0, 0, 2)
    tree_step(1, 0, 2)
    find_segments()
    chain(0, 1)
    to_groups(0, one_hot_from_row(r.dest_row))
    chain(0, 2)
    chain(1, 1)
    tree_step(0, 1, 0)
    chain(1, 2)
    tree_step(1, 1, 0)
    chain(0, 3)
    tree_step(0, 2, 0)
    tree_step(0, 1, 1)
    to_owners(0, one_hot_from_row(r.slot_row))
    chain(1, 3)
    tree_step(0, 3, 0)
    tree_step(1, 2, 0)
    tree_step(0, 2, 1)
    tree_step(0, 1, 2)
    to_heads(1, row_source(r.out_grad))
    tree_step(1, 1, 1)
    tree_step(0, 3, 1)
    tree_step(0, 2, 2)
    take_small()
    tree_step(1, 2, 1)
    tree_step(0, 3, 2)
    tree_step(1, 1, 2)
    tree_step(0, 0, 3)
    tree_step(0, 1, 3)
    tree_step(0, 2, 3)
    tree_step(0, 3, 3)
    assemble_attention(r.packed, r.qkv, r.out)
    tree_step(1, 2, 2)
    rows_here(0)
    take_rows()
    project(r.x, r.qkv, r.bias_qkv, r.proj)
    tree_step(1, 3, 0)
    to_groups(1, one_hot_from_row(r.dest_row))
    tree_step(1, 3, 1)
    attend(r.proj, r.probs, r.context, r.seg_col, r.seg_row)
    to_owners(1, one_hot_from_row(r.slot_row))
    tree_step(1, 3, 2)
    leave_attention(r.x, r.context, r.out, r.vectors, r.attn_res)
    first_norm()
    tree_step(1, 0, 3)
    ffn_up(arrival[0])
    tree_step(1, 1, 3)
    ffn_up(arrival[1])
    tree_step(1, 2, 3)
    ffn_up(arrival[2])
    tree_step(1, 3, 3)
    ffn_up(arrival[3])
    assemble_down()
    ffn_down()
    second_norm()
    to_heads(2, own_rows(r.hidden))
    start_backward()
    rows_here(1)
    second_norm_back()
    sends.finish("weights")
    down_gradient()
    core_start(2)
    ffn_up_back()
    sends.finish(0)
    to_groups(2, one_hot_from_column(r.slot_col, group))
    core_add(2)
    norm_cotangent()
    up_gradient()
    core_start(1)
    first_norm_back()
    context_cotangent()
    to_owners(2, one_hot_from_column(r.dest_col, group))
    attention_back(0, clusters // 2)
    core_add(1)
    attention_back(clusters // 2, clusters)
    tree_down(2, 0)
    row_gradient()
    to_heads(3, own_rows(x_grad))
    out_gradient()
    qkv_gradient()
    core_start(0)
    send_vectors()
    tree_down(2, 1)
    pair_start(2)
    tree_down(1, 0)
    sends.finish(1)
    to_groups(3, one_hot_from_column(r.slot_col, group))
    core_add(0)
    pair_forward(2)
    tree_down(1, 1)
    pair_start(1)
    sum_vectors_over_blk()
    to_owners(3, one_hot_from_column(r.dest_col, group))
    pair_forward(1)
    tree_down(0, 0)
    sum_vectors_over_head()
    pair_add(2)
    shard_copy(2).start()
    tree_down(0, 1)
    direct_start(0)
    rows_here(2)
    row_copy(0).start()
    pair_add(1)
    shard_copy(1).start()
    direct_add(0)
    shard_copy(0).start()
    rows_here(3)
    row_copy(1).start()
    finish()


def fused(blks, heads, fold, tokens, out_grad, weights, vectors, up_bias, perm, seq_lengths):
    micros, rows, width = tokens.shape
    share = weights[0].shape[0]
    part = width * micros // heads
    scratch = fused_scratch(micros, rows, width, blks, heads, share, fold)
    any_space, vmem = pl.BlockSpec(memory_space=pl.ANY), pl.BlockSpec(memory_space=pltpu.VMEM)
    names = ["tokens", "out_grad", "qkv_weight", "out_weight", "up_weight", "down_weight"]
    names += ["vector%d" % i for i in range(8)] + ["up_bias_here", "perm_rows", "seq_lengths"]
    names += ["row_results", "shard_grad", "vec_sum", "from_core"]
    names += list(scratch)
    return pl.pallas_call(
        functools.partial(fused_kernel, names, blks, heads, share, fold),
        name="fused",
        out_shape=(
            jax.ShapeDtypeStruct((2, heads, rows, part), BF16),
            jax.ShapeDtypeStruct((share, 3 * width), BF16),
            jax.ShapeDtypeStruct((16, 128), F32),
            jax.ShapeDtypeStruct((3, heads, blks // 2, share, width), BF16),
        ),
        in_specs=[any_space] * 2 + [vmem] * 14 + [pl.BlockSpec(memory_space=pltpu.SMEM)],
        out_specs=(any_space, any_space, vmem, any_space),
        scratch_shapes=list(scratch.values()),
        compiler_params=pltpu.CompilerParams(
            collective_id=2, has_side_effects=True, vmem_limit_bytes=64 << 20
        ),
    )(
        tokens,
        out_grad,
        *weights[:3],
        weights[3].T,
        *[vector.reshape(1, -1) for vector in vectors],
        up_bias.reshape(-1, 128 if up_bias.shape[0] % 128 == 0 else up_bias.shape[0]),
        perm,
        seq_lengths,
    )[:3]


def unpack_kernel(
    rows_in, shard_in, sums_in, layer_out, x_grad, qkv, out, up, down, up_bias, *rest
):
    vectors, (row_results, shard, sums, sem) = rest[:8], rest[8:]
    micros, rows, width = layer_out.shape
    copies = [
        pltpu.make_async_copy(source, target, sem.at[i])
        for i, (source, target) in enumerate(
            ((sums_in, sums), (shard_in, shard), (rows_in, row_results))
        )
    ]
    for copy in copies:
        copy.start()
    _, heads, _, part = row_results.shape
    splits = heads // micros
    share, short = out.shape
    fold = down.shape[1] // share
    copies[0].wait()
    for i, vector in enumerate(vectors):
        vector[...] = sums[i : i + 1, 0:share]
    bias = jnp.concatenate([sums[8 + j : 9 + j, 0:share] for j in range(fold)], axis=1)
    lanes = up_bias.shape[1]
    for i in range(up_bias.shape[0]):
        up_bias[i : i + 1, :] = bias[:, i * lanes : (i + 1) * lanes]
    copies[1].wait()
    at = 0
    for target in (qkv, out, up):
        target[...] = shard[:, at : at + target.shape[1]].astype(F32)
        at += target.shape[1]
    pieces = [
        shard[:, at + j * short : at + (j + 1) * short].astype(F32) for j in range(fold)
    ]
    down[...] = jnp.concatenate(pieces, axis=0).T
    copies[2].wait()
    for source in range(heads):
        m, which = source // splits, source % splits
        cols = slice(which * part, (which + 1) * part)
        layer_out[m, :, cols] = row_results[0, source]
        x_grad[m, :, cols] = row_results[1, source].astype(F32)


def unpack(micros, width, widths, row_results, shard, sums):
    _, heads, rows, part = row_results.shape
    share = shard.shape[0]
    vmem = pl.BlockSpec(memory_space=pltpu.VMEM)
    shapes = [(share, widths[0]), (share, widths[1]), (share, widths[2])]
    long = widths[3] // widths[1] * share
    lanes = 128 if long % 128 == 0 else long
    shapes += [(widths[1], long), (long // lanes, lanes)]
    shapes += [(1, share)] * 8
    results = pl.pallas_call(
        unpack_kernel,
        name="unpack",
        out_shape=(
            jax.ShapeDtypeStruct((micros, rows, width), BF16),
            jax.ShapeDtypeStruct((micros, rows, width), F32),
        )
        + tuple(jax.ShapeDtypeStruct(shape, F32) for shape in shapes),
        in_specs=[pl.BlockSpec(memory_space=pltpu.HBM)] * 3,
        out_specs=(vmem,) * (2 + len(shapes)),
        scratch_shapes=[
            pltpu.VMEM(row_results.shape, BF16),
            pltpu.VMEM(shard.shape, BF16),
            pltpu.VMEM(sums.shape, F32),
            pltpu.SemaphoreType.DMA((3,)),
        ],
        compiler_params=pltpu.CompilerParams(vmem_limit_bytes=62 << 20),
    )(row_results, shard, sums)
    layer_out, x_grad, qkv, out, up, down, up_bias = results[:7]
    vec = [member.reshape(-1) for member in results[7:]]
    return (
        layer_out,
        x_grad,
        qkv,
        vec[0],
        vec[1],
        out,
        vec[2],
        vec[3],
        vec[4],
        up,
        up_bias.reshape(-1),
        down.T,
        vec[5],
        vec[6],
        vec[7],
    )


def refold(packed, share, other, fold):
    if share == other:
        return packed
    heads, width, wide = packed.shape
    short = wide // fold
    rows = packed.reshape(heads, width // share, share, fold, short).transpose(0, 1, 3, 2, 4)
    rows = rows.reshape(heads, width // other, fold, other, short).transpose(0, 1, 3, 2, 4)
    return rows.reshape(packed.shape)


def body(
    tokens,
    seq_lengths,
    cluster_perm,
    out_grad,
    qkv_weight,
    query_bias,
    value_bias,
    out_weight,
    out_bias,
    attn_gain,
    attn_shift,
    up_weight,
    up_bias,
    down_weight,
    down_bias,
    ffn_gain,
    ffn_shift,
):
    blks, heads = lax.axis_size("blk"), lax.axis_size("head")
    blk, head = lax.axis_index("blk"), lax.axis_index("head")
    micros, rows, width = tokens.shape
    group = rows * heads
    total_rows = cluster_perm.shape[1]
    share = qkv_weight.shape[0]
    folds = down_weight.shape[0] // share
    short = down_weight.shape[1]
    widths = [qkv_weight.shape[1], out_weight.shape[1], up_weight.shape[1], folds * short]
    edges = [sum(widths[:i]) for i in range(5)]

    small = [
        query_bias,
        value_bias,
        out_bias,
        attn_gain,
        attn_shift,
        down_bias,
        ffn_gain,
        ffn_shift,
    ]
    if share % 16 == 0:
        results = fused(
            blks,
            heads,
            folds,
            tokens,
            out_grad,
            (qkv_weight, out_weight, up_weight, down_weight),
            small,
            up_bias,
            cluster_perm,
            seq_lengths,
        )
        return unpack(micros, width, widths, *results)

    shard = jnp.concatenate(
        [qkv_weight, out_weight, up_weight]
        + [down_weight[i * share : (i + 1) * share] for i in range(folds)],
        axis=1,
    )
    lanes = -(-share // 128) * 128
    stacked = jnp.concatenate([jnp.stack(small), up_bias.reshape(folds, share)], axis=0)
    count = stacked.shape[0]
    vectors = jnp.pad(stacked, ((0, -count % 16), (0, lanes - share)))
    perm = cluster_perm.reshape(micros, blks, group)
    full, full_vectors, slots_x, slots_g, dest_col, slot_col = gather_all(
        blks, heads, tokens, out_grad, shard, vectors, perm
    )

    first = blk * group + head * rows
    slots = first + jnp.arange(rows, dtype=jnp.int32)
    ends = jnp.cumsum(seq_lengths, axis=1)
    positions = jnp.arange(total_rows, dtype=jnp.int32)
    segs = jnp.sum((positions[None, :, None] >= ends[:, None, :]).astype(jnp.int32), axis=2)
    slot_segs = jnp.sum(
        jnp.where(cluster_perm[:, None, :] == slots[None, :, None], segs[:, None, :], 0), axis=2
    )

    weights = full.reshape(heads, blks * share, -1)
    tall = share if share % 16 == 0 else width // 8
    if tall != share:
        weights = jnp.concatenate(
            [weights[:, :, : edges[3]], refold(weights[:, :, edges[3] :], share, tall, folds)],
            axis=2,
        )
    spread = full_vectors[:, :count, :share].astype(F32)
    vecs = spread[:, :8].transpose(1, 0, 2).reshape(8, width)
    up_vec = spread[:, 8:count].reshape(1, -1)
    bias_qkv = jnp.concatenate([vecs[0:1], jnp.zeros((1, width), F32), vecs[1:2]], axis=1)
    seg_col = jnp.broadcast_to(slot_segs.reshape(-1, 1), (micros * rows, 128))
    seg_row = slot_segs.reshape(-1, CLUSTER)
    x, proj, probs, context, attn_res, qkv, out = forward_part(
        slots_x, weights, bias_qkv, vecs, seg_col, seg_row
    )
    layer_out, d_attn, g_attn, partial_ffn, vec_ffn, up_vec_grad = ffn_part(
        tall, attn_res, slots_g, weights, vecs, up_vec
    )
    x_grad, partial_attn, vec_attn = backward_part(
        heads, rows, x, proj, probs, context, qkv, out, d_attn, g_attn
    )
    if tall != share:
        partial_ffn = jnp.concatenate(
            [partial_ffn[:, :, :width], refold(partial_ffn[:, :, width:], tall, share, folds)],
            axis=2,
        )
    partial = jnp.concatenate([partial_attn, partial_ffn], axis=2).reshape(full.shape)
    vec_grads = vec_ffn + vec_attn
    vec_parts = jnp.concatenate(
        [vec_grads.reshape(8, blks, share).transpose(1, 0, 2), up_vec_grad.reshape(blks, folds, share)],
        axis=1,
    )
    vec_parts = jnp.pad(vec_parts, ((0, 0), (0, -count % 16), (0, lanes - share)))
    out_rows, grad_rows, shard_grad, vec_sum = reduce_all(
        blks, heads, layer_out, x_grad, partial, vec_parts, dest_col, slot_col
    )
    down_grad = shard_grad[:, edges[3] : edges[4]]
    down_grad = jnp.concatenate(
        [down_grad[:, i * short : (i + 1) * short] for i in range(folds)], axis=0
    )
    vec = [vec_sum[i, :share] for i in range(8)]
    return (
        out_rows,
        grad_rows,
        shard_grad[:, edges[0] : edges[1]],
        vec[0],
        vec[1],
        shard_grad[:, edges[1] : edges[2]],
        vec[2],
        vec[3],
        vec[4],
        shard_grad[:, edges[2] : edges[3]],
        vec_sum[8:count, :share].reshape(-1),
        down_grad,
        vec[5],
        vec[6],
        vec[7],
    )


def solution(mesh):
    return jax.shard_map(
        body,
        mesh=mesh,
        in_specs=(
            P(None, ("blk", "head"), None),
            P(),
            P(),
            P(None, ("blk", "head"), None),
            P("blk", "head"),
            P("blk"),
            P("blk"),
            P("blk", "head"),
            P("blk"),
            P("blk"),
            P("blk"),
            P("blk", "head"),
            P("blk"),
            P("blk", "head"),
            P("blk"),
            P("blk"),
            P("blk"),
        ),
        out_specs=(
            P(None, ("blk", "head"), None),
            P(None, ("blk", "head"), None),
            P("blk", "head"),
            P("blk"),
            P("blk"),
            P("blk", "head"),
            P("blk"),
            P("blk"),
            P("blk"),
            P("blk", "head"),
            P("blk"),
            P("blk", "head"),
            P("blk"),
            P("blk"),
            P("blk"),
        ),
        check_vma=False,
    )
```

```python
import functools
import types

import jax
import jax.numpy as jnp
from jax import lax
from jax.experimental import pallas as pl
from jax.experimental.pallas import tpu as pltpu
from jax.sharding import PartitionSpec as P

HEAD_DIM = 64
CLUSTER = 128
TILE = 512
MESH = pl.DeviceIdType.MESH
BF16 = jnp.bfloat16
F32 = jnp.float32

masked_score = -1e30
norm_epsilon = 1e-05


def bits_of(index, count):
    return [(index // (1 << i)) % 2 for i in range(count)]


def flip(index, mask, bits):
    for i, bit in enumerate(bits):
        if mask & (1 << i):
            index = index + (1 - 2 * bit) * (1 << i)
    return index


def submasks(dims):
    masks = [0]
    for dim in dims:
        masks = masks + [mask | (1 << dim) for mask in masks]
    return masks


def choose(index, values):
    result = values[-1]
    for position in range(len(values) - 2, -1, -1):
        result = jnp.where(index == position, values[position], result)
    return result


class Sends:
    def __init__(self):
        self.pending = []
        self.shared = {}

    def start(self, make, when=None, tag=None, shared=None):
        if when is None:
            make().start()
        else:

            @pl.when(when)
            def _():
                make().start()

        if shared is None:
            self.pending.append((make, when, tag))
        else:
            key, wait = shared
            self.shared[tag, key] = wait

    def finish(self, *tags):
        pending, self.pending = self.pending, []
        for make, when, tag in pending:
            if tags and tag not in tags:
                self.pending.append((make, when, tag))
            elif when is None:
                make().wait_send()
            else:

                @pl.when(when)
                def _(make=make):
                    make().wait_send()

        shared, self.shared = self.shared, {}
        for (tag, key), wait in shared.items():
            if tags and tag not in tags:
                self.shared[tag, key] = wait
            else:
                wait()


def await_bytes(ref, sem):
    pltpu.make_async_copy(ref, ref, sem).wait()


def remote(src, dst, send_sem, recv_sem, device):
    return pltpu.make_async_remote_copy(
        src_ref=src,
        dst_ref=dst,
        send_sem=send_sem,
        recv_sem=recv_sem,
        device_id=device,
        device_id_type=MESH,
    )


def enter(blk, head, blks, heads):
    barrier = pltpu.get_barrier_semaphore()
    for other in range(blks):

        @pl.when(other != blk)
        def _():
            pl.semaphore_signal(barrier, inc=1, device_id=(other, head), device_id_type=MESH)

    for other in range(heads):

        @pl.when(other != head)
        def _():
            pl.semaphore_signal(barrier, inc=1, device_id=(blk, other), device_id_type=MESH)

    pl.semaphore_wait(barrier, blks + heads - 2)


def iota(shape, dim):
    return lax.broadcasted_iota(jnp.int32, shape, dim)


def permute_rows(one_hot_tile, source, target, rows):
    @pl.loop(0, rows // TILE)
    def _(tile):
        start = pl.multiple_of(tile * TILE, TILE)
        chosen = jnp.dot(one_hot_tile(start), source[...], preferred_element_type=F32)
        target[pl.ds(start, TILE), :] = chosen.astype(BF16)


def one_hot_from_row(row_ref):
    def tile(start):
        row = row_ref[0:1, :]
        count = row.shape[1]
        return jnp.where(iota((TILE, count), 0) + start == row, 1.0, 0.0).astype(BF16)

    return tile


def one_hot_from_column(column_ref, count):
    def tile(start):
        column = column_ref[pl.ds(start, TILE), 0:1]
        return jnp.where(iota((TILE, count), 1) == column, 1.0, 0.0).astype(BF16)

    return tile


class RowExchange:
    def __init__(self, sends, blk, head, blks, heads, sems, tensor):
        self.sends, self.blk, self.head, self.blks, self.heads = sends, blk, head, blks, heads
        self.head_send, self.head_recv, self.blk_send, self.blk_recv, self.local = sems
        self.tensor = tensor

    def over_head(self, step, source, target, all_but_one):
        send_sem = self.head_send.at[self.tensor, step]
        for other in range(self.heads):
            make = lambda other=other: remote(
                source(other),
                target(self.head),
                send_sem,
                self.head_recv.at[self.tensor, step],
                (self.blk, other),
            )
            self.sends.start(
                make,
                when=other != self.head,
                tag=self.tensor,
                shared=(("head", step), lambda: await_bytes(all_but_one, send_sem)),
            )

            @pl.when(other == self.head)
            def _():
                pltpu.make_async_copy(
                    source(other), target(other), self.local.at[self.tensor, step]
                ).start()

    def wait_head(self, step, target, all_but_one):
        await_bytes(all_but_one, self.head_recv.at[self.tensor, step])
        await_bytes(target(self.head), self.local.at[self.tensor, step])

    def over_blk(self, source, target, all_but_one):
        send_sem = self.blk_send.at[self.tensor]
        for other in range(self.blks):
            make = lambda other=other: remote(
                source(other),
                target(self.blk),
                send_sem,
                self.blk_recv.at[self.tensor],
                (other, self.head),
            )
            self.sends.start(
                make,
                when=other != self.blk,
                tag=self.tensor,
                shared=("blk", lambda: await_bytes(all_but_one, send_sem)),
            )

            @pl.when(other == self.blk)
            def _():
                pltpu.make_async_copy(
                    source(other), target(other), self.local.at[self.tensor, 2]
                ).start()

    def wait_blk(self, target, all_but_one):
        await_bytes(all_but_one, self.blk_recv.at[self.tensor])
        await_bytes(target(self.blk), self.local.at[self.tensor, 2])


def exchange_sems(blks, heads):
    dma = pltpu.SemaphoreType.DMA
    return [dma((2, 2)), dma((2, 2)), dma((2,)), dma((2,)), dma((2, 3))]


def cumulative(ones_ref, sums_ref, count):
    upper = jnp.where(iota((128, 128), 0) <= iota((128, 128), 1), 1.0, 0.0).astype(BF16)
    carry = jnp.zeros((ones_ref.shape[0], 1), F32)
    for tile in range(count // 128):
        part = ones_ref[:, tile * 128 : (tile + 1) * 128].astype(BF16)
        sums = jnp.dot(part, upper, preferred_element_type=F32) + carry
        sums_ref[:, tile * 128 : (tile + 1) * 128] = sums
        carry = sums[:, 127:128]


def gather_kernel(
    blks,
    heads,
    tokens,
    out_grad,
    shard,
    vectors,
    perm,
    full,
    full_vectors,
    slots_x,
    slots_g,
    dest_col,
    slot_col,
    arrived,
    sorted_rows,
    landed,
    ordered,
    dest_row,
    slot_row,
    ones,
    sums,
    rank_rows,
    head_send,
    head_recv,
    blk_send,
    blk_recv,
    local,
    z_send,
    z_recv,
    tree_send,
    tree_recv,
    vec_send,
    vec_recv,
    own_sem,
):
    blk, head = lax.axis_index("blk"), lax.axis_index("head")
    micros, rows, width = tokens.shape
    splits = heads // micros
    part = width // splits
    group = rows * heads
    pair = group // blks
    levels = blks.bit_length() - 1
    bits = bits_of(blk, levels)
    half = shard.shape[1] // 2
    sends = Sends()
    sems = (head_send, head_recv, blk_send, blk_recv, local)

    enter(blk, head, blks, heads)

    exchanges = [RowExchange(sends, blk, head, blks, heads, sems, i) for i in range(2)]
    sources = (tokens, out_grad)

    def send_rows(i):
        exchanges[i].over_head(
            0,
            lambda other: sources[i].at[
                other // splits, :, (other % splits) * part : (other % splits + 1) * part
            ],
            lambda other: arrived.at[i, pl.ds(pl.multiple_of(other * rows, rows), rows), :],
            arrived.at[i, 0 : group - rows, :],
        )

    send_rows(0)

    def vec_copy(other):
        return remote(
            vectors, full_vectors.at[blk], vec_send.at[other], vec_recv.at[blk], (other, head)
        )

    for other in range(blks):
        sends.start(lambda other=other: vec_copy(other), when=other != blk)
    own_vec = pltpu.make_async_copy(vectors, full_vectors.at[blk], own_sem.at[0])
    own_vec.start()

    orders = [list(range(1, levels)) + [0], list(range(2, levels)) + [1, 0]]
    arrival = [
        choose(
            head,
            [
                sorted([x for x in range(heads) if x != own], key=lambda x: (abs(x - own), x))[j - 1]
                for own in range(heads)
            ],
        )
        if j
        else head
        for j in range(heads)
    ]

    def halves(ref, which):
        return ref.at[:, which * half : (which + 1) * half]

    def tree_step(j, step):
        for which in range(2):
            dims = orders[which]
            if step:
                tree_wait(j, which, step - 1)
            other = flip(blk, 1 << dims[step], bits)
            for mask in submasks(dims[:step]):
                piece = flip(blk, mask, bits)
                target = halves(full.at[arrival[j], piece], which)
                source = halves(shard, which) if j == 0 and mask == 0 else target
                slot = (1 << step) - 1 + submasks(dims[:step]).index(mask)
                make = lambda source=source, target=target, piece=piece, other=other, slot=slot, which=which: remote(
                    source,
                    target,
                    tree_send.at[j, which, slot],
                    tree_recv.at[j, which, piece],
                    (other, head),
                )
                sends.start(make)

    def tree_wait(j, which, step):
        dims = orders[which]
        other = flip(blk, 1 << dims[step], bits)
        for mask in submasks(dims[:step]):
            piece = flip(blk, mask | (1 << dims[step]), bits)
            target = halves(full.at[arrival[j], piece], which)
            remote(
                target,
                target,
                tree_send.at[j, which, 0],
                tree_recv.at[j, which, piece],
                (other, head),
            ).wait_recv()

    def chain(j):
        if j == 0:
            source = shard
            left, right = head > 0, head < heads - 1
        else:
            source = full.at[arrival[j], blk]
            left = (arrival[j] > head) & (head > 0)
            right = (arrival[j] < head) & (head < heads - 1)
            remote(
                source, source, z_send.at[0, 0], z_recv.at[arrival[j]], (blk, head)
            ).wait_recv()
        for side, (condition, step) in enumerate(((left, -1), (right, 1))):
            make = lambda source=source, side=side, step=step: remote(
                source,
                full.at[arrival[j], blk],
                z_send.at[j, side],
                z_recv.at[arrival[j]],
                (blk, jnp.clip(head + step, 0, heads - 1)),
            )
            sends.start(make, when=condition)

    tree_step(0, 0)
    chain(0)
    own_shard = pltpu.make_async_copy(shard, full.at[head, blk], own_sem.at[1])
    own_shard.start()
    send_rows(1)

    micro = head // splits
    own_slots = perm[micro, pl.ds(blk, 1), :]
    ones[...] = jnp.where(iota((blks, group), 0) == own_slots // group, 1.0, 0.0)
    cumulative(ones, sums, group)
    rank = jnp.sum(ones[...] * sums[...], axis=0, keepdims=True).astype(jnp.int32) - 1
    dest = own_slots // group * pair + rank
    dest_row[...] = jnp.broadcast_to(dest, dest_row.shape)
    for tile in range(group // 128):
        block = jnp.broadcast_to(dest[:, tile * 128 : (tile + 1) * 128].astype(F32), (128, 128))
        dest_col[tile * 128 : (tile + 1) * 128, :] = block.T.astype(jnp.int32)

    all_slots = perm[micro]
    ones[...] = jnp.where(all_slots // group == blk, 1.0, 0.0)
    cumulative(ones, sums, group)
    rank_rows[...] = jnp.where(ones[...] > 0, sums[...] - 1, -1.0).astype(jnp.int32)

    @pl.loop(0, blks)
    def _(other):
        ranks = rank_rows[pl.ds(other, 1), :]
        inner = (perm[micro, pl.ds(other, 1), :] % group).astype(F32)
        found = jnp.where(iota((pair, group), 0) == ranks, inner, 0.0)
        column = jnp.sum(found, axis=1, keepdims=True).astype(jnp.int32)
        slot_col[pl.ds(pl.multiple_of(other * pair, pair), pair), :] = jnp.broadcast_to(
            column, (pair, 128)
        )

    for tile in range(group // 128):
        block = slot_col[tile * 128 : (tile + 1) * 128, :].astype(F32)
        slot_row[:, tile * 128 : (tile + 1) * 128] = block.T[0:8, :].astype(jnp.int32)

    def to_groups(i):
        exchanges[i].wait_head(
            0,
            lambda other: arrived.at[i, pl.ds(pl.multiple_of(other * rows, rows), rows), :],
            arrived.at[i, 0 : group - rows, :],
        )
        permute_rows(one_hot_from_row(dest_row), arrived.at[i], sorted_rows.at[i], group)
        exchanges[i].over_blk(
            lambda other: sorted_rows.at[i, pl.ds(other * pair, pair), :],
            lambda other: landed.at[i, pl.ds(pl.multiple_of(other * pair, pair), pair), :],
            landed.at[i, 0 : group - pair, :],
        )

    outs = (slots_x, slots_g)

    def to_slots(i):
        exchanges[i].wait_blk(
            lambda other: landed.at[i, pl.ds(pl.multiple_of(other * pair, pair), pair), :],
            landed.at[i, 0 : group - pair, :],
        )
        permute_rows(one_hot_from_row(slot_row), landed.at[i], ordered.at[i], group)
        exchanges[i].over_head(
            1,
            lambda other: ordered.at[i, pl.ds(other * rows, rows), :],
            lambda other: outs[i].at[other],
            outs[i].at[0 : heads - 1],
        )

    to_groups(0)
    for step in range(1, levels):
        tree_step(0, step)
    for j in range(1, heads):
        chain(j)
        tree_step(j, 0)
        if j == 1:
            to_slots(0)
            to_groups(1)
        if j == 2:
            to_slots(1)
        for step in range(1, levels):
            tree_step(j, step)
    for j in range(heads):
        for which in range(2):
            tree_wait(j, which, levels - 1)

    for i in range(2):
        exchanges[i].wait_head(1, lambda other: outs[i].at[other], outs[i].at[0 : heads - 1])
    for other in range(blks):

        @pl.when(other != blk)
        def _():
            remote(
                vectors,
                full_vectors.at[other],
                vec_send.at[other],
                vec_recv.at[other],
                (other, head),
            ).wait_recv()

    own_vec.wait()
    own_shard.wait()
    sends.finish()


def gather_all(blks, heads, tokens, out_grad, shard, vectors, perm):
    micros, rows, width = tokens.shape
    part = width * micros // heads
    group = rows * heads
    dma = pltpu.SemaphoreType.DMA
    any_space, vmem = pl.BlockSpec(memory_space=pl.ANY), pl.BlockSpec(memory_space=pltpu.VMEM)
    return pl.pallas_call(
        functools.partial(gather_kernel, blks, heads),
        name="gather_all",
        out_shape=(
            jax.ShapeDtypeStruct((heads, blks) + shard.shape, BF16),
            jax.ShapeDtypeStruct((blks,) + vectors.shape, BF16),
            jax.ShapeDtypeStruct((heads, rows, part), BF16),
            jax.ShapeDtypeStruct((heads, rows, part), BF16),
            jax.ShapeDtypeStruct((group, 128), jnp.int32),
            jax.ShapeDtypeStruct((group, 128), jnp.int32),
        ),
        in_specs=[any_space, any_space, any_space, any_space, vmem],
        out_specs=(any_space, any_space, any_space, any_space, vmem, vmem),
        scratch_shapes=[
            pltpu.VMEM((2, group, part), BF16),
            pltpu.VMEM((2, group, part), BF16),
            pltpu.VMEM((2, group, part), BF16),
            pltpu.VMEM((2, group, part), BF16),
            pltpu.VMEM((8, group), jnp.int32),
            pltpu.VMEM((8, group), jnp.int32),
            pltpu.VMEM((blks, group), F32),
            pltpu.VMEM((blks, group), F32),
            pltpu.VMEM((blks, group), jnp.int32),
        ]
        + exchange_sems(blks, heads)
        + [
            dma((heads, 2)),
            dma((heads,)),
            dma((heads, 2, blks)),
            dma((heads, 2, blks)),
            dma((blks,)),
            dma((blks,)),
            dma((2,)),
        ],
        compiler_params=pltpu.CompilerParams(
            collective_id=0, has_side_effects=True, vmem_limit_bytes=32 << 20
        ),
    )(tokens, out_grad, shard, vectors, perm)


def add_into(target, source, width):
    rows = target.shape[0]
    step = 16 if rows % 16 == 0 else rows

    @pl.loop(0, rows // step)
    def _(i):
        at = pl.ds(pl.multiple_of(i * step, step), step)
        for column in range(0, target.shape[1], width):
            cols = slice(column, column + width)
            target[at, cols] = target[at, cols] + source[at, cols]


def reduce_kernel(
    blks,
    heads,
    layer_out,
    x_grad,
    partial,
    vectors,
    dest_col,
    slot_col,
    out_rows,
    grad_rows,
    shard,
    vec_sum,
    total,
    from_core,
    from_tree,
    from_left,
    from_right,
    vec_parts,
    vec_mid,
    vec_heads,
    arrived,
    sorted_rows,
    landed,
    ordered,
    final,
    head_send,
    head_recv,
    blk_send,
    blk_recv,
    local,
    load_sem,
    core_send,
    core_recv,
    tree_send,
    tree_recv,
    left_send,
    left_recv,
    right_send,
    right_recv,
    vec_send,
    vec_recv,
    vec_head_send,
    vec_head_recv,
):
    blk, head = lax.axis_index("blk"), lax.axis_index("head")
    micros, rows, width = out_rows.shape
    splits = heads // micros
    part = width // splits
    group = rows * heads
    pair = group // blks
    levels = blks.bit_length() - 1
    bits = bits_of(blk, levels)
    half = shard.shape[1] // 2
    sends = Sends()
    sems = (head_send, head_recv, blk_send, blk_recv, local)
    exchanges = [RowExchange(sends, blk, head, blks, heads, sems, i) for i in range(2)]
    sources = (layer_out, x_grad)

    enter(blk, head, blks, heads)

    order = []
    for i in range(heads):
        order.append(heads - 1 - i // 2 if i % 2 == 0 else i // 2)

    even = submasks(range(1, levels))
    loads = {}
    for other in order:
        for mask in even:
            piece = flip(blk, mask, bits)
            loads[other, mask] = pltpu.make_async_copy(
                partial.at[other, piece], total.at[other, mask // 2], load_sem.at[other, mask // 2]
            )
            loads[other, mask].start()
            sends.start(
                lambda other=other, mask=mask: remote(
                    partial.at[other, flip(blk, mask | 1, bits)],
                    from_core.at[other, mask // 2],
                    core_send.at[other, mask // 2],
                    core_recv.at[other, mask // 2],
                    (flip(blk, 1, bits), head),
                )
            )

    def rows_to_heads(i):
        exchanges[i].over_head(
            0,
            lambda other: sources[i].at[other],
            lambda other: arrived.at[i, pl.ds(pl.multiple_of(other * rows, rows), rows), :],
            arrived.at[i, 0 : group - rows, :],
        )

    rows_to_heads(0)
    rows_to_heads(1)

    for other in range(blks):
        sends.start(
            lambda other=other: remote(
                vectors.at[other],
                vec_parts.at[blk],
                vec_send.at[other],
                vec_recv.at[blk],
                (other, head),
            ),
            when=other != blk,
        )

    def add_core(other):
        for mask in even:
            loads[other, mask].wait()
            target = from_core.at[other, mask // 2]
            remote(
                target,
                target,
                core_send.at[other, mask // 2],
                core_recv.at[other, mask // 2],
                (flip(blk, 1, bits), head),
            ).wait_recv()
            add_into(total.at[other, mask // 2], target, half)

    orders = [list(range(levels - 1, 0, -1)), [1] + list(range(levels - 1, 1, -1))]

    def cols(ref, which):
        return ref.at[:, which * half : (which + 1) * half]

    def tree_parts(which, step):
        dims = orders[which]
        free = dims[step + 1 :]
        base = sum(1 << (levels - 2 - earlier) for earlier in range(step))
        return dims[step], [(mask, base + i) for i, mask in enumerate(submasks(free))]

    def tree_start(other, step):
        for which in range(2):
            dim, parts = tree_parts(which, step)
            for mask, slot in parts:
                sends.start(
                    lambda which=which, dim=dim, mask=mask, slot=slot: remote(
                        cols(total.at[other, (mask | (1 << dim)) // 2], which),
                        from_tree.at[which, other, slot],
                        tree_send.at[which, other, slot],
                        tree_recv.at[which, other, slot],
                        (flip(blk, 1 << dim, bits), head),
                    )
                )

    def tree_add(other, step):
        for which in range(2):
            dim, parts = tree_parts(which, step)
            for mask, slot in parts:
                source = from_tree.at[which, other, slot]
                remote(
                    source,
                    source,
                    tree_send.at[which, other, slot],
                    tree_recv.at[which, other, slot],
                    (flip(blk, 1 << dim, bits), head),
                ).wait_recv()
                add_into(cols(total.at[other, mask // 2], which), source, half)

    def pass_right(goal):
        target = from_left.at[goal]

        @pl.when((head > 0) & (head <= goal))
        def _():
            remote(
                target, target, left_send.at[goal], left_recv.at[goal], (blk, head)
            ).wait_recv()
            add_into(total.at[goal, 0], target, half)

        sends.start(
            lambda: remote(
                total.at[goal, 0],
                target,
                left_send.at[goal],
                left_recv.at[goal],
                (blk, jnp.minimum(head + 1, heads - 1)),
            ),
            when=head < goal,
        )

    def pass_left(goal):
        target = from_right.at[goal]

        @pl.when((head < heads - 1) & (head >= goal))
        def _():
            remote(
                target, target, right_send.at[goal], right_recv.at[goal], (blk, head)
            ).wait_recv()
            add_into(total.at[goal, 0], target, half)

        sends.start(
            lambda: remote(
                total.at[goal, 0],
                target,
                right_send.at[goal],
                right_recv.at[goal],
                (blk, jnp.maximum(head - 1, 0)),
            ),
            when=head > goal,
        )

    def to_groups(i):
        exchanges[i].wait_head(
            0,
            lambda other: arrived.at[i, pl.ds(pl.multiple_of(other * rows, rows), rows), :],
            arrived.at[i, 0 : group - rows, :],
        )
        permute_rows(one_hot_from_column(slot_col, group), arrived.at[i], sorted_rows.at[i], group)
        exchanges[i].over_blk(
            lambda other: sorted_rows.at[i, pl.ds(other * pair, pair), :],
            lambda other: landed.at[i, pl.ds(pl.multiple_of(other * pair, pair), pair), :],
            landed.at[i, 0 : group - pair, :],
        )

    def to_positions(i):
        exchanges[i].wait_blk(
            lambda other: landed.at[i, pl.ds(pl.multiple_of(other * pair, pair), pair), :],
            landed.at[i, 0 : group - pair, :],
        )
        permute_rows(one_hot_from_column(dest_col, group), landed.at[i], ordered.at[i], group)
        exchanges[i].over_head(
            1,
            lambda other: ordered.at[i, pl.ds(other * rows, rows), :],
            lambda other: final.at[i, other],
            final.at[i, 0 : heads - 1],
        )

    for other in order[:2]:
        add_core(other)
        tree_start(other, 0)
    to_groups(0)
    for other in order[2:]:
        add_core(other)
        tree_start(other, 0)
    to_groups(1)
    for other in order[:2]:
        for step in range(levels - 1):
            tree_add(other, step)
            if step < levels - 2:
                tree_start(other, step + 1)
    to_positions(0)
    for position, other in enumerate(order):
        if position >= 2:
            for step in range(levels - 1):
                tree_add(other, step)
                if step < levels - 2:
                    tree_start(other, step + 1)
        if position == 2:
            to_positions(1)

    vec_mid[...] = vectors[pl.ds(blk, 1)][0]
    for other in range(blks):

        @pl.when(other != blk)
        def _():
            remote(
                vec_parts.at[other],
                vec_parts.at[other],
                vec_send.at[other],
                vec_recv.at[other],
                (other, head),
            ).wait_recv()
            vec_mid[...] += vec_parts[other]

    for other in range(heads):
        sends.start(
            lambda other=other: remote(
                vec_mid,
                vec_heads.at[head],
                vec_head_send.at[other],
                vec_head_recv.at[head],
                (blk, other),
            ),
            when=other != head,
        )

    for i in range(heads):
        goal = heads - 1 - i
        pass_right(goal)
        pass_left(i)

    for own in range(heads):

        @pl.when(own == head)
        def _():
            shard[...] = total[own, 0].astype(F32)

    vec_sum[...] = vec_mid[...]
    for other in range(heads):

        @pl.when(other != head)
        def _():
            remote(
                vec_heads.at[other],
                vec_heads.at[other],
                vec_head_send.at[other],
                vec_head_recv.at[other],
                (blk, other),
            ).wait_recv()
            vec_sum[...] += vec_heads[other]

    for i in range(2):
        exchanges[i].wait_head(1, lambda other: final.at[i, other], final.at[i, 0 : heads - 1])
    for source in range(heads):
        micro, which = source // splits, source % splits
        out_rows[micro, :, which * part : (which + 1) * part] = final[0, source]
        grad_rows[micro, :, which * part : (which + 1) * part] = final[1, source].astype(F32)
    sends.finish()


def reduce_all(blks, heads, layer_out, x_grad, partial, vectors, dest_col, slot_col):
    _, rows, part = layer_out.shape
    micros = 2
    group = rows * heads
    width = part * heads // micros
    size = partial.shape[2:]
    half = size[1] // 2
    dma = pltpu.SemaphoreType.DMA
    any_space, vmem = pl.BlockSpec(memory_space=pl.ANY), pl.BlockSpec(memory_space=pltpu.VMEM)
    vec = vectors.shape[1:]
    return pl.pallas_call(
        functools.partial(reduce_kernel, blks, heads),
        name="reduce_all",
        out_shape=(
            jax.ShapeDtypeStruct((micros, rows, width), BF16),
            jax.ShapeDtypeStruct((micros, rows, width), F32),
            jax.ShapeDtypeStruct(size, F32),
            jax.ShapeDtypeStruct(vec, F32),
        ),
        in_specs=[any_space, any_space, any_space, vmem, vmem, vmem],
        out_specs=(vmem, vmem, vmem, vmem),
        scratch_shapes=[
            pltpu.VMEM((heads, blks // 2) + size, BF16),
            pltpu.VMEM((heads, blks // 2) + size, BF16),
            pltpu.VMEM((2, heads, blks // 2 - 1, size[0], half), BF16),
            pltpu.VMEM((heads,) + size, BF16),
            pltpu.VMEM((heads,) + size, BF16),
            pltpu.VMEM((blks,) + vec, F32),
            pltpu.VMEM(vec, F32),
            pltpu.VMEM((heads,) + vec, F32),
            pltpu.VMEM((2, group, part), BF16),
            pltpu.VMEM((2, group, part), BF16),
            pltpu.VMEM((2, group, part), BF16),
            pltpu.VMEM((2, group, part), BF16),
            pltpu.VMEM((2, heads, rows, part), BF16),
        ]
        + exchange_sems(blks, heads)
        + [
            dma((heads, blks // 2)),
            dma((heads, blks // 2)),
            dma((heads, blks // 2)),
            dma((2, heads, blks // 2 - 1)),
            dma((2, heads, blks // 2 - 1)),
            dma((heads,)),
            dma((heads,)),
            dma((heads,)),
            dma((heads,)),
            dma((blks,)),
            dma((blks,)),
            dma((heads,)),
            dma((heads,)),
        ],
        compiler_params=pltpu.CompilerParams(
            collective_id=1, has_side_effects=True, vmem_limit_bytes=56 << 20
        ),
    )(layer_out, x_grad, partial, vectors, dest_col, slot_col)


def contract(left, right, dims):
    return lax.dot_general(left, right, ((dims[:1], dims[1:]), ((), ())), preferred_element_type=F32)


def assemble_attention(packed, qkv, out):
    heads, width, _ = packed.shape
    wide, narrow = qkv.shape[1] // heads, out.shape[1] // heads

    @pl.loop(0, width // CLUSTER)
    def _(tile):
        rows = pl.ds(pl.multiple_of(tile * CLUSTER, CLUSTER), CLUSTER)
        for head in range(heads):
            qkv[rows, head * wide : (head + 1) * wide] = packed[head, rows, 0:wide]
            out[rows, head * narrow : (head + 1) * narrow] = packed[
                head, rows, wide : wide + narrow
            ]


def column_sum(values):
    return jnp.sum(values, axis=0, keepdims=True)


def row_mean(values):
    return jnp.mean(values, axis=1, keepdims=True)


def normalize(hidden):
    center = hidden - row_mean(hidden)
    scale = lax.rsqrt(row_mean(center * center) + norm_epsilon)
    return center * scale, scale


def norm_derivative(normal, scale, cotangent, gain):
    scaled = cotangent * gain
    return scale * (scaled - row_mean(scaled) - normal * row_mean(scaled * normal))


def forward_kernel(
    slots_x,
    weights,
    bias_qkv,
    vectors,
    seg_col,
    seg_row,
    x,
    proj,
    probs,
    context,
    attn_res,
    qkv,
    out,
    packed,
    sem,
):
    heads, rows, part = slots_x.shape
    tokens, width = x.shape
    splits = width // part
    load = pltpu.make_async_copy(weights.at[:, :, 0 : packed.shape[2]], packed, sem.at[0])
    load.start()
    for source in range(heads):
        micro, which = source // splits, source % splits
        x[micro * rows : (micro + 1) * rows, which * part : (which + 1) * part] = slots_x[source]
    load.wait()
    assemble_attention(packed, qkv, out)
    project(x, qkv, bias_qkv, proj)
    attend(proj, probs, context, seg_col, seg_row)
    leave_attention(x, context, out, vectors, attn_res)


def project(x, qkv, bias_qkv, proj):
    @pl.loop(0, proj.shape[1] // 256, unroll=3)
    def _(tile):
        cols = pl.ds(pl.multiple_of(tile * 256, 256), 256)
        sums = jnp.dot(x[...], qkv[:, cols], preferred_element_type=F32)
        proj[:, cols] = (sums + bias_qkv[:, cols]).astype(BF16)


def two_heads(tile, first):
    zero = jnp.zeros_like(tile)
    return jnp.concatenate([jnp.where(first, tile, zero), jnp.where(first, zero, tile)], axis=0)


def attend(proj, probs, context, seg_col, seg_row):
    tokens, width = context.shape
    first = iota((CLUSTER, 128), 1) < HEAD_DIM

    @pl.loop(0, tokens // CLUSTER)
    def _(cluster):
        rows = pl.ds(pl.multiple_of(cluster * CLUSTER, CLUSTER), CLUSTER)
        column = seg_col[rows, 0:1]
        allowed = jnp.concatenate([column, column], axis=0) == seg_row[pl.ds(cluster, 1), :]
        for pair in range(width // 128):
            at = pair * 128
            q = two_heads(proj[rows, at : at + 128], first)
            k = proj[rows, width + at : width + at + 128]
            v = proj[rows, 2 * width + at : 2 * width + at + 128]
            scores = contract(q, k, (1, 1)) * 0.125
            scores = jnp.where(allowed, scores, masked_score)
            weight = jnp.exp(scores - jnp.max(scores, axis=1, keepdims=True))
            p = (weight / jnp.sum(weight, axis=1, keepdims=True)).astype(BF16)
            probs[cluster, pair] = p
            both = jnp.dot(p, v, preferred_element_type=F32)
            context[rows, at : at + 128] = jnp.where(
                first, both[:CLUSTER], both[CLUSTER:]
            ).astype(BF16)


def leave_attention(x, context, out, vectors, attn_res):
    @pl.loop(0, x.shape[1] // 256)
    def _(tile):
        cols = pl.ds(pl.multiple_of(tile * 256, 256), 256)
        sums = jnp.dot(context[...], out[:, cols], preferred_element_type=F32)
        attn_res[:, cols] = x[:, cols].astype(F32) + sums + vectors[2:3, cols]


def forward_part(slots_x, weights, bias_qkv, vectors, seg_col, seg_row):
    heads, rows, part = slots_x.shape
    width = weights.shape[1]
    tokens = heads * part * rows // width
    vmem = pl.BlockSpec(memory_space=pltpu.VMEM)
    return pl.pallas_call(
        forward_kernel,
        name="forward_part",
        out_shape=(
            jax.ShapeDtypeStruct((tokens, width), BF16),
            jax.ShapeDtypeStruct((tokens, 3 * width), BF16),
            jax.ShapeDtypeStruct((tokens // CLUSTER, width // 128, 2 * CLUSTER, CLUSTER), BF16),
            jax.ShapeDtypeStruct((tokens, width), BF16),
            jax.ShapeDtypeStruct((tokens, width), F32),
            jax.ShapeDtypeStruct((width, 3 * width), BF16),
            jax.ShapeDtypeStruct((width, width), BF16),
        ),
        in_specs=[vmem, pl.BlockSpec(memory_space=pl.ANY), vmem, vmem, vmem, vmem],
        out_specs=(vmem,) * 7,
        scratch_shapes=[
            pltpu.VMEM((heads, width, width), BF16),
            pltpu.SemaphoreType.DMA((1,)),
        ],
        compiler_params=pltpu.CompilerParams(vmem_limit_bytes=48 << 20),
    )(slots_x, weights, bias_qkv, vectors, seg_col, seg_row)


def ffn_kernel(
    share,
    attn_res,
    slots_g,
    weights,
    vectors,
    up_bias,
    layer_out,
    d_attn,
    g_attn,
    partial,
    vec_grads,
    up_bias_grad,
    packed,
    down,
    normed,
    hidden,
    hidden_t,
    active,
    slope,
    g_pre,
    ffn_res,
    g_down,
    sem,
):
    heads, rows, part = slots_g.shape
    tokens, width = attn_res.shape
    ff = active.shape[1]
    fold = ff // width
    short = width // heads
    splits = width // part
    load = pltpu.make_async_copy(weights.at[:, :, width : 3 * width], packed, sem.at[0])
    load.start()
    gain_attn, shift_attn = vectors[3:4, :], vectors[4:5, :]
    bias_down, gain_ffn, shift_ffn = vectors[5:6, :], vectors[6:7, :], vectors[7:8, :]
    vec_grads[...] = jnp.zeros_like(vec_grads)

    def row_tiles(body):
        @pl.loop(0, tokens // CLUSTER)
        def _(tile):
            body(tile, pl.ds(pl.multiple_of(tile * CLUSTER, CLUSTER), CLUSTER))

    def first_norm(tile, at):
        normal, _ = normalize(attn_res[at, :])
        values = normal * gain_attn + shift_attn
        normed[at, :] = values
        hidden[at, :] = values.astype(BF16)

    row_tiles(first_norm)
    hidden_t[...] = hidden[...].T
    load.wait()

    blks = width // share

    @pl.loop(0, blks)
    def _(blk):
        source = pl.ds(pl.multiple_of(blk * share, share), share)
        for j in range(fold):
            target = pl.ds(pl.multiple_of(blk * share * fold + j * share, share), share)
            for head in range(heads):
                down[target, head * short : (head + 1) * short] = packed[
                    head, source, width + j * short : width + (j + 1) * short
                ]

    per_head = width // 256

    @pl.loop(0, ff // 256)
    def _(tile):
        cols = pl.ds(pl.multiple_of(tile * 256, 256), 256)
        inner = pl.ds(pl.multiple_of(tile % per_head * 256, 256), 256)
        pre = jnp.dot(
            hidden[...], packed[tile // per_head, :, inner], preferred_element_type=F32
        )
        pre = pre + up_bias[:, cols]
        below = 0.5 + 0.5 * lax.erf(pre * (0.5**0.5))
        active[:, cols] = (pre * below).astype(BF16)
        slope[:, cols] = below + pre * jnp.exp(-0.5 * pre * pre) * (0.5 / jnp.pi) ** 0.5

    @pl.loop(0, width // 256)
    def _(tile):
        cols = pl.ds(pl.multiple_of(tile * 256, 256), 256)
        sums = jnp.dot(active[...], down[:, cols], preferred_element_type=F32)
        ffn_res[:, cols] = normed[:, cols] + sums + vectors[5:6, cols]

    def second_norm(tile, at):
        normal, scale = normalize(ffn_res[at, :])
        result = (normal * gain_ffn + shift_ffn).astype(BF16)
        micro = tile * CLUSTER // rows
        inner = pl.ds(pl.multiple_of(tile * CLUSTER % rows, CLUSTER), CLUSTER)
        for which in range(splits):
            layer_out[micro * splits + which, inner, :] = result[
                :, which * part : (which + 1) * part
            ]
        cotangent = jnp.concatenate(
            [slots_g[micro * splits + which, inner, :] for which in range(splits)], axis=1
        ).astype(F32)
        d_ffn = norm_derivative(normal, scale, cotangent, gain_ffn)
        low = d_ffn.astype(BF16)
        g_down[at, :] = low
        ffn_res[at, :] = d_ffn
        vec_grads[5:6, :] += column_sum(low.astype(F32))
        vec_grads[6:7, :] += column_sum(cotangent * normal)
        vec_grads[7:8, :] += column_sum(cotangent)

    row_tiles(second_norm)

    @pl.loop(0, ff // 256)
    def _(tile):
        cols = pl.ds(pl.multiple_of(tile * 256, 256), 256)
        inner = pl.ds(pl.multiple_of(tile % per_head * 256, 256), 256)
        d_active = contract(g_down[...], down[cols, :], (1, 1))
        low = (d_active * slope[:, cols]).astype(BF16)
        g_pre[:, cols] = low
        up_bias_grad[:, cols] = column_sum(low.astype(F32))
        up_grad = jnp.dot(hidden_t[...], low, preferred_element_type=F32)
        partial[tile // per_head, :, inner] = up_grad.astype(BF16)

    @pl.loop(0, blks)
    def _(blk):
        wide = share * fold
        cols = pl.ds(pl.multiple_of(blk * wide, wide), wide)
        down_grad = contract(active[:, cols], g_down[...], (0, 0)).astype(BF16)
        target = pl.ds(pl.multiple_of(blk * share, share), share)
        for j in range(fold):
            for head in range(heads):
                partial[head, target, width + j * short : width + (j + 1) * short] = down_grad[
                    j * share : (j + 1) * share, head * short : (head + 1) * short
                ]

    @pl.loop(0, width // 256)
    def _(tile):
        cols = pl.ds(pl.multiple_of(tile * 256, 256), 256)
        sums = ffn_res[:, cols]
        for head in range(heads):
            sums = sums + contract(
                g_pre[:, head * width : (head + 1) * width], packed[head, cols, 0:width], (1, 1)
            )
        normed[:, cols] = sums

    def first_norm_back(tile, at):
        normal, scale = normalize(attn_res[at, :])
        cotangent = normed[at, :]
        grad = norm_derivative(normal, scale, cotangent, gain_attn)
        low = grad.astype(BF16)
        d_attn[at, :] = grad
        g_attn[at, :] = low
        vec_grads[2:3, :] += column_sum(low.astype(F32))
        vec_grads[3:4, :] += column_sum(cotangent * normal)
        vec_grads[4:5, :] += column_sum(cotangent)

    row_tiles(first_norm_back)


def ffn_part(share, attn_res, slots_g, weights, vectors, up_bias):
    heads = weights.shape[0]
    tokens, width = attn_res.shape
    ff = up_bias.shape[1]
    vmem = pl.BlockSpec(memory_space=pltpu.VMEM)
    return pl.pallas_call(
        functools.partial(ffn_kernel, share),
        name="ffn_part",
        out_shape=(
            jax.ShapeDtypeStruct(slots_g.shape, BF16),
            jax.ShapeDtypeStruct((tokens, width), F32),
            jax.ShapeDtypeStruct((tokens, width), BF16),
            jax.ShapeDtypeStruct((heads, width, 2 * width), BF16),
            jax.ShapeDtypeStruct((8, width), F32),
            jax.ShapeDtypeStruct((1, ff), F32),
        ),
        in_specs=[vmem, vmem, pl.BlockSpec(memory_space=pl.ANY), vmem, vmem],
        out_specs=(vmem,) * 6,
        scratch_shapes=[
            pltpu.VMEM((heads, width, 2 * width), BF16),
            pltpu.VMEM((ff, width), BF16),
            pltpu.VMEM((tokens, width), F32),
            pltpu.VMEM((tokens, width), BF16),
            pltpu.VMEM((width, tokens), BF16),
            pltpu.VMEM((tokens, ff), BF16),
            pltpu.VMEM((tokens, ff), F32),
            pltpu.VMEM((tokens, ff), BF16),
            pltpu.VMEM((tokens, width), F32),
            pltpu.VMEM((tokens, width), BF16),
            pltpu.SemaphoreType.DMA((1,)),
        ],
        compiler_params=pltpu.CompilerParams(vmem_limit_bytes=60 << 20),
    )(attn_res, slots_g, weights, vectors, up_bias)


def attend_back(proj, probs, g_context, g_proj, begin=0, end=None):
    tokens, width = g_context.shape
    first = iota((CLUSTER, 128), 1) < HEAD_DIM

    @pl.loop(begin, tokens // CLUSTER if end is None else end)
    def _(cluster):
        rows = pl.ds(pl.multiple_of(cluster * CLUSTER, CLUSTER), CLUSTER)
        for pair in range(width // 128):
            at = pair * 128
            q = two_heads(proj[rows, at : at + 128], first)
            k = proj[rows, width + at : width + at + 128]
            v = proj[rows, 2 * width + at : 2 * width + at + 128]
            g = two_heads(g_context[rows, at : at + 128], first)
            low = probs[cluster, pair]
            p = low.astype(F32)
            dprob = contract(g, v, (1, 1))
            delta = jnp.sum(p * dprob, axis=1, keepdims=True)
            dscore = (p * (dprob - delta)).astype(BF16)
            both = jnp.dot(dscore, k, preferred_element_type=F32)
            g_q = jnp.where(first, both[:CLUSTER], both[CLUSTER:]) * 0.125
            g_k = contract(dscore, q, (0, 0)) * 0.125
            g_v = contract(low, g, (0, 0))
            g_proj[rows, at : at + 128] = g_q.astype(BF16)
            g_proj[rows, width + at : width + at + 128] = g_k.astype(BF16)
            g_proj[rows, 2 * width + at : 2 * width + at + 128] = g_v.astype(BF16)


def backward_kernel(
    x,
    proj,
    probs,
    context,
    qkv,
    out,
    d_attn,
    g_attn,
    x_grad,
    partial,
    vec_grads,
    g_context,
    g_proj,
    x_t,
    natural,
):
    heads, rows, part = x_grad.shape
    tokens, width = x.shape
    splits = width // part
    wide, narrow = 3 * width // heads, width // heads
    g_context[...] = contract(g_attn[...], out[...], (1, 1)).astype(BF16)
    x_t[...] = context[...].T

    def tiles(count, body):
        @pl.loop(0, count)
        def _(tile):
            body(pl.ds(pl.multiple_of(tile * 256, 256), 256))

    def out_grad(cols):
        natural[:, cols] = jnp.dot(
            x_t[...], g_attn[:, cols], preferred_element_type=F32
        ).astype(BF16)

    tiles(width // 256, out_grad)

    @pl.loop(0, width // CLUSTER)
    def _(tile):
        at = pl.ds(pl.multiple_of(tile * CLUSTER, CLUSTER), CLUSTER)
        for head in range(heads):
            partial[head, at, wide : wide + narrow] = natural[
                at, head * narrow : (head + 1) * narrow
            ]

    attend_back(proj, probs, g_context, g_proj)
    x_t[...] = x[...].T

    def qkv_grad(cols):
        natural[:, cols] = jnp.dot(
            x_t[...], g_proj[:, cols], preferred_element_type=F32
        ).astype(BF16)

    tiles(3 * width // 256, qkv_grad)

    @pl.loop(0, width // CLUSTER)
    def _(tile):
        at = pl.ds(pl.multiple_of(tile * CLUSTER, CLUSTER), CLUSTER)
        for head in range(heads):
            partial[head, at, 0:wide] = natural[at, head * wide : (head + 1) * wide]

    vec_grads[...] = jnp.zeros_like(vec_grads)
    vec_grads[0:1, :] = column_sum(g_proj[:, 0:width].astype(F32))
    vec_grads[1:2, :] = column_sum(g_proj[:, 2 * width :].astype(F32))
    for which in range(splits):
        for piece in range(part // 128):
            at = which * part + piece * 128
            sums = d_attn[:, at : at + 128] + contract(g_proj[...], qkv[at : at + 128, :], (1, 1))
            for micro in range(heads // splits):
                x_grad[micro * splits + which, :, piece * 128 : (piece + 1) * 128] = sums[
                    micro * rows : (micro + 1) * rows
                ].astype(BF16)


def backward_part(heads, rows, x, proj, probs, context, qkv, out, d_attn, g_attn):
    tokens, width = x.shape
    part = tokens * width // (heads * rows)
    vmem = pl.BlockSpec(memory_space=pltpu.VMEM)
    return pl.pallas_call(
        backward_kernel,
        name="backward_part",
        out_shape=(
            jax.ShapeDtypeStruct((heads, rows, part), BF16),
            jax.ShapeDtypeStruct((heads, width, width), BF16),
            jax.ShapeDtypeStruct((8, width), F32),
        ),
        in_specs=[vmem] * 8,
        out_specs=(vmem,) * 3,
        scratch_shapes=[
            pltpu.VMEM((tokens, width), BF16),
            pltpu.VMEM((tokens, 3 * width), BF16),
            pltpu.VMEM((width, tokens), BF16),
            pltpu.VMEM((width, 3 * width), BF16),
        ],
        compiler_params=pltpu.CompilerParams(vmem_limit_bytes=48 << 20),
    )(x, proj, probs, context, qkv, out, d_attn, g_attn)


def fused_scratch(micros, rows, width, blks, heads, share, fold):
    dma = pltpu.SemaphoreType.DMA
    vmem = pltpu.VMEM
    tokens = micros * rows
    part = width * micros // heads
    group = rows * heads
    ff = width * fold
    half = width // 2
    kept = blks // 2
    levels = blks.bit_length() - 1
    return dict(
        arrived=vmem((2, group, part), BF16),
        sorted_rows=vmem((2, group, part), BF16),
        landed=vmem((2, group, part), BF16),
        ordered=vmem((2, group, part), BF16),
        slots=vmem((2, heads, rows, part), BF16),
        dest_row=vmem((8, group), jnp.int32),
        slot_row=vmem((8, group), jnp.int32),
        dest_col=vmem((group, 128), jnp.int32),
        slot_col=vmem((group, 128), jnp.int32),
        ones=vmem((blks, group), F32),
        sums=vmem((blks, group), F32),
        rank_rows=vmem((blks, group), jnp.int32),
        seg_col=vmem((tokens, 128), F32),
        seg_row=vmem((8 * (-(-tokens // CLUSTER // 8)), CLUSTER), F32),
        perm=vmem((micros, blks, group), jnp.int32),
        shard=vmem((share, 3 * width), BF16),
        small_sums=vmem((16, 128), F32),
        small=vmem((16, 128), BF16),
        packed=vmem((heads, width, 3 * width), BF16),
        qkv=vmem((width, 3 * width), BF16),
        out=vmem((width, width), BF16),
        down=vmem((ff, width), BF16),
        full_vectors=vmem((blks, 16, 128), BF16),
        vectors=vmem((8, width), F32),
        bias_qkv=vmem((1, 3 * width), F32),
        up_bias=vmem((1, ff), F32),
        vec_grads=vmem((8, width), F32),
        up_bias_grad=vmem((1, ff), F32),
        x=vmem((tokens, width), BF16),
        proj=vmem((tokens, 3 * width), BF16),
        probs=vmem((tokens // CLUSTER, width // 128, 2 * CLUSTER, CLUSTER), BF16),
        context=vmem((tokens, width), BF16),
        attn_res=vmem((tokens, width), F32),
        normed=vmem((tokens, width), F32),
        hidden=vmem((tokens, width), BF16),
        turned=vmem((width, tokens), BF16),
        active=vmem((tokens, ff), BF16),
        slope=vmem((tokens, ff), BF16),
        ffn_res=vmem((tokens, width), F32),
        g_down=vmem((tokens, width), BF16),
        g_attn=vmem((tokens, width), BF16),
        staged=vmem((2, kept, share, width), BF16),
        from_tree=vmem((3, 2, heads, kept - 1, share, half), BF16),
        from_head=vmem((3, heads, share, width), BF16),
        vec_split=vmem((blks, 16, 128), F32),
        vec_parts=vmem((blks, 16, 128), F32),
        vec_mid=vmem((16, 128), F32),
        vec_heads=vmem((heads, 16, 128), F32),
        head_send=dma((4, 2)),
        head_recv=dma((4, 2)),
        blk_send=dma((4,)),
        blk_recv=dma((4,)),
        local=dma((4, 3)),
        z_send=dma((2, heads, 2)),
        z_recv=dma((2, heads)),
        tree_send=dma((2,)),
        tree_recv=dma((2, heads, 2, levels)),
        small_send=dma((3,)),
        small_recv=dma((3,)),
        own_sem=dma((2,)),
        core_send=dma((3,)),
        core_recv=dma((3, heads)),
        stage_sem=dma((2,)),
        down_send=dma((3,)),
        down_recv=dma((3, 2, heads, levels - 1)),
        pair_send=dma((3,)),
        pair_recv=dma((3, heads)),
        out_sem=dma((2, 3)),
    )


def fused_kernel(names, blks, heads, share, fold, *refs):
    r = types.SimpleNamespace(**dict(zip(names, refs)))
    blk, head = lax.axis_index("blk"), lax.axis_index("head")
    micros, rows, width = r.tokens.shape
    tokens = micros * rows
    splits = heads // micros
    part = width // splits
    group = rows * heads
    pair = group // blks
    ff = width * fold
    short = width // heads
    levels = blks.bit_length() - 1
    bits = bits_of(blk, levels)
    sends = Sends()
    sems = (r.head_send, r.head_recv, r.blk_send, r.blk_recv, r.local)
    exchanges = [RowExchange(sends, blk, head, blks, heads, sems, i) for i in range(4)]

    def tiles(count, size):
        def run(body):
            @pl.loop(0, count, unroll=2 if count % 2 == 0 else 1)
            def _(tile):
                body(tile, pl.ds(pl.multiple_of(tile * size, size), size))

        return run

    row_tiles = tiles(tokens // CLUSTER, CLUSTER)


    def head_block(ref, i):
        return lambda other: ref.at[i, pl.ds(pl.multiple_of(other * rows, rows), rows), :]

    def blk_block(ref, i):
        return lambda other: ref.at[i, pl.ds(pl.multiple_of(other * pair, pair), pair), :]

    def head_blocks(ref, i):
        return ref.at[i, 0 : group - rows, :]

    def blk_blocks(ref, i):
        return ref.at[i, 0 : group - pair, :]

    def row_source(ref):
        return lambda other: ref.at[
            other // splits, :, (other % splits) * part : (other % splits + 1) * part
        ]

    def own_rows(ref):
        return lambda other: ref.at[
            other // splits * rows : (other // splits + 1) * rows,
            (other % splits) * part : (other % splits + 1) * part,
        ]

    def to_heads(i, source):
        exchanges[i].over_head(0, source, head_block(r.arrived, i % 2), head_blocks(r.arrived, i % 2))

    def to_groups(i, one_hot):
        exchanges[i].wait_head(0, head_block(r.arrived, i % 2), head_blocks(r.arrived, i % 2))
        permute_rows(one_hot, r.arrived.at[i % 2], r.sorted_rows.at[i % 2], group)
        exchanges[i].over_blk(
            blk_block(r.sorted_rows, i % 2), blk_block(r.landed, i % 2), blk_blocks(r.landed, i % 2)
        )

    def to_owners(i, one_hot):
        exchanges[i].wait_blk(blk_block(r.landed, i % 2), blk_blocks(r.landed, i % 2))
        permute_rows(one_hot, r.landed.at[i % 2], r.ordered.at[i % 2], group)
        exchanges[i].over_head(
            1,
            head_block(r.ordered, i % 2),
            lambda other: r.slots.at[i % 2, other],
            r.slots.at[i % 2, 0 : heads - 1],
        )

    def rows_here(i):
        exchanges[i].wait_head(
            1, lambda other: r.slots.at[i % 2, other], r.slots.at[i % 2, 0 : heads - 1]
        )


    parts = ((0, width), (width, 2 * width))
    orders = [list(range(1, levels)) + [0], list(range(2, levels)) + [1, 0]]
    arrival = [
        choose(
            head,
            [
                sorted([x for x in range(heads) if x != own], key=lambda x: (abs(x - own), x))[j - 1]
                for own in range(heads)
            ],
        )
        if j
        else head
        for j in range(heads)
    ]

    def piece_rows(piece):
        return pl.ds(pl.multiple_of(piece * share, share), share)

    def part_cols(p, which=None):
        base, size = parts[p]
        if which is None:
            return slice(base, base + size)
        return slice(base + which * size // 2, base + (which + 1) * size // 2)

    def tree_wait(p, j, which, step):
        pieces = slice(0, share << step)
        await_bytes(
            r.packed.at[arrival[j], pieces, part_cols(p, which)], r.tree_recv.at[p, j, which, step]
        )

    def forwards(j):
        left = (arrival[j] > head) & (head > 0)
        right = (arrival[j] < head) & (head < heads - 1)
        return left, right

    def chain_wait(p, j):
        target = r.packed.at[arrival[j], piece_rows(blk), part_cols(p)]
        remote(
            target, target, r.z_send.at[p, 0, 0], r.z_recv.at[p, arrival[j]], (blk, head)
        ).wait_recv()

    def tree_step(p, j, step):
        if step == 0 and j:
            left, right = forwards(j)

            @pl.when(jnp.logical_not(left | right))
            def _():
                chain_wait(p, j)

        for which in range(2):
            dims = orders[which]
            if step:
                tree_wait(p, j, which, step - 1)
            if step == levels:
                continue
            other = flip(blk, 1 << dims[step], bits)
            sent = r.packed.at[:, 0 : (blks - 1) * share, part_cols(p)]
            for mask in submasks(dims[:step]):
                piece = flip(blk, mask, bits)
                target = r.packed.at[arrival[j], piece_rows(piece), part_cols(p, which)]
                first = j == 0 and mask == 0
                source = r.shard.at[:, part_cols(p, which)] if first else target
                sends.start(
                    lambda source=source, target=target, other=other, which=which: remote(
                        source,
                        target,
                        r.tree_send.at[p],
                        r.tree_recv.at[p, j, which, step],
                        (other, head),
                    ),
                    tag="weights",
                    shared=(p, lambda: await_bytes(sent, r.tree_send.at[p])),
                )

    def chain(p, j):
        target = r.packed.at[arrival[j], piece_rows(blk), part_cols(p)]
        if j == 0:
            source = r.shard.at[:, part_cols(p)]
            left, right = head > 0, head < heads - 1
        else:
            source = target
            left, right = forwards(j)

            @pl.when(left | right)
            def _():
                chain_wait(p, j)

        for side, (condition, step) in enumerate(((left, -1), (right, 1))):
            sends.start(
                lambda side=side, step=step: remote(
                    source,
                    target,
                    r.z_send.at[p, j, side],
                    r.z_recv.at[p, arrival[j]],
                    (blk, jnp.clip(head + step, 0, heads - 1)),
                ),
                when=condition,
                tag="weights",
            )

    def gain_copy(other, slot):
        return remote(
            r.small, r.full_vectors.at[slot], r.small_send.at[0], r.small_recv.at[0], (other, head)
        )


    order = []
    for i in range(heads):
        order.append(heads - 1 - i // 2 if i % 2 == 0 else i // 2)
    even = submasks(range(1, levels))
    down_orders = [list(range(levels - 1, 0, -1)), [1] + list(range(levels - 1, 1, -1))]
    sibling = flip(blk, 1, bits)

    def group_cols(g, which=None):
        if which is None:
            return slice(g * width, (g + 1) * width)
        return slice(g * width + which * width // 2, g * width + (which + 1) * width // 2)

    def total(g, other, mask, which=None):
        return r.packed.at[other, piece_rows(flip(blk, mask, bits)), group_cols(g, which)]

    def core_start(g):
        sent = r.packed.at[:, 0 : blks // 2 * share, group_cols(g)]
        for other in order:
            for mask in even:
                sends.start(
                    lambda other=other, mask=mask: remote(
                        total(g, other, mask | 1),
                        r.from_core.at[g, other, mask // 2],
                        r.core_send.at[g],
                        r.core_recv.at[g, other],
                        (sibling, head),
                    ),
                    shared=(("core", g), lambda: await_bytes(sent, r.core_send.at[g])),
                )

    def core_load(g, i):
        return pltpu.make_async_copy(
            r.from_core.at[g, order[i]], r.staged.at[i % 2], r.stage_sem.at[i % 2]
        )

    def core_arrived(g, i):
        await_bytes(r.from_core.at[g, order[i]], r.core_recv.at[g, order[i]])
        core_load(g, i).start()

    def core_add(g):
        core_arrived(g, 0)
        for i, other in enumerate(order):
            if i + 1 < heads:
                core_arrived(g, i + 1)
            core_load(g, i).wait()
            for mask in even:
                add_into(total(g, other, mask), r.staged.at[i % 2, mask // 2], width)
            tree_start(g, other, 0)

    def tree_slots(which, step):
        dims = down_orders[which]
        base = sum(1 << (levels - 2 - earlier) for earlier in range(step))
        return dims[step], [(mask, base + i) for i, mask in enumerate(submasks(dims[step + 1 :]))]

    def tree_start(g, other, step):
        sent = r.packed.at[:, 0 : (blks // 2 - 1) * share, group_cols(g)]
        for which in range(2):
            dim, slots = tree_slots(which, step)
            for mask, slot in slots:
                sends.start(
                    lambda which=which, dim=dim, mask=mask, slot=slot: remote(
                        total(g, other, mask | (1 << dim), which),
                        r.from_tree.at[g, which, other, slot],
                        r.down_send.at[g],
                        r.down_recv.at[g, which, other, step],
                        (flip(blk, 1 << dim, bits), head),
                    ),
                    shared=(("down", g), lambda: await_bytes(sent, r.down_send.at[g])),
                )

    def tree_add(g, other, step):
        for which in range(2):
            _, slots = tree_slots(which, step)
            first, count = slots[0][1], len(slots)
            await_bytes(
                r.from_tree.at[g, which, other, first : first + count],
                r.down_recv.at[g, which, other, step],
            )
            for mask, slot in slots:
                add_into(
                    total(g, other, mask, which), r.from_tree.at[g, which, other, slot], width // 2
                )
        if step < levels - 2:
            tree_start(g, other, step + 1)

    def tree_down(g, step):
        for other in order:
            tree_add(g, other, step)

    partner = head + 1 - 2 * (head % 2)
    others = range(1, heads // 2)

    def far(distance):
        return (head + 2 * distance) % heads

    def far_partner(distance):
        return (partner + 2 * distance) % heads

    def sum_copy(g, goal, slot, device):
        return remote(
            total(g, goal, 0),
            r.from_head.at[g, slot],
            r.pair_send.at[g],
            r.pair_recv.at[g, slot],
            (blk, device),
        )

    def sum_start(g, goal, slot, device, when=None):
        sent = r.packed.at[0, 0 : (heads - 1) * share, group_cols(g)]
        sends.start(
            lambda: sum_copy(g, goal, slot, device),
            when=when,
            shared=(("pair", g), lambda: await_bytes(sent, r.pair_send.at[g])),
        )

    def sum_add(g, goal, slot):
        await_bytes(r.from_head.at[g, slot], r.pair_recv.at[g, slot])
        add_into(total(g, goal, 0), r.from_head.at[g, slot], width)

    def direct_start(g):
        for goal in range(heads):
            sum_start(g, goal, head, goal, when=goal != head)

    def direct_add(g):
        for source in range(heads):

            @pl.when(source != head)
            def _():
                sum_add(g, head, source)

    def pair_start(g):
        sum_start(g, partner, 0, partner)
        for distance in others:
            sum_start(g, far_partner(distance), distance, partner)

    def pair_forward(g):
        for distance in others:
            sum_add(g, far(distance), distance)
            sum_start(g, far(distance), heads // 2 + distance, far(distance))

    def pair_add(g):
        sum_add(g, head, 0)
        for distance in others:
            sum_add(g, head, heads // 2 + distance)


    micro = head // splits

    def find_destinations():
        own_slots = r.perm[micro, pl.ds(blk, 1), :]
        r.ones[...] = jnp.where(iota((blks, group), 0) == own_slots // group, 1.0, 0.0)
        cumulative(r.ones, r.sums, group)
        rank = column_sum(r.ones[...] * r.sums[...]).astype(jnp.int32) - 1
        dest = own_slots // group * pair + rank
        r.dest_row[...] = jnp.broadcast_to(dest, r.dest_row.shape)
        for tile in range(group // 128):
            block = jnp.broadcast_to(dest[:, tile * 128 : (tile + 1) * 128].astype(F32), (128, 128))
            r.dest_col[tile * 128 : (tile + 1) * 128, :] = block.T.astype(jnp.int32)

    def find_slots():
        r.ones[...] = jnp.where(r.perm[micro] // group == blk, 1.0, 0.0)
        cumulative(r.ones, r.sums, group)
        r.rank_rows[...] = jnp.where(r.ones[...] > 0, r.sums[...] - 1, -1.0).astype(jnp.int32)

        @pl.loop(0, blks)
        def _(other):
            ranks = r.rank_rows[pl.ds(other, 1), :]
            inner = (r.perm[micro, pl.ds(other, 1), :] % group).astype(F32)
            found = jnp.where(iota((pair, group), 0) == ranks, inner, 0.0)
            column = jnp.sum(found, axis=1, keepdims=True).astype(jnp.int32)
            r.slot_col[pl.ds(pl.multiple_of(other * pair, pair), pair), :] = jnp.broadcast_to(
                column, (pair, 128)
            )

        for tile in range(group // 128):
            block = r.slot_col[tile * 128 : (tile + 1) * 128, :].astype(F32)
            r.slot_row[:, tile * 128 : (tile + 1) * 128] = block.T[0:8, :].astype(jnp.int32)

    def find_segments():
        first = blk * group + head * rows
        for m in range(micros):
            ends = []
            for s in range(r.seq_lengths.shape[1]):
                ends.append(r.seq_lengths[m, s] + (ends[-1] if ends else 0))
            for tile in range(rows // CLUSTER):
                slot = iota((CLUSTER, group), 0) + (first + tile * CLUSTER)

                def add(other, sums):
                    position = iota((1, group), 1) + other * group
                    segment = jnp.zeros((1, group), F32)
                    for end in ends:
                        segment = segment + jnp.where(position >= end, 1.0, 0.0)
                    here = r.perm[m, pl.ds(other, 1), :] == slot
                    found = jnp.where(here, segment, 0.0)
                    return sums + sum(
                        found[:, i * 128 : (i + 1) * 128] for i in range(group // 128)
                    )

                sums = lax.fori_loop(0, blks, add, jnp.zeros((CLUSTER, 128), F32))
                column = jnp.broadcast_to(
                    jnp.sum(sums, axis=1, keepdims=True), (CLUSTER, 128)
                )
                cluster = m * (rows // CLUSTER) + tile
                r.seg_col[cluster * CLUSTER : (cluster + 1) * CLUSTER, :] = column
                r.seg_row[cluster : cluster + 1, :] = column.T[0:1, :]

    def spread_vectors():
        for b in range(blks):
            small = r.full_vectors[b].astype(F32)
            r.vectors[:, b * share : (b + 1) * share] = small[0:8, 0:share]
            for j in range(fold):
                at = (b * fold + j) * share
                r.up_bias[:, at : at + share] = small[8 + j : 9 + j, 0:share]
        r.bias_qkv[:, 0:width] = r.vectors[0:1, :]
        r.bias_qkv[:, width : 2 * width] = jnp.zeros((1, width), F32)
        r.bias_qkv[:, 2 * width :] = r.vectors[1:2, :]


    def take_rows():
        for source in range(heads):
            m, which = source // splits, source % splits
            r.x[m * rows : (m + 1) * rows, which * part : (which + 1) * part] = r.slots[0, source]

    def assemble_down():
        @pl.loop(0, width // share)
        def _(b):
            source = piece_rows(b)
            for j in range(fold):
                at = b * share * fold + j * share
                target = pl.ds(pl.multiple_of(at, share), share)
                for h in range(heads):
                    base = 2 * width + j * short
                    r.down[target, h * short : (h + 1) * short] = r.packed[
                        h, source, base : base + short
                    ]

    per_head = width // 256

    def first_norm():
        @row_tiles
        def _(tile, at):
            normal, _ = normalize(r.attn_res[at, :])
            values = normal * r.vectors[3:4, :] + r.vectors[4:5, :]
            r.normed[at, :] = values
            r.hidden[at, :] = values.astype(BF16)

        r.turned[...] = r.hidden[...].T

    def ffn_up(h):
        @tiles(per_head, 256)
        def _(tile, inner):
            inner = pl.ds(pl.multiple_of(width + tile * 256, 256), 256)
            cols = pl.ds(pl.multiple_of(h * width + tile * 256, 256), 256)
            pre = jnp.dot(r.hidden[...], r.packed[h, :, inner], preferred_element_type=F32)
            pre = pre + r.up_bias[:, cols]
            below = 0.5 + 0.5 * lax.erf(pre * (0.5**0.5))
            r.active[:, cols] = (pre * below).astype(BF16)
            bell = jnp.exp(-0.5 * pre * pre) * (0.5 / jnp.pi) ** 0.5
            r.slope[:, cols] = (below + pre * bell).astype(BF16)

    def ffn_down():
        @tiles(width // 256, 256)
        def _(tile, cols):
            sums = jnp.dot(r.active[...], r.down[:, cols], preferred_element_type=F32)
            r.ffn_res[:, cols] = r.normed[:, cols] + sums + r.vectors[5:6, cols]

    def inner_rows(tile):
        return tile * CLUSTER // rows, pl.ds(pl.multiple_of(tile * CLUSTER % rows, CLUSTER), CLUSTER)

    def second_norm():
        @row_tiles
        def _(tile, at):
            normal, _ = normalize(r.ffn_res[at, :])
            result = (normal * r.vectors[6:7, :] + r.vectors[7:8, :]).astype(BF16)
            r.hidden[at, :] = result

    def second_norm_back():
        @row_tiles
        def _(tile, at):
            normal, scale = normalize(r.ffn_res[at, :])
            m, inner = inner_rows(tile)
            cotangent = jnp.concatenate(
                [r.slots[1, m * splits + which, inner, :] for which in range(splits)], axis=1
            ).astype(F32)
            d_ffn = norm_derivative(normal, scale, cotangent, r.vectors[6:7, :])
            low = d_ffn.astype(BF16)
            r.g_down[at, :] = low
            r.ffn_res[at, :] = d_ffn
            r.vec_grads[5:6, :] += column_sum(low.astype(F32))
            r.vec_grads[6:7, :] += column_sum(cotangent * normal)
            r.vec_grads[7:8, :] += column_sum(cotangent)

    def down_gradient():
        @pl.loop(0, width // share, unroll=2)
        def _(b):
            wide = share * fold
            cols = pl.ds(pl.multiple_of(b * wide, wide), wide)
            turned = r.active[:, cols].T
            target = piece_rows(b)
            for which in range(2):
                grad = jnp.dot(
                    turned,
                    r.g_down[:, which * width // 2 : (which + 1) * width // 2],
                    preferred_element_type=F32,
                ).astype(BF16)
                for j in range(fold):
                    for h in range(heads // 2):
                        base = 2 * width + j * short
                        r.packed[which * heads // 2 + h, target, base : base + short] = grad[
                            j * share : (j + 1) * share, h * short : (h + 1) * short
                        ]

    def ffn_up_back():
        @tiles(ff // 256, 256)
        def _(tile, cols):
            d_active = contract(r.g_down[...], r.down[cols, :], (1, 1))
            low = (d_active * r.slope[:, cols].astype(F32)).astype(BF16)
            r.slope[:, cols] = low
            r.up_bias_grad[:, cols] = column_sum(low.astype(F32))

    def norm_cotangent():
        @tiles(width // 256, 256)
        def _(tile, cols):
            sums = r.ffn_res[:, cols]
            for h in range(heads):
                sums = sums + contract(
                    r.slope[:, h * width : (h + 1) * width],
                    r.packed[h, cols, width : 2 * width],
                    (1, 1),
                )
            r.normed[:, cols] = sums

    def up_gradient():
        @tiles(ff // 256, 256)
        def _(tile, cols):
            inner = pl.ds(pl.multiple_of(width + tile % per_head * 256, 256), 256)
            grad = jnp.dot(r.turned[...], r.slope[:, cols], preferred_element_type=F32)
            r.packed[tile // per_head, :, inner] = grad.astype(BF16)

    def first_norm_back():
        @row_tiles
        def _(tile, at):
            normal, scale = normalize(r.attn_res[at, :])
            cotangent = r.normed[at, :]
            grad = norm_derivative(normal, scale, cotangent, r.vectors[3:4, :])
            low = grad.astype(BF16)
            r.attn_res[at, :] = grad
            r.g_attn[at, :] = low
            r.vec_grads[2:3, :] += column_sum(low.astype(F32))
            r.vec_grads[3:4, :] += column_sum(cotangent * normal)
            r.vec_grads[4:5, :] += column_sum(cotangent)

    g_context = r.g_down
    x_grad = r.g_down
    g_proj = r.active
    wide = 3 * width // heads

    def out_gradient():
        r.turned[...] = r.context[...].T
        for h in range(heads):
            grad = jnp.dot(
                r.turned[...],
                r.g_attn[:, h * short : (h + 1) * short],
                preferred_element_type=F32,
            )
            r.packed[h, :, wide : wide + short] = grad.astype(BF16)

    def context_cotangent():
        @tiles(width // 256, 256)
        def _(tile, cols):
            g_context[:, cols] = contract(r.g_attn[...], r.out[cols, :], (1, 1)).astype(BF16)

    def qkv_gradient():
        r.turned[...] = r.x[...].T

        @tiles(width // 256, 256)
        def _(tile, at):
            for h in range(heads):
                grad = jnp.dot(
                    r.turned[at, :], g_proj[:, h * wide : (h + 1) * wide], preferred_element_type=F32
                )
                r.packed[h, at, 0:wide] = grad.astype(BF16)

        r.vec_grads[0:1, :] = column_sum(g_proj[:, 0:width].astype(F32))
        r.vec_grads[1:2, :] = column_sum(g_proj[:, 2 * width : 3 * width].astype(F32))

    def row_gradient():
        for which in range(splits):
            for piece in range(part // 128):
                at = which * part + piece * 128
                sums = r.attn_res[:, at : at + 128] + contract(
                    g_proj[:, 0 : 3 * width], r.qkv[at : at + 128, :], (1, 1)
                )
                x_grad[:, at : at + 128] = sums.astype(BF16)


    def split_vectors():
        r.vec_split[...] = jnp.zeros_like(r.vec_split)
        for b in range(blks):
            r.vec_split[b, 0:8, 0:share] = r.vec_grads[:, b * share : (b + 1) * share]
            for j in range(fold):
                at = (b * fold + j) * share
                r.vec_split[b, 8 + j : 9 + j, 0:share] = r.up_bias_grad[:, at : at + share]

    def vec_copy(other, slot):
        return remote(
            r.vec_split.at[other],
            r.vec_parts.at[slot],
            r.small_send.at[1],
            r.small_recv.at[1],
            (other, head),
        )

    def vec_head_copy(other, slot):
        return remote(
            r.vec_mid,
            r.vec_heads.at[slot],
            r.small_send.at[2],
            r.small_recv.at[2],
            (blk, other),
        )

    def place_slots():
        for m in range(micros):
            for b in range(blks):
                r.perm[m, b : b + 1, :] = r.perm_rows[m : m + 1, b * group : (b + 1) * group]

    def pack_shard():
        at = 0
        for source in (r.qkv_weight, r.out_weight, r.up_weight):
            r.shard[:, at : at + source.shape[1]] = source[...]
            at += source.shape[1]
        turned = r.down_weight[...].T
        for j in range(fold):
            r.shard[:, at + j * short : at + (j + 1) * short] = turned[
                j * share : (j + 1) * share
            ]

    def pack_small():
        r.small_sums[...] = jnp.zeros_like(r.small_sums)
        for i in range(8):
            r.small_sums[i : i + 1, 0:share] = getattr(r, "vector%d" % i)[...].astype(F32)
        bias = r.up_bias_here[...].astype(F32)
        bias = jnp.concatenate([bias[i : i + 1] for i in range(bias.shape[0])], axis=1)
        for j in range(fold):
            r.small_sums[8 + j : 9 + j, 0:share] = bias[:, j * share : (j + 1) * share]
        r.small[...] = r.small_sums[...].astype(BF16)

    def send_small():
        sent = r.full_vectors.at[0 : blks - 1]
        for other in range(blks):
            sends.start(
                lambda other=other: gain_copy(other, blk),
                when=other != blk,
                shared=("gain", lambda: await_bytes(sent, r.small_send.at[0])),
            )
        own_gain.start()
        own_shard.start()

    def take_small():
        await_bytes(r.full_vectors.at[0 : blks - 1], r.small_recv.at[0])
        own_gain.wait()
        own_shard.wait()
        spread_vectors()

    def send_vectors():
        split_vectors()
        sent = r.vec_parts.at[0 : blks - 1]
        for other in range(blks):
            sends.start(
                lambda other=other: vec_copy(other, blk),
                when=other != blk,
                shared=("vec", lambda: await_bytes(sent, r.small_send.at[1])),
            )

    def sum_vectors_over_blk():
        await_bytes(r.vec_parts.at[0 : blks - 1], r.small_recv.at[1])
        r.vec_mid[...] = jnp.zeros_like(r.vec_mid)
        for other in range(blks):

            @pl.when(other != blk)
            def _():
                r.vec_mid[...] += r.vec_parts[other]

        r.vec_mid[...] += r.vec_split[pl.ds(blk, 1)][0]
        sent = r.vec_heads.at[0 : heads - 1]
        for other in range(heads):
            sends.start(
                lambda other=other: vec_head_copy(other, head),
                when=other != head,
                shared=("vec head", lambda: await_bytes(sent, r.small_send.at[2])),
            )

    def sum_vectors_over_head():
        await_bytes(r.vec_heads.at[0 : heads - 1], r.small_recv.at[2])
        r.vec_sum[...] = r.vec_mid[...]
        for other in range(heads):

            @pl.when(other != head)
            def _():
                r.vec_sum[...] += r.vec_heads[other]

    own_gain = pltpu.make_async_copy(r.small, r.full_vectors.at[blk], r.own_sem.at[0])
    own_shard = pltpu.make_async_copy(
        r.shard, r.packed.at[head, piece_rows(blk), :], r.own_sem.at[1]
    )

    def start_backward():
        r.vec_grads[...] = jnp.zeros_like(r.vec_grads)

    clusters = tokens // CLUSTER

    def attention_back(begin, end):
        attend_back(r.proj, r.probs, g_context, g_proj, begin, end)

    def row_copy(i):
        return pltpu.make_async_copy(r.slots.at[i], r.row_results.at[i], r.out_sem.at[0, i])

    def shard_copy(g):
        return pltpu.make_async_copy(
            r.packed.at[head, piece_rows(blk), group_cols(g)],
            r.shard_grad.at[:, group_cols(g)],
            r.out_sem.at[1, g],
        )

    def finish():
        for i in range(2):
            row_copy(i).wait()
        for g in range(3):
            shard_copy(g).wait()
        sends.finish()


    enter(blk, head, blks, heads)
    to_heads(0, row_source(r.tokens))
    pack_shard()
    chain(0, 0)
    tree_step(0, 0, 0)
    tree_step(1, 0, 0)
    pack_small()
    send_small()
    place_slots()
    find_destinations()
    tree_step(0, 0, 1)
    chain(1, 0)
    tree_step(1, 0, 1)
    find_slots()
    tree_step(0, 0, 2)
    tree_step(1, 0, 2)
    find_segments()
    chain(0, 1)
    to_groups(0, one_hot_from_row(r.dest_row))
    chain(0, 2)
    chain(1, 1)
    tree_step(0, 1, 0)
    chain(1, 2)
    tree_step(1, 1, 0)
    chain(0, 3)
    tree_step(0, 2, 0)
    tree_step(0, 1, 1)
    to_owners(0, one_hot_from_row(r.slot_row))
    chain(1, 3)
    tree_step(0, 3, 0)
    tree_step(1, 2, 0)
    tree_step(0, 2, 1)
    tree_step(0, 1, 2)
    to_heads(1, row_source(r.out_grad))
    tree_step(1, 1, 1)
    tree_step(0, 3, 1)
    tree_step(0, 2, 2)
    take_small()
    tree_step(1, 2, 1)
    tree_step(0, 3, 2)
    tree_step(1, 1, 2)
    tree_step(0, 0, 3)
    tree_step(0, 1, 3)
    tree_step(0, 2, 3)
    tree_step(0, 3, 3)
    assemble_attention(r.packed, r.qkv, r.out)
    tree_step(1, 2, 2)
    tree_step(1, 3, 0)
    rows_here(0)
    take_rows()
    project(r.x, r.qkv, r.bias_qkv, r.proj)
    to_groups(1, one_hot_from_row(r.dest_row))
    attend(r.proj, r.probs, r.context, r.seg_col, r.seg_row)
    tree_step(1, 3, 1)
    to_owners(1, one_hot_from_row(r.slot_row))
    tree_step(1, 3, 2)
    leave_attention(r.x, r.context, r.out, r.vectors, r.attn_res)
    first_norm()
    tree_step(1, 0, 3)
    ffn_up(arrival[0])
    tree_step(1, 1, 3)
    ffn_up(arrival[1])
    tree_step(1, 2, 3)
    ffn_up(arrival[2])
    tree_step(1, 3, 3)
    ffn_up(arrival[3])
    assemble_down()
    ffn_down()
    second_norm()
    to_heads(2, own_rows(r.hidden))
    start_backward()
    rows_here(1)
    second_norm_back()
    sends.finish("weights")
    down_gradient()
    core_start(2)
    ffn_up_back()
    norm_cotangent()
    sends.finish(0)
    to_groups(2, one_hot_from_column(r.slot_col, group))
    core_add(2)
    up_gradient()
    core_start(1)
    first_norm_back()
    context_cotangent()
    to_owners(2, one_hot_from_column(r.dest_col, group))
    attention_back(0, clusters // 2)
    core_add(1)
    attention_back(clusters // 2, clusters)
    tree_down(2, 0)
    row_gradient()
    to_heads(3, own_rows(x_grad))
    out_gradient()
    qkv_gradient()
    core_start(0)
    send_vectors()
    tree_down(2, 1)
    pair_start(2)
    tree_down(1, 0)
    sends.finish(1)
    to_groups(3, one_hot_from_column(r.slot_col, group))
    core_add(0)
    pair_forward(2)
    tree_down(1, 1)
    pair_start(1)
    sum_vectors_over_blk()
    to_owners(3, one_hot_from_column(r.dest_col, group))
    pair_forward(1)
    tree_down(0, 0)
    sum_vectors_over_head()
    pair_add(2)
    shard_copy(2).start()
    tree_down(0, 1)
    direct_start(0)
    rows_here(2)
    row_copy(0).start()
    pair_add(1)
    shard_copy(1).start()
    direct_add(0)
    shard_copy(0).start()
    rows_here(3)
    row_copy(1).start()
    finish()


def fused(blks, heads, fold, tokens, out_grad, weights, vectors, up_bias, perm, seq_lengths):
    micros, rows, width = tokens.shape
    share = weights[0].shape[0]
    part = width * micros // heads
    scratch = fused_scratch(micros, rows, width, blks, heads, share, fold)
    any_space, vmem = pl.BlockSpec(memory_space=pl.ANY), pl.BlockSpec(memory_space=pltpu.VMEM)
    names = ["tokens", "out_grad", "qkv_weight", "out_weight", "up_weight", "down_weight"]
    names += ["vector%d" % i for i in range(8)] + ["up_bias_here", "perm_rows", "seq_lengths"]
    names += ["row_results", "shard_grad", "vec_sum", "from_core"]
    names += list(scratch)
    return pl.pallas_call(
        functools.partial(fused_kernel, names, blks, heads, share, fold),
        name="fused",
        out_shape=(
            jax.ShapeDtypeStruct((2, heads, rows, part), BF16),
            jax.ShapeDtypeStruct((share, 3 * width), BF16),
            jax.ShapeDtypeStruct((16, 128), F32),
            jax.ShapeDtypeStruct((3, heads, blks // 2, share, width), BF16),
        ),
        in_specs=[any_space] * 2 + [vmem] * 14 + [pl.BlockSpec(memory_space=pltpu.SMEM)],
        out_specs=(any_space, any_space, vmem, any_space),
        scratch_shapes=list(scratch.values()),
        compiler_params=pltpu.CompilerParams(
            collective_id=2, has_side_effects=True, vmem_limit_bytes=64 << 20
        ),
    )(
        tokens,
        out_grad,
        *weights[:3],
        weights[3].T,
        *[vector.reshape(1, -1) for vector in vectors],
        up_bias.reshape(-1, 128 if up_bias.shape[0] % 128 == 0 else up_bias.shape[0]),
        perm,
        seq_lengths,
    )[:3]


def unpack_kernel(
    rows_in, shard_in, sums_in, layer_out, x_grad, qkv, out, up, down, up_bias, *rest
):
    vectors, (row_results, shard, sums, sem) = rest[:8], rest[8:]
    micros, rows, width = layer_out.shape
    copies = [
        pltpu.make_async_copy(source, target, sem.at[i])
        for i, (source, target) in enumerate(
            ((sums_in, sums), (shard_in, shard), (rows_in, row_results))
        )
    ]
    for copy in copies:
        copy.start()
    _, heads, _, part = row_results.shape
    splits = heads // micros
    share, short = out.shape
    fold = down.shape[1] // share
    copies[0].wait()
    for i, vector in enumerate(vectors):
        vector[...] = sums[i : i + 1, 0:share]
    bias = jnp.concatenate([sums[8 + j : 9 + j, 0:share] for j in range(fold)], axis=1)
    lanes = up_bias.shape[1]
    for i in range(up_bias.shape[0]):
        up_bias[i : i + 1, :] = bias[:, i * lanes : (i + 1) * lanes]
    copies[1].wait()
    at = 0
    for target in (qkv, out, up):
        target[...] = shard[:, at : at + target.shape[1]].astype(F32)
        at += target.shape[1]
    pieces = [
        shard[:, at + j * short : at + (j + 1) * short].astype(F32) for j in range(fold)
    ]
    down[...] = jnp.concatenate(pieces, axis=0).T
    copies[2].wait()
    for source in range(heads):
        m, which = source // splits, source % splits
        cols = slice(which * part, (which + 1) * part)
        layer_out[m, :, cols] = row_results[0, source]
        x_grad[m, :, cols] = row_results[1, source].astype(F32)


def unpack(micros, width, widths, row_results, shard, sums):
    _, heads, rows, part = row_results.shape
    share = shard.shape[0]
    vmem = pl.BlockSpec(memory_space=pltpu.VMEM)
    shapes = [(share, widths[0]), (share, widths[1]), (share, widths[2])]
    long = widths[3] // widths[1] * share
    lanes = 128 if long % 128 == 0 else long
    shapes += [(widths[1], long), (long // lanes, lanes)]
    shapes += [(1, share)] * 8
    results = pl.pallas_call(
        unpack_kernel,
        name="unpack",
        out_shape=(
            jax.ShapeDtypeStruct((micros, rows, width), BF16),
            jax.ShapeDtypeStruct((micros, rows, width), F32),
        )
        + tuple(jax.ShapeDtypeStruct(shape, F32) for shape in shapes),
        in_specs=[pl.BlockSpec(memory_space=pltpu.HBM)] * 3,
        out_specs=(vmem,) * (2 + len(shapes)),
        scratch_shapes=[
            pltpu.VMEM(row_results.shape, BF16),
            pltpu.VMEM(shard.shape, BF16),
            pltpu.VMEM(sums.shape, F32),
            pltpu.SemaphoreType.DMA((3,)),
        ],
        compiler_params=pltpu.CompilerParams(vmem_limit_bytes=62 << 20),
    )(row_results, shard, sums)
    layer_out, x_grad, qkv, out, up, down, up_bias = results[:7]
    vec = [member.reshape(-1) for member in results[7:]]
    return (
        layer_out,
        x_grad,
        qkv,
        vec[0],
        vec[1],
        out,
        vec[2],
        vec[3],
        vec[4],
        up,
        up_bias.reshape(-1),
        down.T,
        vec[5],
        vec[6],
        vec[7],
    )


def refold(packed, share, other, fold):
    if share == other:
        return packed
    heads, width, wide = packed.shape
    short = wide // fold
    rows = packed.reshape(heads, width // share, share, fold, short).transpose(0, 1, 3, 2, 4)
    rows = rows.reshape(heads, width // other, fold, other, short).transpose(0, 1, 3, 2, 4)
    return rows.reshape(packed.shape)


def body(
    tokens,
    seq_lengths,
    cluster_perm,
    out_grad,
    qkv_weight,
    query_bias,
    value_bias,
    out_weight,
    out_bias,
    attn_gain,
    attn_shift,
    up_weight,
    up_bias,
    down_weight,
    down_bias,
    ffn_gain,
    ffn_shift,
):
    blks, heads = lax.axis_size("blk"), lax.axis_size("head")
    blk, head = lax.axis_index("blk"), lax.axis_index("head")
    micros, rows, width = tokens.shape
    group = rows * heads
    total_rows = cluster_perm.shape[1]
    share = qkv_weight.shape[0]
    folds = down_weight.shape[0] // share
    short = down_weight.shape[1]
    widths = [qkv_weight.shape[1], out_weight.shape[1], up_weight.shape[1], folds * short]
    edges = [sum(widths[:i]) for i in range(5)]

    small = [
        query_bias,
        value_bias,
        out_bias,
        attn_gain,
        attn_shift,
        down_bias,
        ffn_gain,
        ffn_shift,
    ]
    if share % 16 == 0:
        results = fused(
            blks,
            heads,
            folds,
            tokens,
            out_grad,
            (qkv_weight, out_weight, up_weight, down_weight),
            small,
            up_bias,
            cluster_perm,
            seq_lengths,
        )
        return unpack(micros, width, widths, *results)

    shard = jnp.concatenate(
        [qkv_weight, out_weight, up_weight]
        + [down_weight[i * share : (i + 1) * share] for i in range(folds)],
        axis=1,
    )
    lanes = -(-share // 128) * 128
    stacked = jnp.concatenate([jnp.stack(small), up_bias.reshape(folds, share)], axis=0)
    count = stacked.shape[0]
    vectors = jnp.pad(stacked, ((0, -count % 16), (0, lanes - share)))
    perm = cluster_perm.reshape(micros, blks, group)
    full, full_vectors, slots_x, slots_g, dest_col, slot_col = gather_all(
        blks, heads, tokens, out_grad, shard, vectors, perm
    )

    first = blk * group + head * rows
    slots = first + jnp.arange(rows, dtype=jnp.int32)
    ends = jnp.cumsum(seq_lengths, axis=1)
    positions = jnp.arange(total_rows, dtype=jnp.int32)
    segs = jnp.sum((positions[None, :, None] >= ends[:, None, :]).astype(jnp.int32), axis=2)
    slot_segs = jnp.sum(
        jnp.where(cluster_perm[:, None, :] == slots[None, :, None], segs[:, None, :], 0), axis=2
    )

    weights = full.reshape(heads, blks * share, -1)
    tall = share if share % 16 == 0 else width // 8
    if tall != share:
        weights = jnp.concatenate(
            [weights[:, :, : edges[3]], refold(weights[:, :, edges[3] :], share, tall, folds)],
            axis=2,
        )
    spread = full_vectors[:, :count, :share].astype(F32)
    vecs = spread[:, :8].transpose(1, 0, 2).reshape(8, width)
    up_vec = spread[:, 8:count].reshape(1, -1)
    bias_qkv = jnp.concatenate([vecs[0:1], jnp.zeros((1, width), F32), vecs[1:2]], axis=1)
    seg_col = jnp.broadcast_to(slot_segs.reshape(-1, 1), (micros * rows, 128))
    seg_row = slot_segs.reshape(-1, CLUSTER)
    x, proj, probs, context, attn_res, qkv, out = forward_part(
        slots_x, weights, bias_qkv, vecs, seg_col, seg_row
    )
    layer_out, d_attn, g_attn, partial_ffn, vec_ffn, up_vec_grad = ffn_part(
        tall, attn_res, slots_g, weights, vecs, up_vec
    )
    x_grad, partial_attn, vec_attn = backward_part(
        heads, rows, x, proj, probs, context, qkv, out, d_attn, g_attn
    )
    if tall != share:
        partial_ffn = jnp.concatenate(
            [partial_ffn[:, :, :width], refold(partial_ffn[:, :, width:], tall, share, folds)],
            axis=2,
        )
    partial = jnp.concatenate([partial_attn, partial_ffn], axis=2).reshape(full.shape)
    vec_grads = vec_ffn + vec_attn
    vec_parts = jnp.concatenate(
        [vec_grads.reshape(8, blks, share).transpose(1, 0, 2), up_vec_grad.reshape(blks, folds, share)],
        axis=1,
    )
    vec_parts = jnp.pad(vec_parts, ((0, 0), (0, -count % 16), (0, lanes - share)))
    out_rows, grad_rows, shard_grad, vec_sum = reduce_all(
        blks, heads, layer_out, x_grad, partial, vec_parts, dest_col, slot_col
    )
    down_grad = shard_grad[:, edges[3] : edges[4]]
    down_grad = jnp.concatenate(
        [down_grad[:, i * short : (i + 1) * short] for i in range(folds)], axis=0
    )
    vec = [vec_sum[i, :share] for i in range(8)]
    return (
        out_rows,
        grad_rows,
        shard_grad[:, edges[0] : edges[1]],
        vec[0],
        vec[1],
        shard_grad[:, edges[1] : edges[2]],
        vec[2],
        vec[3],
        vec[4],
        shard_grad[:, edges[2] : edges[3]],
        vec_sum[8:count, :share].reshape(-1),
        down_grad,
        vec[5],
        vec[6],
        vec[7],
    )


def solution(mesh):
    return jax.shard_map(
        body,
        mesh=mesh,
        in_specs=(
            P(None, ("blk", "head"), None),
            P(),
            P(),
            P(None, ("blk", "head"), None),
            P("blk", "head"),
            P("blk"),
            P("blk"),
            P("blk", "head"),
            P("blk"),
            P("blk"),
            P("blk"),
            P("blk", "head"),
            P("blk"),
            P("blk", "head"),
            P("blk"),
            P("blk"),
            P("blk"),
        ),
        out_specs=(
            P(None, ("blk", "head"), None),
            P(None, ("blk", "head"), None),
            P("blk", "head"),
            P("blk"),
            P("blk"),
            P("blk", "head"),
            P("blk"),
            P("blk"),
            P("blk"),
            P("blk", "head"),
            P("blk"),
            P("blk", "head"),
            P("blk"),
            P("blk"),
            P("blk"),
        ),
        check_vma=False,
    )
```
